32 devices in a mesh: ulysses: 2 (over y), blk: 16 (over z, x, core).
Axes of the slice: x: 2, y: 2, z: 4, core: 2. Of those that a mesh axis runs over, the one named last changes fastest.
Arguments:
- tokens: bfloat16 [4096, 768], P(('ulysses', 'blk')), may hold values from -6 to 6
- condition: float32 [128], replicated, may hold values from -6 to 6
- ada_weight: bfloat16 [128, 4608], P(None, ('ulysses', 'blk')), may hold values from -0.25 to 0.25
- ada_bias: bfloat16 [4608], P(('ulysses', 'blk')), may hold values from -3 to 3
- first_gain: bfloat16 [768], P(('ulysses', 'blk')), may hold values from 0.099609375 to 1.8984375
- second_gain: bfloat16 [768], P(('ulysses', 'blk')), may hold values from 0.099609375 to 1.8984375
- project_weight: bfloat16 [768, 2304], P(None, ('ulysses', 'blk')), may hold values from -0.21875 to 0.21875
- output_weight: bfloat16 [768, 768], P(('ulysses', 'blk')), may hold values from -4 to 4
- expand_weight: bfloat16 [768, 3072], P(None, ('ulysses', 'blk')), may hold values from -0.21875 to 0.21875
- expand_bias: bfloat16 [3072], P(('ulysses', 'blk')), may hold values from -3 to 3
- reduce_weight: bfloat16 [3072, 768], P(('ulysses', 'blk')), may hold values from -0.109375 to 0.109375
- reduce_bias: bfloat16 [768], P(('ulysses', 'blk')), may hold values from -1.75 to 1.75
- cotangent: bfloat16 [4096, 768], P(('ulysses', 'blk')), may hold values from -6 to 6
Outputs:
- result: bfloat16 [4096, 768], P(('ulysses', 'blk'))
- grad_tokens: float32 [4096, 768], P(('ulysses', 'blk'))
- grad_condition: float32 [128], replicated
- grad_ada_weight: float32 [128, 4608], P(None, ('ulysses', 'blk'))
- grad_ada_bias: float32 [4608], P(('ulysses', 'blk'))
- grad_first_gain: float32 [768], P(('ulysses', 'blk'))
- grad_second_gain: float32 [768], P(('ulysses', 'blk'))
- grad_project_weight: float32 [768, 2304], P(None, ('ulysses', 'blk'))
- grad_output_weight: float32 [768, 768], P(('ulysses', 'blk'))
- grad_expand_weight: float32 [768, 3072], P(None, ('ulysses', 'blk'))
- grad_expand_bias: float32 [3072], P(('ulysses', 'blk'))
- grad_reduce_weight: float32 [3072, 768], P(('ulysses', 'blk'))
- grad_reduce_bias: float32 [768], P(('ulysses', 'blk'))
The draws below stay inside these ranges and needn't reach their ends.
All inputs are finite; a program needn't handle non-finite values.
Results may differ from the reference program's by a relative error of at most 0.025.
Values may be sent and summed in bfloat16 or wider, within the bound.
A program may use at most 320 MiB of HBM per device.

```python
import math
import jax
import jax.numpy as jnp
from jax import lax

D = 768
HEAD_DIM = 64
FF = 3072
COND = 128
SEQS = 2
SEQLEN = 2048
TOKENS = 4096


def shard_levels(key, dims, shards, smallest, high):
    level, own = 1.0, jax.random.fold_in(key, 6)
    for position, parts in shards:
        steps = jnp.exp(jax.random.uniform(jax.random.fold_in(own, position), (parts,), jnp.float32, smallest / len(shards), high / len(shards)))
        level = level * jnp.repeat(steps, dims[position] // parts).reshape([-1 if axis == position else 1 for axis in range(len(dims))])
    return level


def centred(rng, dims, width, limit, cuts=(), kind=jnp.bfloat16):
    gain = shard_levels(rng, dims, cuts, -0.22, 0.18) if cuts else 1.0
    values = jax.random.normal(rng, dims, jnp.float32) * width * gain
    return jnp.minimum(jnp.maximum(values, -limit), limit).astype(kind)


def setup_inputs(seed: int = 0) -> dict:
    keys = jax.random.split(jax.random.key(seed), 14)
    tokens = centred(keys[0], (TOKENS, D), 1.0, 6.0, ((0, 32),))
    condition = centred(keys[1], (COND,), 1.0, 6.0, (), jnp.float32)
    ada_weight = centred(keys[2], (COND, 6 * D), (4 * COND) ** -0.5, 0.25, ((1, 32),))
    ada_bias = centred(keys[3], (6 * D,), 0.5, 3.0, ((0, 32),))
    first_gain = jnp.clip(1.0 + 0.18 * jax.random.normal(keys[4], (D,), jnp.float32), 0.099609375, 1.8984375).astype(jnp.bfloat16)
    second_gain = jnp.clip(1.0 + 0.18 * jax.random.normal(keys[5], (D,), jnp.float32), 0.099609375, 1.8984375).astype(jnp.bfloat16)
    project_weight = centred(keys[6], (D, 3 * D), D ** -0.5, 0.21875, ((1, 32),))
    output_weight = centred(keys[7], (D, D), (0.4 * SEQLEN ** 0.5 * D ** -0.5), 4.0, ((0, 32),))
    expand_weight = centred(keys[8], (D, FF), D ** -0.5, 0.21875, ((1, 32),))
    expand_bias = centred(keys[9], (FF,), 0.5, 3.0, ((0, 32),))
    reduce_weight = centred(keys[10], (FF, D), FF ** -0.5, 0.109375, ((0, 32),))
    reduce_bias = centred(keys[11], (D,), 0.3, 1.75, ((0, 32),))
    cotangent = centred(keys[12], (TOKENS, D), 1.0, 6.0, ((0, 32),))
    return dict(tokens=tokens, condition=condition, ada_weight=ada_weight, ada_bias=ada_bias, first_gain=first_gain, second_gain=second_gain, project_weight=project_weight, output_weight=output_weight, expand_weight=expand_weight, expand_bias=expand_bias, reduce_weight=reduce_weight, reduce_bias=reduce_bias, cotangent=cotangent)


@jax.custom_vjp
def low(v):
    return lax.optimization_barrier(v.astype(jnp.bfloat16)).astype(jnp.float32)

@jax.custom_vjp
def low_back(v):
    return v

def low_keep(v):
    return (low(v), None)

def low_pass(kept, grad):
    return (grad,)

def back_keep(v):
    return (v, None)

def back_low(kept, grad):
    return (low(grad),)
low.defvjp(low_keep, low_pass)
low_back.defvjp(back_keep, back_low)
eps = 1e-05
highest = lax.Precision.HIGHEST

def round_pair(value):
    return low_back(low(value))

def layer_norm(value):
    center = value - lax.optimization_barrier(jnp.mean(value, axis=-1, keepdims=True))
    spread = lax.optimization_barrier(jnp.mean(center * center, axis=-1, keepdims=True))
    return center * lax.rsqrt(spread + eps)

def rotary_tables(positions, head_dim):
    half_dim = head_dim // 2
    frequency = jnp.exp(jnp.arange(half_dim, dtype=jnp.float32) * (-2.0 * math.log(10000.0) / head_dim))
    angles = positions[:, None] * frequency[None, :]
    return (jnp.cos(angles)[:, None, :], jnp.sin(angles)[:, None, :])

def rotate(value, cosine, sine):
    half_dim = value.shape[-1] // 2
    first = value[..., :half_dim]
    second = value[..., half_dim:]
    return jnp.concatenate([first * cosine - second * sine, second * cosine + first * sine], axis=-1)

def attend_sequence(query_rot, key_rot, value_heads):
    seq_len = query_rot.shape[0]
    head_count = query_rot.shape[1]
    query_block = math.gcd(seq_len, 256)
    query_blocks = query_rot.reshape(seq_len // query_block, query_block, head_count, HEAD_DIM)

    def attend(block_rows):
        scores = low_back(jnp.einsum('qhd,khd->hqk', block_rows, key_rot, precision=highest) * HEAD_DIM ** (-0.5))
        maximum = lax.optimization_barrier(jnp.max(scores, axis=-1, keepdims=True))
        weights = jnp.exp(scores - maximum)
        shares = weights / lax.optimization_barrier(jnp.sum(weights, axis=-1, keepdims=True))
        return jnp.einsum('hqk,khd->qhd', low(shares), value_heads, precision=highest)
    return lax.map(jax.checkpoint(attend), query_blocks).reshape(seq_len, head_count * HEAD_DIM)

def forward(tokens, condition, ada_weight, ada_bias, first_gain, second_gain, project_weight, output_weight, expand_weight, expand_bias, reduce_weight, reduce_bias):
    length = tokens.shape[0]
    model_width = tokens.shape[1]
    head_count = model_width // HEAD_DIM
    seq_len = length // SEQS
    modulation = jnp.dot(condition, ada_weight, precision=highest) + ada_bias
    shift_one, scale_one, gate_one, shift_two, scale_two, gate_two = jnp.split(modulation, 6)
    mixed_one = low(layer_norm(tokens) * first_gain * (1.0 + scale_one) + shift_one)
    projected = jnp.dot(mixed_one, project_weight, precision=highest)
    query_raw = round_pair(projected[:, :model_width]).reshape(SEQS, seq_len, head_count, HEAD_DIM)
    key_raw = round_pair(projected[:, model_width:2 * model_width]).reshape(SEQS, seq_len, head_count, HEAD_DIM)
    value_raw = round_pair(projected[:, 2 * model_width:]).reshape(SEQS, seq_len, head_count, HEAD_DIM)
    cosine, sine = rotary_tables(jnp.arange(seq_len, dtype=jnp.float32), HEAD_DIM)
    pieces = []
    for index in range(SEQS):
        query_rot = low(rotate(query_raw[index], cosine, sine))
        key_rot = low(rotate(key_raw[index], cosine, sine))
        pieces.append(attend_sequence(query_rot, key_rot, value_raw[index]))
    attended = round_pair(jnp.concatenate(pieces, axis=0))
    attn_branch = low_back(jnp.dot(attended, output_weight, precision=highest))
    middle = tokens + gate_one * attn_branch
    mixed_two = low(layer_norm(middle) * second_gain * (1.0 + scale_two) + shift_two)
    hidden = low_back(jnp.dot(mixed_two, expand_weight, precision=highest) + expand_bias)
    activated = low(jax.nn.gelu(hidden, approximate=True))
    mlp_branch = low_back(jnp.dot(activated, reduce_weight, precision=highest) + reduce_bias)
    return middle + gate_two * mlp_branch

def reference(tokens, condition, ada_weight, ada_bias, first_gain, second_gain, project_weight, output_weight, expand_weight, expand_bias, reduce_weight, reduce_bias, cotangent):
    result, pullback = jax.vjp(forward, tokens.astype(jnp.float32), condition.astype(jnp.float32), ada_weight.astype(jnp.float32), ada_bias.astype(jnp.float32), first_gain.astype(jnp.float32), second_gain.astype(jnp.float32), project_weight.astype(jnp.float32), output_weight.astype(jnp.float32), expand_weight.astype(jnp.float32), expand_bias.astype(jnp.float32), reduce_weight.astype(jnp.float32), reduce_bias.astype(jnp.float32))
    grads_all = pullback(cotangent.astype(jnp.float32))
    return (result.astype(jnp.bfloat16), grads_all[0], grads_all[1], grads_all[2], grads_all[3], grads_all[4], grads_all[5], grads_all[6], grads_all[7], grads_all[8], grads_all[9], grads_all[10], grads_all[11])
```

```python
from functools import partial
import math

import jax
import jax.numpy as jnp
import numpy as np
from jax import lax
from jax.experimental import pallas as pl
from jax.experimental.pallas import tpu as pltpu
from jax.sharding import PartitionSpec as P

HEAD_DIM = 64


eps = 1e-05
highest = lax.Precision.HIGHEST


def layer_norm(value):
    center = value - jnp.mean(value, axis=-1, keepdims=True)
    inverse = lax.rsqrt(jnp.mean(center * center, axis=-1, keepdims=True) + eps)
    return (center * inverse, inverse)


def norm_back(grad_normed, normed, inverse):
    first = jnp.mean(grad_normed, axis=-1, keepdims=True)
    second = jnp.mean(grad_normed * normed, axis=-1, keepdims=True)
    return inverse * (grad_normed - first - normed * second)


def rotary_tables(positions, head_dim):
    half_dim = head_dim // 2
    frequency = jnp.exp(
        jnp.arange(half_dim, dtype=jnp.float32) * (-2.0 * math.log(10000.0) / head_dim)
    )
    angles = positions[:, None] * frequency[None, :]
    return (jnp.cos(angles)[:, None, :], jnp.sin(angles)[:, None, :])


def rotate(value, cosine, sine):
    half_dim = value.shape[-1] // 2
    first = value[..., :half_dim]
    second = value[..., half_dim:]
    return jnp.concatenate(
        [first * cosine - second * sine, second * cosine + first * sine], axis=-1
    )


def rotate_back(grad_value, cosine, sine):
    half_dim = grad_value.shape[-1] // 2
    first = grad_value[..., :half_dim]
    second = grad_value[..., half_dim:]
    return jnp.concatenate(
        [first * cosine + second * sine, second * cosine - first * sine], axis=-1
    )


def over_blocks(block_step, carried, pieces, key_block):
    length = pieces[0].shape[1]
    complete = length // key_block
    stacked = tuple(
        (
            jnp.moveaxis(
                member.reshape((member.shape[0], complete, key_block) + member.shape[2:]), 1, 0
            )
            for member in pieces
        )
    )
    offsets = jnp.arange(complete, dtype=jnp.int32) * key_block

    def scan_step(carried_in, inputs):
        return (block_step(carried_in, inputs[:-1], inputs[-1]), None)

    carried, unused = lax.scan(scan_step, carried, stacked + (offsets,))
    return carried


def on_device(
    tokens,
    condition,
    ada_weight,
    ada_bias,
    first_gain,
    second_gain,
    project_weight,
    output_weight,
    expand_weight,
    expand_bias,
    reduce_weight,
    reduce_bias,
    cotangent,
):
    row_count = tokens.shape[0]
    model_width = tokens.shape[1]
    cycle_size = lax.axis_size("blk")
    cycle_place = lax.axis_index("blk")
    seq_count = lax.axis_size("ulysses")
    (
        ada_full,
        ada_shift,
        gain_one,
        gain_two,
        project_full,
        output_full,
        expand_full,
        expand_shift,
        reduce_full,
        reduce_shift,
    ) = (
        lax.all_gather(ada_weight, ("ulysses", "blk"), axis=1, tiled=True),
        lax.all_gather(ada_bias, ("ulysses", "blk"), axis=0, tiled=True),
        lax.all_gather(first_gain, ("ulysses", "blk"), axis=0, tiled=True),
        lax.all_gather(second_gain, ("ulysses", "blk"), axis=0, tiled=True),
        lax.all_gather(project_weight, ("ulysses", "blk"), axis=1, tiled=True),
        lax.all_gather(output_weight, ("ulysses", "blk"), axis=0, tiled=True),
        lax.all_gather(expand_weight, ("ulysses", "blk"), axis=1, tiled=True),
        lax.all_gather(expand_bias, ("ulysses", "blk"), axis=0, tiled=True),
        lax.all_gather(reduce_weight, ("ulysses", "blk"), axis=0, tiled=True),
        lax.all_gather(reduce_bias, ("ulysses", "blk"), axis=0, tiled=True),
    )
    ada_float = ada_full.astype(jnp.float32)
    modulation = jnp.dot(condition, ada_float, precision=highest) + ada_shift.astype(jnp.float32)
    shift_one, scale_one, gate_one, shift_two, scale_two, gate_two = jnp.split(modulation, 6)
    gain_one_f = gain_one.astype(jnp.float32)
    gain_two_f = gain_two.astype(jnp.float32)
    inputs = tokens.astype(jnp.float32)
    normed_one, inverse_one = layer_norm(inputs)
    gain_first = gain_one_f * (1.0 + scale_one)
    mixed_one = (normed_one * gain_first + shift_one).astype(jnp.bfloat16)
    projected = jnp.dot(mixed_one, project_full, preferred_element_type=jnp.float32)
    packed = projected.astype(jnp.bfloat16).reshape(row_count, 3, model_width)
    regrouped = lax.all_to_all(packed, "ulysses", split_axis=2, concat_axis=0, tiled=True)
    local_rows = regrouped.shape[0]
    local_width = regrouped.shape[2]
    head_count = local_width // HEAD_DIM
    by_seq = regrouped.reshape(seq_count, row_count, 3, local_width)
    positions = cycle_place * row_count + jnp.arange(row_count, dtype=jnp.int32)
    cosine, sine = rotary_tables(positions.astype(jnp.float32), HEAD_DIM)
    query_rot = rotate(
        by_seq[:, :, 0].astype(jnp.float32).reshape(seq_count, row_count, head_count, HEAD_DIM),
        cosine,
        sine,
    ).astype(jnp.bfloat16)
    key_rot = rotate(
        by_seq[:, :, 1].astype(jnp.float32).reshape(seq_count, row_count, head_count, HEAD_DIM),
        cosine,
        sine,
    ).astype(jnp.bfloat16)
    value_flat = by_seq[:, :, 2]
    value_own = value_flat.reshape(seq_count, row_count, head_count, HEAD_DIM)
    key_flat = key_rot.reshape(seq_count, row_count, local_width)
    score_scale = HEAD_DIM ** (-0.5)
    key_block = row_count * -(-512 // row_count)

    def attend_step(carried, pieces, offset):
        maximum, denominator, weighted = carried
        key_rows = pieces[0].reshape(seq_count, -1, head_count, HEAD_DIM)
        value_rows = pieces[1].reshape(seq_count, -1, head_count, HEAD_DIM)
        scores = (
            jnp.einsum("sqhd,skhd->shqk", query_rot, key_rows, preferred_element_type=jnp.float32)
            * score_scale
        )
        new_maximum = jnp.maximum(maximum, jnp.max(scores, axis=-1))
        weights = jnp.exp(scores - new_maximum[..., None])
        factor = jnp.exp(maximum - new_maximum)
        denominator = denominator * factor + jnp.sum(weights, axis=-1)
        weighted = weighted * jnp.transpose(factor, (0, 2, 1))[..., None] + jnp.einsum(
            "shqk,skhd->sqhd",
            weights.astype(jnp.bfloat16),
            value_rows,
            preferred_element_type=jnp.float32,
        )
        return (new_maximum, denominator, weighted)

    start_state = (
        jnp.full((seq_count, head_count, row_count), -1e30, jnp.float32),
        jnp.zeros((seq_count, head_count, row_count), jnp.float32),
        jnp.zeros((seq_count, row_count, head_count, HEAD_DIM), jnp.float32),
    )
    maximum, denominator, weighted = over_blocks(
        attend_step,
        start_state,
        (
            lax.all_gather(key_flat, "blk", axis=1, tiled=True),
            lax.all_gather(value_flat, "blk", axis=1, tiled=True),
        ),
        key_block,
    )
    log_total = maximum + jnp.log(denominator)
    attended = (
        (weighted / jnp.transpose(denominator, (0, 2, 1))[..., None])
        .astype(jnp.bfloat16)
        .reshape(local_rows, local_width)
    )
    attended_tokens = lax.all_to_all(attended, "ulysses", split_axis=0, concat_axis=1, tiled=True)
    attn_branch = jnp.dot(attended_tokens, output_full, preferred_element_type=jnp.float32)
    middle = inputs + gate_one * attn_branch
    normed_two, inverse_two = layer_norm(middle)
    gain_second = gain_two_f * (1.0 + scale_two)
    mixed_two = (normed_two * gain_second + shift_two).astype(jnp.bfloat16)
    hidden = jnp.dot(
        mixed_two, expand_full, preferred_element_type=jnp.float32
    ) + expand_shift.astype(jnp.float32)
    activated, gelu_back = jax.vjp(partial(jax.nn.gelu, approximate=True), hidden)
    activated_low = activated.astype(jnp.bfloat16)
    mlp_branch = jnp.dot(
        activated_low, reduce_full, preferred_element_type=jnp.float32
    ) + reduce_shift.astype(jnp.float32)
    result = (middle + gate_two * mlp_branch).astype(jnp.bfloat16)
    grad_result = cotangent.astype(jnp.float32)
    grad_gate_two = jnp.sum(grad_result * mlp_branch, axis=0)
    grad_branch = (gate_two * grad_result).astype(jnp.bfloat16)
    grad_reduce = jnp.einsum(
        "tf,td->fd", activated_low, grad_branch, preferred_element_type=jnp.float32
    )
    grad_reduce_shift = jnp.sum(grad_branch.astype(jnp.float32), axis=0)
    grad_activated = jnp.einsum(
        "td,fd->tf", grad_branch, reduce_full, preferred_element_type=jnp.float32
    )
    grad_hidden = gelu_back(grad_activated)[0].astype(jnp.bfloat16)
    grad_expand = jnp.einsum(
        "td,tf->df", mixed_two, grad_hidden, preferred_element_type=jnp.float32
    )
    grad_expand_shift = jnp.sum(grad_hidden.astype(jnp.float32), axis=0)
    grad_mixed_two = jnp.einsum(
        "tf,df->td", grad_hidden, expand_full, preferred_element_type=jnp.float32
    )
    grad_shift_two = jnp.sum(grad_mixed_two, axis=0)
    grad_scale_two = jnp.sum(grad_mixed_two * normed_two * gain_two_f, axis=0)
    grad_gain_two = jnp.sum(grad_mixed_two * normed_two * (1.0 + scale_two), axis=0)
    grad_middle = grad_result + norm_back(grad_mixed_two * gain_second, normed_two, inverse_two)
    grad_gate_one = jnp.sum(grad_middle * attn_branch, axis=0)
    grad_attn = (gate_one * grad_middle).astype(jnp.bfloat16)
    grad_output = jnp.einsum(
        "tc,td->cd", attended_tokens, grad_attn, preferred_element_type=jnp.float32
    )
    grad_heads = jnp.einsum(
        "td,cd->tc", grad_attn, output_full, preferred_element_type=jnp.float32
    ).astype(jnp.bfloat16)
    grad_local = lax.all_to_all(grad_heads, "ulysses", split_axis=1, concat_axis=0, tiled=True)
    grad_local_heads = grad_local.reshape(seq_count, row_count, head_count, HEAD_DIM)
    row_dots = jnp.sum(
        (grad_local.astype(jnp.float32) * attended.astype(jnp.float32)).reshape(
            seq_count, row_count, head_count, HEAD_DIM
        ),
        axis=-1,
    )
    row_dots_t = jnp.transpose(row_dots, (0, 2, 1))

    def query_step(carried, pieces, offset):
        key_rows = pieces[0].reshape(seq_count, -1, head_count, HEAD_DIM)
        value_rows = pieces[1].reshape(seq_count, -1, head_count, HEAD_DIM)
        scores = (
            jnp.einsum("sqhd,skhd->shqk", query_rot, key_rows, preferred_element_type=jnp.float32)
            * score_scale
        )
        shares = jnp.exp(scores - log_total[..., None])
        grad_shares = jnp.einsum(
            "sqhd,skhd->shqk", grad_local_heads, value_rows, preferred_element_type=jnp.float32
        )
        grad_scores = (shares * (grad_shares - row_dots_t[..., None])).astype(jnp.bfloat16)
        return (
            carried
            + jnp.einsum(
                "shqk,skhd->sqhd", grad_scores, key_rows, preferred_element_type=jnp.float32
            )
            * score_scale
        )

    grad_query_rot = over_blocks(
        query_step,
        jnp.zeros((seq_count, row_count, head_count, HEAD_DIM), jnp.float32),
        (
            lax.all_gather(key_flat, "blk", axis=1, tiled=True),
            lax.all_gather(value_flat, "blk", axis=1, tiled=True),
        ),
        key_block,
    )

    def key_step(carried, pieces, offset):
        grad_keys_acc, grad_values_acc = carried
        query_rows = pieces[0].reshape(seq_count, -1, head_count, HEAD_DIM)
        slope_rows = pieces[1].reshape(seq_count, -1, head_count, HEAD_DIM)
        scores = (
            jnp.einsum("sqhd,skhd->shqk", query_rows, key_rot, preferred_element_type=jnp.float32)
            * score_scale
        )
        shares = jnp.exp(scores - jnp.transpose(pieces[2], (0, 2, 1))[..., None])
        grad_values_acc = grad_values_acc + jnp.einsum(
            "shqk,sqhd->skhd",
            shares.astype(jnp.bfloat16),
            slope_rows,
            preferred_element_type=jnp.float32,
        )
        grad_shares = jnp.einsum(
            "sqhd,skhd->shqk", slope_rows, value_own, preferred_element_type=jnp.float32
        )
        grad_scores = (
            shares * (grad_shares - jnp.transpose(pieces[3], (0, 2, 1))[..., None])
        ).astype(jnp.bfloat16)
        grad_keys_acc = (
            grad_keys_acc
            + jnp.einsum(
                "shqk,sqhd->skhd", grad_scores, query_rows, preferred_element_type=jnp.float32
            )
            * score_scale
        )
        return (grad_keys_acc, grad_values_acc)

    query_wide = query_rot.reshape(seq_count, row_count, local_width)
    slope_wide = grad_local.reshape(seq_count, row_count, local_width)
    key_init = (
        jnp.zeros((seq_count, row_count, head_count, HEAD_DIM), jnp.float32),
        jnp.zeros((seq_count, row_count, head_count, HEAD_DIM), jnp.float32),
    )
    grad_key_rot, grad_value_sum = over_blocks(
        key_step,
        key_init,
        (
            lax.all_gather(query_wide.astype(jnp.float32), "blk", axis=1, tiled=True).astype(
                jnp.bfloat16
            ),
            lax.all_gather(slope_wide.astype(jnp.float32), "blk", axis=1, tiled=True).astype(
                jnp.bfloat16
            ),
            lax.all_gather(jnp.transpose(log_total, (0, 2, 1)), "blk", axis=1, tiled=True),
            lax.all_gather(row_dots, "blk", axis=1, tiled=True),
        ),
        key_block,
    )
    grad_query = (
        rotate_back(grad_query_rot, cosine, sine)
        .astype(jnp.bfloat16)
        .reshape(local_rows, local_width)
    )
    grad_key = (
        rotate_back(grad_key_rot, cosine, sine)
        .astype(jnp.bfloat16)
        .reshape(local_rows, local_width)
    )
    grad_value = grad_value_sum.astype(jnp.bfloat16).reshape(local_rows, local_width)
    grad_packed = jnp.stack([grad_query, grad_key, grad_value], axis=1)
    grad_tokens_qkv = lax.all_to_all(
        grad_packed, "ulysses", split_axis=0, concat_axis=2, tiled=True
    ).reshape(row_count, 3 * model_width)
    grad_project = jnp.einsum(
        "tc,tk->ck", mixed_one, grad_tokens_qkv, preferred_element_type=jnp.float32
    )
    grad_mixed_one = jnp.einsum(
        "tk,ck->tc", grad_tokens_qkv, project_full, preferred_element_type=jnp.float32
    )
    grad_shift_one = jnp.sum(grad_mixed_one, axis=0)
    grad_scale_one = jnp.sum(grad_mixed_one * normed_one * gain_one_f, axis=0)
    grad_gain_one = jnp.sum(grad_mixed_one * normed_one * (1.0 + scale_one), axis=0)
    grad_input = grad_middle + norm_back(grad_mixed_one * gain_first, normed_one, inverse_one)
    mod_terms = jnp.concatenate(
        [
            grad_shift_one,
            grad_scale_one,
            grad_gate_one,
            grad_shift_two,
            grad_scale_two,
            grad_gate_two,
        ]
    )
    grad_modulation = lax.psum(mod_terms, ("ulysses", "blk"))
    grad_condition = jnp.dot(ada_float, grad_modulation, precision=highest)
    piece_width = ada_weight.shape[1]
    flat_index = lax.axis_index("ulysses") * cycle_size + cycle_place
    mod_piece = lax.dynamic_slice_in_dim(grad_modulation, flat_index * piece_width, piece_width, 0)
    grad_ada = condition[:, None] * mod_piece[None, :]
    shards = (
        lax.psum_scatter(grad_gain_one, ("ulysses", "blk"), scatter_dimension=0, tiled=True),
        lax.psum_scatter(grad_gain_two, ("ulysses", "blk"), scatter_dimension=0, tiled=True),
        lax.psum_scatter(grad_project, ("ulysses", "blk"), scatter_dimension=1, tiled=True),
        lax.psum_scatter(grad_output, ("ulysses", "blk"), scatter_dimension=0, tiled=True),
        lax.psum_scatter(grad_expand, ("ulysses", "blk"), scatter_dimension=1, tiled=True),
        lax.psum_scatter(grad_expand_shift, ("ulysses", "blk"), scatter_dimension=0, tiled=True),
        lax.psum_scatter(grad_reduce, ("ulysses", "blk"), scatter_dimension=0, tiled=True),
        lax.psum_scatter(grad_reduce_shift, ("ulysses", "blk"), scatter_dimension=0, tiled=True),
    )
    return (
        result,
        grad_input,
        grad_condition,
        grad_ada,
        mod_piece,
        shards[0],
        shards[1],
        shards[2],
        shards[3],
        shards[4],
        shards[5],
        shards[6],
        shards[7],
    )


MESH = pl.DeviceIdType.MESH
Y, ZH, ZL, X, C = 16, 8, 4, 2, 1
TP = (0, X, ZL, X + ZL)
DP = (0, C, Y, Y + C, ZH, ZH + C, ZH + Y, ZH + Y + C)
BLK = 128
f32 = jnp.float32
bf16 = jnp.bfloat16


def place():
    blk = lax.axis_index("blk")
    return (lax.axis_index("ulysses"), blk // 8, (blk // 4) % 2, (blk // 2) % 2, blk % 2)


def flip(offset):
    return tuple(
        1 - bit if (offset // weight) % 2 else bit
        for bit, weight in zip(place(), (Y, ZH, ZL, X, C))
    )


def peer(offset):
    y, zh, zl, x, c = flip(offset)
    return (y, zh * 8 + zl * 4 + x * 2 + c)


def peer_loop(offset):
    y, zh, zl, x, c = (
        (bit + (offset // weight) % 2) % 2 for bit, weight in zip(place(), (Y, ZH, ZL, X, C))
    )
    return (y, zh * 8 + zl * 4 + x * 2 + c)


def flat(device):
    return device[0] * 16 + device[1]


def share(offset):
    y, zh, zl, x, c = flip(offset)
    return zh * 4 + y * 2 + c


def enter(offsets):
    barrier = pltpu.get_barrier_semaphore()
    for offset in offsets:
        pl.semaphore_signal(barrier, inc=1, device_id=peer(offset), device_id_type=MESH)
    pl.semaphore_wait(barrier, len(offsets))


def remote(source, target, send_sem, recv_sem, offset):
    return pltpu.make_async_remote_copy(
        src_ref=source,
        dst_ref=target,
        send_sem=send_sem,
        recv_sem=recv_sem,
        device_id=peer(offset),
        device_id_type=MESH,
    )


def dot_nn(a, b):
    return jnp.dot(a, b, preferred_element_type=f32)


def dot_nt(a, b):
    return lax.dot_general(a, b, (((1,), (1,)), ((), ())), preferred_element_type=f32)


def dot_tn(a, b):
    return lax.dot_general(a, b, (((0,), (0,)), ((), ())), preferred_element_type=f32)


class Gather:
    def __init__(self, buffer, send_sem, recv_sem):
        self.buffer, self.send_sem, self.recv_sem = buffer, send_sem, recv_sem
        self.sent = []

    def send(self, have, to):
        slot = self.buffer.at[share(have)]
        index = len(self.sent)
        copy = remote(
            slot, slot, self.send_sem.at[index], self.recv_sem.at[DP.index(have + to)], to
        )
        copy.start()
        self.sent.append(copy)

    def arrive(self, what):
        slot = self.buffer.at[share(what)]
        remote(
            slot, slot, self.send_sem.at[0], self.recv_sem.at[DP.index(what)], C
        ).wait_recv()

    def first(self):
        self.send(0, ZH)
        self.send(0, Y)
        self.send(0, C)

    def second(self):
        self.arrive(ZH)
        self.send(ZH, Y)
        self.send(ZH, C)

    def third(self):
        self.arrive(Y)
        self.send(Y, C)
        self.arrive(ZH + Y)
        self.send(ZH + Y, C)

    def last(self):
        for what in (C, Y + C, ZH + C, ZH + Y + C):
            self.arrive(what)
        for copy in self.sent:
            copy.wait_send()


def turn(value, cosine, sine):
    lane = lax.broadcasted_iota(jnp.int32, value.shape, 1)
    swapped = jnp.where(
        lane < HEAD_DIM // 2,
        pltpu.roll(value, BLK - HEAD_DIM // 2, 1),
        pltpu.roll(value, HEAD_DIM // 2, 1),
    )
    return value * cosine + swapped * sine


def head_rows(first, count, low):
    for row in range(first, first + count, 8):
        yield row - first, (row // HEAD_DIM) * BLK + row % HEAD_DIM + (0 if low else HEAD_DIM)


def forward_kernel(
    tokens_ref, cotangent_ref, condition_ref, ada_ref, rows_ref, chunk_ref, mlp_e_ref, mlp_r_ref,
    cos_hbm, sin_hbm,
    mods_ref, attn_ref, mixed_ref, query_ref, kv_ref, att_ref, logt_ref, weight_ref,
    cot_ref, expand_ref, reduce_ref, cos_ref, sin_ref,
    vec_own, vecs, chunks, tok, mod_row, gain_rows, state_m, state_l, acc, part_send, part_recv,
    vec_ss, vec_rs, chunk_ss, chunk_rs, local_sem, tok_ss, tok_rs, cot_ss, cot_rs,
    a_ss, a_rs, e_ss, e_rs, r_ss, r_rs, kv_ss, kv_rs, part_ss, part_rs,
):
    rows = tokens_ref.shape[0]
    width = tokens_ref.shape[1]
    heads = query_ref.shape[1] // BLK
    me = flat(peer(0))
    tables = []
    for slot in range(4):
        start = pl.multiple_of(peer(TP[slot])[1] * rows, rows)
        for which, (source, target) in enumerate(((cos_hbm, cos_ref), (sin_hbm, sin_ref))):
            copy = pltpu.make_async_copy(
                source.at[pl.ds(start, rows)],
                target.at[pl.ds(slot * rows, rows)],
                local_sem.at[4 + slot * 2 + which],
            )
            copy.start()
            tables.append(copy)
    piece = jnp.sum(condition_ref[...] * ada_ref[...].astype(f32), axis=0, keepdims=True)
    vec_own[...] = rows_ref[...]
    vec_own[0:1, 0 : ada_ref.shape[1]] += piece
    mod_shift = (me % 8) * 16
    gain_shift = ((3 * me) % 16) * 8
    vec_own[0:8, :] = pltpu.roll(vec_own[0:8, :], mod_shift, 1)
    vec_own[8:16, :] = pltpu.roll(vec_own[8:16, :], gain_shift, 1)
    vec_own[16:24, :] = pltpu.roll(vec_own[16:24, :], gain_shift, 1)
    vec_own[24:32, :] = pltpu.roll(vec_own[24:32, :], gain_shift, 1)
    for index in range(1, 4):
        vec_own[index : index + 1, :] = vec_own[8 * index : 8 * index + 1, :]
    vecs[me] = vec_own[0:8, :]
    tok[0] = tokens_ref[...]
    cot_ref[0] = cotangent_ref[...]
    own = share(0)
    expand_ref[own] = mlp_e_ref[...]
    reduce_ref[own] = mlp_r_ref[...]

    enter(range(1, 32))

    targets = []
    for index in range(4):
        if index < 3:
            number = 3 * me + index
            part, place_in = number // 32, number % 32
        else:
            part, place_in = 3, me
        rank, slot = place_in // 8, place_in % 8
        device = (
            (slot // 2) % 2,
            (slot // 4) * 8 + (rank // 2) * 4 + (rank % 2) * 2 + slot % 2,
        )
        targets.append((part, slot, device, flat(device) == me))

    def chunk_copies(index):
        part, slot, device, stays = targets[index]
        far = pltpu.make_async_remote_copy(
            src_ref=chunk_ref.at[index],
            dst_ref=chunks.at[slot, part],
            send_sem=chunk_ss.at[index],
            recv_sem=chunk_rs.at[index],
            device_id=device,
            device_id_type=MESH,
        )
        near = pltpu.make_async_copy(
            chunk_ref.at[index], chunks.at[slot, part], local_sem.at[index]
        )
        return far, near, stays

    for index in range(4):
        far, near, stays = chunk_copies(index)

        @pl.when(jnp.logical_not(stays))
        def _():
            far.start()

        @pl.when(stays)
        def _():
            near.start()

    def vec_copy(offset):
        return pltpu.make_async_remote_copy(
            src_ref=vecs.at[me],
            dst_ref=vecs.at[me],
            send_sem=vec_ss.at[offset],
            recv_sem=vec_rs.at[offset],
            device_id=peer_loop(offset),
            device_id_type=MESH,
        )

    @pl.loop(1, 32)
    def _(offset):
        vec_copy(offset).start()

    token_copies = [
        remote(tok.at[0], tok.at[slot], tok_ss.at[slot], tok_rs.at[slot], TP[slot])
        for slot in range(1, 4)
    ]
    for copy in token_copies:
        copy.start()

    for index in range(4):
        far, near, stays = chunk_copies(index)

        @pl.when(jnp.logical_not(stays))
        def _():
            far.wait()

        @pl.when(stays)
        def _():
            near.wait()

    gather_a = Gather(chunks, a_ss, a_rs)
    gather_e = Gather(expand_ref, e_ss, e_rs)
    gather_r = Gather(reduce_ref, r_ss, r_rs)
    gather_a.first()

    @pl.loop(1, 32)
    def _(offset):
        other = flat(peer_loop(offset))
        copy = pltpu.make_async_remote_copy(
            src_ref=vecs.at[other],
            dst_ref=vecs.at[other],
            send_sem=vec_ss.at[offset],
            recv_sem=vec_rs.at[offset],
            device_id=peer_loop(offset),
            device_id_type=MESH,
        )
        copy.wait()

    mod_row[...] = jnp.zeros_like(mod_row)
    gain_rows[...] = jnp.zeros_like(gain_rows)
    for index in range(32):
        tile = (9 * index) // 8 * BLK
        mod_row[0:1, tile : tile + 2 * BLK] += vecs[index, 0:1, :]
        tile = (3 * index) // 16 * BLK
        gain_rows[0:8, tile : tile + 2 * BLK] += vecs[index]
    for index in range(6):
        mods_ref[index : index + 1, :] = mod_row[0:1, index * width : (index + 1) * width]
    for index in range(3):
        mods_ref[6 + index : 7 + index, :] = gain_rows[index + 1 : index + 2, 0:width]
    mods_ref[9:16, :] = jnp.zeros((7, width), f32)

    shift_one = mods_ref[0:1, :]
    gain_first = mods_ref[6:7, :] * (1.0 + mods_ref[1:2, :])
    gather_a.second()
    for slot in range(4):
        if slot:
            token_copies[slot - 1].wait()
        normed, _unused = layer_norm(tok[slot].astype(f32))
        mixed_ref[slot * rows : (slot + 1) * rows, :] = (normed * gain_first + shift_one).astype(
            bf16
        )
    gather_a.third()
    cot_copies = [
        remote(cot_ref.at[0], cot_ref.at[slot], cot_ss.at[slot], cot_rs.at[slot], TP[slot])
        for slot in range(1, 4)
    ]
    for copy in cot_copies:
        copy.start()
    gather_e.first()
    gather_r.first()
    gather_a.last()
    zero = jnp.zeros((HEAD_DIM, width), bf16)
    half = heads * BLK
    for head in range(heads):
        weight_ref[head * BLK + HEAD_DIM : (head + 1) * BLK, :] = zero
        weight_ref[2 * half + head * BLK : 2 * half + head * BLK + HEAD_DIM, :] = zero
    count = chunks.shape[2]
    for slot in range(8):
        for part, base, low in ((0, 0, True), (1, half, True), (2, half, False), (3, 2 * half, False)):
            for row, target in head_rows(slot * count, count, low):
                weight_ref[base + target : base + target + 8, :] = chunks[slot, part, row : row + 8, :]

    for copy in tables:
        copy.wait()

    @pl.loop(0, 4)
    def _(slot):
        here = pl.ds(pl.multiple_of(slot * rows, rows), rows)
        mixed = mixed_ref[here, :]
        cosine, sine = cos_ref[here, :], sin_ref[here, :]
        for head in range(heads):
            lanes = slice(head * BLK, (head + 1) * BLK)
            query = dot_nt(mixed, weight_ref[lanes, :]).astype(bf16).astype(f32)
            query_ref[here, lanes] = (
                turn(query, cosine, sine).astype(bf16).astype(f32) * (HEAD_DIM ** (-0.5))
            ).astype(bf16)
            both = dot_nt(mixed, weight_ref[half + head * BLK : half + (head + 1) * BLK, :])
            kv_ref[0, here, lanes] = turn(both.astype(bf16).astype(f32), cosine, sine).astype(bf16)

    kv_copies = [
        remote(kv_ref.at[0], kv_ref.at[2], kv_ss.at[0], kv_rs.at[2], ZH),
        remote(kv_ref.at[0], kv_ref.at[1], kv_ss.at[1], kv_rs.at[1], C),
    ]
    for copy in kv_copies:
        copy.start()

    state_m[...] = jnp.full_like(state_m, -1e30)
    state_l[...] = jnp.zeros_like(state_l)
    acc[...] = jnp.zeros_like(acc)

    def attend(slot):
        @pl.loop(0, heads)
        def _(head):
            lanes = pl.ds(pl.multiple_of(head * BLK, BLK), BLK)
            keys = kv_ref[slot, :, lanes]
            scores = dot_nt(keys, query_ref[:, lanes])
            before = state_m[head]
            maximum = jnp.maximum(before, jnp.max(scores, axis=0, keepdims=True))
            weights = jnp.exp(scores - maximum)
            factor = jnp.exp(before - maximum)
            state_m[head] = maximum
            state_l[head] = state_l[head] * factor + jnp.sum(weights, axis=0, keepdims=True)
            acc[head] = acc[head] * factor + dot_tn(keys, weights.astype(bf16))

    attend(0)
    kv_copies[1].wait_recv()
    attend(1)
    kv_copies[0].wait_recv()
    forwarded = remote(kv_ref.at[2], kv_ref.at[3], kv_ss.at[2], kv_rs.at[3], C)
    forwarded.start()
    attend(2)
    forwarded.wait_recv()
    attend(3)
    gather_e.second()
    gather_r.second()

    row = lax.broadcasted_iota(jnp.int32, (BLK, acc.shape[2]), 0)
    for head in range(heads):
        value = jnp.where(row < HEAD_DIM, 0.0, acc[head] / state_l[head])
        att_ref[head * BLK : (head + 1) * BLK, :] = value.astype(bf16)
        logt_ref[head] = state_m[head] + jnp.log(state_l[head])

    part_copies = []
    for slot in (3, 2, 1, 0):
        here = slice(slot * rows, (slot + 1) * rows)
        partial_sum = dot_tn(att_ref[:, here], weight_ref[2 * half : 3 * half, :])
        if slot:
            part_send[slot - 1] = partial_sum.astype(bf16)
            copy = remote(
                part_send.at[slot - 1], part_recv.at[slot - 1],
                part_ss.at[slot], part_rs.at[slot], TP[slot],
            )
            copy.start()
            part_copies.append(copy)
        else:
            attn_ref[...] = partial_sum
    gather_e.third()
    gather_r.third()
    for copy in part_copies:
        copy.wait()
    attn_ref[...] += (
        part_recv[0].astype(f32) + part_recv[1].astype(f32) + part_recv[2].astype(f32)
    )
    gather_e.last()
    gather_r.last()
    for copy in kv_copies:
        copy.wait_send()
    forwarded.wait_send()
    for copy in cot_copies:
        copy.wait()


def gelu_pair(hidden):
    scale = math.sqrt(2.0 / math.pi)
    square = hidden * hidden
    bend = jnp.tanh(scale * hidden * (1.0 + 0.044715 * square))
    half = 0.5 * (1.0 + bend)
    slope = half + 0.5 * hidden * (1.0 - bend * bend) * (
        scale * (1.0 + 3.0 * 0.044715 * square)
    )
    return hidden * half, slope


def mlp_kernel(
    tokens_ref, mods_ref, attn_ref, cot_ref, expand_in, reduce_in,
    mlp_ref, gm_ref, middle_ref, expand_grad, reduce_grad,
    expand_ref, reduce_ref, mix, branch, active, grad_hid, mlp_send, mlp_recv, gm_send, gm_recv,
    mix_ss, mix_rs, mlp_ss, mlp_rs, gm_ss, gm_rs,
):
    rows, width = tokens_ref.shape
    units = expand_ref.shape[0]
    per = units // 8
    enter(TP[1:])
    gate_one, shift_two, scale_two, gate_two = (
        mods_ref[index : index + 1, :] for index in (2, 3, 4, 5)
    )
    middle = tokens_ref[...].astype(f32) + gate_one * attn_ref[...]
    middle_ref[...] = middle
    normed, _unused = layer_norm(middle)
    gain = mods_ref[7:8, :] * (1.0 + scale_two)
    mixed = (normed * gain + shift_two).astype(bf16)
    lane = lax.broadcasted_iota(jnp.int32, (rows, BLK), 1)
    ones = jnp.where(lane == 0, 1.0, 0.0).astype(bf16)
    for slot in range(4):
        mix[slot, :, width:] = ones
    mix[0, :, :width] = mixed
    mix_copies = [
        remote(
            mix.at[0, :, pl.ds(0, width)], mix.at[slot, :, pl.ds(0, width)],
            mix_ss.at[slot], mix_rs.at[slot], TP[slot],
        )
        for slot in range(1, 4)
    ]
    for copy in mix_copies:
        copy.start()
    for index in range(8):
        expand_ref[index * per : (index + 1) * per, :] = expand_in[index]
        reduce_ref[index * per : (index + 1) * per, :] = reduce_in[index]

    copies = []
    for slot in range(4):
        here = slice(slot * rows, (slot + 1) * rows)
        if slot:
            mix_copies[slot - 1].wait_recv()
        grad_branch = (gate_two * cot_ref[slot].astype(f32)).astype(bf16)
        branch[here, :] = grad_branch
        hidden = dot_nt(mix[slot], expand_ref[...])
        activated, slope = gelu_pair(hidden)
        activated = activated.astype(bf16)
        active[here, :] = activated
        grad_hidden = (dot_nt(grad_branch, reduce_ref[...]) * slope).astype(bf16)
        grad_hid[here, :] = grad_hidden
        gm_part = dot_nn(grad_hidden, expand_ref[:, :width])
        mlp_part = dot_nn(activated, reduce_ref[...])
        if slot:
            gm_send[slot - 1] = gm_part.astype(bf16)
            mlp_send[slot - 1] = mlp_part.astype(bf16)
            for source, target, ss, rs in (
                (gm_send, gm_recv, gm_ss, gm_rs), (mlp_send, mlp_recv, mlp_ss, mlp_rs),
            ):
                copy = remote(
                    source.at[slot - 1], target.at[slot - 1], ss.at[slot], rs.at[slot], TP[slot]
                )
                copy.start()
                copies.append(copy)
        else:
            gm_ref[...] = gm_part
            mlp_ref[...] = mlp_part + mods_ref[8:9, :]

    @pl.loop(0, units // BLK)
    def _(index):
        lanes = pl.ds(pl.multiple_of(index * BLK, BLK), BLK)
        grad_reduce = dot_tn(active[:, lanes], branch[...])
        reduce_grad[lanes, :] = grad_reduce.astype(bf16)
        left = grad_hid[:, lanes]
        total = dot_tn(left, mix[0:4].reshape(4 * rows, width + BLK))
        expand_grad[lanes, :] = total.astype(bf16)

    for copy in mix_copies:
        copy.wait_send()
    for copy in copies:
        copy.wait()
    for slot in range(3):
        gm_ref[...] += gm_recv[slot].astype(f32)
        mlp_ref[...] += mlp_recv[slot].astype(f32)


class Scatter:
    def __init__(self, blocks, from_core, from_y, from_z, send_sem, recv_sem):
        self.blocks, self.send_sem, self.recv_sem = blocks, send_sem, recv_sem
        self.place = {C: from_core, Y: from_y, ZH: from_z}
        self.base = {C: 0, Y: 4, ZH: 6}
        self.sent = []

    def step(self, to, kept):
        copies = []
        for index, offset in enumerate(kept):
            number = self.base[to] + index
            copy = remote(
                self.blocks.at[share(offset + to)], self.place[to].at[index],
                self.send_sem.at[number], self.recv_sem.at[number], to,
            )
            copy.start()
            copies.append(copy)
        self.sent.append((to, kept, copies))

    def add(self):
        to, kept, copies = self.sent[-1]
        for index, offset in enumerate(kept):
            copies[index].wait_recv()
            slot = share(offset)
            self.blocks[slot] = (
                self.blocks[slot].astype(f32) + self.place[to][index].astype(f32)
            ).astype(bf16)

    def finish(self):
        for _to, _kept, copies in self.sent:
            for copy in copies:
                copy.wait_send()


KEPT = ((C, (0, Y, ZH, Y + ZH)), (Y, (0, ZH)), (ZH, (0,)))


def column_sum(value):
    return jnp.sum(value, axis=0, keepdims=True)


def backward_kernel(
    tokens_ref, cotangent_ref, mods_ref, attn_ref, middle_ref, mlp_ref, gm_ref,
    mixed_ref, query_ref, kv_ref, att_ref, logt_ref, weight_ref, cos_ref, sin_ref,
    expand_in, reduce_in, condition_ref, ada_ref,
    result_ref, gtok_ref, gcond_ref, gvec_ref, gexp_ref, gred_ref, gchunk_ref,
    gattn, dout, dout_t, rdots, dq, dkv, dkv_send, dkv_recv, dqkv, part_send, part_recv,
    gmid, blocks_e, blocks_r, blocks_a, wide, from_e, from_r, from_a, from_e2, from_r2, from_a2,
    from_e3, from_r3, from_a3, rowsum, vec_send, vec_recv, cond_send, cond_recv, chunk_send,
    chunk_recv,
    ga_ss, ga_rs, dkv_ss, dkv_rs, part_ss, part_rs, e_ss, e_rs, r_ss, r_rs, a_ss, a_rs,
    vec_ss, vec_rs, cond_ss, cond_rs, chunk_ss, chunk_rs, local_sem,
):
    rows, width = tokens_ref.shape
    heads = query_ref.shape[1] // BLK
    half = heads * BLK
    per = expand_in.shape[0] // 8
    me = flat(peer(0))
    enter(range(1, 32))
    shift_one, scale_one, gate_one, shift_two, scale_two, gate_two, gain_one, gain_two = (
        mods_ref[index : index + 1, :] for index in range(8)
    )
    cot = cotangent_ref[...].astype(f32)
    middle = middle_ref[...]
    mlp_branch = mlp_ref[...]
    grad_mixed = gm_ref[...]
    normed, inverse = layer_norm(middle)
    gain = gain_two * (1.0 + scale_two)
    grad_middle = cot + norm_back(grad_mixed * gain, normed, inverse)
    gmid[...] = grad_middle
    gattn[0] = (gate_one * grad_middle).astype(bf16)
    ga_copies = [
        remote(gattn.at[0], gattn.at[slot], ga_ss.at[slot], ga_rs.at[slot], TP[slot])
        for slot in range(1, 4)
    ]
    for copy in ga_copies:
        copy.start()
    for index in range(8):
        here = slice(index * per, (index + 1) * per)
        blocks_e[index] = expand_in[here, :]
        blocks_r[index] = reduce_in[here, :]
    scatter_e = Scatter(blocks_e, from_e, from_e2, from_e3, e_ss, e_rs)
    scatter_r = Scatter(blocks_r, from_r, from_r2, from_r3, r_ss, r_rs)
    scatter_e.step(*KEPT[0])
    scatter_r.step(*KEPT[0])
    result_ref[...] = (middle + gate_two * mlp_branch).astype(bf16)
    weighted = column_sum(grad_mixed * normed)
    rowsum[2:3, :] = column_sum(grad_middle * attn_ref[...])
    rowsum[3:4, :] = column_sum(grad_mixed)
    rowsum[4:5, :] = weighted * gain_two
    rowsum[5:6, :] = column_sum(cot * mlp_branch)
    rowsum[7:8, :] = weighted * (1.0 + scale_two)
    rowsum[8:9, :] = column_sum((gate_two * cot).astype(bf16).astype(f32))

    for slot in range(4):
        if slot:
            ga_copies[slot - 1].wait_recv()
        here = slice(slot * rows, (slot + 1) * rows)
        values = dot_nt(gattn[slot], weight_ref[2 * half :, :]).astype(bf16).astype(f32)
        dout[here, :] = values.astype(bf16)
        for head in range(heads):
            lanes = slice(head * BLK, (head + 1) * BLK)
            turned = values[:, lanes].T
            dout_t[lanes, here] = turned.astype(bf16)
            rdots[head, :, here] = column_sum(turned * att_ref[lanes, here].astype(f32))
    scatter_e.add()
    scatter_r.add()
    scatter_e.step(*KEPT[1])
    scatter_r.step(*KEPT[1])

    dq[...] = jnp.zeros_like(dq)

    def back(slot):
        @pl.loop(0, heads)
        def _(head):
            lanes = pl.ds(pl.multiple_of(head * BLK, BLK), BLK)
            keys = kv_ref[slot, :, lanes]
            query = query_ref[:, lanes]
            shares = jnp.exp(dot_nt(keys, query) - logt_ref[head])
            grad_shares = dot_nn(keys, dout_t[lanes, :])
            grad_scores = (shares * (grad_shares - rdots[head])).astype(bf16)
            dkv[:, lanes] = dot_nn(grad_scores, query) + dot_nn(
                shares.astype(bf16), dout[:, lanes]
            )
            dq[head] += dot_tn(keys, grad_scores)

    dkv_copies = []

    def dkv_copy(index, offset):
        copy = remote(
            dkv_send.at[index], dkv_recv.at[index], dkv_ss.at[index], dkv_rs.at[index], offset
        )
        copy.start()
        dkv_copies.append(copy)

    back(3)
    dkv_send[0] = dkv[...].astype(bf16)
    dkv_copy(0, C)
    back(2)
    dkv_copies[0].wait_recv()
    dkv_send[1] = (dkv[...] + dkv_recv[0].astype(f32)).astype(bf16)
    dkv_copy(1, ZH)
    back(1)
    dkv_send[2] = dkv[...].astype(bf16)
    dkv_copy(2, C)
    back(0)
    count = blocks_a.shape[2]

    def spread(part, base, low):
        for slot in range(8):
            for row, target in head_rows(slot * count, count, low):
                blocks_a[slot, part, row : row + 8, :] = wide[
                    base + target : base + target + 8, :
                ].astype(bf16)

    @pl.loop(0, heads)
    def _(head):
        lanes = pl.ds(pl.multiple_of(head * BLK, BLK), BLK)
        wide[lanes, :] = dot_nn(att_ref[lanes, :], gattn[0:4].reshape(4 * rows, width))

    spread(3, 0, False)
    scatter_e.add()
    scatter_r.add()
    scatter_e.step(*KEPT[2])
    scatter_r.step(*KEPT[2])
    for head in range(heads):
        lanes = slice(head * BLK, (head + 1) * BLK)
        value = dq[head].T * (HEAD_DIM ** (-0.5))
        dqkv[:, lanes] = turn(value, cos_ref[...], -sin_ref[...]).astype(bf16)
    dkv_copies[2].wait_recv()
    dkv[...] += dkv_recv[2].astype(f32)
    dkv_copies[1].wait_recv()
    for head in range(heads):
        lanes = slice(head * BLK, (head + 1) * BLK)
        value = dkv[:, lanes] + dkv_recv[1, :, lanes].astype(f32)
        dqkv[:, half + head * BLK : half + (head + 1) * BLK] = turn(
            value, cos_ref[...], -sin_ref[...]
        ).astype(bf16)

    part_copies = []
    for slot in (3, 2, 1, 0):
        here = slice(slot * rows, (slot + 1) * rows)
        partial_sum = dot_nn(dqkv[here, :], weight_ref[0 : 2 * half, :])
        if slot:
            part_send[slot - 1] = partial_sum.astype(bf16)
            copy = remote(
                part_send.at[slot - 1], part_recv.at[slot - 1],
                part_ss.at[slot], part_rs.at[slot], TP[slot],
            )
            copy.start()
            part_copies.append(copy)
        else:
            gtok_ref[...] = partial_sum

    @pl.loop(0, 2 * heads)
    def _(head):
        lanes = pl.ds(pl.multiple_of(head * BLK, BLK), BLK)
        wide[lanes, :] = dot_tn(dqkv[:, lanes], mixed_ref[...])

    spread(0, 0, True)
    spread(1, half, True)
    spread(2, half, False)
    scatter_a = Scatter(blocks_a, from_a, from_a2, from_a3, a_ss, a_rs)
    scatter_a.step(*KEPT[0])
    for copy in part_copies:
        copy.wait()
    grad_mixed_one = (
        gtok_ref[...]
        + part_recv[0].astype(f32) + part_recv[1].astype(f32) + part_recv[2].astype(f32)
    )
    scatter_a.add()
    scatter_a.step(*KEPT[1])
    normed_one, inverse_one = layer_norm(tokens_ref[...].astype(f32))
    gain_first = gain_one * (1.0 + scale_one)
    gtok_ref[...] = gmid[...] + norm_back(grad_mixed_one * gain_first, normed_one, inverse_one)
    weighted = column_sum(grad_mixed_one * normed_one)
    rowsum[0:1, :] = column_sum(grad_mixed_one)
    rowsum[1:2, :] = weighted * gain_one
    rowsum[6:7, :] = weighted * (1.0 + scale_one)
    vec_send[...] = jnp.zeros_like(vec_send)
    tiles = width // BLK
    for owner in range(32):
        for tile in range(2):
            at = (9 * owner) // 8 + tile
            vec_send[owner, 0:1, tile * BLK : (tile + 1) * BLK] = rowsum[
                at // tiles : at // tiles + 1, (at % tiles) * BLK : (at % tiles + 1) * BLK
            ]
            at = (3 * owner) // 16 + tile
            if at < tiles:
                vec_send[owner, 1:4, tile * BLK : (tile + 1) * BLK] = rowsum[
                    6:9, at * BLK : (at + 1) * BLK
                ]

    def vec_copy(offset):
        return pltpu.make_async_remote_copy(
            src_ref=vec_send.at[flat(peer_loop(offset))],
            dst_ref=vec_recv.at[offset],
            send_sem=vec_ss.at[offset],
            recv_sem=vec_rs.at[offset],
            device_id=peer_loop(offset),
            device_id_type=MESH,
        )

    @pl.loop(1, 32)
    def _(offset):
        vec_copy(offset).start()

    scatter_e.add()
    scatter_r.add()
    own = share(0)
    gexp_ref[...] = blocks_e[own].astype(f32)
    gred_ref[...] = blocks_r[own].astype(f32)
    scatter_a.add()
    scatter_a.step(*KEPT[2])
    vec_recv[0] = vec_send[me]

    @pl.loop(1, 32)
    def _(offset):
        vec_copy(offset).wait()

    total = jnp.zeros(vec_recv.shape[1:], f32)
    for index in range(32):
        total = total + vec_recv[index]
    mod_shift = (me % 8) * 16
    gain_shift = ((3 * me) % 16) * 8
    gvec_ref[0:8, :] = pltpu.roll(total, (256 - mod_shift) % 256, 1)
    gvec_ref[8:16, :] = pltpu.roll(total, (256 - gain_shift) % 256, 1)
    piece = ada_ref.shape[1]
    cond_send[...] = lax.dot_general(
        gvec_ref[0:8, 0:piece], ada_ref[...].astype(f32), (((1,), (1,)), ((), ())),
        preferred_element_type=f32, precision=highest,
    )

    def cond_copy(offset):
        return pltpu.make_async_remote_copy(
            src_ref=cond_send.at[pl.ds(0, 1)],
            dst_ref=cond_recv.at[offset],
            send_sem=cond_ss.at[offset],
            recv_sem=cond_rs.at[offset],
            device_id=peer_loop(offset),
            device_id_type=MESH,
        )

    @pl.loop(1, 32)
    def _(offset):
        cond_copy(offset).start()

    scatter_a.add()
    chunk_send[...] = blocks_a[own]
    place_in = 8 * ((me // 4) % 2 * 2 + (me // 2) % 2) + own

    def chunk_copies(part):
        if part < 3:
            number = 32 * part + place_in
            owner, slot = number // 3, number % 3
        else:
            owner, slot = place_in, 3
        stays = owner == me
        far = pltpu.make_async_remote_copy(
            src_ref=chunk_send.at[part], dst_ref=chunk_recv.at[slot],
            send_sem=chunk_ss.at[part], recv_sem=chunk_rs.at[slot],
            device_id=(owner // 16, owner % 16), device_id_type=MESH,
        )
        near = pltpu.make_async_copy(
            chunk_send.at[part], chunk_recv.at[slot], local_sem.at[part]
        )
        return far, near, stays

    for part in range(4):
        far, near, stays = chunk_copies(part)

        @pl.when(jnp.logical_not(stays))
        def _():
            far.start()

        @pl.when(stays)
        def _():
            near.start()

    @pl.loop(1, 32)
    def _(offset):
        cond_copy(offset).wait()

    cond_recv[0] = cond_send[0:1, :]
    gradient = jnp.zeros((1, BLK), f32)
    for index in range(32):
        gradient = gradient + cond_recv[index]
    gcond_ref[...] = gradient

    for part in range(4):
        far, near, stays = chunk_copies(part)

        @pl.when(jnp.logical_not(stays))
        def _():
            far.wait_send()

        @pl.when(stays)
        def _():
            near.wait()

    for slot in range(4):
        if slot < 3:
            number = 3 * me + slot
            part, place_of = number // 32, number % 32
        else:
            part, place_of = 3, me
        rank, dp = place_of // 8, place_of % 8
        keeper = ((dp // 2) % 2) * 16 + (dp // 4) * 8 + (rank // 2) * 4 + (rank % 2) * 2 + dp % 2

        @pl.when(keeper != me)
        def _():
            pltpu.make_async_remote_copy(
                src_ref=chunk_send.at[slot], dst_ref=chunk_recv.at[slot],
                send_sem=chunk_ss.at[slot], recv_sem=chunk_rs.at[slot],
                device_id=(keeper // 16, keeper % 16), device_id_type=MESH,
            ).wait_recv()

    gchunk_ref[...] = chunk_recv[...].astype(f32)
    for copy in ga_copies:
        copy.wait_send()
    for copy in dkv_copies:
        copy.wait_send()
    scatter_e.finish()
    scatter_r.finish()
    scatter_a.finish()


def rotary_blocks(length):
    half_dim = HEAD_DIM // 2
    frequency = np.exp(
        np.arange(half_dim, dtype=np.float32) * np.float32(-2.0 * math.log(10000.0) / HEAD_DIM)
    ).astype(np.float32)
    angles = (np.arange(length, dtype=np.float32)[:, None] * frequency[None, :]).astype(np.float32)
    cosine, sine = np.cos(angles.astype(np.float64)), np.sin(angles.astype(np.float64))
    one, zero = np.ones((length, HEAD_DIM)), np.zeros((length, HEAD_DIM))
    return (
        np.concatenate([cosine, cosine, one], axis=1).astype(np.float32),
        np.concatenate([-sine, sine, zero], axis=1).astype(np.float32),
    )


def vmem(*shape, kind=jnp.bfloat16):
    return pltpu.VMEM(shape, kind)


def dma(*count):
    return pltpu.SemaphoreType.DMA(count)


def call(body, outs, scratch, number, operands, hbm=()):
    whole = pl.BlockSpec(memory_space=pltpu.VMEM)
    return pl.pallas_call(
        body,
        out_shape=tuple(jax.ShapeDtypeStruct(shape, kind) for shape, kind in outs),
        in_specs=[
            pl.BlockSpec(memory_space=pl.ANY) if index in hbm else whole
            for index in range(len(operands))
        ],
        out_specs=tuple(whole for _ in outs),
        scratch_shapes=scratch,
        compiler_params=pltpu.CompilerParams(
            collective_id=number, has_side_effects=True, vmem_limit_bytes=60 * 2**20
        ),
    )(*operands)


def on_device_fast(
    tokens, condition, ada_weight, ada_bias, first_gain, second_gain, project_weight,
    output_weight, expand_weight, expand_bias, reduce_weight, reduce_bias, cotangent,
):
    rows, width = tokens.shape
    cycle = lax.axis_size("blk")
    group = 4 * rows
    heads = width // HEAD_DIM // 4
    half = heads * BLK
    per = reduce_weight.shape[0]
    units = 8 * per
    count = output_weight.shape[0]
    piece = ada_weight.shape[1]

    def line(value):
        return jnp.pad(value.astype(f32)[None, :], ((0, 7), (0, 256 - value.shape[0])))

    lines = jnp.concatenate(
        [line(ada_bias), line(first_gain), line(second_gain), line(reduce_bias)], axis=0
    )
    chunk = jnp.concatenate(
        [project_weight.T.reshape(3, count, width), output_weight[None]], axis=0
    )
    expand_rows = jnp.concatenate(
        [expand_weight.T, expand_bias[:, None], jnp.zeros((per, BLK - 1), bf16)], axis=1
    )
    column = condition[:, None]
    cosine, sine = (jnp.asarray(table) for table in rotary_blocks(cycle * rows))
    (
        mods, attn, mixed, query, kv, att, logt, weight, cot_all, expand_all, reduce_all,
        cos_rows, sin_rows,
    ) = call(
        forward_kernel,
        [
            ((16, width), f32), ((rows, width), f32), ((group, width), bf16),
            ((group, half), bf16), ((4, group, half), bf16), ((half, group), bf16),
            ((heads, 1, group), f32), ((3 * half, width), bf16), ((4, rows, width), bf16),
            ((8, per, width + BLK), bf16), ((8, per, width), bf16),
            ((group, BLK), f32), ((group, BLK), f32),
        ],
        [
            vmem(32, 256, kind=f32), vmem(32, 8, 256, kind=f32), vmem(8, 4, count, width),
            vmem(4, rows, width), vmem(1, 6 * width, kind=f32), vmem(8, width + BLK, kind=f32),
            vmem(heads, 1, group, kind=f32), vmem(heads, 1, group, kind=f32),
            vmem(heads, BLK, group, kind=f32), vmem(3, rows, width), vmem(3, rows, width),
            dma(32), dma(32), dma(4), dma(4), dma(12), dma(4), dma(4), dma(4), dma(4),
            dma(8), dma(8), dma(8), dma(8), dma(8), dma(8), dma(4), dma(4), dma(4), dma(4),
        ],
        1,
        (
            tokens, cotangent, column, ada_weight, lines, chunk, expand_rows, reduce_weight,
            cosine, sine,
        ),
        hbm=(8, 9),
    )
    mlp, grad_mixed, middle, expand_grad, reduce_grad = call(
        mlp_kernel,
        [
            ((rows, width), f32), ((rows, width), f32), ((rows, width), f32),
            ((units, width + BLK), bf16), ((units, width), bf16),
        ],
        [
            vmem(units, width + BLK), vmem(units, width), vmem(4, rows, width + BLK),
            vmem(group, width), vmem(group, units), vmem(group, units),
            vmem(3, rows, width), vmem(3, rows, width), vmem(3, rows, width),
            vmem(3, rows, width),
            dma(4), dma(4), dma(4), dma(4), dma(4), dma(4),
        ],
        2,
        (tokens, mods, attn, cot_all, expand_all, reduce_all),
    )
    result, grad_tokens, grad_condition, grad_vec, grad_expand, grad_reduce, grad_chunk = call(
        backward_kernel,
        [
            ((rows, width), bf16), ((rows, width), f32), ((1, BLK), f32), ((16, 256), f32),
            ((per, width + BLK), f32), ((per, width), f32), ((4, count, width), f32),
        ],
        [
            vmem(4, rows, width), vmem(group, half), vmem(half, group),
            vmem(heads, 1, group, kind=f32), vmem(heads, BLK, group, kind=f32),
            vmem(group, half, kind=f32), vmem(3, group, half), vmem(3, group, half),
            vmem(group, 2 * half), vmem(3, rows, width), vmem(3, rows, width),
            vmem(rows, width, kind=f32), vmem(8, per, width + BLK), vmem(8, per, width),
            vmem(8, 4, count, width), vmem(2 * half, width, kind=f32),
            vmem(4, per, width + BLK), vmem(4, per, width), vmem(4, 4, count, width),
            vmem(2, per, width + BLK), vmem(2, per, width), vmem(2, 4, count, width),
            vmem(1, per, width + BLK), vmem(1, per, width), vmem(1, 4, count, width),
            vmem(16, width, kind=f32), vmem(32, 8, 256, kind=f32), vmem(32, 8, 256, kind=f32),
            vmem(8, BLK, kind=f32), vmem(32, 1, BLK, kind=f32), vmem(4, count, width),
            vmem(4, count, width),
            dma(4), dma(4), dma(4), dma(4), dma(4), dma(4), dma(7), dma(7), dma(7), dma(7),
            dma(7), dma(7), dma(32), dma(32), dma(32), dma(32), dma(4), dma(4), dma(4),
        ],
        3,
        (
            tokens, cotangent, mods, attn, middle, mlp, grad_mixed, mixed, query, kv, att, logt,
            weight, cos_rows, sin_rows, expand_grad, reduce_grad, column, ada_weight,
        ),
    )
    mod_piece = grad_vec[0, :piece]
    return (
        result,
        grad_tokens,
        grad_condition.reshape(-1),
        condition[:, None] * mod_piece[None, :],
        mod_piece,
        grad_vec[9, :count],
        grad_vec[10, :count],
        grad_chunk[:3].reshape(3 * count, width).T,
        grad_chunk[3],
        grad_expand[:, :width].T,
        grad_expand[:, width],
        grad_reduce,
        grad_vec[11, :count],
    )


def solution(mesh):
    return jax.shard_map(
        on_device_fast if mesh.shape["ulysses"] * mesh.shape["blk"] == 32 else on_device,
        mesh=mesh,
        in_specs=(
            P(("ulysses", "blk"), None),
            P(),
            P(None, ("ulysses", "blk")),
            P(("ulysses", "blk")),
            P(("ulysses", "blk")),
            P(("ulysses", "blk")),
            P(None, ("ulysses", "blk")),
            P(("ulysses", "blk"), None),
            P(None, ("ulysses", "blk")),
            P(("ulysses", "blk")),
            P(("ulysses", "blk"), None),
            P(("ulysses", "blk")),
            P(("ulysses", "blk"), None),
        ),
        out_specs=(
            P(("ulysses", "blk"), None),
            P(("ulysses", "blk"), None),
            P(),
            P(None, ("ulysses", "blk")),
            P(("ulysses", "blk")),
            P(("ulysses", "blk")),
            P(("ulysses", "blk")),
            P(None, ("ulysses", "blk")),
            P(("ulysses", "blk"), None),
            P(None, ("ulysses", "blk")),
            P(("ulysses", "blk")),
            P(("ulysses", "blk"), None),
            P(("ulysses", "blk")),
        ),
        check_vma=False,
    )
```

```python
from functools import partial
import math
import types

import jax
import jax.numpy as jnp
import numpy as np
from jax import lax
from jax.experimental import pallas as pl
from jax.experimental.pallas import tpu as pltpu
from jax.sharding import PartitionSpec as P

HEAD_DIM = 64


eps = 1e-05
highest = lax.Precision.HIGHEST


def layer_norm(value):
    center = value - jnp.mean(value, axis=-1, keepdims=True)
    inverse = lax.rsqrt(jnp.mean(center * center, axis=-1, keepdims=True) + eps)
    return (center * inverse, inverse)


def norm_back(grad_normed, normed, inverse):
    first = jnp.mean(grad_normed, axis=-1, keepdims=True)
    second = jnp.mean(grad_normed * normed, axis=-1, keepdims=True)
    return inverse * (grad_normed - first - normed * second)


def rotary_tables(positions, head_dim):
    half_dim = head_dim // 2
    frequency = jnp.exp(
        jnp.arange(half_dim, dtype=jnp.float32) * (-2.0 * math.log(10000.0) / head_dim)
    )
    angles = positions[:, None] * frequency[None, :]
    return (jnp.cos(angles)[:, None, :], jnp.sin(angles)[:, None, :])


def rotate(value, cosine, sine):
    half_dim = value.shape[-1] // 2
    first = value[..., :half_dim]
    second = value[..., half_dim:]
    return jnp.concatenate(
        [first * cosine - second * sine, second * cosine + first * sine], axis=-1
    )


def rotate_back(grad_value, cosine, sine):
    half_dim = grad_value.shape[-1] // 2
    first = grad_value[..., :half_dim]
    second = grad_value[..., half_dim:]
    return jnp.concatenate(
        [first * cosine + second * sine, second * cosine - first * sine], axis=-1
    )


def over_blocks(block_step, carried, pieces, key_block):
    length = pieces[0].shape[1]
    complete = length // key_block
    stacked = tuple(
        (
            jnp.moveaxis(
                member.reshape((member.shape[0], complete, key_block) + member.shape[2:]), 1, 0
            )
            for member in pieces
        )
    )
    offsets = jnp.arange(complete, dtype=jnp.int32) * key_block

    def scan_step(carried_in, inputs):
        return (block_step(carried_in, inputs[:-1], inputs[-1]), None)

    carried, unused = lax.scan(scan_step, carried, stacked + (offsets,))
    return carried


def on_device(
    tokens,
    condition,
    ada_weight,
    ada_bias,
    first_gain,
    second_gain,
    project_weight,
    output_weight,
    expand_weight,
    expand_bias,
    reduce_weight,
    reduce_bias,
    cotangent,
):
    row_count = tokens.shape[0]
    model_width = tokens.shape[1]
    cycle_size = lax.axis_size("blk")
    cycle_place = lax.axis_index("blk")
    seq_count = lax.axis_size("ulysses")
    (
        ada_full,
        ada_shift,
        gain_one,
        gain_two,
        project_full,
        output_full,
        expand_full,
        expand_shift,
        reduce_full,
        reduce_shift,
    ) = (
        lax.all_gather(ada_weight, ("ulysses", "blk"), axis=1, tiled=True),
        lax.all_gather(ada_bias, ("ulysses", "blk"), axis=0, tiled=True),
        lax.all_gather(first_gain, ("ulysses", "blk"), axis=0, tiled=True),
        lax.all_gather(second_gain, ("ulysses", "blk"), axis=0, tiled=True),
        lax.all_gather(project_weight, ("ulysses", "blk"), axis=1, tiled=True),
        lax.all_gather(output_weight, ("ulysses", "blk"), axis=0, tiled=True),
        lax.all_gather(expand_weight, ("ulysses", "blk"), axis=1, tiled=True),
        lax.all_gather(expand_bias, ("ulysses", "blk"), axis=0, tiled=True),
        lax.all_gather(reduce_weight, ("ulysses", "blk"), axis=0, tiled=True),
        lax.all_gather(reduce_bias, ("ulysses", "blk"), axis=0, tiled=True),
    )
    ada_float = ada_full.astype(jnp.float32)
    modulation = jnp.dot(condition, ada_float, precision=highest) + ada_shift.astype(jnp.float32)
    shift_one, scale_one, gate_one, shift_two, scale_two, gate_two = jnp.split(modulation, 6)
    gain_one_f = gain_one.astype(jnp.float32)
    gain_two_f = gain_two.astype(jnp.float32)
    inputs = tokens.astype(jnp.float32)
    normed_one, inverse_one = layer_norm(inputs)
    gain_first = gain_one_f * (1.0 + scale_one)
    mixed_one = (normed_one * gain_first + shift_one).astype(jnp.bfloat16)
    projected = jnp.dot(mixed_one, project_full, preferred_element_type=jnp.float32)
    packed = projected.astype(jnp.bfloat16).reshape(row_count, 3, model_width)
    regrouped = lax.all_to_all(packed, "ulysses", split_axis=2, concat_axis=0, tiled=True)
    local_rows = regrouped.shape[0]
    local_width = regrouped.shape[2]
    head_count = local_width // HEAD_DIM
    by_seq = regrouped.reshape(seq_count, row_count, 3, local_width)
    positions = cycle_place * row_count + jnp.arange(row_count, dtype=jnp.int32)
    cosine, sine = rotary_tables(positions.astype(jnp.float32), HEAD_DIM)
    query_rot = rotate(
        by_seq[:, :, 0].astype(jnp.float32).reshape(seq_count, row_count, head_count, HEAD_DIM),
        cosine,
        sine,
    ).astype(jnp.bfloat16)
    key_rot = rotate(
        by_seq[:, :, 1].astype(jnp.float32).reshape(seq_count, row_count, head_count, HEAD_DIM),
        cosine,
        sine,
    ).astype(jnp.bfloat16)
    value_flat = by_seq[:, :, 2]
    value_own = value_flat.reshape(seq_count, row_count, head_count, HEAD_DIM)
    key_flat = key_rot.reshape(seq_count, row_count, local_width)
    score_scale = HEAD_DIM ** (-0.5)
    key_block = row_count * -(-512 // row_count)

    def attend_step(carried, pieces, offset):
        maximum, denominator, weighted = carried
        key_rows = pieces[0].reshape(seq_count, -1, head_count, HEAD_DIM)
        value_rows = pieces[1].reshape(seq_count, -1, head_count, HEAD_DIM)
        scores = (
            jnp.einsum("sqhd,skhd->shqk", query_rot, key_rows, preferred_element_type=jnp.float32)
            * score_scale
        )
        new_maximum = jnp.maximum(maximum, jnp.max(scores, axis=-1))
        weights = jnp.exp(scores - new_maximum[..., None])
        factor = jnp.exp(maximum - new_maximum)
        denominator = denominator * factor + jnp.sum(weights, axis=-1)
        weighted = weighted * jnp.transpose(factor, (0, 2, 1))[..., None] + jnp.einsum(
            "shqk,skhd->sqhd",
            weights.astype(jnp.bfloat16),
            value_rows,
            preferred_element_type=jnp.float32,
        )
        return (new_maximum, denominator, weighted)

    start_state = (
        jnp.full((seq_count, head_count, row_count), -1e30, jnp.float32),
        jnp.zeros((seq_count, head_count, row_count), jnp.float32),
        jnp.zeros((seq_count, row_count, head_count, HEAD_DIM), jnp.float32),
    )
    maximum, denominator, weighted = over_blocks(
        attend_step,
        start_state,
        (
            lax.all_gather(key_flat, "blk", axis=1, tiled=True),
            lax.all_gather(value_flat, "blk", axis=1, tiled=True),
        ),
        key_block,
    )
    log_total = maximum + jnp.log(denominator)
    attended = (
        (weighted / jnp.transpose(denominator, (0, 2, 1))[..., None])
        .astype(jnp.bfloat16)
        .reshape(local_rows, local_width)
    )
    attended_tokens = lax.all_to_all(attended, "ulysses", split_axis=0, concat_axis=1, tiled=True)
    attn_branch = jnp.dot(attended_tokens, output_full, preferred_element_type=jnp.float32)
    middle = inputs + gate_one * attn_branch
    normed_two, inverse_two = layer_norm(middle)
    gain_second = gain_two_f * (1.0 + scale_two)
    mixed_two = (normed_two * gain_second + shift_two).astype(jnp.bfloat16)
    hidden = jnp.dot(
        mixed_two, expand_full, preferred_element_type=jnp.float32
    ) + expand_shift.astype(jnp.float32)
    activated, gelu_back = jax.vjp(partial(jax.nn.gelu, approximate=True), hidden)
    activated_low = activated.astype(jnp.bfloat16)
    mlp_branch = jnp.dot(
        activated_low, reduce_full, preferred_element_type=jnp.float32
    ) + reduce_shift.astype(jnp.float32)
    result = (middle + gate_two * mlp_branch).astype(jnp.bfloat16)
    grad_result = cotangent.astype(jnp.float32)
    grad_gate_two = jnp.sum(grad_result * mlp_branch, axis=0)
    grad_branch = (gate_two * grad_result).astype(jnp.bfloat16)
    grad_reduce = jnp.einsum(
        "tf,td->fd", activated_low, grad_branch, preferred_element_type=jnp.float32
    )
    grad_reduce_shift = jnp.sum(grad_branch.astype(jnp.float32), axis=0)
    grad_activated = jnp.einsum(
        "td,fd->tf", grad_branch, reduce_full, preferred_element_type=jnp.float32
    )
    grad_hidden = gelu_back(grad_activated)[0].astype(jnp.bfloat16)
    grad_expand = jnp.einsum(
        "td,tf->df", mixed_two, grad_hidden, preferred_element_type=jnp.float32
    )
    grad_expand_shift = jnp.sum(grad_hidden.astype(jnp.float32), axis=0)
    grad_mixed_two = jnp.einsum(
        "tf,df->td", grad_hidden, expand_full, preferred_element_type=jnp.float32
    )
    grad_shift_two = jnp.sum(grad_mixed_two, axis=0)
    grad_scale_two = jnp.sum(grad_mixed_two * normed_two * gain_two_f, axis=0)
    grad_gain_two = jnp.sum(grad_mixed_two * normed_two * (1.0 + scale_two), axis=0)
    grad_middle = grad_result + norm_back(grad_mixed_two * gain_second, normed_two, inverse_two)
    grad_gate_one = jnp.sum(grad_middle * attn_branch, axis=0)
    grad_attn = (gate_one * grad_middle).astype(jnp.bfloat16)
    grad_output = jnp.einsum(
        "tc,td->cd", attended_tokens, grad_attn, preferred_element_type=jnp.float32
    )
    grad_heads = jnp.einsum(
        "td,cd->tc", grad_attn, output_full, preferred_element_type=jnp.float32
    ).astype(jnp.bfloat16)
    grad_local = lax.all_to_all(grad_heads, "ulysses", split_axis=1, concat_axis=0, tiled=True)
    grad_local_heads = grad_local.reshape(seq_count, row_count, head_count, HEAD_DIM)
    row_dots = jnp.sum(
        (grad_local.astype(jnp.float32) * attended.astype(jnp.float32)).reshape(
            seq_count, row_count, head_count, HEAD_DIM
        ),
        axis=-1,
    )
    row_dots_t = jnp.transpose(row_dots, (0, 2, 1))

    def query_step(carried, pieces, offset):
        key_rows = pieces[0].reshape(seq_count, -1, head_count, HEAD_DIM)
        value_rows = pieces[1].reshape(seq_count, -1, head_count, HEAD_DIM)
        scores = (
            jnp.einsum("sqhd,skhd->shqk", query_rot, key_rows, preferred_element_type=jnp.float32)
            * score_scale
        )
        shares = jnp.exp(scores - log_total[..., None])
        grad_shares = jnp.einsum(
            "sqhd,skhd->shqk", grad_local_heads, value_rows, preferred_element_type=jnp.float32
        )
        grad_scores = (shares * (grad_shares - row_dots_t[..., None])).astype(jnp.bfloat16)
        return (
            carried
            + jnp.einsum(
                "shqk,skhd->sqhd", grad_scores, key_rows, preferred_element_type=jnp.float32
            )
            * score_scale
        )

    grad_query_rot = over_blocks(
        query_step,
        jnp.zeros((seq_count, row_count, head_count, HEAD_DIM), jnp.float32),
        (
            lax.all_gather(key_flat, "blk", axis=1, tiled=True),
            lax.all_gather(value_flat, "blk", axis=1, tiled=True),
        ),
        key_block,
    )

    def key_step(carried, pieces, offset):
        grad_keys_acc, grad_values_acc = carried
        query_rows = pieces[0].reshape(seq_count, -1, head_count, HEAD_DIM)
        slope_rows = pieces[1].reshape(seq_count, -1, head_count, HEAD_DIM)
        scores = (
            jnp.einsum("sqhd,skhd->shqk", query_rows, key_rot, preferred_element_type=jnp.float32)
            * score_scale
        )
        shares = jnp.exp(scores - jnp.transpose(pieces[2], (0, 2, 1))[..., None])
        grad_values_acc = grad_values_acc + jnp.einsum(
            "shqk,sqhd->skhd",
            shares.astype(jnp.bfloat16),
            slope_rows,
            preferred_element_type=jnp.float32,
        )
        grad_shares = jnp.einsum(
            "sqhd,skhd->shqk", slope_rows, value_own, preferred_element_type=jnp.float32
        )
        grad_scores = (
            shares * (grad_shares - jnp.transpose(pieces[3], (0, 2, 1))[..., None])
        ).astype(jnp.bfloat16)
        grad_keys_acc = (
            grad_keys_acc
            + jnp.einsum(
                "shqk,sqhd->skhd", grad_scores, query_rows, preferred_element_type=jnp.float32
            )
            * score_scale
        )
        return (grad_keys_acc, grad_values_acc)

    query_wide = query_rot.reshape(seq_count, row_count, local_width)
    slope_wide = grad_local.reshape(seq_count, row_count, local_width)
    key_init = (
        jnp.zeros((seq_count, row_count, head_count, HEAD_DIM), jnp.float32),
        jnp.zeros((seq_count, row_count, head_count, HEAD_DIM), jnp.float32),
    )
    grad_key_rot, grad_value_sum = over_blocks(
        key_step,
        key_init,
        (
            lax.all_gather(query_wide.astype(jnp.float32), "blk", axis=1, tiled=True).astype(
                jnp.bfloat16
            ),
            lax.all_gather(slope_wide.astype(jnp.float32), "blk", axis=1, tiled=True).astype(
                jnp.bfloat16
            ),
            lax.all_gather(jnp.transpose(log_total, (0, 2, 1)), "blk", axis=1, tiled=True),
            lax.all_gather(row_dots, "blk", axis=1, tiled=True),
        ),
        key_block,
    )
    grad_query = (
        rotate_back(grad_query_rot, cosine, sine)
        .astype(jnp.bfloat16)
        .reshape(local_rows, local_width)
    )
    grad_key = (
        rotate_back(grad_key_rot, cosine, sine)
        .astype(jnp.bfloat16)
        .reshape(local_rows, local_width)
    )
    grad_value = grad_value_sum.astype(jnp.bfloat16).reshape(local_rows, local_width)
    grad_packed = jnp.stack([grad_query, grad_key, grad_value], axis=1)
    grad_tokens_qkv = lax.all_to_all(
        grad_packed, "ulysses", split_axis=0, concat_axis=2, tiled=True
    ).reshape(row_count, 3 * model_width)
    grad_project = jnp.einsum(
        "tc,tk->ck", mixed_one, grad_tokens_qkv, preferred_element_type=jnp.float32
    )
    grad_mixed_one = jnp.einsum(
        "tk,ck->tc", grad_tokens_qkv, project_full, preferred_element_type=jnp.float32
    )
    grad_shift_one = jnp.sum(grad_mixed_one, axis=0)
    grad_scale_one = jnp.sum(grad_mixed_one * normed_one * gain_one_f, axis=0)
    grad_gain_one = jnp.sum(grad_mixed_one * normed_one * (1.0 + scale_one), axis=0)
    grad_input = grad_middle + norm_back(grad_mixed_one * gain_first, normed_one, inverse_one)
    mod_terms = jnp.concatenate(
        [
            grad_shift_one,
            grad_scale_one,
            grad_gate_one,
            grad_shift_two,
            grad_scale_two,
            grad_gate_two,
        ]
    )
    grad_modulation = lax.psum(mod_terms, ("ulysses", "blk"))
    grad_condition = jnp.dot(ada_float, grad_modulation, precision=highest)
    piece_width = ada_weight.shape[1]
    flat_index = lax.axis_index("ulysses") * cycle_size + cycle_place
    mod_piece = lax.dynamic_slice_in_dim(grad_modulation, flat_index * piece_width, piece_width, 0)
    grad_ada = condition[:, None] * mod_piece[None, :]
    shards = (
        lax.psum_scatter(grad_gain_one, ("ulysses", "blk"), scatter_dimension=0, tiled=True),
        lax.psum_scatter(grad_gain_two, ("ulysses", "blk"), scatter_dimension=0, tiled=True),
        lax.psum_scatter(grad_project, ("ulysses", "blk"), scatter_dimension=1, tiled=True),
        lax.psum_scatter(grad_output, ("ulysses", "blk"), scatter_dimension=0, tiled=True),
        lax.psum_scatter(grad_expand, ("ulysses", "blk"), scatter_dimension=1, tiled=True),
        lax.psum_scatter(grad_expand_shift, ("ulysses", "blk"), scatter_dimension=0, tiled=True),
        lax.psum_scatter(grad_reduce, ("ulysses", "blk"), scatter_dimension=0, tiled=True),
        lax.psum_scatter(grad_reduce_shift, ("ulysses", "blk"), scatter_dimension=0, tiled=True),
    )
    return (
        result,
        grad_input,
        grad_condition,
        grad_ada,
        mod_piece,
        shards[0],
        shards[1],
        shards[2],
        shards[3],
        shards[4],
        shards[5],
        shards[6],
        shards[7],
    )


MESH = pl.DeviceIdType.MESH
Y, ZH, ZL, X, C = 16, 8, 4, 2, 1
TP = (0, X, ZL, X + ZL)
DP = (0, C, Y, Y + C, ZH, ZH + C, ZH + Y, ZH + Y + C)
BLK = 128
f32 = jnp.float32
bf16 = jnp.bfloat16


def place():
    blk = lax.axis_index("blk")
    return (lax.axis_index("ulysses"), blk // 8, (blk // 4) % 2, (blk // 2) % 2, blk % 2)


def flip(offset):
    return tuple(
        1 - bit if (offset // weight) % 2 else bit
        for bit, weight in zip(place(), (Y, ZH, ZL, X, C))
    )


def device_at(y, zh, zl, x, c):
    return (y, zh * 8 + zl * 4 + x * 2 + c)


def peer(offset):
    return device_at(*flip(offset))


def peer_loop(offset):
    return device_at(
        *(
            (bit + (offset // weight) % 2) % 2
            for bit, weight in zip(place(), (Y, ZH, ZL, X, C))
        )
    )


def flat(device):
    return device[0] * 16 + device[1]


def share(offset):
    y, zh, zl, x, c = flip(offset)
    return zh * 4 + y * 2 + c


def rank(offset):
    y, zh, zl, x, c = flip(offset)
    return zl * 2 + x


def member(which, slot):
    return device_at((slot // 2) % 2, slot // 4, which // 2, which % 2, slot % 2)


def enter(offsets):
    barrier = pltpu.get_barrier_semaphore()
    for offset in offsets:
        pl.semaphore_signal(barrier, inc=1, device_id=peer(offset), device_id_type=MESH)
    pl.semaphore_wait(barrier, len(offsets))


def remote_to(source, target, send_sem, recv_sem, device):
    return pltpu.make_async_remote_copy(
        src_ref=source,
        dst_ref=target,
        send_sem=send_sem,
        recv_sem=recv_sem,
        device_id=device,
        device_id_type=MESH,
    )


def remote(source, target, send_sem, recv_sem, offset):
    return remote_to(source, target, send_sem, recv_sem, peer(offset))


def dot_nn(a, b):
    return jnp.dot(a, b, preferred_element_type=f32)


def dot_nt(a, b):
    return lax.dot_general(a, b, (((1,), (1,)), ((), ())), preferred_element_type=f32)


def dot_tn(a, b):
    return lax.dot_general(a, b, (((0,), (0,)), ((), ())), preferred_element_type=f32)


def exact(a, b, contract):
    return lax.dot_general(
        a, b, (contract, ((), ())), preferred_element_type=f32, precision=highest
    )


def column_sum(value):
    return jnp.sum(value, axis=0, keepdims=True)


class Gather:
    def __init__(self, view, send_sem, recv_sem):
        self.view, self.send_sem, self.recv_sem = view, send_sem, recv_sem
        self.sent = []

    def send(self, have, to):
        slot = self.view(share(have))
        index = len(self.sent)
        copy = remote(
            slot, slot, self.send_sem.at[index], self.recv_sem.at[DP.index(have + to)], to
        )
        copy.start()
        self.sent.append(copy)

    def arrive(self, what):
        slot = self.view(share(what))
        remote(
            slot, slot, self.send_sem.at[0], self.recv_sem.at[DP.index(what)], C
        ).wait_recv()

    def near(self):
        self.send(0, Y)
        self.send(0, C)

    def far(self):
        self.send(0, ZH)

    def second(self):
        self.arrive(ZH)
        self.send(ZH, Y)
        self.send(ZH, C)

    def third(self):
        self.arrive(Y)
        self.send(Y, C)
        self.arrive(ZH + Y)
        self.send(ZH + Y, C)

    def last(self):
        for what in (C, Y + C, ZH + C, ZH + Y + C):
            self.arrive(what)

    def finish(self):
        for copy in self.sent:
            copy.wait_send()


class Scatter:
    KEPT = {C: (0, Y, ZH, Y + ZH), Y: (0, ZH), ZH: (0,)}

    def __init__(self, view, inbox, send_sem, recv_sem):
        self.view, self.inbox = view, inbox
        self.send_sem, self.recv_sem = send_sem, recv_sem
        self.base = {C: 0, Y: 4, ZH: 6}
        self.copies = {}

    def step(self, to):
        self.copies[to] = []
        for index, offset in enumerate(self.KEPT[to]):
            number = self.base[to] + index
            copy = remote(
                self.view(share(offset + to)), self.inbox(number),
                self.send_sem.at[number], self.recv_sem.at[number], to,
            )
            copy.start()
            self.copies[to].append(copy)

    def add(self, to):
        for index, offset in enumerate(self.KEPT[to]):
            self.copies[to][index].wait_recv()
            block = self.view(share(offset))
            block[...] = (
                block[...].astype(f32) + self.inbox(self.base[to] + index)[...].astype(f32)
            ).astype(bf16)

    def finish(self):
        for copies in self.copies.values():
            for copy in copies:
                copy.wait_send()


def turn(value, cosine, sine):
    lane = lax.broadcasted_iota(jnp.int32, value.shape, 1)
    swapped = jnp.where(
        lane < HEAD_DIM // 2,
        pltpu.roll(value, BLK - HEAD_DIM // 2, 1),
        pltpu.roll(value, HEAD_DIM // 2, 1),
    )
    return value * cosine + swapped * sine


def head_rows(first, count, low):
    for row in range(first, first + count, 8):
        yield row - first, row // HEAD_DIM, row % HEAD_DIM + (0 if low else HEAD_DIM)


def gelu_pair(hidden):
    scale = math.sqrt(2.0 / math.pi)
    square = hidden * hidden
    bend = jnp.tanh(scale * hidden * (1.0 + 0.044715 * square))
    half = 0.5 * (1.0 + bend)
    slope = half + 0.5 * hidden * (1.0 - bend * bend) * (
        scale * (1.0 + 3.0 * 0.044715 * square)
    )
    return hidden * half, slope


def to_column(row):
    count = row.shape[1]
    one = lax.broadcasted_iota(jnp.int32, (count, count), 0)
    two = lax.broadcasted_iota(jnp.int32, (count, count), 1)
    return jnp.sum(jnp.where(one == two, row, 0.0), axis=1, keepdims=True)


def to_row(column):
    count = column.shape[0]
    one = lax.broadcasted_iota(jnp.int32, (count, count), 0)
    two = lax.broadcasted_iota(jnp.int32, (count, count), 1)
    return jnp.sum(jnp.where(one == two, column, 0.0), axis=0, keepdims=True)


def block_kernel(names, *refs):
    s = types.SimpleNamespace(**dict(zip(names, refs)))
    rows, width = s.tokens.shape
    heads = s.query.shape[0]
    count = s.output_weight.shape[0]
    per = s.reduce_weight.shape[0]
    units = 8 * per
    scale = HEAD_DIM ** (-0.5)
    me = flat(peer(0))
    own = share(0)
    my_rank = rank(0)

    def here(slot):
        return slice(slot * rows, (slot + 1) * rows)

    tables = []
    for slot in range(4):
        start = pl.multiple_of(peer(TP[slot])[1] * rows, rows)
        for which, (source, target) in enumerate(((s.cos_hbm, s.cos), (s.sin_hbm, s.sin))):
            copy = pltpu.make_async_copy(
                source.at[pl.ds(start, rows)],
                target.at[pl.ds(slot * rows, rows)],
                s.table_sem.at[slot * 2 + which],
            )
            copy.start()
            tables.append(copy)
    piece = s.ada.shape[0]
    s.vec_own[...] = jnp.zeros_like(s.vec_own)
    s.vec_own[0:8, 0:piece] = exact(
        jnp.broadcast_to(s.condition[...], (8, s.condition.shape[1])),
        s.ada[...].astype(f32), ((1,), (1,)),
    )
    s.vec_own[0:1, 0:piece] += s.ada_bias[...].astype(f32)
    for index, ref in enumerate((s.first_gain, s.second_gain, s.reduce_bias)):
        s.vec_own[8 + index : 9 + index, 0:count] = ref[...].astype(f32)
    mod_shift = (me % 8) * 16
    gain_shift = ((3 * me) % 16) * 8
    s.vecs[me, 0:1, :] = pltpu.roll(s.vec_own[0:8, :], mod_shift, 1)[0:1, :]
    s.vecs[me, 1:4, :] = pltpu.roll(s.vec_own[8:16, :], gain_shift, 1)[0:3, :]
    s.cot[0] = s.cotangent[...]
    s.expand[own, :, 0:width] = s.expand_weight[...]
    lane = lax.broadcasted_iota(jnp.int32, (per, BLK), 1)
    s.expand[own, :, width:] = jnp.where(
        lane == 0, to_column(s.expand_bias[...].astype(f32)), 0.0
    ).astype(bf16)
    s.reduce[own] = s.reduce_weight[...]
    s.outw[me] = s.output_weight[...]

    enter(range(1, 32))

    def chunk_out(index):
        number = 3 * me + index
        part, place_in = number // 32, number % 32
        slot = place_in % 8
        device = member(place_in // 8, slot)
        target = s.chunks.at[slot, part]
        far = remote_to(
            s.project_weight.at[index], target, s.chunk_ss.at[index], s.chunk_rs.at[index], device
        )
        near = pltpu.make_async_copy(s.project_weight.at[index], target, s.local_sem.at[index])
        return far, near, flat(device) == me

    for index in range(3):
        far, near, stays = chunk_out(index)

        @pl.when(jnp.logical_not(stays))
        def _():
            far.start()

        @pl.when(stays)
        def _():
            near.start()

    def vec_copy(offset, device):
        return remote_to(
            s.vecs.at[device], s.vecs.at[device], s.vec_ss.at[offset], s.vec_rs.at[offset],
            peer_loop(offset),
        )

    @pl.loop(1, 32)
    def _(offset):
        vec_copy(offset, me).start()

    token_copies = [
        remote(s.tokens, s.tok.at[slot], s.tok_ss.at[slot], s.tok_rs.at[slot], TP[slot])
        for slot in range(1, 4)
    ]
    for copy in token_copies:
        copy.start()

    for index in range(3):
        far, near, stays = chunk_out(index)

        @pl.when(jnp.logical_not(stays))
        def _():
            far.wait()

        @pl.when(stays)
        def _():
            near.wait()

    gather_kv = Gather(lambda slot: s.chunks.at[slot, pl.ds(1, 2)], s.akv_ss, s.akv_rs)
    gather_q = Gather(lambda slot: s.chunks.at[slot, 0], s.aq_ss, s.aq_rs)
    gather_e = Gather(lambda slot: s.expand.at[slot], s.e_ss, s.e_rs)
    gather_r = Gather(lambda slot: s.reduce.at[slot], s.r_ss, s.r_rs)
    gather_kv.far()
    gather_kv.near()
    gather_q.far()
    gather_q.near()
    outw_sent = []

    def outw_copy(have, to, number):
        slot = s.outw.at[flat(peer(have))]
        return remote(slot, slot, s.o_ss.at[number], s.o_rs.at[number], to)

    def outw_send(have, to, number):
        copy = outw_copy(have, to, number)
        copy.start()
        outw_sent.append(copy)

    def outw_arrive(what, number):
        outw_copy(what, C, number).wait_recv()

    outw_send(0, ZH, 0)

    @pl.loop(1, 32)
    def _(offset):
        vec_copy(offset, flat(peer_loop(offset))).wait()

    s.mod_row[...] = jnp.zeros_like(s.mod_row)
    s.gain_rows[...] = jnp.zeros_like(s.gain_rows)
    for index in range(32):
        tile = (9 * index) // 8 * BLK
        s.mod_row[0:1, tile : tile + 2 * BLK] += s.vecs[index, 0:1, :]
        tile = (3 * index) // 16 * BLK
        s.gain_rows[0:3, tile : tile + 2 * BLK] += s.vecs[index, 1:4, :]
    shift_one, scale_one, gate_one, shift_two, scale_two, gate_two = range(6)
    for index in range(6):
        s.mods[index : index + 1, :] = s.mod_row[0:1, index * width : (index + 1) * width]
    s.mods[6:9, :] = s.gain_rows[0:3, 0:width]
    s.mods[9:10, :] = s.mods[6:7, :] * (1.0 + s.mods[scale_one : scale_one + 1, :])
    s.mods[10:11, :] = s.mods[7:8, :] * (1.0 + s.mods[scale_two : scale_two + 1, :])

    def mod(index):
        return s.mods[index : index + 1, :]

    gather_kv.second()
    gather_q.second()
    outw_arrive(ZH, 0)
    outw_send(0, Y, 1)
    outw_send(ZH, Y, 2)
    for slot in range(4):
        if slot:
            token_copies[slot - 1].wait()
        source = s.tok[slot] if slot else s.tokens[...]
        normed, _unused = layer_norm(source.astype(f32))
        s.mixed[here(slot), :] = (normed * mod(9) + mod(shift_one)).astype(bf16)
    gather_kv.third()
    gather_q.third()
    cot_copies = [
        remote(s.cot.at[0], s.cot.at[slot], s.cot_ss.at[slot], s.cot_rs.at[slot], TP[slot])
        for slot in range(1, 4)
    ]
    for copy in cot_copies:
        copy.start()
    gather_e.near()
    gather_r.near()
    zero = jnp.zeros((HEAD_DIM, width), bf16)
    for head in range(heads):
        s.weight[head, HEAD_DIM:, :] = zero

    def assemble(part, base, low):
        for slot in range(8):
            for row, head, target in head_rows(slot * count, count, low):
                s.weight[base + head, target : target + 8, :] = s.chunks[
                    slot, part, row : row + 8, :
                ]

    gather_kv.last()
    assemble(1, heads, True)
    assemble(2, heads, False)
    for copy in tables:
        copy.wait()
    kv_far = [
        remote(s.kv.at[0, head], s.kv.at[2, head], s.kv_ss.at[head], s.kv_rs.at[head], ZH)
        for head in range(heads)
    ]
    kv_near = [
        remote(
            s.kv.at[0, head], s.kv.at[1, head], s.kv_ss.at[heads + head],
            s.kv_rs.at[heads + head], C,
        )
        for head in range(heads)
    ]
    for head in range(heads):
        both = dot_nt(s.mixed[...], s.weight[heads + head]).astype(bf16).astype(f32)
        s.kv[0, head] = turn(both, s.cos[...], s.sin[...]).astype(bf16)
        kv_far[head].start()
        kv_near[head].start()
    gather_q.last()
    assemble(0, 0, True)
    for head in range(heads):
        query = dot_nt(s.mixed[...], s.weight[head]).astype(bf16).astype(f32)
        query = turn(query, s.cos[...], s.sin[...]).astype(bf16).astype(f32)
        s.query[head] = (query * scale).astype(bf16)
    outw_arrive(Y, 1)
    outw_arrive(Y + ZH, 2)
    number = 3
    for slot in range(1, 4):
        for have in (0, ZH, Y, Y + ZH):
            outw_send(have, TP[slot], number)
            number += 1

    s.state_m[...] = jnp.full_like(s.state_m, -1e30)
    s.state_l[...] = jnp.zeros_like(s.state_l)
    s.acc[...] = jnp.zeros_like(s.acc)

    def attend(slot, head):
        keys = s.kv[slot, head]
        scores = dot_nt(keys, s.query[head])
        before = s.state_m[head]
        maximum = jnp.maximum(before, jnp.max(scores, axis=0, keepdims=True))
        weights = jnp.exp(scores - maximum)
        factor = jnp.exp(before - maximum)
        s.state_m[head] = maximum
        s.state_l[head] = s.state_l[head] * factor + column_sum(weights)
        s.acc[head] = s.acc[head] * factor + dot_tn(keys, weights.astype(bf16))

    for head in range(heads):
        kv_near[head].wait_recv()

    @pl.loop(0, heads)
    def _(head):
        attend(0, head)
        attend(1, head)

    number = 3
    for slot in range(1, 4):
        for have in (0, ZH, Y, Y + ZH):
            outw_arrive(have + TP[slot], number)
            number += 1
    for tp in TP:
        for have in (0, ZH, Y, Y + ZH):
            outw_send(have + tp, C, number)
            number += 1

    def kv_forward(head):
        return remote(
            s.kv.at[2, head], s.kv.at[3, head], s.kv_ss.at[2 * heads + head],
            s.kv_rs.at[2 * heads + head], C,
        )

    @pl.loop(0, heads)
    def _(head):
        remote(
            s.kv.at[0, head], s.kv.at[2, head], s.kv_ss.at[head], s.kv_rs.at[head], ZH
        ).wait_recv()
        forward = kv_forward(head)
        forward.start()
        attend(2, head)
        forward.wait_recv()
        attend(3, head)
        value = (s.acc[head] / s.state_l[head]).astype(bf16)
        s.att[head] = value[HEAD_DIM:, :]
        s.logt[head] = s.state_m[head] + jnp.log(s.state_l[head])

    gather_e.far()
    gather_r.far()

    for slot in range(4):
        for head in range(heads):
            s.att_send[slot, head] = s.att[head, :, here(slot)]
    att_copies = [
        remote(
            s.att_send.at[slot], s.att_all.at[my_rank], s.att_ss.at[slot], s.att_rs.at[slot],
            TP[slot],
        )
        for slot in range(1, 4)
    ]
    for copy in att_copies:
        copy.start()
    s.att_all[my_rank] = s.att_send[0]
    number = 15
    for tp in TP:
        for have in (0, ZH, Y, Y + ZH):
            outw_arrive(have + tp + C, number)
            number += 1
    for index in range(32):
        s.out_full[index * count : (index + 1) * count, :] = s.outw[index]
    for slot in range(1, 4):
        where = s.att_all.at[rank(TP[slot])]
        remote(where, where, s.att_ss.at[slot], s.att_rs.at[slot], TP[slot]).wait_recv()
    s.attn[...] = dot_tn(s.att_all[...].reshape(width, rows), s.out_full[...])
    s.middle[...] = s.tokens[...].astype(f32) + mod(gate_one) * s.attn[...]
    normed, inverse = layer_norm(s.middle[...])
    s.normed[...] = normed
    s.inverse[...] = inverse
    s.mix[0, :, :width] = (normed * mod(10) + mod(shift_two)).astype(bf16)
    mix_copies = [
        remote(
            s.mix.at[0, :, pl.ds(0, width)], s.mix.at[slot, :, pl.ds(0, width)],
            s.mix_ss.at[slot], s.mix_rs.at[slot], TP[slot],
        )
        for slot in range(1, 4)
    ]
    for copy in mix_copies:
        copy.start()
    gather_e.second()
    lane = lax.broadcasted_iota(jnp.int32, (rows, BLK), 1)
    ones = jnp.where(lane == 0, 1.0, 0.0).astype(bf16)
    for slot in range(4):
        if slot:
            cot_copies[slot - 1].wait()
        s.mix[slot, :, width:] = ones
        s.branch[here(slot), :] = (mod(gate_two) * s.cot[slot].astype(f32)).astype(bf16)
    gather_e.third()
    gather_r.second()
    gather_e.last()
    for index in range(8):
        s.expand_full[index * per : (index + 1) * per, :] = s.expand[index]
    gather_r.third()
    gather_r.last()
    for index in range(8):
        s.reduce_full[index * per : (index + 1) * per, :] = s.reduce[index]

    gm_copies, mlp_copies = [], []
    for slot in range(4):
        if slot:
            mix_copies[slot - 1].wait_recv()
        hidden = dot_nt(s.mix[slot], s.expand_full[...])
        activated, slope = gelu_pair(hidden)
        activated = activated.astype(bf16)
        s.active[here(slot), :] = activated
        grad_hidden = (dot_nt(s.branch[here(slot), :], s.reduce_full[...]) * slope).astype(bf16)
        s.grad_hid[here(slot), :] = grad_hidden
        gm_part = dot_nn(grad_hidden, s.expand_full[:, :width])
        if slot:
            s.gm_send[slot - 1] = gm_part.astype(bf16)
            copy = remote(
                s.gm_send.at[slot - 1], s.gm_recv.at[slot - 1], s.gm_ss.at[slot],
                s.gm_rs.at[slot], TP[slot],
            )
            copy.start()
            gm_copies.append(copy)
        else:
            s.grad_mixed[...] = gm_part
    for slot in range(4):
        mlp_part = dot_nn(s.active[here(slot), :], s.reduce_full[...])
        if slot:
            s.mlp_send[slot - 1] = mlp_part.astype(bf16)
            copy = remote(
                s.mlp_send.at[slot - 1], s.mlp_recv.at[slot - 1], s.mlp_ss.at[slot],
                s.mlp_rs.at[slot], TP[slot],
            )
            copy.start()
            mlp_copies.append(copy)
        else:
            s.mlp[...] = mlp_part + mod(8)
    for copy in gm_copies:
        copy.wait()
    grad_mixed = (
        s.grad_mixed[...]
        + s.gm_recv[0].astype(f32) + s.gm_recv[1].astype(f32) + s.gm_recv[2].astype(f32)
    )
    cot = s.cotangent[...].astype(f32)
    normed = s.normed[...]
    grad_middle = cot + norm_back(grad_mixed * mod(10), normed, s.inverse[...])
    s.gmid[...] = grad_middle
    grad_attn = (mod(gate_one) * grad_middle).astype(bf16)
    s.gattn[0] = grad_attn
    s.dout_send[...] = dot_nt(s.out_full[...], grad_attn).astype(bf16).reshape(
        s.dout_send.shape
    )
    dout_copies = [
        remote(
            s.dout_send.at[rank(TP[slot])], s.dout_recv.at[slot], s.dout_ss.at[slot],
            s.dout_rs.at[slot], TP[slot],
        )
        for slot in range(1, 4)
    ]
    for copy in dout_copies:
        copy.start()
    s.dout_recv[0] = s.dout_send[my_rank]
    ga_copies = [
        remote(s.gattn.at[0], s.gattn.at[slot], s.ga_ss.at[slot], s.ga_rs.at[slot], TP[slot])
        for slot in range(1, 4)
    ]
    for copy in ga_copies:
        copy.start()
    weighted = column_sum(grad_mixed * normed)
    s.rowsum[2:3, :] = column_sum(grad_middle * s.attn[...])
    s.rowsum[3:4, :] = column_sum(grad_mixed)
    s.rowsum[4:5, :] = weighted * mod(7)
    s.rowsum[7:8, :] = weighted * (1.0 + mod(scale_two))
    s.rowsum[8:9, :] = column_sum(s.branch[here(0), :].astype(f32))

    for index in range(units // BLK):
        lanes = slice(index * BLK, (index + 1) * BLK)
        s.wide[lanes, 0:width] = dot_tn(s.active[:, lanes], s.branch[...])
    for index in range(8):
        s.blocks_r[index] = s.wide[index * per : (index + 1) * per, 0:width].astype(bf16)
    scatter_r = Scatter(lambda slot: s.blocks_r.at[slot], lambda k: s.from_r.at[k], s.sr_ss, s.sr_rs)
    scatter_r.step(C)
    for index in range(units // BLK):
        lanes = slice(index * BLK, (index + 1) * BLK)
        s.wide[lanes, :] = dot_tn(
            s.grad_hid[:, lanes], s.mix[...].reshape(4 * rows, width + BLK)
        )
    for index in range(8):
        s.blocks_e[index] = s.wide[index * per : (index + 1) * per, :].astype(bf16)
    scatter_e = Scatter(lambda slot: s.blocks_e.at[slot], lambda k: s.from_e.at[k], s.se_ss, s.se_rs)
    scatter_e.step(C)
    scatter_r.add(C)
    scatter_r.step(Y)

    s.dout_t[...] = jnp.zeros_like(s.dout_t)
    for slot in range(4):
        if slot:
            dout_copies[slot - 1].wait()
        for head in range(heads):
            s.dout_t[head, HEAD_DIM:, here(slot)] = s.dout_recv[slot, head]
    for head in range(heads):
        value = s.dout_t[head].astype(f32)
        s.dout[head] = value.T.astype(bf16)
        s.rdots[head] = column_sum(value[HEAD_DIM:, :] * s.att[head].astype(f32))
    scatter_e.add(C)
    scatter_e.step(Y)
    s.dq[...] = jnp.zeros_like(s.dq)

    def back(slot, head):
        keys = s.kv[slot, head]
        query = s.query[head]
        shares = jnp.exp(dot_nt(keys, query) - s.logt[head])
        grad_shares = dot_nn(keys, s.dout_t[head])
        grad_scores = (shares * (grad_shares - s.rdots[head])).astype(bf16)
        s.dq[head] += dot_tn(keys, grad_scores)
        return dot_nn(grad_scores, query) + dot_nn(shares.astype(bf16), s.dout[head])

    def dkv_copy(stage, head, offset):
        index = stage * heads + head
        return remote(
            s.dkv_send.at[index], s.dkv_recv.at[index], s.dkv_ss.at[index], s.dkv_rs.at[index],
            offset,
        )

    @pl.loop(0, heads)
    def _(head):
        s.dkv_send[head] = back(3, head).astype(bf16)
        first = dkv_copy(0, head, C)
        first.start()
        part = back(2, head)
        first.wait_recv()
        s.dkv_send[heads + head] = (part + s.dkv_recv[head].astype(f32)).astype(bf16)
        dkv_copy(1, head, ZH).start()

    @pl.loop(0, heads)
    def _(head):
        s.dkv_send[2 * heads + head] = back(1, head).astype(bf16)
        dkv_copy(2, head, C).start()
        s.dkv[head] = back(0, head)
        value = s.dq[head].T * scale
        s.dqkv[head] = turn(value, s.cos[...], -s.sin[...]).astype(bf16)

    for copy in ga_copies:
        copy.wait()
    gattn = s.gattn[...].reshape(4 * rows, width)

    def spread(part, low, of):
        for slot in range(8):
            for row, head, target in head_rows(slot * count, count, low):
                s.blocks_a[slot, part, row : row + 8, :] = s.wide[
                    of * heads * BLK + head * BLK + target
                    : of * heads * BLK + head * BLK + target + 8, 0:width
                ].astype(bf16)

    for head in range(heads):
        s.wide[head * BLK + HEAD_DIM : (head + 1) * BLK, 0:width] = dot_nn(s.att[head], gattn)
    spread(3, False, 0)
    for head in range(heads):
        at = (heads + head) * BLK
        s.wide[at : at + BLK, 0:width] = dot_tn(s.dqkv[head], s.mixed[...])
    spread(0, True, 1)

    def scatter_part(part, ss, rs):
        return Scatter(
            lambda slot: s.blocks_a.at[slot, part],
            lambda k: s.from_a.at[k, part],
            ss, rs,
        )

    scatter_o = scatter_part(3, s.so_ss, s.so_rs)
    scatter_q = scatter_part(0, s.sq_ss, s.sq_rs)
    scatter_k = scatter_part(1, s.sk_ss, s.sk_rs)
    scatter_v = scatter_part(2, s.sv_ss, s.sv_rs)
    scatter_o.step(C)
    scatter_q.step(C)
    scatter_r.add(Y)
    scatter_e.add(Y)
    for copy in mlp_copies:
        copy.wait()
    mlp_branch = (
        s.mlp[...]
        + s.mlp_recv[0].astype(f32) + s.mlp_recv[1].astype(f32) + s.mlp_recv[2].astype(f32)
    )
    s.result[...] = (s.middle[...] + mod(gate_two) * mlp_branch).astype(bf16)
    s.rowsum[5:6, :] = column_sum(s.cotangent[...].astype(f32) * mlp_branch)
    query_part = dot_nn(s.dqkv[0], s.weight[0])
    for head in range(1, heads):
        query_part = query_part + dot_nn(s.dqkv[head], s.weight[head])
    s.part[...] = query_part
    scatter_o.add(C)
    scatter_q.add(C)
    scatter_o.step(Y)
    scatter_q.step(Y)

    for head in range(heads):
        dkv_copy(2, head, C).wait_recv()
        s.dkv[head] += s.dkv_recv[2 * heads + head].astype(f32)
    for head in range(heads):
        dkv_copy(1, head, ZH).wait_recv()
        value = s.dkv[head] + s.dkv_recv[heads + head].astype(f32)
        s.dqkv[heads + head] = turn(value, s.cos[...], -s.sin[...]).astype(bf16)
    scatter_r.step(ZH)
    scatter_e.step(ZH)

    kv_part = s.part[...]
    for head in range(heads, 2 * heads):
        kv_part = kv_part + dot_nn(s.dqkv[head], s.weight[head])
    part_copies = []
    for slot in (3, 2, 1):
        s.part_send[slot - 1] = kv_part[here(slot), :].astype(bf16)
        copy = remote(
            s.part_send.at[slot - 1], s.part_recv.at[slot - 1], s.part_ss.at[slot],
            s.part_rs.at[slot], TP[slot],
        )
        copy.start()
        part_copies.append(copy)
    s.grad_mixed[...] = kv_part[here(0), :]
    for head in range(heads):
        s.wide[head * BLK : (head + 1) * BLK, 0:width] = dot_tn(
            s.dqkv[heads + head], s.mixed[...]
        )
    spread(1, True, 0)
    spread(2, False, 0)
    scatter_k.step(C)
    scatter_v.step(C)
    scatter_o.add(Y)
    scatter_q.add(Y)

    def chunk_back(part, half):
        slot = half * 4 + own % 4
        place_in = 8 * my_rank + slot
        if part < 3:
            number = 32 * part + place_in
            owner, at = number // 3, number % 3
        else:
            owner, at = place_in, 3
        zh = own // 4
        index = part * 2 + half
        source = s.blocks_a.at[slot, part]
        target = s.owned.at[zh, at]
        far = remote_to(
            source, target, s.back_ss.at[index], s.back_rs.at[zh * 4 + at],
            (owner // 16, owner % 16),
        )
        near = pltpu.make_async_copy(source, target, s.local_sem.at[index])
        return far, near, owner == me

    def chunks_back(parts, act):
        for part in parts:
            for half in range(2):
                far, near, stays = chunk_back(part, half)

                @pl.when(jnp.logical_not(stays))
                def _():
                    far.start() if act else far.wait_send()

                @pl.when(stays)
                def _():
                    near.start() if act else near.wait()

    chunks_back((0, 3), True)
    scatter_k.add(C)
    scatter_v.add(C)
    scatter_k.step(Y)
    scatter_v.step(Y)
    for copy in part_copies:
        copy.wait()
    grad_mixed_one = (
        s.grad_mixed[...]
        + s.part_recv[0].astype(f32) + s.part_recv[1].astype(f32) + s.part_recv[2].astype(f32)
    )
    normed_one, inverse_one = layer_norm(s.tokens[...].astype(f32))
    weighted = column_sum(grad_mixed_one * normed_one)
    s.rowsum[0:1, :] = column_sum(grad_mixed_one)
    s.rowsum[1:2, :] = weighted * mod(6)
    s.rowsum[6:7, :] = weighted * (1.0 + mod(scale_one))
    tiles = width // BLK
    s.vec_send[...] = jnp.zeros_like(s.vec_send)
    for owner in range(32):
        for tile in range(2):
            lanes = slice(tile * BLK, (tile + 1) * BLK)
            at = (9 * owner) // 8 + tile
            s.vec_send[owner, 0:1, lanes] = s.rowsum[
                at // tiles : at // tiles + 1, (at % tiles) * BLK : (at % tiles + 1) * BLK
            ]
            at = (3 * owner) // 16 + tile
            if at < tiles:
                s.vec_send[owner, 1:4, lanes] = s.rowsum[6:9, at * BLK : (at + 1) * BLK]

    def sum_copy(offset):
        return remote_to(
            s.vec_send.at[flat(peer_loop(offset))], s.vec_recv.at[offset],
            s.sum_ss.at[offset], s.sum_rs.at[offset], peer_loop(offset),
        )

    @pl.loop(1, 32)
    def _(offset):
        sum_copy(offset).start()

    scatter_k.add(Y)
    scatter_v.add(Y)
    chunks_back((1, 2), True)
    s.grad_tokens[...] = s.gmid[...] + norm_back(
        grad_mixed_one * mod(9), normed_one, inverse_one
    )
    s.vec_recv[0] = s.vec_send[me]

    @pl.loop(1, 32)
    def _(offset):
        sum_copy(offset).wait()

    total = jnp.zeros(s.vec_recv.shape[1:], f32)
    for index in range(32):
        total = total + s.vec_recv[index]
    s.vec_own[0:4, :] = total
    s.vec_own[8:12, :] = total
    s.sums[0:8, :] = pltpu.roll(s.vec_own[0:8, :], (256 - mod_shift) % 256, 1)
    s.sums[8:16, :] = pltpu.roll(s.vec_own[8:16, :], (256 - gain_shift) % 256, 1)
    s.cond_send[...] = exact(s.sums[0:8, 0:piece], s.ada[...].astype(f32), ((1,), (0,)))

    def cond_copy(offset):
        return remote_to(
            s.cond_send.at[pl.ds(0, 1)], s.cond_recv.at[offset], s.cond_ss.at[offset],
            s.cond_rs.at[offset], peer_loop(offset),
        )

    @pl.loop(1, 32)
    def _(offset):
        cond_copy(offset).start()

    s.grad_r[0] = s.blocks_r[own]
    s.grad_e[0] = s.blocks_e[own]
    for index, scatter, target in ((0, scatter_r, s.grad_r), (1, scatter_e, s.grad_e)):
        scatter.copies[ZH][0].wait_recv()
        target[1] = scatter.inbox(6)[...]

    @pl.loop(1, 32)
    def _(offset):
        cond_copy(offset).wait()

    gradient = s.cond_send[0:1, :]
    for index in range(1, 32):
        gradient = gradient + s.cond_recv[index]
    s.grad_cond[...] = gradient

    chunks_back(range(4), False)
    for at in range(4):
        if at < 3:
            number = 3 * me + at
            part, place_in = number // 32, number % 32
        else:
            part, place_in = 3, me
        slot = place_in % 8
        for zh in range(2):
            keeper = flat(member(place_in // 8, zh * 4 + slot % 4))

            @pl.when(keeper != me)
            def _():
                target = s.owned.at[zh, at]
                remote(
                    target, target, s.back_ss.at[0], s.back_rs.at[zh * 4 + at], C
                ).wait_recv()

    for copies in (kv_far, kv_near, mix_copies, outw_sent, att_copies):
        for copy in copies:
            copy.wait_send()
    for gather in (gather_kv, gather_q, gather_e, gather_r):
        gather.finish()
    for scatter in (scatter_e, scatter_r, scatter_o, scatter_q, scatter_k, scatter_v):
        scatter.finish()

    @pl.loop(0, heads)
    def _(head):
        kv_forward(head).wait_send()
        dkv_copy(0, head, C).wait_send()
        dkv_copy(1, head, ZH).wait_send()
        dkv_copy(2, head, C).wait_send()


def finish_kernel(
    result, grad_tokens, grad_cond, sums, grad_e, grad_r, owned, condition,
    result_out, tokens_out, cond_out, ada_out, ada_bias_out, first_out, second_out, project_out,
    output_out, expand_out, expand_bias_out, reduce_out, reduce_bias_out,
):
    width = result.shape[1]
    count = output_out.shape[0]
    piece = ada_out.shape[0]
    result_out[...] = result[...]
    tokens_out[...] = grad_tokens[...]
    cond_out[...] = grad_cond[...]
    first = lax.broadcasted_iota(jnp.int32, (8, piece), 0) == 0
    row = jnp.where(first, sums[0:8, 0:piece], 0.0)
    ada_out[...] = exact(
        row, jnp.broadcast_to(condition[...], (8, condition.shape[1])), ((0,), (0,))
    )
    ada_bias_out[...] = sums[0:1, 0:piece]
    first_out[...] = sums[9:10, 0:count]
    second_out[...] = sums[10:11, 0:count]
    reduce_bias_out[...] = sums[11:12, 0:count]
    both = owned[0].astype(f32) + owned[1].astype(f32)
    project_out[...] = both[0:3]
    output_out[...] = both[3]
    expand = grad_e[0].astype(f32) + grad_e[1].astype(f32)
    expand_out[...] = expand[:, 0:width]
    expand_bias_out[...] = to_row(expand[:, width : width + 1])
    reduce_out[...] = grad_r[0].astype(f32) + grad_r[1].astype(f32)


def rotary_blocks(length):
    half_dim = HEAD_DIM // 2
    frequency = np.exp(
        np.arange(half_dim, dtype=np.float32) * np.float32(-2.0 * math.log(10000.0) / HEAD_DIM)
    ).astype(np.float32)
    angles = (np.arange(length, dtype=np.float32)[:, None] * frequency[None, :]).astype(np.float32)
    cosine, sine = np.cos(angles.astype(np.float64)), np.sin(angles.astype(np.float64))
    one, zero = np.ones((length, HEAD_DIM)), np.zeros((length, HEAD_DIM))
    return (
        np.concatenate([cosine, cosine, one], axis=1).astype(np.float32),
        np.concatenate([-sine, sine, zero], axis=1).astype(np.float32),
    )


def on_device_fast(
    tokens, condition, ada_weight, ada_bias, first_gain, second_gain, project_weight,
    output_weight, expand_weight, expand_bias, reduce_weight, reduce_bias, cotangent,
):
    rows, width = tokens.shape
    group = 4 * rows
    heads = width // HEAD_DIM // 4
    per = reduce_weight.shape[0]
    units = 8 * per
    count = output_weight.shape[0]
    piece = ada_weight.shape[1]
    wide = width + BLK
    cosine, sine = (
        jnp.asarray(table) for table in rotary_blocks(lax.axis_size("blk") * rows)
    )
    line = condition[None, :]
    inputs = dict(
        tokens=tokens, cotangent=cotangent, condition=line, ada=ada_weight.T,
        ada_bias=ada_bias[None, :], first_gain=first_gain[None, :],
        second_gain=second_gain[None, :], reduce_bias=reduce_bias[None, :],
        expand_bias=expand_bias[None, :],
        project_weight=project_weight.T.reshape(3, count, width), output_weight=output_weight,
        expand_weight=expand_weight.T, reduce_weight=reduce_weight, cos_hbm=cosine, sin_hbm=sine,
    )
    outputs = dict(
        result=((rows, width), bf16), grad_tokens=((rows, width), f32),
        grad_cond=((1, line.shape[1]), f32), sums=((16, 256), f32),
        grad_e=((2, per, wide), bf16), grad_r=((2, per, width), bf16),
        owned=((2, 4, count, width), bf16),
    )
    head_block = (group, BLK)
    scratch = dict(
        cos=(head_block, f32), sin=(head_block, f32), vec_own=((16, 256), f32),
        vecs=((32, 4, 256), f32), mod_row=((1, 6 * width), f32), gain_rows=((3, wide), f32),
        mods=((16, width), f32), chunks=((8, 3, count, width), bf16),
        tok=((4, rows, width), bf16), cot=((4, rows, width), bf16),
        expand=((8, per, wide), bf16), reduce=((8, per, width), bf16),
        outw=((32, count, width), bf16), out_full=((width, width), bf16),
        weight=((2 * heads, BLK, width), bf16), mixed=((group, width), bf16),
        query=((heads,) + head_block, bf16), kv=((4, heads) + head_block, bf16),
        state_m=((heads, 1, group), f32), state_l=((heads, 1, group), f32),
        acc=((heads, BLK, group), f32), att=((heads, HEAD_DIM, group), bf16),
        logt=((heads, 1, group), f32), att_send=((4, heads, HEAD_DIM, rows), bf16),
        att_all=((4, heads, HEAD_DIM, rows), bf16), attn=((rows, width), f32),
        middle=((rows, width), f32), normed=((rows, width), f32), inverse=((rows, 1), f32),
        mix=((4, rows, wide), bf16), branch=((group, width), bf16),
        expand_full=((units, wide), bf16), reduce_full=((units, width), bf16),
        active=((group, units), bf16), grad_hid=((group, units), bf16),
        gm_send=((3, rows, width), bf16), gm_recv=((3, rows, width), bf16),
        mlp_send=((3, rows, width), bf16), mlp_recv=((3, rows, width), bf16),
        grad_mixed=((rows, width), f32), mlp=((rows, width), f32), gmid=((rows, width), f32),
        gattn=((4, rows, width), bf16), dout_send=((4, heads, HEAD_DIM, rows), bf16),
        dout_recv=((4, heads, HEAD_DIM, rows), bf16), rowsum=((16, width), f32),
        wide=((units, wide), f32), blocks_r=((8, per, width), bf16),
        blocks_e=((8, per, wide), bf16), blocks_a=((8, 4, count, width), bf16),
        from_r=((7, per, width), bf16), from_e=((7, per, wide), bf16),
        from_a=((6, 4, count, width), bf16), dout_t=((heads, BLK, group), bf16),
        dout=((heads,) + head_block, bf16), rdots=((heads, 1, group), f32),
        dq=((heads, BLK, group), f32), dkv=((heads,) + head_block, f32),
        dkv_send=((3 * heads,) + head_block, bf16), dkv_recv=((3 * heads,) + head_block, bf16),
        dqkv=((2 * heads,) + head_block, bf16), part=((group, width), f32),
        part_send=((3, rows, width), bf16), part_recv=((3, rows, width), bf16),
        vec_send=((32, 4, 256), f32), vec_recv=((32, 4, 256), f32),
        cond_send=((8, line.shape[1]), f32), cond_recv=((32, 1, line.shape[1]), f32),
    )
    semaphores = dict(
        table_sem=8, local_sem=8, chunk_ss=3, chunk_rs=3, vec_ss=32, vec_rs=32, tok_ss=4,
        tok_rs=4, akv_ss=8, akv_rs=8, aq_ss=8, aq_rs=8, e_ss=8, e_rs=8, r_ss=8, r_rs=8, o_ss=31,
        o_rs=31, cot_ss=4, cot_rs=4, kv_ss=3 * heads, kv_rs=3 * heads, att_ss=4, att_rs=4,
        mix_ss=4, mix_rs=4, gm_ss=4, gm_rs=4, mlp_ss=4, mlp_rs=4, dout_ss=4, dout_rs=4, ga_ss=4,
        ga_rs=4, sr_ss=7, sr_rs=7, se_ss=7, se_rs=7, so_ss=6, so_rs=6, sq_ss=6, sq_rs=6, sk_ss=6,
        sk_rs=6, sv_ss=6, sv_rs=6, dkv_ss=3 * heads, dkv_rs=3 * heads, part_ss=4, part_rs=4,
        back_ss=8, back_rs=8, sum_ss=32, sum_rs=32, cond_ss=32, cond_rs=32,
    )
    whole = pl.BlockSpec(memory_space=pltpu.VMEM)
    names = (*inputs, *outputs, *scratch, *semaphores)
    staged = pl.pallas_call(
        partial(block_kernel, names),
        out_shape=tuple(jax.ShapeDtypeStruct(*spec) for spec in outputs.values()),
        in_specs=[
            pl.BlockSpec(memory_space=pl.ANY) if name.endswith("_hbm") else whole
            for name in inputs
        ],
        out_specs=tuple(whole for _ in outputs),
        scratch_shapes=[pltpu.VMEM(*spec) for spec in scratch.values()]
        + [pltpu.SemaphoreType.DMA((number,)) for number in semaphores.values()],
        compiler_params=pltpu.CompilerParams(
            collective_id=1, has_side_effects=True, vmem_limit_bytes=62 * 2**20
        ),
    )(*inputs.values())
    (
        result, grad_tokens, grad_condition, grad_ada, grad_ada_bias, grad_first, grad_second,
        grad_project, grad_output, grad_expand, grad_expand_bias, grad_reduce, grad_reduce_bias,
    ) = pl.pallas_call(
        finish_kernel,
        out_shape=tuple(
            jax.ShapeDtypeStruct(shape, kind)
            for shape, kind in (
                ((rows, width), bf16), ((rows, width), f32), (line.shape, f32),
                ((piece, line.shape[1]), f32), ((1, piece), f32), ((1, count), f32),
                ((1, count), f32), ((3, count, width), f32), ((count, width), f32),
                ((per, width), f32), ((1, per), f32), ((per, width), f32), ((1, count), f32),
            )
        ),
        in_specs=[whole] * 8,
        out_specs=(whole,) * 13,
    )(*staged, line)
    return (
        result,
        grad_tokens,
        grad_condition.reshape(-1),
        grad_ada.T,
        grad_ada_bias.reshape(-1),
        grad_first.reshape(-1),
        grad_second.reshape(-1),
        grad_project.reshape(3 * count, width).T,
        grad_output,
        grad_expand.T,
        grad_expand_bias.reshape(-1),
        grad_reduce,
        grad_reduce_bias.reshape(-1),
    )


def solution(mesh):
    return jax.shard_map(
        on_device_fast if mesh.shape["ulysses"] * mesh.shape["blk"] == 32 else on_device,
        mesh=mesh,
        in_specs=(
            P(("ulysses", "blk"), None),
            P(),
            P(None, ("ulysses", "blk")),
            P(("ulysses", "blk")),
            P(("ulysses", "blk")),
            P(("ulysses", "blk")),
            P(None, ("ulysses", "blk")),
            P(("ulysses", "blk"), None),
            P(None, ("ulysses", "blk")),
            P(("ulysses", "blk")),
            P(("ulysses", "blk"), None),
            P(("ulysses", "blk")),
            P(("ulysses", "blk"), None),
        ),
        out_specs=(
            P(("ulysses", "blk"), None),
            P(("ulysses", "blk"), None),
            P(),
            P(None, ("ulysses", "blk")),
            P(("ulysses", "blk")),
            P(("ulysses", "blk")),
            P(("ulysses", "blk")),
            P(None, ("ulysses", "blk")),
            P(("ulysses", "blk"), None),
            P(None, ("ulysses", "blk")),
            P(("ulysses", "blk")),
            P(("ulysses", "blk"), None),
            P(("ulysses", "blk")),
        ),
        check_vma=False,
    )
```

```python
from functools import partial
import itertools
import math
import types

import jax
import jax.numpy as jnp
import numpy as np
from jax import lax
from jax.experimental import pallas as pl
from jax.experimental.pallas import tpu as pltpu
from jax.sharding import PartitionSpec as P

HEAD_DIM = 64
BOTH = ("ulysses", "blk")


eps = 1e-05
highest = lax.Precision.HIGHEST


def layer_norm(value):
    center = value - jnp.mean(value, axis=-1, keepdims=True)
    inverse = lax.rsqrt(jnp.mean(center * center, axis=-1, keepdims=True) + eps)
    return (center * inverse, inverse)


def norm_back(grad_normed, normed, inverse):
    first = jnp.mean(grad_normed, axis=-1, keepdims=True)
    second = jnp.mean(grad_normed * normed, axis=-1, keepdims=True)
    return inverse * (grad_normed - first - normed * second)


def rotary_tables(positions, head_dim):
    half_dim = head_dim // 2
    frequency = jnp.exp(
        jnp.arange(half_dim, dtype=jnp.float32) * (-2.0 * math.log(10000.0) / head_dim)
    )
    angles = positions[:, None] * frequency[None, :]
    return (jnp.cos(angles)[:, None, :], jnp.sin(angles)[:, None, :])


def rotate(value, cosine, sine):
    half_dim = value.shape[-1] // 2
    first = value[..., :half_dim]
    second = value[..., half_dim:]
    return jnp.concatenate(
        [first * cosine - second * sine, second * cosine + first * sine], axis=-1
    )


def rotate_back(grad_value, cosine, sine):
    half_dim = grad_value.shape[-1] // 2
    first = grad_value[..., :half_dim]
    second = grad_value[..., half_dim:]
    return jnp.concatenate(
        [first * cosine + second * sine, second * cosine - first * sine], axis=-1
    )


def over_blocks(block_step, carried, pieces, key_block):
    length = pieces[0].shape[1]
    complete = length // key_block
    stacked = tuple(
        (
            jnp.moveaxis(
                member.reshape((member.shape[0], complete, key_block) + member.shape[2:]), 1, 0
            )
            for member in pieces
        )
    )
    offsets = jnp.arange(complete, dtype=jnp.int32) * key_block

    def scan_step(carried_in, inputs):
        return (block_step(carried_in, inputs[:-1], inputs[-1]), None)

    carried, unused = lax.scan(scan_step, carried, stacked + (offsets,))
    return carried


def on_device(
    tokens,
    condition,
    ada_weight,
    ada_bias,
    first_gain,
    second_gain,
    project_weight,
    output_weight,
    expand_weight,
    expand_bias,
    reduce_weight,
    reduce_bias,
    cotangent,
):
    row_count = tokens.shape[0]
    model_width = tokens.shape[1]
    cycle_size = lax.axis_size("blk")
    cycle_place = lax.axis_index("blk")
    seq_count = lax.axis_size("ulysses")
    (
        ada_full,
        ada_shift,
        gain_one,
        gain_two,
        project_full,
        output_full,
        expand_full,
        expand_shift,
        reduce_full,
        reduce_shift,
    ) = (
        lax.all_gather(ada_weight, BOTH, axis=1, tiled=True),
        lax.all_gather(ada_bias, BOTH, axis=0, tiled=True),
        lax.all_gather(first_gain, BOTH, axis=0, tiled=True),
        lax.all_gather(second_gain, BOTH, axis=0, tiled=True),
        lax.all_gather(project_weight, BOTH, axis=1, tiled=True),
        lax.all_gather(output_weight, BOTH, axis=0, tiled=True),
        lax.all_gather(expand_weight, BOTH, axis=1, tiled=True),
        lax.all_gather(expand_bias, BOTH, axis=0, tiled=True),
        lax.all_gather(reduce_weight, BOTH, axis=0, tiled=True),
        lax.all_gather(reduce_bias, BOTH, axis=0, tiled=True),
    )
    ada_float = ada_full.astype(jnp.float32)
    modulation = jnp.dot(condition, ada_float, precision=highest) + ada_shift.astype(jnp.float32)
    shift_one, scale_one, gate_one, shift_two, scale_two, gate_two = jnp.split(modulation, 6)
    gain_one_f = gain_one.astype(jnp.float32)
    gain_two_f = gain_two.astype(jnp.float32)
    inputs = tokens.astype(jnp.float32)
    normed_one, inverse_one = layer_norm(inputs)
    gain_first = gain_one_f * (1.0 + scale_one)
    mixed_one = (normed_one * gain_first + shift_one).astype(jnp.bfloat16)
    projected = jnp.dot(mixed_one, project_full, preferred_element_type=jnp.float32)
    packed = projected.astype(jnp.bfloat16).reshape(row_count, 3, model_width)
    regrouped = lax.all_to_all(packed, "ulysses", split_axis=2, concat_axis=0, tiled=True)
    local_rows = regrouped.shape[0]
    local_width = regrouped.shape[2]
    head_count = local_width // HEAD_DIM
    by_seq = regrouped.reshape(seq_count, row_count, 3, local_width)
    positions = cycle_place * row_count + jnp.arange(row_count, dtype=jnp.int32)
    cosine, sine = rotary_tables(positions.astype(jnp.float32), HEAD_DIM)
    query_rot = rotate(
        by_seq[:, :, 0].astype(jnp.float32).reshape(seq_count, row_count, head_count, HEAD_DIM),
        cosine,
        sine,
    ).astype(jnp.bfloat16)
    key_rot = rotate(
        by_seq[:, :, 1].astype(jnp.float32).reshape(seq_count, row_count, head_count, HEAD_DIM),
        cosine,
        sine,
    ).astype(jnp.bfloat16)
    value_flat = by_seq[:, :, 2]
    value_own = value_flat.reshape(seq_count, row_count, head_count, HEAD_DIM)
    key_flat = key_rot.reshape(seq_count, row_count, local_width)
    score_scale = HEAD_DIM ** (-0.5)
    key_block = row_count * -(-512 // row_count)

    def attend_step(carried, pieces, offset):
        maximum, denominator, weighted = carried
        key_rows = pieces[0].reshape(seq_count, -1, head_count, HEAD_DIM)
        value_rows = pieces[1].reshape(seq_count, -1, head_count, HEAD_DIM)
        scores = (
            jnp.einsum("sqhd,skhd->shqk", query_rot, key_rows, preferred_element_type=jnp.float32)
            * score_scale
        )
        new_maximum = jnp.maximum(maximum, jnp.max(scores, axis=-1))
        weights = jnp.exp(scores - new_maximum[..., None])
        factor = jnp.exp(maximum - new_maximum)
        denominator = denominator * factor + jnp.sum(weights, axis=-1)
        weighted = weighted * jnp.transpose(factor, (0, 2, 1))[..., None] + jnp.einsum(
            "shqk,skhd->sqhd",
            weights.astype(jnp.bfloat16),
            value_rows,
            preferred_element_type=jnp.float32,
        )
        return (new_maximum, denominator, weighted)

    start_state = (
        jnp.full((seq_count, head_count, row_count), -1e30, jnp.float32),
        jnp.zeros((seq_count, head_count, row_count), jnp.float32),
        jnp.zeros((seq_count, row_count, head_count, HEAD_DIM), jnp.float32),
    )
    maximum, denominator, weighted = over_blocks(
        attend_step,
        start_state,
        (
            lax.all_gather(key_flat, "blk", axis=1, tiled=True),
            lax.all_gather(value_flat, "blk", axis=1, tiled=True),
        ),
        key_block,
    )
    log_total = maximum + jnp.log(denominator)
    attended = (
        (weighted / jnp.transpose(denominator, (0, 2, 1))[..., None])
        .astype(jnp.bfloat16)
        .reshape(local_rows, local_width)
    )
    attended_tokens = lax.all_to_all(attended, "ulysses", split_axis=0, concat_axis=1, tiled=True)
    attn_branch = jnp.dot(attended_tokens, output_full, preferred_element_type=jnp.float32)
    middle = inputs + gate_one * attn_branch
    normed_two, inverse_two = layer_norm(middle)
    gain_second = gain_two_f * (1.0 + scale_two)
    mixed_two = (normed_two * gain_second + shift_two).astype(jnp.bfloat16)
    hidden = jnp.dot(
        mixed_two, expand_full, preferred_element_type=jnp.float32
    ) + expand_shift.astype(jnp.float32)
    activated, gelu_back = jax.vjp(partial(jax.nn.gelu, approximate=True), hidden)
    activated_low = activated.astype(jnp.bfloat16)
    mlp_branch = jnp.dot(
        activated_low, reduce_full, preferred_element_type=jnp.float32
    ) + reduce_shift.astype(jnp.float32)
    result = (middle + gate_two * mlp_branch).astype(jnp.bfloat16)
    grad_result = cotangent.astype(jnp.float32)
    grad_gate_two = jnp.sum(grad_result * mlp_branch, axis=0)
    grad_branch = (gate_two * grad_result).astype(jnp.bfloat16)
    grad_reduce = jnp.einsum(
        "tf,td->fd", activated_low, grad_branch, preferred_element_type=jnp.float32
    )
    grad_reduce_shift = jnp.sum(grad_branch.astype(jnp.float32), axis=0)
    grad_activated = jnp.einsum(
        "td,fd->tf", grad_branch, reduce_full, preferred_element_type=jnp.float32
    )
    grad_hidden = gelu_back(grad_activated)[0].astype(jnp.bfloat16)
    grad_expand = jnp.einsum(
        "td,tf->df", mixed_two, grad_hidden, preferred_element_type=jnp.float32
    )
    grad_expand_shift = jnp.sum(grad_hidden.astype(jnp.float32), axis=0)
    grad_mixed_two = jnp.einsum(
        "tf,df->td", grad_hidden, expand_full, preferred_element_type=jnp.float32
    )
    grad_shift_two = jnp.sum(grad_mixed_two, axis=0)
    grad_scale_two = jnp.sum(grad_mixed_two * normed_two * gain_two_f, axis=0)
    grad_gain_two = jnp.sum(grad_mixed_two * normed_two * (1.0 + scale_two), axis=0)
    grad_middle = grad_result + norm_back(grad_mixed_two * gain_second, normed_two, inverse_two)
    grad_gate_one = jnp.sum(grad_middle * attn_branch, axis=0)
    grad_attn = (gate_one * grad_middle).astype(jnp.bfloat16)
    grad_output = jnp.einsum(
        "tc,td->cd", attended_tokens, grad_attn, preferred_element_type=jnp.float32
    )
    grad_heads = jnp.einsum(
        "td,cd->tc", grad_attn, output_full, preferred_element_type=jnp.float32
    ).astype(jnp.bfloat16)
    grad_local = lax.all_to_all(grad_heads, "ulysses", split_axis=1, concat_axis=0, tiled=True)
    grad_local_heads = grad_local.reshape(seq_count, row_count, head_count, HEAD_DIM)
    row_dots = jnp.sum(
        (grad_local.astype(jnp.float32) * attended.astype(jnp.float32)).reshape(
            seq_count, row_count, head_count, HEAD_DIM
        ),
        axis=-1,
    )
    row_dots_t = jnp.transpose(row_dots, (0, 2, 1))

    def query_step(carried, pieces, offset):
        key_rows = pieces[0].reshape(seq_count, -1, head_count, HEAD_DIM)
        value_rows = pieces[1].reshape(seq_count, -1, head_count, HEAD_DIM)
        scores = (
            jnp.einsum("sqhd,skhd->shqk", query_rot, key_rows, preferred_element_type=jnp.float32)
            * score_scale
        )
        shares = jnp.exp(scores - log_total[..., None])
        grad_shares = jnp.einsum(
            "sqhd,skhd->shqk", grad_local_heads, value_rows, preferred_element_type=jnp.float32
        )
        grad_scores = (shares * (grad_shares - row_dots_t[..., None])).astype(jnp.bfloat16)
        return (
            carried
            + jnp.einsum(
                "shqk,skhd->sqhd", grad_scores, key_rows, preferred_element_type=jnp.float32
            )
            * score_scale
        )

    grad_query_rot = over_blocks(
        query_step,
        jnp.zeros((seq_count, row_count, head_count, HEAD_DIM), jnp.float32),
        (
            lax.all_gather(key_flat, "blk", axis=1, tiled=True),
            lax.all_gather(value_flat, "blk", axis=1, tiled=True),
        ),
        key_block,
    )

    def key_step(carried, pieces, offset):
        grad_keys_acc, grad_values_acc = carried
        query_rows = pieces[0].reshape(seq_count, -1, head_count, HEAD_DIM)
        slope_rows = pieces[1].reshape(seq_count, -1, head_count, HEAD_DIM)
        scores = (
            jnp.einsum("sqhd,skhd->shqk", query_rows, key_rot, preferred_element_type=jnp.float32)
            * score_scale
        )
        shares = jnp.exp(scores - jnp.transpose(pieces[2], (0, 2, 1))[..., None])
        grad_values_acc = grad_values_acc + jnp.einsum(
            "shqk,sqhd->skhd",
            shares.astype(jnp.bfloat16),
            slope_rows,
            preferred_element_type=jnp.float32,
        )
        grad_shares = jnp.einsum(
            "sqhd,skhd->shqk", slope_rows, value_own, preferred_element_type=jnp.float32
        )
        grad_scores = (
            shares * (grad_shares - jnp.transpose(pieces[3], (0, 2, 1))[..., None])
        ).astype(jnp.bfloat16)
        grad_keys_acc = (
            grad_keys_acc
            + jnp.einsum(
                "shqk,sqhd->skhd", grad_scores, query_rows, preferred_element_type=jnp.float32
            )
            * score_scale
        )
        return (grad_keys_acc, grad_values_acc)

    query_wide = query_rot.reshape(seq_count, row_count, local_width)
    slope_wide = grad_local.reshape(seq_count, row_count, local_width)
    key_init = (
        jnp.zeros((seq_count, row_count, head_count, HEAD_DIM), jnp.float32),
        jnp.zeros((seq_count, row_count, head_count, HEAD_DIM), jnp.float32),
    )
    grad_key_rot, grad_value_sum = over_blocks(
        key_step,
        key_init,
        (
            lax.all_gather(query_wide.astype(jnp.float32), "blk", axis=1, tiled=True).astype(
                jnp.bfloat16
            ),
            lax.all_gather(slope_wide.astype(jnp.float32), "blk", axis=1, tiled=True).astype(
                jnp.bfloat16
            ),
            lax.all_gather(jnp.transpose(log_total, (0, 2, 1)), "blk", axis=1, tiled=True),
            lax.all_gather(row_dots, "blk", axis=1, tiled=True),
        ),
        key_block,
    )
    grad_query = (
        rotate_back(grad_query_rot, cosine, sine)
        .astype(jnp.bfloat16)
        .reshape(local_rows, local_width)
    )
    grad_key = (
        rotate_back(grad_key_rot, cosine, sine)
        .astype(jnp.bfloat16)
        .reshape(local_rows, local_width)
    )
    grad_value = grad_value_sum.astype(jnp.bfloat16).reshape(local_rows, local_width)
    grad_packed = jnp.stack([grad_query, grad_key, grad_value], axis=1)
    grad_tokens_qkv = lax.all_to_all(
        grad_packed, "ulysses", split_axis=0, concat_axis=2, tiled=True
    ).reshape(row_count, 3 * model_width)
    grad_project = jnp.einsum(
        "tc,tk->ck", mixed_one, grad_tokens_qkv, preferred_element_type=jnp.float32
    )
    grad_mixed_one = jnp.einsum(
        "tk,ck->tc", grad_tokens_qkv, project_full, preferred_element_type=jnp.float32
    )
    grad_shift_one = jnp.sum(grad_mixed_one, axis=0)
    grad_scale_one = jnp.sum(grad_mixed_one * normed_one * gain_one_f, axis=0)
    grad_gain_one = jnp.sum(grad_mixed_one * normed_one * (1.0 + scale_one), axis=0)
    grad_input = grad_middle + norm_back(grad_mixed_one * gain_first, normed_one, inverse_one)
    mod_terms = jnp.concatenate(
        [
            grad_shift_one,
            grad_scale_one,
            grad_gate_one,
            grad_shift_two,
            grad_scale_two,
            grad_gate_two,
        ]
    )
    grad_modulation = lax.psum(mod_terms, BOTH)
    grad_condition = jnp.dot(ada_float, grad_modulation, precision=highest)
    piece_width = ada_weight.shape[1]
    flat_index = lax.axis_index("ulysses") * cycle_size + cycle_place
    mod_piece = lax.dynamic_slice_in_dim(grad_modulation, flat_index * piece_width, piece_width, 0)
    grad_ada = condition[:, None] * mod_piece[None, :]
    shards = (
        lax.psum_scatter(grad_gain_one, BOTH, scatter_dimension=0, tiled=True),
        lax.psum_scatter(grad_gain_two, BOTH, scatter_dimension=0, tiled=True),
        lax.psum_scatter(grad_project, BOTH, scatter_dimension=1, tiled=True),
        lax.psum_scatter(grad_output, BOTH, scatter_dimension=0, tiled=True),
        lax.psum_scatter(grad_expand, BOTH, scatter_dimension=1, tiled=True),
        lax.psum_scatter(grad_expand_shift, BOTH, scatter_dimension=0, tiled=True),
        lax.psum_scatter(grad_reduce, BOTH, scatter_dimension=0, tiled=True),
        lax.psum_scatter(grad_reduce_shift, BOTH, scatter_dimension=0, tiled=True),
    )
    return (
        result,
        grad_input,
        grad_condition,
        grad_ada,
        mod_piece,
        shards[0],
        shards[1],
        shards[2],
        shards[3],
        shards[4],
        shards[5],
        shards[6],
        shards[7],
    )


MESH = pl.DeviceIdType.MESH
Y, ZH, ZL, X, C = 16, 8, 4, 2, 1
ATTN = (0, X, ZH, X + ZH)
MLP = (0, X, ZL, X + ZL)
BLK = 128
f32 = jnp.float32
bf16 = jnp.bfloat16


def place():
    blk = lax.axis_index("blk")
    return (lax.axis_index("ulysses"), blk // 8, (blk // 4) % 2, (blk // 2) % 2, blk % 2)


def flip(offset):
    return tuple(
        1 - bit if (offset // weight) % 2 else bit
        for bit, weight in zip(place(), (Y, ZH, ZL, X, C))
    )


def device_at(y, zh, zl, x, c):
    return (y, zh * 8 + zl * 4 + x * 2 + c)


def peer(offset):
    return device_at(*flip(offset))


def peer_loop(offset):
    return device_at(
        *(
            (bit + (offset // weight) % 2) % 2
            for bit, weight in zip(place(), (Y, ZH, ZL, X, C))
        )
    )


def flat(device):
    return device[0] * 16 + device[1]


def share(offset, far):
    y, zh, zl, x, c = flip(offset)
    return c * 4 + y * 2 + (zl if far == ZL else zh)


def rank(offset):
    y, zh, zl, x, c = flip(offset)
    return zh * 2 + x


def member(which, slot):
    return device_at((slot // 2) % 2, which // 2, slot % 2, which % 2, slot // 4)


def greet(offsets):
    barrier = pltpu.get_barrier_semaphore()
    for offset in offsets:
        pl.semaphore_signal(barrier, inc=1, device_id=peer(offset), device_id_type=MESH)
    return lambda: pl.semaphore_wait(barrier, len(offsets))


def remote_to(source, target, send_sem, recv_sem, device):
    return pltpu.make_async_remote_copy(
        src_ref=source,
        dst_ref=target,
        send_sem=send_sem,
        recv_sem=recv_sem,
        device_id=device,
        device_id_type=MESH,
    )


def remote(source, target, send_sem, recv_sem, offset):
    return remote_to(source, target, send_sem, recv_sem, peer(offset))


def dot_nn(a, b):
    return jnp.dot(a, b, preferred_element_type=f32)


def dot_nt(a, b):
    return lax.dot_general(a, b, (((1,), (1,)), ((), ())), preferred_element_type=f32)


def dot_tn(a, b):
    return lax.dot_general(a, b, (((0,), (0,)), ((), ())), preferred_element_type=f32)


def exact(a, b, contract):
    return lax.dot_general(
        a, b, (contract, ((), ())), preferred_element_type=f32, precision=highest
    )


def column_sum(value):
    return jnp.sum(value, axis=0, keepdims=True)


class Gather:
    def __init__(self, view, send_sem, recv_sem, far, pieces):
        own, core = share(0, far), share(C, far)
        z, y = share(far, far), share(Y, far)
        both = share(Y + far, far)
        half = own // 4 * 4
        other = core // 4 * 4
        self.out = [
            remote(view(own, 1), view(own, 1), send_sem.at[1], recv_sem.at[1], Y),
            remote(view(z, 1), view(z, 1), send_sem.at[2], recv_sem.at[2], Y),
            remote(view(half, 4), view(half, 4), send_sem.at[3], recv_sem.at[3], C),
        ]
        self.parts = [
            tuple(
                remote(
                    piece(view(where, 1)), piece(view(where, 1)), send_sem.at[index],
                    recv_sem.at[index], far,
                )
                for where in (own, z)
            )
            for index, piece in zip((0, 4), pieces)
        ]
        self.into = [
            remote(view(where, size), view(where, size), send_sem.at[index], recv_sem.at[index], to)
            for index, where, size, to in ((1, y, 1, Y), (2, both, 1, Y), (3, other, 4, C))
        ]

    def near(self):
        self.out[0].start()

    def far(self, which=0):
        self.parts[which][0].start()

    def second(self):
        for _out, into in self.parts:
            into.wait_recv()
        self.out[1].start()

    def third(self):
        self.into[0].wait_recv()
        self.into[1].wait_recv()
        self.out[2].start()

    def last(self):
        self.into[2].wait_recv()

    def finish(self):
        for copy in self.out:
            copy.wait_send()
        for out, _into in self.parts:
            out.wait_send()


class Spread:
    def __init__(self, view, place_of, order, send_sem, recv_sem):
        self.out, self.into = [], []
        size = 1
        for index, to in enumerate(order):
            mine, other = (place_of(flip(to_where)) // size * size for to_where in (0, to))
            sems = (send_sem.at[index], recv_sem.at[index])
            self.out.append(remote(view(mine, size), view(mine, size), *sems, to))
            self.into.append(remote(view(other, size), view(other, size), *sems, to))
            size *= 2

    def step(self, index):
        if index:
            self.into[index - 1].wait_recv()
        self.out[index].start()

    def last(self):
        self.into[-1].wait_recv()

    def finish(self):
        for copy in self.out:
            copy.wait_send()


class Scatter:
    def __init__(self, view, inbox, send_sem, recv_sem, far):
        self.view, self.inbox = view, inbox
        own = share(0, far)
        core, y, z = share(C, far), share(Y, far), share(far, far)
        self.plan = {
            C: (core // 4 * 4, own // 4 * 4, 4, 0), Y: (y // 2 * 2, own // 2 * 2, 2, 4),
            far: (z, own, 1, 6),
        }
        self.send_sem, self.recv_sem = send_sem, recv_sem
        self.copies = {}

    def step(self, to):
        goes, _stays, size, slot = self.plan[to]
        index = len(self.copies)
        self.copies[to] = remote(
            self.view(goes, size), self.inbox(slot, size), self.send_sem.at[index],
            self.recv_sem.at[index], to,
        )
        self.copies[to].start()

    def add(self, to):
        self.copies[to].wait_recv()
        _goes, stays, size, slot = self.plan[to]
        block = self.view(stays, size)
        block[...] = (
            block[...].astype(f32) + self.inbox(slot, size)[...].astype(f32)
        ).astype(bf16)

    def finish(self):
        for copy in self.copies.values():
            copy.wait_send()


class Total:
    def __init__(self, first, mid, last, send_sem, recv_sem):
        self.first, self.mid, self.last = first, mid, last
        y, zh, zl, x, c = place()
        self.own = (y * 2 + zh, zl * 2 + x, c)
        self.copies = [
            remote(
                ref.at[own], ref.at[own], send_sem.at[3 * which + index],
                recv_sem.at[3 * which + index], to,
            )
            for which, (ref, own, offsets) in enumerate(
                (
                    (first, self.own[0], (Y, ZH, Y + ZH)), (last, self.own[1], (ZL, X, ZL + X)),
                    (mid, self.own[2], (C,)),
                )
            )
            for index, to in enumerate(offsets)
        ]

    def start(self, value):
        self.first[self.own[0]] = value
        for copy in self.copies[0:3]:
            copy.start()

    def second(self):
        for copy in self.copies[0:3]:
            copy.wait_recv()
        self.mid[self.own[2]] = self.first[0] + self.first[1] + self.first[2] + self.first[3]
        self.copies[6].start()

    def third(self):
        self.copies[6].wait_recv()
        self.last[self.own[1]] = self.mid[0] + self.mid[1]
        for copy in self.copies[3:6]:
            copy.start()

    def result(self):
        for copy in self.copies[3:6]:
            copy.wait_recv()
        return self.last[0] + self.last[1] + self.last[2] + self.last[3]

    def finish(self):
        for copy in self.copies:
            copy.wait_send()


def turn(value, cosine, sine):
    lane = lax.broadcasted_iota(jnp.int32, value.shape, 1)
    swapped = jnp.where(
        lane < HEAD_DIM // 2,
        pltpu.roll(value, BLK - HEAD_DIM // 2, 1),
        pltpu.roll(value, HEAD_DIM // 2, 1),
    )
    return value * cosine + swapped * sine


def head_rows(first, count, low):
    for row in range(first, first + count, 8):
        yield row - first, row // HEAD_DIM, row % HEAD_DIM + (0 if low else HEAD_DIM)


def gelu_pair(hidden):
    scale = math.sqrt(2.0 / math.pi)
    square = hidden * hidden
    bend = jnp.tanh(scale * hidden * (1.0 + 0.044715 * square))
    half = 0.5 * (1.0 + bend)
    slope = half + 0.5 * hidden * (1.0 - bend * bend) * (
        scale * (1.0 + 3.0 * 0.044715 * square)
    )
    return hidden * half, slope


def to_column(row):
    count = row.shape[1]
    one = lax.broadcasted_iota(jnp.int32, (count, count), 0)
    two = lax.broadcasted_iota(jnp.int32, (count, count), 1)
    return jnp.sum(jnp.where(one == two, row, 0.0), axis=1, keepdims=True)


def to_row(column):
    count = column.shape[0]
    one = lax.broadcasted_iota(jnp.int32, (count, count), 0)
    two = lax.broadcasted_iota(jnp.int32, (count, count), 1)
    return jnp.sum(jnp.where(one == two, column, 0.0), axis=0, keepdims=True)


def block_kernel(names, *refs):
    s = types.SimpleNamespace(**dict(zip(names, refs)))
    rows, width = s.tokens.shape
    wide = width + BLK
    heads = s.query.shape[0]
    count = s.output_weight_hbm.shape[0]
    per = s.reduce_weight_hbm.shape[0]
    units = 8 * per
    scale = HEAD_DIM ** (-0.5)
    me = flat(peer(0))
    own, own_mlp = share(0, ZL), share(0, ZH)
    my_rank = rank(0)

    def here(slot):
        return slice(slot * rows, (slot + 1) * rows)

    loads = {}

    def load(name, target=None):
        number = len(loads)
        copy = pltpu.make_async_copy(
            getattr(s, name + "_hbm"), getattr(s, name) if target is None else target,
            s.load_sem.at[number],
        )
        copy.start()
        loads[name] = copy

    for name in (
        "ada", "condition", "ada_bias", "first_gain", "second_gain", "reduce_bias",
        "project_weight",
    ):
        load(name)
    def out_place(bits):
        y, zh, zl, x, c = bits
        return c * 16 + y * 8 + zh * 4 + zl * 2 + x

    entered = greet(range(1, 32))
    piece = s.ada.shape[0]
    for name in ("ada", "condition", "ada_bias", "first_gain", "second_gain", "reduce_bias"):
        loads[name].wait()
    for index in range(width // BLK):
        s.adaw[out_place(flip(0)), :, index * BLK : (index + 1) * BLK] = s.ada[
            index * count : (index + 1) * count, :
        ]
    s.vec_own[...] = jnp.zeros_like(s.vec_own)
    s.vec_own[0:8, 0:piece] = exact(
        jnp.broadcast_to(s.condition[...], (8, s.condition.shape[1])),
        s.ada[...].astype(f32), ((1,), (1,)),
    )
    s.vec_own[0:1, 0:piece] += s.ada_bias[...].astype(f32)
    for index, ref in enumerate((s.first_gain, s.second_gain, s.reduce_bias)):
        s.vec_own[8 + index : 9 + index, 0:count] = ref[...].astype(f32)
    mod_shift = (me % 8) * 16
    gain_shift = ((3 * me) % 16) * 8
    y, zh, zl, x, c = place()
    vec_own = y * 16 + x * 8 + c * 4 + zh * 2 + zl
    s.vecs[vec_own, 0:1, :] = pltpu.roll(s.vec_own[0:8, :], mod_shift, 1)[0:1, :]
    s.vecs[vec_own, 1:4, :] = pltpu.roll(s.vec_own[8:16, :], gain_shift, 1)[0:3, :]
    lane = lax.broadcasted_iota(jnp.int32, (rows, BLK), 1)
    ones = jnp.where(lane == 0, 1.0, 0.0).astype(bf16)
    for slot in range(4):
        s.mix[slot, :, width:] = ones
        s.plain[here(slot), width:] = ones
    loads["project_weight"].wait()
    entered()

    def token_copy(have, to):
        slot = ATTN.index(have + to)
        return remote(
            s.tok.at[ATTN.index(have)] if have else s.tokens, s.tok.at[slot],
            s.tok_ss.at[slot], s.tok_rs.at[slot], to,
        )

    token_copies = [token_copy(0, X), token_copy(0, ZH), token_copy(ZH, X)]
    vec_steps = []
    for index, (size, offsets) in enumerate(
        ((1, (ZL, ZH, ZL + ZH)), (4, (C, X, X + C)), (16, (Y,)))
    ):
        where = s.vecs.at[pl.ds(vec_own // size * size, size)]
        vec_steps.append(
            [
                remote(
                    where, where, s.vec_ss.at[3 * index + number], s.vec_rs.at[3 * index + number],
                    to,
                )
                for number, to in enumerate(offsets)
            ]
        )

    def vec_step(index):
        for copy in vec_steps[index - 1] if index else ():
            copy.wait_recv()
        for copy in vec_steps[index] if index < 3 else ():
            copy.start()

    vec_step(0)
    def chunk_out(index):
        number = 3 * me + index
        part, place_in = number // 32, number % 32
        slot = place_in % 8
        device = member(place_in // 8, slot)
        target = s.chunks.at[slot, part]
        far = remote_to(
            s.project_weight.at[index], target, s.chunk_ss.at[index], s.chunk_rs.at[index], device
        )
        near = pltpu.make_async_copy(s.project_weight.at[index], target, s.local_sem.at[index])
        return far, near, flat(device) == me

    for index in range(3):
        far, near, stays = chunk_out(index)

        @pl.when(jnp.logical_not(stays))
        def _():
            far.start()

        @pl.when(stays)
        def _():
            near.start()

    for name in ("tokens", "expand_bias"):
        load(name)
    load("expand_weight", s.er.at[own_mlp, :, pl.ds(0, width)])
    load("reduce_weight", s.er.at[own_mlp, :, pl.ds(wide, width)])

    load("output_weight", s.outw.at[out_place(flip(0))])
    load("cotangent", s.cot.at[0])
    tables = []
    for slot in range(4):
        start = pl.multiple_of(peer(ATTN[slot])[1] * rows, rows)
        copy = pltpu.make_async_copy(
            s.table_hbm.at[pl.ds(start, rows)], s.table.at[pl.ds(slot * rows, rows)],
            s.table_sem.at[slot],
        )
        copy.start()
        tables.append(copy)
    gather_er = Gather(
        lambda slot, size: s.er.at[pl.ds(slot, size)], s.er_ss, s.er_rs, ZH,
        (
            lambda v: v.at[:, :, pl.ds(wide, width)],
            lambda v: v.at[:, :, pl.ds(0, wide)],
        ),
    )
    loads["expand_bias"].wait()
    lane = lax.broadcasted_iota(jnp.int32, (per, BLK), 1)
    s.er[own_mlp, :, width:wide] = jnp.where(
        lane == 0, to_column(s.expand_bias[...].astype(f32)), 0.0
    ).astype(bf16)
    zero = jnp.zeros((HEAD_DIM, width), bf16)
    for head in range(heads):
        s.weight[head, HEAD_DIM:, :] = zero
    s.state_m[...] = jnp.full_like(s.state_m, -1e30)
    s.state_l[...] = jnp.zeros_like(s.state_l)
    s.acc[...] = jnp.zeros_like(s.acc)
    spread_out = Spread(
        lambda slot, size: s.outw.at[pl.ds(slot, size)], out_place, (X, ZL, ZH, Y, C),
        s.o_ss, s.o_rs,
    )
    spread_ada = Spread(
        lambda slot, size: s.adaw.at[pl.ds(slot, size)], out_place, (X, ZL, ZH, Y, C),
        s.ada_ss, s.ada_rs,
    )
    for name in ("expand_weight", "reduce_weight", "output_weight", "cotangent", "tokens"):
        loads[name].wait()
    vec_step(1)
    gather_er.far(0)
    spread_out.step(0)
    spread_ada.step(0)

    for index in range(3):
        far, near, stays = chunk_out(index)

        @pl.when(jnp.logical_not(stays))
        def _():
            far.wait()

        @pl.when(stays)
        def _():
            near.wait()

    gather_a = Gather(
        lambda slot, size: s.chunks.at[pl.ds(slot, size)], s.a_ss, s.a_rs, ZL, (lambda v: v,)
    )
    def cot_copy(have, to):
        slot = MLP.index(have + to)
        return remote(
            s.cot.at[MLP.index(have)], s.cot.at[slot], s.cot_ss.at[slot], s.cot_rs.at[slot], to
        )

    cot_copies = [cot_copy(0, X), cot_copy(0, ZL), cot_copy(ZL, X)]
    gather_a.far()
    gather_a.near()
    token_copies[1].start()
    token_copies[0].start()
    vec_step(2)
    spread_out.step(1)
    spread_ada.step(1)
    gather_a.second()
    cot_copies[1].start()
    vec_step(3)
    s.mod_row[...] = jnp.zeros_like(s.mod_row)
    s.gain_rows[...] = jnp.zeros_like(s.gain_rows)
    for index in range(32):
        y, zh, zl, x, c = ((index // weight) % 2 for weight in (Y, ZH, ZL, X, C))
        found = y * 16 + x * 8 + c * 4 + zh * 2 + zl
        tile = (9 * index) // 8 * BLK
        s.mod_row[0:1, tile : tile + 2 * BLK] += s.vecs[found, 0:1, :]
        tile = (3 * index) // 16 * BLK
        s.gain_rows[0:3, tile : tile + 2 * BLK] += s.vecs[found, 1:4, :]
    shift_one, scale_one, gate_one, shift_two, scale_two, gate_two = range(6)
    for index in range(6):
        s.mods[index : index + 1, :] = s.mod_row[0:1, index * width : (index + 1) * width]
    s.mods[6:9, :] = s.gain_rows[0:3, 0:width]
    s.mods[9:10, :] = s.mods[6:7, :] * (1.0 + s.mods[scale_one : scale_one + 1, :])
    s.mods[10:11, :] = s.mods[7:8, :] * (1.0 + s.mods[scale_two : scale_two + 1, :])

    def mod(index):
        return s.mods[index : index + 1, :]

    for slot in range(4):
        if slot == 1 or slot == 3:
            token_copies[slot - 1].wait_recv()
        if slot == 2:
            token_copies[1].wait_recv()
            token_copies[2].start()
            cot_copies[0].start()
            spread_out.step(2)
            gather_er.far(1)
            gather_er.near()
            gather_a.third()
        source = s.tok[slot] if slot else s.tokens[...]
        normed, _unused = layer_norm(source.astype(f32))
        s.mixed[here(slot), :] = (normed * mod(9) + mod(shift_one)).astype(bf16)
        s.plain[here(slot), 0:width] = normed.astype(bf16)
    def assemble(part, base, low):
        for slot in range(8):
            for row, head, target in head_rows(slot * count, count, low):
                s.weight[base + head, target : target + 8, :] = s.chunks[
                    slot, part, row : row + 8, :
                ]

    gather_a.last()
    assemble(1, heads, True)
    assemble(2, heads, False)
    for copy in tables:
        copy.wait()
    kv_far = [
        remote(s.kv.at[0, head], s.kv.at[2, head], s.kv_ss.at[head], s.kv_rs.at[head], ZL)
        for head in range(heads)
    ]
    kv_near = [
        remote(
            s.kv.at[0, head], s.kv.at[1, head], s.kv_ss.at[heads + head],
            s.kv_rs.at[heads + head], C,
        )
        for head in range(heads)
    ]
    for head in range(heads):
        both = dot_nt(s.mixed[...], s.weight[heads + head]).astype(bf16).astype(f32)
        s.kv[0, head] = turn(both, s.table[:, 0:BLK], s.table[:, BLK:]).astype(bf16)
        kv_far[head].start()
        kv_near[head].start()
    assemble(0, 0, True)
    for head in range(heads):
        query = dot_nt(s.mixed[...], s.weight[head]).astype(bf16).astype(f32)
        query = turn(query, s.table[:, 0:BLK], s.table[:, BLK:]).astype(bf16).astype(f32)
        s.query[head] = (query * scale).astype(bf16)
    cot_copies[1].wait_recv()
    cot_copies[2].start()


    def attend(slot, head):
        keys = s.kv[slot, head]
        scores = dot_nt(keys, s.query[head])
        before = s.state_m[head]
        maximum = jnp.maximum(before, jnp.max(scores, axis=0, keepdims=True))
        weights = jnp.exp(scores - maximum)
        factor = jnp.exp(before - maximum)
        s.state_m[head] = maximum
        s.state_l[head] = s.state_l[head] * factor + column_sum(weights)
        s.acc[head] = s.acc[head] * factor + dot_tn(keys, weights.astype(bf16))

    for head in range(heads):
        kv_near[head].wait_recv()

    @pl.loop(0, heads)
    def _(head):
        attend(0, head)
        attend(1, head)

    def kv_forward(head):
        return remote(
            s.kv.at[2, head], s.kv.at[3, head], s.kv_ss.at[2 * heads + head],
            s.kv_rs.at[2 * heads + head], C,
        )

    @pl.loop(0, heads)
    def _(head):
        remote(
            s.kv.at[0, head], s.kv.at[2, head], s.kv_ss.at[head], s.kv_rs.at[head], ZL
        ).wait_recv()
        forward = kv_forward(head)
        forward.start()

        @pl.when(head == 1)
        def _():
            spread_out.step(3)
            gather_er.second()

        attend(2, head)
        forward.wait_recv()
        attend(3, head)
        value = (s.acc[head] / s.state_l[head]).astype(bf16)
        s.att[head] = value[HEAD_DIM:, :]
        s.logt[head] = s.state_m[head] + jnp.log(s.state_l[head])

    for slot in range(4):
        for head in range(heads):
            s.att_send[slot, head] = s.att[head, :, here(slot)]
    att_copies = [
        remote(
            s.att_send.at[slot], s.att_all.at[my_rank], s.att_ss.at[slot], s.att_rs.at[slot],
            ATTN[slot],
        )
        for slot in range(1, 4)
    ]
    for copy in att_copies:
        copy.start()
    s.att_all[my_rank] = s.att_send[0]
    spread_out.step(4)
    gather_er.third()
    spread_out.last()
    for y in range(2):
        for zh, zl, x, c in itertools.product(range(2), repeat=4):
            at = (y * 16 + zh * 8 + zl * 4 + x * 2 + c) * count
            s.out_full[at : at + count, :] = s.outw[c * 16 + y * 8 + zh * 4 + zl * 2 + x]
    for slot in range(1, 4):
        where = s.att_all.at[rank(ATTN[slot])]
        remote(where, where, s.att_ss.at[slot], s.att_rs.at[slot], ATTN[slot]).wait_recv()
    s.attn[...] = dot_tn(s.att_all[...].reshape(width, rows), s.out_full[...])
    s.middle[...] = s.tokens[...].astype(f32) + mod(gate_one) * s.attn[...]
    normed, inverse = layer_norm(s.middle[...])
    s.normed[...] = normed
    s.inverse[...] = inverse
    s.mix[0, :, :width] = (normed * mod(10) + mod(shift_two)).astype(bf16)
    mix_copies = [
        remote(
            s.mix.at[0, :, pl.ds(0, width)], s.mix.at[slot, :, pl.ds(0, width)],
            s.mix_ss.at[slot], s.mix_rs.at[slot], MLP[slot],
        )
        for slot in range(1, 4)
    ]
    for copy in mix_copies[0:2]:
        copy.start()
    for slot in range(4):
        if slot == 1 or slot == 3:
            cot_copies[slot - 1].wait_recv()
        s.branch[here(slot), :] = (mod(gate_two) * s.cot[slot].astype(f32)).astype(bf16)
    gather_er.last()

    def expand(lanes=wide):
        return s.er[:, :, 0:lanes].reshape(units, lanes)

    def reduce():
        return s.er[:, :, wide:].reshape(units, width)

    spread_ada.step(2)
    gm_copies = [
        remote(
            s.gm_send.at[slot - 1], s.gm_recv.at[slot - 1], s.gm_ss.at[slot], s.gm_rs.at[slot],
            MLP[slot],
        )
        for slot in range(1, 4)
    ]
    for first, last in ((0, 1), (1, 3), (3, 4)):
        for slot in range(first, last):
            if slot:
                mix_copies[slot - 1].wait_recv()
        if first == 1:
            mix_copies[2].start()
        these = slice(first * rows, last * rows)
        mixed_two = s.mix[first:last].reshape((last - first) * rows, wide)
        activated, slope = gelu_pair(dot_nt(mixed_two, expand()))
        s.active[these, :] = activated.astype(bf16)
        grad_hidden = (dot_nt(s.branch[these, :], reduce()) * slope).astype(bf16)
        s.grad_hid[these, :] = grad_hidden
        gm_part = dot_nn(grad_hidden, expand(width))
        for slot in range(first, last):
            part = gm_part[(slot - first) * rows : (slot - first + 1) * rows, :]
            if slot:
                s.gm_send[slot - 1] = part.astype(bf16)
                gm_copies[slot - 1].start()
            else:
                s.grad_mixed[...] = part
    for index in range(units // BLK):
        lanes = slice(index * BLK, (index + 1) * BLK)
        s.wide[lanes, 0:width] = dot_tn(s.active[:, lanes], s.branch[...])
    for index in range(8):
        s.blocks_r[index] = s.wide[index * per : (index + 1) * per, 0:width].astype(bf16)
    scatter_r = Scatter(
        lambda slot, size: s.blocks_r.at[pl.ds(slot, size)],
        lambda slot, size: s.from_r.at[pl.ds(slot, size)], s.sr_ss, s.sr_rs, ZH
    )
    scatter_r.step(C)
    for index in range(units // BLK):
        lanes = slice(index * BLK, (index + 1) * BLK)
        s.wide[lanes, :] = dot_tn(
            s.grad_hid[:, lanes], s.mix[...].reshape(4 * rows, width + BLK)
        )
    scatter_r.add(C)
    scatter_r.step(Y)
    for index in range(8):
        s.blocks_e[index] = s.wide[index * per : (index + 1) * per, :].astype(bf16)
    scatter_e = Scatter(
        lambda slot, size: s.blocks_e.at[pl.ds(slot, size)],
        lambda slot, size: s.from_e.at[pl.ds(slot, size)], s.se_ss, s.se_rs, ZH
    )
    scatter_e.step(C)
    def mlp_copy(slot, number, to):
        return remote(
            s.mlp_send.at[slot], s.mlp_recv.at[number], s.mlp_ss.at[slot], s.mlp_rs.at[number], to
        )

    mlp_copies = [mlp_copy(2, 2, X), mlp_copy(0, 0, X), mlp_copy(1, 1, ZL)]

    def mlp_part(slot):
        return dot_nn(s.active[here(slot), :], reduce())

    s.mlp_send[2] = mlp_part(3).astype(bf16)
    s.mlp_send[0] = mlp_part(1).astype(bf16)
    s.mlp[...] = mlp_part(0) + mod(8)
    s.mlp_near[...] = mlp_part(2)
    for copy in gm_copies:
        copy.wait()
    grad_mixed = (
        s.grad_mixed[...]
        + s.gm_recv[0].astype(f32) + s.gm_recv[1].astype(f32) + s.gm_recv[2].astype(f32)
    )
    cot = s.cot[0].astype(f32)
    normed = s.normed[...]
    grad_middle = cot + norm_back(grad_mixed * mod(10), normed, s.inverse[...])
    s.gmid[...] = grad_middle
    grad_attn = (mod(gate_one) * grad_middle).astype(bf16)
    s.gattn[0] = grad_attn
    s.dout_send[...] = dot_nt(s.out_full[...], grad_attn).astype(bf16).reshape(
        s.dout_send.shape
    )
    dout_copies = [
        remote(
            s.dout_send.at[rank(ATTN[slot])], s.dout_recv.at[slot], s.dout_ss.at[slot],
            s.dout_rs.at[slot], ATTN[slot],
        )
        for slot in range(1, 4)
    ]
    for copy in dout_copies:
        copy.start()
    s.dout_recv[0] = s.dout_send[my_rank]
    def ga_copy(have, to):
        slot = ATTN.index(have + to)
        return remote(
            s.gattn.at[ATTN.index(have)], s.gattn.at[slot], s.ga_ss.at[slot], s.ga_rs.at[slot], to
        )

    ga_copies = [ga_copy(0, X), ga_copy(0, ZH), ga_copy(ZH, X)]
    weighted = column_sum(grad_mixed * normed)
    s.rowsum[2:3, :] = column_sum(grad_middle * s.attn[...])
    s.rowsum[3:4, :] = column_sum(grad_mixed)
    s.rowsum[4:5, :] = weighted * mod(7)
    s.rowsum[7:8, :] = weighted * (1.0 + mod(scale_two))
    s.rowsum[8:9, :] = column_sum(s.branch[here(0), :].astype(f32))
    scatter_e.add(C)
    scatter_e.step(Y)

    s.dout_t[...] = jnp.zeros_like(s.dout_t)
    for slot in range(4):
        if slot:
            dout_copies[slot - 1].wait()
        if slot == 3:
            ga_copies[1].start()
            mlp_copies[0].start()
        for head in range(heads):
            s.dout_t[head, HEAD_DIM:, here(slot)] = s.dout_recv[slot, head]
    for head in range(heads):
        value = s.dout_t[head].astype(f32)
        s.dout[head] = value.T.astype(bf16)
        s.rdots[head] = column_sum(value[HEAD_DIM:, :] * s.att[head].astype(f32))
    scatter_r.add(Y)
    scatter_r.step(ZH)
    ga_copies[0].start()
    mlp_copies[1].start()
    s.dq[...] = jnp.zeros_like(s.dq)

    def back(slot, head):
        keys = s.kv[slot, head]
        query = s.query[head]
        shares = jnp.exp(dot_nt(keys, query) - s.logt[head])
        grad_shares = dot_nn(keys, s.dout_t[head])
        grad_scores = (shares * (grad_shares - s.rdots[head])).astype(bf16)
        s.dq[head] += dot_tn(keys, grad_scores)
        return dot_nn(grad_scores, query) + dot_nn(shares.astype(bf16), s.dout[head])

    def dkv_copy(stage, head, offset):
        index = stage * heads + head
        return remote(
            s.dkv_send.at[index], s.dkv_recv.at[index], s.dkv_ss.at[index], s.dkv_rs.at[index],
            offset,
        )

    @pl.loop(0, heads)
    def _(head):
        s.dkv_send[head] = back(3, head).astype(bf16)
        first = dkv_copy(0, head, C)
        first.start()
        part = back(2, head)
        first.wait_recv()
        s.dkv_send[heads + head] = (part + s.dkv_recv[head].astype(f32)).astype(bf16)
        dkv_copy(1, head, ZL).start()

    scatter_e.add(Y)
    scatter_e.step(ZH)
    spread_ada.step(3)
    mlp_copies[0].wait_recv()
    s.mlp_send[1] = (s.mlp_near[...] + s.mlp_recv[2].astype(f32)).astype(bf16)
    mlp_copies[2].start()

    @pl.loop(0, heads)
    def _(head):
        @pl.when(head == 1)
        def _():
            ga_copies[1].wait_recv()
            ga_copies[2].start()

        s.dkv_send[2 * heads + head] = back(1, head).astype(bf16)
        dkv_copy(2, head, C).start()
        s.dkv[head] = back(0, head)
        value = s.dq[head].T * scale
        s.dqkv[head] = turn(value, s.table[:, 0:BLK], -s.table[:, BLK:]).astype(bf16)

    spread_ada.step(4)
    query_part = dot_nn(s.dqkv[0], s.weight[0])
    for head in range(1, heads):
        query_part = query_part + dot_nn(s.dqkv[head], s.weight[head])
    s.part[...] = query_part
    for head in range(heads):
        dkv_copy(2, head, C).wait_recv()
        s.dkv[head] += s.dkv_recv[2 * heads + head].astype(f32)
    for head in range(heads):
        dkv_copy(1, head, ZL).wait_recv()
        value = s.dkv[head] + s.dkv_recv[heads + head].astype(f32)
        s.dqkv[heads + head] = turn(value, s.table[:, 0:BLK], -s.table[:, BLK:]).astype(bf16)
    kv_part = s.part[...]
    for head in range(heads, 2 * heads):
        kv_part = kv_part + dot_nn(s.dqkv[head], s.weight[head])

    def part_copy(slot, number, to):
        return remote(
            s.part_send.at[slot], s.part_recv.at[number], s.part_ss.at[slot],
            s.part_rs.at[number], to,
        )

    def part_half(slot, number, to, half):
        lines = pl.ds(half * (rows // 2), rows // 2)
        return remote(
            s.part_send.at[slot, lines], s.part_recv.at[number, lines],
            s.part_ss.at[slot + 3 * half], s.part_rs.at[number + 3 * half], to,
        )

    relays = [(part_half(2, 2, X, half), part_half(1, 1, ZH, half)) for half in range(2)]
    part_copies = [part_copy(0, 0, X)]
    s.part_send[2] = kv_part[here(3), :].astype(bf16)
    for half in range(2):
        relays[half][0].start()
    s.part_send[0] = kv_part[here(1), :].astype(bf16)
    s.part[here(2), :] = kv_part[here(2), :]
    s.grad_mixed[...] = kv_part[here(0), :]

    s.norm_sum[...] = jnp.zeros_like(s.norm_sum)
    s.rowsum[9:16, :] = jnp.zeros((7, width), f32)
    for head in range(2 * heads):
        moment = dot_tn(s.dqkv[head], s.plain[...])
        weights = s.weight[head].astype(f32)
        s.norm_sum[0:1, :] += column_sum(weights * moment[:, width : width + 1])
        s.norm_sum[1:2, :] += column_sum(weights * moment[:, 0:width])
    s.rowsum[0:1, :] = s.norm_sum[0:1, :]
    s.rowsum[1:2, :] = s.norm_sum[1:2, :] * mod(6)
    s.rowsum[6:7, :] = s.norm_sum[1:2, :] * (1.0 + mod(scale_one))
    for index in (1, 2):
        mlp_copies[index].wait_recv()
    mlp_branch = s.mlp[...] + s.mlp_recv[0].astype(f32) + s.mlp_recv[1].astype(f32)
    s.result[...] = (s.middle[...] + mod(gate_two) * mlp_branch).astype(bf16)
    s.rowsum[5:6, :] = column_sum(s.cot[0].astype(f32) * mlp_branch)
    spread_ada.last()
    for y in range(2):
        for zh, zl, x, c in itertools.product(range(2), repeat=4):
            at = (y * 16 + zh * 8 + zl * 4 + x * 2 + c) * piece
            for index in range(width // BLK):
                s.ada_full[at + index * count : at + (index + 1) * count, :] = s.adaw[
                    c * 16 + y * 8 + zh * 4 + zl * 2 + x, :,
                    index * BLK : (index + 1) * BLK,
                ]
    high = s.rowsum[0:8, :].astype(bf16)
    low = (s.rowsum[0:8, :] - high.astype(f32)).astype(bf16)
    both = jnp.concatenate([high, low], axis=0)
    terms = jnp.zeros((1, BLK), f32)
    for index in range(6):
        found = dot_nn(both, s.ada_full[index * width : (index + 1) * width, :])
        terms = terms + found[index : index + 1, :] + found[8 + index : 9 + index, :]
    s.rowsum[9:10, 0:BLK] = terms
    totals = Total(s.sum_first, s.sum_mid, s.sum_last, s.sum_ss, s.sum_rs)
    totals.start(s.rowsum[...])

    ga_copies[0].wait_recv()
    ga_copies[2].wait_recv()
    gattn = s.gattn[...].reshape(4 * rows, width)

    def spread(part, low, of):
        for slot in range(8):
            for row, head, target in head_rows(slot * count, count, low):
                s.blocks_a[slot, part, row : row + 8, :] = s.wide[
                    of * heads * BLK + head * BLK + target
                    : of * heads * BLK + head * BLK + target + 8, 0:width
                ].astype(bf16)

    for head in range(heads):
        s.wide[head * BLK : (head + 1) * BLK, 0:width] = dot_tn(s.dqkv[head], s.mixed[...])
        at = (heads + head) * BLK
        s.wide[at : at + BLK, 0:width] = dot_tn(s.dqkv[heads + head], s.mixed[...])
    spread(0, True, 0)
    spread(1, True, 1)
    spread(2, False, 1)
    totals.second()
    for head in range(heads):
        s.wide[head * BLK + HEAD_DIM : (head + 1) * BLK, 0:width] = dot_nn(s.att[head], gattn)
    spread(3, False, 0)
    scatter_a = Scatter(
        lambda slot, size: s.blocks_a.at[pl.ds(slot, size)],
        lambda slot, size: s.from_a.at[pl.ds(slot, size)],
        s.sa_ss, s.sa_rs, ZL,
    )
    scatter_a.step(C)
    totals.third()
    for half in range(2):
        lines = slice(half * (rows // 2), (half + 1) * (rows // 2))
        relays[half][0].wait_recv()
        s.part_send[1, lines, :] = (
            s.part[2 * rows + lines.start : 2 * rows + lines.stop, :]
            + s.part_recv[2, lines, :].astype(f32)
        ).astype(bf16)
        relays[half][1].start()
    part_copies[0].start()
    scatter_a.add(C)
    scatter_a.step(Y)

    def chunk_back(part, half):
        slot = own // 2 * 2 + half
        place_in = 8 * my_rank + slot
        if part < 3:
            number = 32 * part + place_in
            owner, at = number // 3, number % 3
        else:
            owner, at = place_in, 3
        z = own % 2
        index = part * 2 + half
        source = s.blocks_a.at[slot, part]
        target = s.owned.at[z, at]
        far = remote_to(
            source, target, s.back_ss.at[index], s.back_rs.at[z * 4 + at],
            (owner // 16, owner % 16),
        )
        near = pltpu.make_async_copy(source, target, s.local_sem.at[index])
        return far, near, owner == me

    def chunks_back(parts, act):
        for part in parts:
            for half in range(2):
                far, near, stays = chunk_back(part, half)

                @pl.when(jnp.logical_not(stays))
                def _():
                    far.start() if act else far.wait_send()

                @pl.when(stays)
                def _():
                    near.start() if act else near.wait()

    sums = totals.result()
    for index in range(6):
        for tile in range(width // BLK):
            s.tiles[index * (width // BLK) + tile] = sums[
                index : index + 1, tile * BLK : (tile + 1) * BLK
            ]
    for tile in range(width // BLK):
        s.gain_tiles[tile] = sums[6:9, tile * BLK : (tile + 1) * BLK]
    s.gain_tiles[width // BLK] = jnp.zeros((3, BLK), f32)
    s.vec_own[...] = jnp.zeros_like(s.vec_own)
    for tile in range(2):
        lanes = slice(tile * BLK, (tile + 1) * BLK)
        s.vec_own[0:1, lanes] = s.tiles[(9 * me) // 8 + tile]
        s.vec_own[9:12, lanes] = s.gain_tiles[(3 * me) // 16 + tile]
    s.sums[0:8, :] = pltpu.roll(s.vec_own[0:8, :], (256 - mod_shift) % 256, 1)
    s.sums[8:16, :] = pltpu.roll(s.vec_own[8:16, :], (256 - gain_shift) % 256, 1)
    s.grad_cond[...] = sums[9:10, 0:BLK]
    scatter_a.add(Y)
    chunks_back(range(4), True)
    normed_one, inverse_one = layer_norm(s.tokens[...].astype(f32))
    s.grad_r[0] = s.blocks_r[own_mlp]
    s.grad_e[0] = s.blocks_e[own_mlp]
    for scatter, target in ((scatter_r, s.grad_r), (scatter_e, s.grad_e)):
        scatter.copies[ZH].wait_recv()
        target[1] = scatter.inbox(6, 1)[0]
    part_copies[0].wait_recv()
    for half in range(2):
        relays[half][1].wait_recv()
    grad_mixed_one = (
        s.grad_mixed[...] + s.part_recv[0].astype(f32) + s.part_recv[1].astype(f32)
    )
    s.grad_tokens[...] = s.gmid[...] + norm_back(
        grad_mixed_one * mod(9), normed_one, inverse_one
    )

    chunks_back(range(4), False)
    for at in range(4):
        if at < 3:
            number = 3 * me + at
            part, place_in = number // 32, number % 32
        else:
            part, place_in = 3, me
        slot = place_in % 8
        for z in range(2):
            keeper = flat(member(place_in // 8, slot // 2 * 2 + z))

            @pl.when(keeper != me)
            def _():
                target = s.owned.at[z, at]
                remote(
                    target, target, s.back_ss.at[0], s.back_rs.at[z * 4 + at], C
                ).wait_recv()

    for copies in (
        kv_far, kv_near, cot_copies, mix_copies, att_copies, ga_copies, mlp_copies, token_copies,
        part_copies, *relays, *vec_steps,
    ):
        for copy in copies:
            copy.wait_send()
    for group in (
        gather_a, gather_er, spread_out, spread_ada, scatter_e, scatter_r, scatter_a, totals,
    ):
        group.finish()

    @pl.loop(0, heads)
    def _(head):
        kv_forward(head).wait_send()
        dkv_copy(0, head, C).wait_send()
        dkv_copy(1, head, ZL).wait_send()
        dkv_copy(2, head, C).wait_send()


def finish_kernel(
    result, grad_tokens, grad_cond, sums, grad_e, grad_r, owned, condition,
    result_out, tokens_out, cond_out, ada_out, ada_bias_out, first_out, second_out, project_out,
    output_out, expand_out, expand_bias_out, reduce_out, reduce_bias_out,
):
    width = result.shape[1]
    count = output_out.shape[0]
    piece = ada_out.shape[0]
    result_out[...] = result[...]
    tokens_out[...] = grad_tokens[...]
    cond_out[...] = grad_cond[...]
    first = lax.broadcasted_iota(jnp.int32, (8, piece), 0) == 0
    row = jnp.where(first, sums[0:8, 0:piece], 0.0)
    ada_out[...] = exact(
        row, jnp.broadcast_to(condition[...], (8, condition.shape[1])), ((0,), (0,))
    )
    ada_bias_out[...] = sums[0:1, 0:piece]
    first_out[...] = sums[9:10, 0:count]
    second_out[...] = sums[10:11, 0:count]
    reduce_bias_out[...] = sums[11:12, 0:count]
    both = owned[0].astype(f32) + owned[1].astype(f32)
    project_out[...] = both[0:3]
    output_out[...] = both[3]
    expand = grad_e[0].astype(f32) + grad_e[1].astype(f32)
    expand_out[...] = expand[:, 0:width]
    expand_bias_out[...] = to_row(expand[:, width : width + 1])
    reduce_out[...] = grad_r[0].astype(f32) + grad_r[1].astype(f32)


def rotary_blocks(length):
    half_dim = HEAD_DIM // 2
    frequency = np.exp(
        np.arange(half_dim, dtype=np.float32) * np.float32(-2.0 * math.log(10000.0) / HEAD_DIM)
    ).astype(np.float32)
    angles = (np.arange(length, dtype=np.float32)[:, None] * frequency[None, :]).astype(np.float32)
    cosine, sine = np.cos(angles.astype(np.float64)), np.sin(angles.astype(np.float64))
    one, zero = np.ones((length, HEAD_DIM)), np.zeros((length, HEAD_DIM))
    return np.concatenate([cosine, cosine, one, -sine, sine, zero], axis=1).astype(np.float32)


def on_device_fast(
    tokens, condition, ada_weight, ada_bias, first_gain, second_gain, project_weight,
    output_weight, expand_weight, expand_bias, reduce_weight, reduce_bias, cotangent,
):
    rows, width = tokens.shape
    group = 4 * rows
    heads = width // HEAD_DIM // 4
    per = reduce_weight.shape[0]
    units = 8 * per
    count = output_weight.shape[0]
    piece = ada_weight.shape[1]
    wide = width + BLK
    table = jnp.asarray(rotary_blocks(lax.axis_size("blk") * rows))
    line = condition[None, :]
    inputs = dict(
        tokens=tokens, cotangent=cotangent, condition=line, ada=ada_weight.T,
        ada_bias=ada_bias, first_gain=first_gain[None, :],
        second_gain=second_gain[None, :], reduce_bias=reduce_bias[None, :],
        expand_bias=expand_bias[None, :],
        project_weight=project_weight.T.reshape(3, count, width), output_weight=output_weight,
        expand_weight=expand_weight.T, reduce_weight=reduce_weight, table=table,
    )
    outputs = dict(
        result=((rows, width), bf16), grad_tokens=((rows, width), f32),
        grad_cond=((1, line.shape[1]), f32), sums=((16, 256), f32),
        grad_e=((2, per, wide), bf16), grad_r=((2, per, width), bf16),
        owned=((2, 4, count, width), bf16),
    )
    head_block = (group, BLK)
    kept = {
        name: (inputs[name].shape, inputs[name].dtype)
        for name in (
            "tokens", "condition", "ada", "ada_bias", "first_gain", "second_gain", "reduce_bias",
            "expand_bias", "project_weight",
        )
    }
    scratch = dict(
        **kept,
        table=((group, 2 * BLK), f32), vec_own=((16, 256), f32),
        vecs=((32, 4, 256), f32), mod_row=((1, 6 * width), f32), gain_rows=((3, wide), f32),
        mods=((16, width), f32), chunks=((8, 3, count, width), bf16),
        tok=((4, rows, width), bf16), cot=((4, rows, width), bf16),
        er=((8, per, wide + width), bf16),
        outw=((32, count, width), bf16), adaw=((32, count, width), bf16), ada_full=((6 * width, BLK), bf16), out_full=((width, width), bf16),
        weight=((2 * heads, BLK, width), bf16), mixed=((group, width), bf16),
        query=((heads,) + head_block, bf16), kv=((4, heads) + head_block, bf16),
        state_m=((heads, 1, group), f32), state_l=((heads, 1, group), f32),
        acc=((heads, BLK, group), f32), att=((heads, HEAD_DIM, group), bf16),
        logt=((heads, 1, group), f32), att_send=((4, heads, HEAD_DIM, rows), bf16),
        att_all=((4, heads, HEAD_DIM, rows), bf16), attn=((rows, width), f32),
        middle=((rows, width), f32), normed=((rows, width), f32), inverse=((rows, 1), f32),
        mix=((4, rows, wide), bf16), branch=((group, width), bf16),
        active=((group, units), bf16), grad_hid=((group, units), bf16),
        gm_send=((3, rows, width), bf16), gm_recv=((3, rows, width), bf16),
        mlp_send=((3, rows, width), bf16), mlp_recv=((3, rows, width), bf16),
        grad_mixed=((rows, width), f32), mlp=((rows, width), f32), gmid=((rows, width), f32),
        gattn=((4, rows, width), bf16), dout_send=((4, heads, HEAD_DIM, rows), bf16),
        dout_recv=((4, heads, HEAD_DIM, rows), bf16), rowsum=((16, width), f32),
        wide=((units, wide), f32), blocks_r=((8, per, width), bf16),
        blocks_e=((8, per, wide), bf16), blocks_a=((8, 4, count, width), bf16),
        from_r=((7, per, width), bf16), from_e=((7, per, wide), bf16),
        from_a=((6, 4, count, width), bf16), dout_t=((heads, BLK, group), bf16),
        dout=((heads,) + head_block, bf16), rdots=((heads, 1, group), f32),
        dq=((heads, BLK, group), f32), dkv=((heads,) + head_block, f32),
        dkv_send=((3 * heads,) + head_block, bf16), dkv_recv=((3 * heads,) + head_block, bf16),
        dqkv=((2 * heads,) + head_block, bf16), part=((group, width), f32),
        part_send=((3, rows, width), bf16), part_recv=((3, rows, width), bf16),
        plain=((group, wide), bf16), norm_sum=((8, width), f32),
        sum_first=((4, 16, width), f32), sum_mid=((2, 16, width), f32),
        sum_last=((4, 16, width), f32), tiles=((6 * width // BLK, 1, BLK), f32),
        gain_tiles=((width // BLK + 1, 3, BLK), f32),
        mlp_near=((rows, width), f32),
    )
    semaphores = dict(
        load_sem=16, table_sem=4, local_sem=8, chunk_ss=3, chunk_rs=3, vec_ss=7, vec_rs=7,
        tok_ss=4, tok_rs=4, a_ss=4, a_rs=4, er_ss=5, er_rs=5, o_ss=5, o_rs=5, ada_ss=5, ada_rs=5, cot_ss=4, cot_rs=4,
        kv_ss=3 * heads, kv_rs=3 * heads, att_ss=4, att_rs=4, mix_ss=4, mix_rs=4, gm_ss=4,
        gm_rs=4, mlp_ss=4, mlp_rs=4, dout_ss=4, dout_rs=4, ga_ss=4, ga_rs=4, sr_ss=3, sr_rs=3,
        se_ss=3, se_rs=3, sa_ss=2, sa_rs=2, dkv_ss=3 * heads,
        dkv_rs=3 * heads, part_ss=6, part_rs=6, back_ss=8, back_rs=8, sum_ss=7, sum_rs=7,
    )
    whole = pl.BlockSpec(memory_space=pltpu.VMEM)
    names = (*(name + "_hbm" for name in inputs), *outputs, *scratch, *semaphores)
    staged = pl.pallas_call(
        partial(block_kernel, names),
        out_shape=tuple(jax.ShapeDtypeStruct(*spec) for spec in outputs.values()),
        in_specs=[pl.BlockSpec(memory_space=pl.ANY)] * len(inputs),
        out_specs=tuple(whole for _ in outputs),
        scratch_shapes=[pltpu.VMEM(*spec) for spec in scratch.values()]
        + [pltpu.SemaphoreType.DMA((number,)) for number in semaphores.values()],
        compiler_params=pltpu.CompilerParams(
            collective_id=1, has_side_effects=True, vmem_limit_bytes=62 * 2**20
        ),
    )(*inputs.values())
    (
        result, grad_tokens, grad_condition, grad_ada, grad_ada_bias, grad_first, grad_second,
        grad_project, grad_output, grad_expand, grad_expand_bias, grad_reduce, grad_reduce_bias,
    ) = pl.pallas_call(
        finish_kernel,
        out_shape=tuple(
            jax.ShapeDtypeStruct(shape, kind)
            for shape, kind in (
                ((rows, width), bf16), ((rows, width), f32), (line.shape, f32),
                ((piece, line.shape[1]), f32), ((1, piece), f32), ((1, count), f32),
                ((1, count), f32), ((3, count, width), f32), ((count, width), f32),
                ((per, width), f32), ((1, per), f32), ((per, width), f32), ((1, count), f32),
            )
        ),
        in_specs=[whole] * 8,
        out_specs=(whole,) * 13,
    )(*staged, line)
    return (
        result,
        grad_tokens,
        grad_condition.reshape(-1),
        grad_ada.T,
        grad_ada_bias.reshape(-1),
        grad_first.reshape(-1),
        grad_second.reshape(-1),
        grad_project.reshape(3 * count, width).T,
        grad_output,
        grad_expand.T,
        grad_expand_bias.reshape(-1),
        grad_reduce,
        grad_reduce_bias.reshape(-1),
    )


def solution(mesh):
    return jax.shard_map(
        on_device_fast if mesh.shape["ulysses"] * mesh.shape["blk"] == 32 else on_device,
        mesh=mesh,
        in_specs=(
            P(BOTH, None),
            P(),
            P(None, BOTH),
            P(BOTH),
            P(BOTH),
            P(BOTH),
            P(None, BOTH),
            P(BOTH, None),
            P(None, BOTH),
            P(BOTH),
            P(BOTH, None),
            P(BOTH),
            P(BOTH, None),
        ),
        out_specs=(
            P(BOTH, None),
            P(BOTH, None),
            P(),
            P(None, BOTH),
            P(BOTH),
            P(BOTH),
            P(BOTH),
            P(None, BOTH),
            P(BOTH, None),
            P(None, BOTH),
            P(BOTH),
            P(BOTH, None),
            P(BOTH),
        ),
        check_vma=False,
    )
```

```python
from functools import partial
import itertools
import math
import types

import jax
import jax.numpy as jnp
import numpy as np
from jax import lax
from jax.experimental import pallas as pl
from jax.experimental.pallas import tpu as pltpu
from jax.sharding import PartitionSpec as P

HEAD_DIM = 64
BOTH = ("ulysses", "blk")


eps = 1e-05
highest = lax.Precision.HIGHEST


def layer_norm(value):
    center = value - jnp.mean(value, axis=-1, keepdims=True)
    inverse = lax.rsqrt(jnp.mean(center * center, axis=-1, keepdims=True) + eps)
    return (center * inverse, inverse)


def norm_back(grad_normed, normed, inverse):
    first = jnp.mean(grad_normed, axis=-1, keepdims=True)
    second = jnp.mean(grad_normed * normed, axis=-1, keepdims=True)
    return inverse * (grad_normed - first - normed * second)


def rotary_tables(positions, head_dim):
    half_dim = head_dim // 2
    frequency = jnp.exp(
        jnp.arange(half_dim, dtype=jnp.float32) * (-2.0 * math.log(10000.0) / head_dim)
    )
    angles = positions[:, None] * frequency[None, :]
    return (jnp.cos(angles)[:, None, :], jnp.sin(angles)[:, None, :])


def rotate(value, cosine, sine):
    half_dim = value.shape[-1] // 2
    first = value[..., :half_dim]
    second = value[..., half_dim:]
    return jnp.concatenate(
        [first * cosine - second * sine, second * cosine + first * sine], axis=-1
    )


def rotate_back(grad_value, cosine, sine):
    half_dim = grad_value.shape[-1] // 2
    first = grad_value[..., :half_dim]
    second = grad_value[..., half_dim:]
    return jnp.concatenate(
        [first * cosine + second * sine, second * cosine - first * sine], axis=-1
    )


def over_blocks(block_step, carried, pieces, key_block):
    length = pieces[0].shape[1]
    complete = length // key_block
    stacked = tuple(
        (
            jnp.moveaxis(
                member.reshape((member.shape[0], complete, key_block) + member.shape[2:]), 1, 0
            )
            for member in pieces
        )
    )
    offsets = jnp.arange(complete, dtype=jnp.int32) * key_block

    def scan_step(carried_in, inputs):
        return (block_step(carried_in, inputs[:-1], inputs[-1]), None)

    carried, unused = lax.scan(scan_step, carried, stacked + (offsets,))
    return carried


def on_device(
    tokens,
    condition,
    ada_weight,
    ada_bias,
    first_gain,
    second_gain,
    project_weight,
    output_weight,
    expand_weight,
    expand_bias,
    reduce_weight,
    reduce_bias,
    cotangent,
):
    row_count = tokens.shape[0]
    model_width = tokens.shape[1]
    cycle_size = lax.axis_size("blk")
    cycle_place = lax.axis_index("blk")
    seq_count = lax.axis_size("ulysses")
    (
        ada_full,
        ada_shift,
        gain_one,
        gain_two,
        project_full,
        output_full,
        expand_full,
        expand_shift,
        reduce_full,
        reduce_shift,
    ) = (
        lax.all_gather(ada_weight, BOTH, axis=1, tiled=True),
        lax.all_gather(ada_bias, BOTH, axis=0, tiled=True),
        lax.all_gather(first_gain, BOTH, axis=0, tiled=True),
        lax.all_gather(second_gain, BOTH, axis=0, tiled=True),
        lax.all_gather(project_weight, BOTH, axis=1, tiled=True),
        lax.all_gather(output_weight, BOTH, axis=0, tiled=True),
        lax.all_gather(expand_weight, BOTH, axis=1, tiled=True),
        lax.all_gather(expand_bias, BOTH, axis=0, tiled=True),
        lax.all_gather(reduce_weight, BOTH, axis=0, tiled=True),
        lax.all_gather(reduce_bias, BOTH, axis=0, tiled=True),
    )
    ada_float = ada_full.astype(jnp.float32)
    modulation = jnp.dot(condition, ada_float, precision=highest) + ada_shift.astype(jnp.float32)
    shift_one, scale_one, gate_one, shift_two, scale_two, gate_two = jnp.split(modulation, 6)
    gain_one_f = gain_one.astype(jnp.float32)
    gain_two_f = gain_two.astype(jnp.float32)
    inputs = tokens.astype(jnp.float32)
    normed_one, inverse_one = layer_norm(inputs)
    gain_first = gain_one_f * (1.0 + scale_one)
    mixed_one = (normed_one * gain_first + shift_one).astype(jnp.bfloat16)
    projected = jnp.dot(mixed_one, project_full, preferred_element_type=jnp.float32)
    packed = projected.astype(jnp.bfloat16).reshape(row_count, 3, model_width)
    regrouped = lax.all_to_all(packed, "ulysses", split_axis=2, concat_axis=0, tiled=True)
    local_rows = regrouped.shape[0]
    local_width = regrouped.shape[2]
    head_count = local_width // HEAD_DIM
    by_seq = regrouped.reshape(seq_count, row_count, 3, local_width)
    positions = cycle_place * row_count + jnp.arange(row_count, dtype=jnp.int32)
    cosine, sine = rotary_tables(positions.astype(jnp.float32), HEAD_DIM)
    query_rot = rotate(
        by_seq[:, :, 0].astype(jnp.float32).reshape(seq_count, row_count, head_count, HEAD_DIM),
        cosine,
        sine,
    ).astype(jnp.bfloat16)
    key_rot = rotate(
        by_seq[:, :, 1].astype(jnp.float32).reshape(seq_count, row_count, head_count, HEAD_DIM),
        cosine,
        sine,
    ).astype(jnp.bfloat16)
    value_flat = by_seq[:, :, 2]
    value_own = value_flat.reshape(seq_count, row_count, head_count, HEAD_DIM)
    key_flat = key_rot.reshape(seq_count, row_count, local_width)
    score_scale = HEAD_DIM ** (-0.5)
    key_block = row_count * -(-512 // row_count)

    def attend_step(carried, pieces, offset):
        maximum, denominator, weighted = carried
        key_rows = pieces[0].reshape(seq_count, -1, head_count, HEAD_DIM)
        value_rows = pieces[1].reshape(seq_count, -1, head_count, HEAD_DIM)
        scores = (
            jnp.einsum("sqhd,skhd->shqk", query_rot, key_rows, preferred_element_type=jnp.float32)
            * score_scale
        )
        new_maximum = jnp.maximum(maximum, jnp.max(scores, axis=-1))
        weights = jnp.exp(scores - new_maximum[..., None])
        factor = jnp.exp(maximum - new_maximum)
        denominator = denominator * factor + jnp.sum(weights, axis=-1)
        weighted = weighted * jnp.transpose(factor, (0, 2, 1))[..., None] + jnp.einsum(
            "shqk,skhd->sqhd",
            weights.astype(jnp.bfloat16),
            value_rows,
            preferred_element_type=jnp.float32,
        )
        return (new_maximum, denominator, weighted)

    start_state = (
        jnp.full((seq_count, head_count, row_count), -1e30, jnp.float32),
        jnp.zeros((seq_count, head_count, row_count), jnp.float32),
        jnp.zeros((seq_count, row_count, head_count, HEAD_DIM), jnp.float32),
    )
    maximum, denominator, weighted = over_blocks(
        attend_step,
        start_state,
        (
            lax.all_gather(key_flat, "blk", axis=1, tiled=True),
            lax.all_gather(value_flat, "blk", axis=1, tiled=True),
        ),
        key_block,
    )
    log_total = maximum + jnp.log(denominator)
    attended = (
        (weighted / jnp.transpose(denominator, (0, 2, 1))[..., None])
        .astype(jnp.bfloat16)
        .reshape(local_rows, local_width)
    )
    attended_tokens = lax.all_to_all(attended, "ulysses", split_axis=0, concat_axis=1, tiled=True)
    attn_branch = jnp.dot(attended_tokens, output_full, preferred_element_type=jnp.float32)
    middle = inputs + gate_one * attn_branch
    normed_two, inverse_two = layer_norm(middle)
    gain_second = gain_two_f * (1.0 + scale_two)
    mixed_two = (normed_two * gain_second + shift_two).astype(jnp.bfloat16)
    hidden = jnp.dot(
        mixed_two, expand_full, preferred_element_type=jnp.float32
    ) + expand_shift.astype(jnp.float32)
    activated, gelu_back = jax.vjp(partial(jax.nn.gelu, approximate=True), hidden)
    activated_low = activated.astype(jnp.bfloat16)
    mlp_branch = jnp.dot(
        activated_low, reduce_full, preferred_element_type=jnp.float32
    ) + reduce_shift.astype(jnp.float32)
    result = (middle + gate_two * mlp_branch).astype(jnp.bfloat16)
    grad_result = cotangent.astype(jnp.float32)
    grad_gate_two = jnp.sum(grad_result * mlp_branch, axis=0)
    grad_branch = (gate_two * grad_result).astype(jnp.bfloat16)
    grad_reduce = jnp.einsum(
        "tf,td->fd", activated_low, grad_branch, preferred_element_type=jnp.float32
    )
    grad_reduce_shift = jnp.sum(grad_branch.astype(jnp.float32), axis=0)
    grad_activated = jnp.einsum(
        "td,fd->tf", grad_branch, reduce_full, preferred_element_type=jnp.float32
    )
    grad_hidden = gelu_back(grad_activated)[0].astype(jnp.bfloat16)
    grad_expand = jnp.einsum(
        "td,tf->df", mixed_two, grad_hidden, preferred_element_type=jnp.float32
    )
    grad_expand_shift = jnp.sum(grad_hidden.astype(jnp.float32), axis=0)
    grad_mixed_two = jnp.einsum(
        "tf,df->td", grad_hidden, expand_full, preferred_element_type=jnp.float32
    )
    grad_shift_two = jnp.sum(grad_mixed_two, axis=0)
    grad_scale_two = jnp.sum(grad_mixed_two * normed_two * gain_two_f, axis=0)
    grad_gain_two = jnp.sum(grad_mixed_two * normed_two * (1.0 + scale_two), axis=0)
    grad_middle = grad_result + norm_back(grad_mixed_two * gain_second, normed_two, inverse_two)
    grad_gate_one = jnp.sum(grad_middle * attn_branch, axis=0)
    grad_attn = (gate_one * grad_middle).astype(jnp.bfloat16)
    grad_output = jnp.einsum(
        "tc,td->cd", attended_tokens, grad_attn, preferred_element_type=jnp.float32
    )
    grad_heads = jnp.einsum(
        "td,cd->tc", grad_attn, output_full, preferred_element_type=jnp.float32
    ).astype(jnp.bfloat16)
    grad_local = lax.all_to_all(grad_heads, "ulysses", split_axis=1, concat_axis=0, tiled=True)
    grad_local_heads = grad_local.reshape(seq_count, row_count, head_count, HEAD_DIM)
    row_dots = jnp.sum(
        (grad_local.astype(jnp.float32) * attended.astype(jnp.float32)).reshape(
            seq_count, row_count, head_count, HEAD_DIM
        ),
        axis=-1,
    )
    row_dots_t = jnp.transpose(row_dots, (0, 2, 1))

    def query_step(carried, pieces, offset):
        key_rows = pieces[0].reshape(seq_count, -1, head_count, HEAD_DIM)
        value_rows = pieces[1].reshape(seq_count, -1, head_count, HEAD_DIM)
        scores = (
            jnp.einsum("sqhd,skhd->shqk", query_rot, key_rows, preferred_element_type=jnp.float32)
            * score_scale
        )
        shares = jnp.exp(scores - log_total[..., None])
        grad_shares = jnp.einsum(
            "sqhd,skhd->shqk", grad_local_heads, value_rows, preferred_element_type=jnp.float32
        )
        grad_scores = (shares * (grad_shares - row_dots_t[..., None])).astype(jnp.bfloat16)
        return (
            carried
            + jnp.einsum(
                "shqk,skhd->sqhd", grad_scores, key_rows, preferred_element_type=jnp.float32
            )
            * score_scale
        )

    grad_query_rot = over_blocks(
        query_step,
        jnp.zeros((seq_count, row_count, head_count, HEAD_DIM), jnp.float32),
        (
            lax.all_gather(key_flat, "blk", axis=1, tiled=True),
            lax.all_gather(value_flat, "blk", axis=1, tiled=True),
        ),
        key_block,
    )

    def key_step(carried, pieces, offset):
        grad_keys_acc, grad_values_acc = carried
        query_rows = pieces[0].reshape(seq_count, -1, head_count, HEAD_DIM)
        slope_rows = pieces[1].reshape(seq_count, -1, head_count, HEAD_DIM)
        scores = (
            jnp.einsum("sqhd,skhd->shqk", query_rows, key_rot, preferred_element_type=jnp.float32)
            * score_scale
        )
        shares = jnp.exp(scores - jnp.transpose(pieces[2], (0, 2, 1))[..., None])
        grad_values_acc = grad_values_acc + jnp.einsum(
            "shqk,sqhd->skhd",
            shares.astype(jnp.bfloat16),
            slope_rows,
            preferred_element_type=jnp.float32,
        )
        grad_shares = jnp.einsum(
            "sqhd,skhd->shqk", slope_rows, value_own, preferred_element_type=jnp.float32
        )
        grad_scores = (
            shares * (grad_shares - jnp.transpose(pieces[3], (0, 2, 1))[..., None])
        ).astype(jnp.bfloat16)
        grad_keys_acc = (
            grad_keys_acc
            + jnp.einsum(
                "shqk,sqhd->skhd", grad_scores, query_rows, preferred_element_type=jnp.float32
            )
            * score_scale
        )
        return (grad_keys_acc, grad_values_acc)

    query_wide = query_rot.reshape(seq_count, row_count, local_width)
    slope_wide = grad_local.reshape(seq_count, row_count, local_width)
    key_init = (
        jnp.zeros((seq_count, row_count, head_count, HEAD_DIM), jnp.float32),
        jnp.zeros((seq_count, row_count, head_count, HEAD_DIM), jnp.float32),
    )
    grad_key_rot, grad_value_sum = over_blocks(
        key_step,
        key_init,
        (
            lax.all_gather(query_wide.astype(jnp.float32), "blk", axis=1, tiled=True).astype(
                jnp.bfloat16
            ),
            lax.all_gather(slope_wide.astype(jnp.float32), "blk", axis=1, tiled=True).astype(
                jnp.bfloat16
            ),
            lax.all_gather(jnp.transpose(log_total, (0, 2, 1)), "blk", axis=1, tiled=True),
            lax.all_gather(row_dots, "blk", axis=1, tiled=True),
        ),
        key_block,
    )
    grad_query = (
        rotate_back(grad_query_rot, cosine, sine)
        .astype(jnp.bfloat16)
        .reshape(local_rows, local_width)
    )
    grad_key = (
        rotate_back(grad_key_rot, cosine, sine)
        .astype(jnp.bfloat16)
        .reshape(local_rows, local_width)
    )
    grad_value = grad_value_sum.astype(jnp.bfloat16).reshape(local_rows, local_width)
    grad_packed = jnp.stack([grad_query, grad_key, grad_value], axis=1)
    grad_tokens_qkv = lax.all_to_all(
        grad_packed, "ulysses", split_axis=0, concat_axis=2, tiled=True
    ).reshape(row_count, 3 * model_width)
    grad_project = jnp.einsum(
        "tc,tk->ck", mixed_one, grad_tokens_qkv, preferred_element_type=jnp.float32
    )
    grad_mixed_one = jnp.einsum(
        "tk,ck->tc", grad_tokens_qkv, project_full, preferred_element_type=jnp.float32
    )
    grad_shift_one = jnp.sum(grad_mixed_one, axis=0)
    grad_scale_one = jnp.sum(grad_mixed_one * normed_one * gain_one_f, axis=0)
    grad_gain_one = jnp.sum(grad_mixed_one * normed_one * (1.0 + scale_one), axis=0)
    grad_input = grad_middle + norm_back(grad_mixed_one * gain_first, normed_one, inverse_one)
    mod_terms = jnp.concatenate(
        [
            grad_shift_one,
            grad_scale_one,
            grad_gate_one,
            grad_shift_two,
            grad_scale_two,
            grad_gate_two,
        ]
    )
    grad_modulation = lax.psum(mod_terms, BOTH)
    grad_condition = jnp.dot(ada_float, grad_modulation, precision=highest)
    piece_width = ada_weight.shape[1]
    flat_index = lax.axis_index("ulysses") * cycle_size + cycle_place
    mod_piece = lax.dynamic_slice_in_dim(grad_modulation, flat_index * piece_width, piece_width, 0)
    grad_ada = condition[:, None] * mod_piece[None, :]
    shards = (
        lax.psum_scatter(grad_gain_one, BOTH, scatter_dimension=0, tiled=True),
        lax.psum_scatter(grad_gain_two, BOTH, scatter_dimension=0, tiled=True),
        lax.psum_scatter(grad_project, BOTH, scatter_dimension=1, tiled=True),
        lax.psum_scatter(grad_output, BOTH, scatter_dimension=0, tiled=True),
        lax.psum_scatter(grad_expand, BOTH, scatter_dimension=1, tiled=True),
        lax.psum_scatter(grad_expand_shift, BOTH, scatter_dimension=0, tiled=True),
        lax.psum_scatter(grad_reduce, BOTH, scatter_dimension=0, tiled=True),
        lax.psum_scatter(grad_reduce_shift, BOTH, scatter_dimension=0, tiled=True),
    )
    return (
        result,
        grad_input,
        grad_condition,
        grad_ada,
        mod_piece,
        shards[0],
        shards[1],
        shards[2],
        shards[3],
        shards[4],
        shards[5],
        shards[6],
        shards[7],
    )


MESH = pl.DeviceIdType.MESH
Y, ZH, ZL, X, C = 16, 8, 4, 2, 1
ATTN = (0, X, ZH, X + ZH)
MLP = (0, X, ZL, X + ZL)
BLK = 128
f32 = jnp.float32
bf16 = jnp.bfloat16


def place():
    blk = lax.axis_index("blk")
    return (lax.axis_index("ulysses"), blk // 8, (blk // 4) % 2, (blk // 2) % 2, blk % 2)


def flip(offset):
    return tuple(
        1 - bit if (offset // weight) % 2 else bit
        for bit, weight in zip(place(), (Y, ZH, ZL, X, C))
    )


def device_at(y, zh, zl, x, c):
    return (y, zh * 8 + zl * 4 + x * 2 + c)


def peer(offset):
    return device_at(*flip(offset))


def peer_loop(offset):
    return device_at(
        *(
            (bit + (offset // weight) % 2) % 2
            for bit, weight in zip(place(), (Y, ZH, ZL, X, C))
        )
    )


def flat(device):
    return device[0] * 16 + device[1]


def share(offset, far):
    y, zh, zl, x, c = flip(offset)
    return c * 4 + y * 2 + (zl if far == ZL else zh)


def rank(offset):
    y, zh, zl, x, c = flip(offset)
    return zh * 2 + x


def member(which, slot):
    return device_at((slot // 2) % 2, which // 2, slot % 2, which % 2, slot // 4)


def greet(offsets):
    barrier = pltpu.get_barrier_semaphore()
    for offset in offsets:
        pl.semaphore_signal(barrier, inc=1, device_id=peer(offset), device_id_type=MESH)
    return lambda: pl.semaphore_wait(barrier, len(offsets))


def remote_to(source, target, send_sem, recv_sem, device):
    return pltpu.make_async_remote_copy(
        src_ref=source,
        dst_ref=target,
        send_sem=send_sem,
        recv_sem=recv_sem,
        device_id=device,
        device_id_type=MESH,
    )


def remote(source, target, send_sem, recv_sem, offset):
    return remote_to(source, target, send_sem, recv_sem, peer(offset))


def dot_nn(a, b):
    return jnp.dot(a, b, preferred_element_type=f32)


def dot_nt(a, b):
    return lax.dot_general(a, b, (((1,), (1,)), ((), ())), preferred_element_type=f32)


def dot_tn(a, b):
    return lax.dot_general(a, b, (((0,), (0,)), ((), ())), preferred_element_type=f32)


def exact(a, b, contract):
    return lax.dot_general(
        a, b, (contract, ((), ())), preferred_element_type=f32, precision=highest
    )


def column_sum(value):
    return jnp.sum(value, axis=0, keepdims=True)


class Gather:
    def __init__(self, view, send_sem, recv_sem, far, pieces):
        own, core = share(0, far), share(C, far)
        z, y = share(far, far), share(Y, far)
        both = share(Y + far, far)
        half = own // 4 * 4
        other = core // 4 * 4
        self.out = [
            remote(view(own, 1), view(own, 1), send_sem.at[1], recv_sem.at[1], Y),
            remote(view(z, 1), view(z, 1), send_sem.at[2], recv_sem.at[2], Y),
            remote(view(half, 4), view(half, 4), send_sem.at[3], recv_sem.at[3], C),
        ]
        self.parts = [
            tuple(
                remote(
                    piece(view(where, 1)), piece(view(where, 1)), send_sem.at[index],
                    recv_sem.at[index], far,
                )
                for where in (own, z)
            )
            for index, piece in zip((0, 4), pieces)
        ]
        self.into = [
            remote(view(where, size), view(where, size), send_sem.at[index], recv_sem.at[index], to)
            for index, where, size, to in ((1, y, 1, Y), (2, both, 1, Y), (3, other, 4, C))
        ]

    def near(self):
        self.out[0].start()

    def far(self, which=0):
        self.parts[which][0].start()

    def second(self):
        for _out, into in self.parts:
            into.wait_recv()
        self.out[1].start()

    def third(self):
        self.into[0].wait_recv()
        self.into[1].wait_recv()
        self.out[2].start()

    def last(self):
        self.into[2].wait_recv()

    def finish(self):
        for copy in self.out:
            copy.wait_send()
        for out, _into in self.parts:
            out.wait_send()


class Spread:
    def __init__(self, view, place_of, order, send_sem, recv_sem):
        self.out, self.into = [], []
        size = 1
        for index, to in enumerate(order):
            mine, other = (place_of(flip(to_where)) // size * size for to_where in (0, to))
            sems = (send_sem.at[index], recv_sem.at[index])
            self.out.append(remote(view(mine, size), view(mine, size), *sems, to))
            self.into.append(remote(view(other, size), view(other, size), *sems, to))
            size *= 2

    def step(self, index):
        if index:
            self.into[index - 1].wait_recv()
        self.out[index].start()

    def last(self):
        self.into[-1].wait_recv()

    def finish(self):
        for copy in self.out:
            copy.wait_send()


class Scatter:
    def __init__(self, view, inbox, send_sem, recv_sem, far):
        self.view, self.inbox = view, inbox
        own = share(0, far)
        core, y, z = share(C, far), share(Y, far), share(far, far)
        self.plan = {
            C: (core // 4 * 4, own // 4 * 4, 4, 0), Y: (y // 2 * 2, own // 2 * 2, 2, 4),
            far: (z, own, 1, 6),
        }
        self.send_sem, self.recv_sem = send_sem, recv_sem
        self.copies = {}

    def step(self, to):
        goes, _stays, size, slot = self.plan[to]
        index = len(self.copies)
        self.copies[to] = remote(
            self.view(goes, size), self.inbox(slot, size), self.send_sem.at[index],
            self.recv_sem.at[index], to,
        )
        self.copies[to].start()

    def add(self, to):
        self.copies[to].wait_recv()
        _goes, stays, size, slot = self.plan[to]
        block = self.view(stays, size)
        block[...] = (
            block[...].astype(f32) + self.inbox(slot, size)[...].astype(f32)
        ).astype(bf16)

    def finish(self):
        for copy in self.copies.values():
            copy.wait_send()


class Total:
    def __init__(self, halves, inbox, first, last, send_sem, recv_sem):
        self.halves, self.inbox, self.first, self.last = halves, inbox, first, last
        y, zh, zl, x, c = place()
        self.core = c
        self.own = (y * 2 + zh, zl * 2 + x)
        sems = [(send_sem.at[index], recv_sem.at[index]) for index in range(8)]
        self.copies = [
            remote(ref.at[own], ref.at[own], *sems[3 * which + index], to)
            for which, (ref, own, offsets) in enumerate(
                ((first, self.own[0], (Y, ZH, Y + ZH)), (last, self.own[1], (ZL, X, ZL + X)))
            )
            for index, to in enumerate(offsets)
        ]
        self.copies.append(remote(halves.at[1 - c], inbox.at[0], *sems[6], C))
        self.copies.append(remote(inbox.at[1 + c], inbox.at[1 + c], *sems[7], C))

    def start(self):
        self.copies[6].start()

    def second(self):
        self.copies[6].wait_recv()
        self.first[self.own[0]] = self.halves[self.core] + self.inbox[0]
        for copy in self.copies[0:3]:
            copy.start()

    def third(self):
        for copy in self.copies[0:3]:
            copy.wait_recv()
        self.last[self.own[1]] = (
            self.first[0] + self.first[1] + self.first[2] + self.first[3]
        )
        for copy in self.copies[3:6]:
            copy.start()

    def fourth(self):
        for copy in self.copies[3:6]:
            copy.wait_recv()
        self.inbox[1 + self.core] = self.last[0] + self.last[1] + self.last[2] + self.last[3]
        self.copies[7].start()

    def result(self):
        self.copies[7].wait_recv()
        return jnp.concatenate([self.inbox[1], self.inbox[2]], axis=0)

    def finish(self):
        for copy in self.copies:
            copy.wait_send()


def turn(value, cosine, sine):
    lane = lax.broadcasted_iota(jnp.int32, value.shape, 1)
    swapped = jnp.where(
        lane < HEAD_DIM // 2,
        pltpu.roll(value, BLK - HEAD_DIM // 2, 1),
        pltpu.roll(value, HEAD_DIM // 2, 1),
    )
    return value * cosine + swapped * sine


def head_rows(first, count, low):
    for row in range(first, first + count, 8):
        yield row - first, row // HEAD_DIM, row % HEAD_DIM + (0 if low else HEAD_DIM)


def gelu_pair(hidden):
    scale = math.sqrt(2.0 / math.pi)
    square = hidden * hidden
    bend = jnp.tanh(scale * hidden * (1.0 + 0.044715 * square))
    half = 0.5 * (1.0 + bend)
    slope = half + 0.5 * hidden * (1.0 - bend * bend) * (
        scale * (1.0 + 3.0 * 0.044715 * square)
    )
    return hidden * half, slope


def to_column(row):
    count = row.shape[1]
    one = lax.broadcasted_iota(jnp.int32, (count, count), 0)
    two = lax.broadcasted_iota(jnp.int32, (count, count), 1)
    return jnp.sum(jnp.where(one == two, row, 0.0), axis=1, keepdims=True)


def to_row(column):
    count = column.shape[0]
    one = lax.broadcasted_iota(jnp.int32, (count, count), 0)
    two = lax.broadcasted_iota(jnp.int32, (count, count), 1)
    return jnp.sum(jnp.where(one == two, column, 0.0), axis=0, keepdims=True)


def block_kernel(names, *refs):
    s = types.SimpleNamespace(**dict(zip(names, refs)))
    rows, width = s.tokens.shape
    wide = width + BLK
    heads = s.query.shape[0]
    count = s.output_weight_hbm.shape[0]
    per = s.reduce_weight_hbm.shape[0]
    units = 8 * per
    scale = HEAD_DIM ** (-0.5)
    me = flat(peer(0))
    own, own_mlp = share(0, ZL), share(0, ZH)
    my_rank = rank(0)

    def here(slot):
        return slice(slot * rows, (slot + 1) * rows)

    loads = {}

    def load(name, target=None):
        number = len(loads)
        copy = pltpu.make_async_copy(
            getattr(s, name + "_hbm"), getattr(s, name) if target is None else target,
            s.load_sem.at[number],
        )
        copy.start()
        loads[name] = copy

    for name in (
        "ada", "condition", "ada_bias", "first_gain", "second_gain", "reduce_bias",
        "project_weight",
    ):
        load(name)
    def out_place(bits):
        y, zh, zl, x, c = bits
        return c * 16 + y * 8 + zh * 4 + zl * 2 + x

    entered = greet(range(1, 32))
    piece = s.ada.shape[0]
    for name in ("ada", "condition", "ada_bias", "first_gain", "second_gain", "reduce_bias"):
        loads[name].wait()
    for index in range(width // BLK):
        s.adaw[out_place(flip(0)), :, index * BLK : (index + 1) * BLK] = s.ada[
            index * count : (index + 1) * count, :
        ]
    s.vec_own[...] = jnp.zeros_like(s.vec_own)
    s.vec_own[0:8, 0:piece] = exact(
        jnp.broadcast_to(s.condition[...], (8, s.condition.shape[1])),
        s.ada[...].astype(f32), ((1,), (1,)),
    )
    s.vec_own[0:1, 0:piece] += s.ada_bias[...].astype(f32)
    for index, ref in enumerate((s.first_gain, s.second_gain, s.reduce_bias)):
        s.vec_own[8 + index : 9 + index, 0:count] = ref[...].astype(f32)
    mod_shift = (me % 8) * 16
    gain_shift = ((3 * me) % 16) * 8
    y, zh, zl, x, c = place()
    vec_own = y * 16 + x * 8 + c * 4 + zh * 2 + zl
    s.vecs[vec_own, 0:1, :] = pltpu.roll(s.vec_own[0:8, :], mod_shift, 1)[0:1, :]
    s.vecs[vec_own, 1:4, :] = pltpu.roll(s.vec_own[8:16, :], gain_shift, 1)[0:3, :]
    lane = lax.broadcasted_iota(jnp.int32, (rows, BLK), 1)
    ones = jnp.where(lane == 0, 1.0, 0.0).astype(bf16)
    for slot in range(4):
        s.mix[slot, :, width:] = ones
        s.plain[here(slot), width:] = ones
    loads["project_weight"].wait()
    entered()

    def token_copy(have, to):
        slot = ATTN.index(have + to)
        return remote(
            s.tok.at[ATTN.index(have)] if have else s.tokens, s.tok.at[slot],
            s.tok_ss.at[slot], s.tok_rs.at[slot], to,
        )

    token_copies = [token_copy(0, X), token_copy(0, ZH), token_copy(ZH, X)]
    vec_steps = []
    for index, (size, offsets) in enumerate(
        ((1, (ZL, ZH, ZL + ZH)), (4, (C, X, X + C)), (16, (Y,)))
    ):
        where = s.vecs.at[pl.ds(vec_own // size * size, size)]
        vec_steps.append(
            [
                remote(
                    where, where, s.vec_ss.at[3 * index + number], s.vec_rs.at[3 * index + number],
                    to,
                )
                for number, to in enumerate(offsets)
            ]
        )

    def vec_step(index):
        for copy in vec_steps[index - 1] if index else ():
            copy.wait_recv()
        for copy in vec_steps[index] if index < 3 else ():
            copy.start()

    vec_step(0)
    def chunk_out(index):
        number = 3 * me + index
        part, place_in = number // 32, number % 32
        slot = place_in % 8
        device = member(place_in // 8, slot)
        target = s.chunks.at[slot, part]
        far = remote_to(
            s.project_weight.at[index], target, s.chunk_ss.at[index], s.chunk_rs.at[index], device
        )
        near = pltpu.make_async_copy(s.project_weight.at[index], target, s.local_sem.at[index])
        return far, near, flat(device) == me

    for index in range(3):
        far, near, stays = chunk_out(index)

        @pl.when(jnp.logical_not(stays))
        def _():
            far.start()

        @pl.when(stays)
        def _():
            near.start()

    for name in ("tokens", "expand_bias"):
        load(name)
    load("expand_weight", s.er.at[own_mlp, :, pl.ds(0, width)])
    load("reduce_weight", s.er.at[own_mlp, :, pl.ds(wide, width)])

    load("output_weight", s.outw.at[out_place(flip(0))])
    load("cotangent", s.cot.at[0])
    tables = []
    for slot in range(4):
        start = pl.multiple_of(peer(ATTN[slot])[1] * rows, rows)
        copy = pltpu.make_async_copy(
            s.table_hbm.at[pl.ds(start, rows)], s.table.at[pl.ds(slot * rows, rows)],
            s.table_sem.at[slot],
        )
        copy.start()
        tables.append(copy)
    gather_er = Gather(
        lambda slot, size: s.er.at[pl.ds(slot, size)], s.er_ss, s.er_rs, ZH,
        (
            lambda v: v.at[:, :, pl.ds(wide, width)],
            lambda v: v.at[:, :, pl.ds(0, wide)],
        ),
    )
    loads["expand_bias"].wait()
    lane = lax.broadcasted_iota(jnp.int32, (per, BLK), 1)
    s.er[own_mlp, :, width:wide] = jnp.where(
        lane == 0, to_column(s.expand_bias[...].astype(f32)), 0.0
    ).astype(bf16)
    zero = jnp.zeros((HEAD_DIM, width), bf16)
    for head in range(heads):
        s.weight[head, HEAD_DIM:, :] = zero
    s.state_m[...] = jnp.full_like(s.state_m, -1e30)
    s.state_l[...] = jnp.zeros_like(s.state_l)
    s.acc[...] = jnp.zeros_like(s.acc)
    spread_out = Spread(
        lambda slot, size: s.outw.at[pl.ds(slot, size)], out_place, (X, ZL, ZH, Y, C),
        s.o_ss, s.o_rs,
    )
    spread_ada = Spread(
        lambda slot, size: s.adaw.at[pl.ds(slot, size)], out_place, (X, ZL, ZH, Y, C),
        s.ada_ss, s.ada_rs,
    )
    for name in ("expand_weight", "reduce_weight", "output_weight", "cotangent", "tokens"):
        loads[name].wait()
    vec_step(1)
    spread_out.step(0)
    spread_ada.step(0)

    for index in range(3):
        far, near, stays = chunk_out(index)

        @pl.when(jnp.logical_not(stays))
        def _():
            far.wait()

        @pl.when(stays)
        def _():
            near.wait()

    gather_a = Gather(
        lambda slot, size: s.chunks.at[pl.ds(slot, size)], s.a_ss, s.a_rs, ZL, (lambda v: v,)
    )
    def cot_copy(have, to):
        slot = MLP.index(have + to)
        return remote(
            s.cot.at[MLP.index(have)], s.cot.at[slot], s.cot_ss.at[slot], s.cot_rs.at[slot], to
        )

    cot_copies = [cot_copy(0, X), cot_copy(0, ZL), cot_copy(ZL, X)]
    gather_a.far()
    gather_a.near()
    token_copies[1].start()
    token_copies[0].start()
    vec_step(2)
    spread_out.step(1)
    spread_ada.step(1)
    gather_a.second()
    cot_copies[1].start()
    vec_step(3)
    s.mod_row[...] = jnp.zeros_like(s.mod_row)
    s.gain_rows[...] = jnp.zeros_like(s.gain_rows)
    for index in range(32):
        y, zh, zl, x, c = ((index // weight) % 2 for weight in (Y, ZH, ZL, X, C))
        found = y * 16 + x * 8 + c * 4 + zh * 2 + zl
        tile = (9 * index) // 8 * BLK
        s.mod_row[0:1, tile : tile + 2 * BLK] += s.vecs[found, 0:1, :]
        tile = (3 * index) // 16 * BLK
        s.gain_rows[0:3, tile : tile + 2 * BLK] += s.vecs[found, 1:4, :]
    shift_one, scale_one, gate_one, shift_two, scale_two, gate_two = range(6)
    for index in range(6):
        s.mods[index : index + 1, :] = s.mod_row[0:1, index * width : (index + 1) * width]
    s.mods[6:9, :] = s.gain_rows[0:3, 0:width]
    s.mods[9:10, :] = s.mods[6:7, :] * (1.0 + s.mods[scale_one : scale_one + 1, :])
    s.mods[10:11, :] = s.mods[7:8, :] * (1.0 + s.mods[scale_two : scale_two + 1, :])

    def mod(index):
        return s.mods[index : index + 1, :]

    for slot in range(4):
        if slot == 1 or slot == 3:
            token_copies[slot - 1].wait_recv()
        if slot == 2:
            token_copies[1].wait_recv()
            token_copies[2].start()
            cot_copies[0].start()
            spread_out.step(2)
            gather_er.far(0)
            gather_er.near()
            gather_a.third()
        source = s.tok[slot] if slot else s.tokens[...]
        normed, _unused = layer_norm(source.astype(f32))
        s.mixed[here(slot), :] = (normed * mod(9) + mod(shift_one)).astype(bf16)
        s.plain[here(slot), 0:width] = normed.astype(bf16)
    def assemble(part, base, low):
        for slot in range(8):
            for row, head, target in head_rows(slot * count, count, low):
                s.weight[base + head, target : target + 8, :] = s.chunks[
                    slot, part, row : row + 8, :
                ]

    gather_er.far(1)
    gather_a.last()
    assemble(1, heads, True)
    assemble(2, heads, False)
    for copy in tables:
        copy.wait()
    kv_far = [
        remote(s.kv.at[0, head], s.kv.at[2, head], s.kv_ss.at[head], s.kv_rs.at[head], ZL)
        for head in range(heads)
    ]
    kv_near = [
        remote(
            s.kv.at[0, head], s.kv.at[1, head], s.kv_ss.at[heads + head],
            s.kv_rs.at[heads + head], C,
        )
        for head in range(heads)
    ]
    for head in range(heads):
        both = dot_nt(s.mixed[...], s.weight[heads + head]).astype(bf16).astype(f32)
        s.kv[0, head] = turn(both, s.table[:, 0:BLK], s.table[:, BLK:]).astype(bf16)
        kv_far[head].start()
        kv_near[head].start()
    assemble(0, 0, True)
    for head in range(heads):
        query = dot_nt(s.mixed[...], s.weight[head]).astype(bf16).astype(f32)
        query = turn(query, s.table[:, 0:BLK], s.table[:, BLK:]).astype(bf16).astype(f32)
        s.query[head] = (query * scale).astype(bf16)
    cot_copies[1].wait_recv()
    cot_copies[2].start()
    spread_out.step(3)


    def attend(slot, head):
        keys = s.kv[slot, head]
        scores = dot_nt(keys, s.query[head])
        before = s.state_m[head]
        maximum = jnp.maximum(before, jnp.max(scores, axis=0, keepdims=True))
        weights = jnp.exp(scores - maximum)
        factor = jnp.exp(before - maximum)
        s.state_m[head] = maximum
        s.state_l[head] = s.state_l[head] * factor + column_sum(weights)
        s.acc[head] = s.acc[head] * factor + dot_tn(keys, weights.astype(bf16))

    for head in range(heads):
        kv_near[head].wait_recv()

    @pl.loop(0, heads)
    def _(head):
        attend(0, head)
        attend(1, head)

    def kv_forward(head):
        return remote(
            s.kv.at[2, head], s.kv.at[3, head], s.kv_ss.at[2 * heads + head],
            s.kv_rs.at[2 * heads + head], C,
        )

    @pl.loop(0, heads)
    def _(head):
        remote(
            s.kv.at[0, head], s.kv.at[2, head], s.kv_ss.at[head], s.kv_rs.at[head], ZL
        ).wait_recv()
        forward = kv_forward(head)
        forward.start()

        @pl.when(head == 1)
        def _():
            gather_er.second()

        attend(2, head)
        forward.wait_recv()
        attend(3, head)
        value = (s.acc[head] / s.state_l[head]).astype(bf16)
        s.att[head] = value[HEAD_DIM:, :]
        s.logt[head] = s.state_m[head] + jnp.log(s.state_l[head])

    for slot in range(4):
        for head in range(heads):
            s.att_send[slot, head] = s.att[head, :, here(slot)]
    att_copies = [
        remote(
            s.att_send.at[slot], s.att_all.at[my_rank], s.att_ss.at[slot], s.att_rs.at[slot],
            ATTN[slot],
        )
        for slot in range(1, 4)
    ]
    for copy in att_copies:
        copy.start()
    s.att_all[my_rank] = s.att_send[0]
    spread_out.step(4)
    gather_er.third()
    spread_out.last()
    for y in range(2):
        for zh, zl, x, c in itertools.product(range(2), repeat=4):
            at = (y * 16 + zh * 8 + zl * 4 + x * 2 + c) * count
            s.out_full[at : at + count, :] = s.outw[c * 16 + y * 8 + zh * 4 + zl * 2 + x]
    for slot in range(1, 4):
        where = s.att_all.at[rank(ATTN[slot])]
        remote(where, where, s.att_ss.at[slot], s.att_rs.at[slot], ATTN[slot]).wait_recv()
    s.attn[...] = dot_tn(s.att_all[...].reshape(width, rows), s.out_full[...])
    s.middle[...] = s.tokens[...].astype(f32) + mod(gate_one) * s.attn[...]
    normed, inverse = layer_norm(s.middle[...])
    s.normed[...] = normed
    s.inverse[...] = inverse
    s.mix[0, :, :width] = (normed * mod(10) + mod(shift_two)).astype(bf16)
    mix_copies = [
        remote(
            s.mix.at[0, :, pl.ds(0, width)], s.mix.at[slot, :, pl.ds(0, width)],
            s.mix_ss.at[slot], s.mix_rs.at[slot], MLP[slot],
        )
        for slot in range(1, 4)
    ]
    for copy in mix_copies[0:2]:
        copy.start()
    for slot in range(4):
        if slot == 1 or slot == 3:
            cot_copies[slot - 1].wait_recv()
        s.branch[here(slot), :] = (mod(gate_two) * s.cot[slot].astype(f32)).astype(bf16)
    gather_er.last()

    def expand(lanes=wide):
        return s.er[:, :, 0:lanes].reshape(units, lanes)

    def reduce():
        return s.er[:, :, wide:].reshape(units, width)

    spread_ada.step(2)
    gm_copies = [
        remote(
            s.gm_send.at[slot - 1], s.gm_recv.at[slot - 1], s.gm_ss.at[slot], s.gm_rs.at[slot],
            MLP[slot],
        )
        for slot in range(1, 4)
    ]
    for first, last in ((0, 1), (1, 3), (3, 4)):
        for slot in range(first, last):
            if slot:
                mix_copies[slot - 1].wait_recv()
        if first == 1:
            mix_copies[2].start()
        these = slice(first * rows, last * rows)
        mixed_two = s.mix[first:last].reshape((last - first) * rows, wide)
        activated, slope = gelu_pair(dot_nt(mixed_two, expand()))
        s.active[these, :] = activated.astype(bf16)
        grad_hidden = (dot_nt(s.branch[these, :], reduce()) * slope).astype(bf16)
        s.grad_hid[these, :] = grad_hidden
        gm_part = dot_nn(grad_hidden, expand(width))
        for slot in range(first, last):
            part = gm_part[(slot - first) * rows : (slot - first + 1) * rows, :]
            if slot:
                s.gm_send[slot - 1] = part.astype(bf16)
                gm_copies[slot - 1].start()
            else:
                s.grad_mixed[...] = part
    for index in range(units // BLK):
        lanes = slice(index * BLK, (index + 1) * BLK)
        s.wide[lanes, 0:width] = dot_tn(s.active[:, lanes], s.branch[...])
    for index in range(8):
        s.blocks_r[index] = s.wide[index * per : (index + 1) * per, 0:width].astype(bf16)
    scatter_r = Scatter(
        lambda slot, size: s.blocks_r.at[pl.ds(slot, size)],
        lambda slot, size: s.from_r.at[pl.ds(slot, size)], s.sr_ss, s.sr_rs, ZH
    )
    scatter_r.step(C)
    for index in range(units // BLK):
        lanes = slice(index * BLK, (index + 1) * BLK)
        s.wide[lanes, :] = dot_tn(
            s.grad_hid[:, lanes], s.mix[...].reshape(4 * rows, width + BLK)
        )
    scatter_r.add(C)
    scatter_r.step(Y)
    for index in range(8):
        s.blocks_e[index] = s.wide[index * per : (index + 1) * per, :].astype(bf16)
    scatter_e = Scatter(
        lambda slot, size: s.blocks_e.at[pl.ds(slot, size)],
        lambda slot, size: s.from_e.at[pl.ds(slot, size)], s.se_ss, s.se_rs, ZH
    )
    scatter_e.step(C)
    def mlp_copy(slot, number, to):
        return remote(
            s.mlp_send.at[slot], s.mlp_recv.at[number], s.mlp_ss.at[slot], s.mlp_rs.at[number], to
        )

    mlp_copies = [mlp_copy(2, 2, X), mlp_copy(0, 0, X), mlp_copy(1, 1, ZL)]

    def mlp_part(slot):
        return dot_nn(s.active[here(slot), :], reduce())

    s.mlp_send[2] = mlp_part(3).astype(bf16)
    s.mlp_send[0] = mlp_part(1).astype(bf16)
    s.mlp[...] = mlp_part(0) + mod(8)
    s.mlp_near[...] = mlp_part(2)
    for index in range(units // BLK):
        lanes = slice(index * BLK, (index + 1) * BLK)
        s.wide[lanes, 0:width] = dot_tn(s.active[:, lanes], s.cot[...].reshape(4 * rows, width))
    gate_sum = mod(8) * column_sum(s.cot[0].astype(f32))
    for index in range(8):
        gate_sum = gate_sum + column_sum(
            s.er[index, :, wide:].astype(f32) * s.wide[index * per : (index + 1) * per, 0:width]
        )
    s.rowsum[5:6, :] = gate_sum
    for copy in gm_copies:
        copy.wait()
    mlp_copies[0].start()
    grad_mixed = (
        s.grad_mixed[...]
        + s.gm_recv[0].astype(f32) + s.gm_recv[1].astype(f32) + s.gm_recv[2].astype(f32)
    )
    cot = s.cot[0].astype(f32)
    normed = s.normed[...]
    grad_middle = cot + norm_back(grad_mixed * mod(10), normed, s.inverse[...])
    s.gmid[...] = grad_middle
    grad_attn = (mod(gate_one) * grad_middle).astype(bf16)
    s.gattn[0] = grad_attn
    s.dout_send[...] = dot_nt(s.out_full[...], grad_attn).astype(bf16).reshape(
        s.dout_send.shape
    )
    dout_copies = [
        remote(
            s.dout_send.at[rank(ATTN[slot])], s.dout_recv.at[slot], s.dout_ss.at[slot],
            s.dout_rs.at[slot], ATTN[slot],
        )
        for slot in range(1, 4)
    ]
    for copy in dout_copies:
        copy.start()
    s.dout_recv[0] = s.dout_send[my_rank]
    def ga_copy(have, to):
        slot = ATTN.index(have + to)
        return remote(
            s.gattn.at[ATTN.index(have)], s.gattn.at[slot], s.ga_ss.at[slot], s.ga_rs.at[slot], to
        )

    ga_copies = [ga_copy(0, X), ga_copy(0, ZH), ga_copy(ZH, X)]
    weighted = column_sum(grad_mixed * normed)
    s.rowsum[2:3, :] = column_sum(grad_middle * s.attn[...])
    s.rowsum[3:4, :] = column_sum(grad_mixed)
    s.rowsum[4:5, :] = weighted * mod(7)
    s.rowsum[7:8, :] = weighted * (1.0 + mod(scale_two))
    s.rowsum[8:9, :] = column_sum(s.branch[here(0), :].astype(f32))
    scatter_e.add(C)
    scatter_e.step(Y)

    s.dout_t[...] = jnp.zeros_like(s.dout_t)
    for slot in range(4):
        if slot:
            dout_copies[slot - 1].wait()
        if slot == 3:
            ga_copies[1].start()
        for head in range(heads):
            s.dout_t[head, HEAD_DIM:, here(slot)] = s.dout_recv[slot, head]
    for head in range(heads):
        value = s.dout_t[head].astype(f32)
        s.dout[head] = value.T.astype(bf16)
        s.rdots[head] = column_sum(value[HEAD_DIM:, :] * s.att[head].astype(f32))
    scatter_r.add(Y)
    scatter_r.step(ZH)
    ga_copies[0].start()
    mlp_copies[1].start()
    s.dq[...] = jnp.zeros_like(s.dq)

    def back(slot, head):
        keys = s.kv[slot, head]
        query = s.query[head]
        shares = jnp.exp(dot_nt(keys, query) - s.logt[head])
        grad_shares = dot_nn(keys, s.dout_t[head])
        grad_scores = (shares * (grad_shares - s.rdots[head])).astype(bf16)
        s.dq[head] += dot_tn(keys, grad_scores)
        return dot_nn(grad_scores, query) + dot_nn(shares.astype(bf16), s.dout[head])

    def dkv_copy(stage, head, offset):
        index = stage * heads + head
        return remote(
            s.dkv_send.at[index], s.dkv_recv.at[index], s.dkv_ss.at[index], s.dkv_rs.at[index],
            offset,
        )

    @pl.loop(0, heads)
    def _(head):
        s.dkv_send[head] = back(3, head).astype(bf16)
        first = dkv_copy(0, head, C)
        first.start()
        part = back(2, head)
        first.wait_recv()
        s.dkv_send[heads + head] = (part + s.dkv_recv[head].astype(f32)).astype(bf16)
        dkv_copy(1, head, ZL).start()

    spread_ada.step(3)

    @pl.loop(0, heads)
    def _(head):
        @pl.when(head == 1)
        def _():
            ga_copies[1].wait_recv()
            ga_copies[2].start()

        s.dkv_send[2 * heads + head] = back(1, head).astype(bf16)
        dkv_copy(2, head, C).start()
        s.dkv[head] = back(0, head)
        value = s.dq[head].T * scale
        s.dqkv[head] = turn(value, s.table[:, 0:BLK], -s.table[:, BLK:]).astype(bf16)

    spread_ada.step(4)
    query_part = dot_nn(s.dqkv[0], s.weight[0])
    for head in range(1, heads):
        query_part = query_part + dot_nn(s.dqkv[head], s.weight[head])
    s.part[...] = query_part
    ga_copies[0].wait_recv()
    ga_copies[2].wait_recv()
    gattn = s.gattn[...].reshape(4 * rows, width)

    def spread(part, low, of):
        for slot in range(8):
            for row, head, target in head_rows(slot * count, count, low):
                s.blocks_a[(part + 1) % 4 // 2, slot, (part + 1) % 2, row : row + 8, :] = s.wide[
                    of * heads * BLK + head * BLK + target
                    : of * heads * BLK + head * BLK + target + 8, 0:width
                ].astype(bf16)

    def scatter_pair(pair, ss, rs):
        return Scatter(
            lambda slot, size: s.blocks_a.at[pair, pl.ds(slot, size)],
            lambda slot, size: s.from_a.at[pair, pl.ds(slot, size)],
            ss, rs, ZL,
        )

    for head in range(heads):
        s.wide[head * BLK + HEAD_DIM : (head + 1) * BLK, 0:width] = dot_nn(s.att[head], gattn)
        at = (heads + head) * BLK
        s.wide[at : at + BLK, 0:width] = dot_tn(s.dqkv[head], s.mixed[...])
    spread(3, False, 0)
    spread(0, True, 1)
    scatter_oq = scatter_pair(0, s.soq_ss, s.soq_rs)
    scatter_kv = scatter_pair(1, s.skv_ss, s.skv_rs)
    scatter_oq.step(C)
    for head in range(heads):
        dkv_copy(2, head, C).wait_recv()
        s.dkv[head] += s.dkv_recv[2 * heads + head].astype(f32)
    scatter_e.add(Y)
    for head in range(heads):
        dkv_copy(1, head, ZL).wait_recv()
        value = s.dkv[head] + s.dkv_recv[heads + head].astype(f32)
        s.dqkv[heads + head] = turn(value, s.table[:, 0:BLK], -s.table[:, BLK:]).astype(bf16)
    kv_part = s.part[...]
    for head in range(heads, 2 * heads):
        kv_part = kv_part + dot_nn(s.dqkv[head], s.weight[head])

    def part_copy(slot, number, to):
        return remote(
            s.part_send.at[slot], s.part_recv.at[number], s.part_ss.at[slot],
            s.part_rs.at[number], to,
        )

    def part_half(slot, number, to, half):
        lines = pl.ds(half * (rows // 2), rows // 2)
        return remote(
            s.part_send.at[slot, lines], s.part_recv.at[number, lines],
            s.part_ss.at[slot + 3 * half], s.part_rs.at[number + 3 * half], to,
        )

    relays = [(part_half(2, 2, X, half), part_half(1, 1, ZH, half)) for half in range(2)]
    part_copies = [part_copy(0, 0, X)]
    s.part_send[2] = kv_part[here(3), :].astype(bf16)
    for half in range(2):
        relays[half][0].start()
    scatter_e.step(ZH)
    mlp_copies[0].wait_recv()
    s.mlp_send[1] = (s.mlp_near[...] + s.mlp_recv[2].astype(f32)).astype(bf16)
    mlp_copies[2].start()
    s.part_send[0] = kv_part[here(1), :].astype(bf16)
    s.part[here(2), :] = kv_part[here(2), :]
    s.grad_mixed[...] = kv_part[here(0), :]

    scatter_oq.add(C)
    scatter_oq.step(Y)

    s.norm_sum[...] = jnp.zeros_like(s.norm_sum)
    s.rowsum[9:16, :] = jnp.zeros((7, width), f32)
    for head in range(2 * heads):
        moment = dot_tn(s.dqkv[head], s.plain[...])
        weights = s.weight[head].astype(f32)
        s.norm_sum[0:1, :] += column_sum(weights * moment[:, width : width + 1])
        s.norm_sum[1:2, :] += column_sum(weights * moment[:, 0:width])
    s.rowsum[0:1, :] = s.norm_sum[0:1, :]
    s.rowsum[1:2, :] = s.norm_sum[1:2, :] * mod(6)
    s.rowsum[6:7, :] = s.norm_sum[1:2, :] * (1.0 + mod(scale_one))
    spread_ada.last()
    for y in range(2):
        for zh, zl, x, c in itertools.product(range(2), repeat=4):
            at = (y * 16 + zh * 8 + zl * 4 + x * 2 + c) * piece
            for index in range(width // BLK):
                s.ada_full[at + index * count : at + (index + 1) * count, :] = s.adaw[
                    c * 16 + y * 8 + zh * 4 + zl * 2 + x, :,
                    index * BLK : (index + 1) * BLK,
                ]
    high = s.rowsum[0:8, :].astype(bf16)
    low = (s.rowsum[0:8, :] - high.astype(f32)).astype(bf16)
    both = jnp.concatenate([high, low], axis=0)
    terms = jnp.zeros((1, BLK), f32)
    for index in range(6):
        found = dot_nn(both, s.ada_full[index * width : (index + 1) * width, :])
        terms = terms + found[index : index + 1, :] + found[8 + index : 9 + index, :]
    s.rowsum[9:10, 0:BLK] = terms
    totals = Total(s.sum_halves, s.sum_inbox, s.sum_first, s.sum_last, s.sum_ss, s.sum_rs)
    s.sum_halves[0] = s.rowsum[0:8, :]
    s.sum_halves[1] = s.rowsum[8:16, :]
    totals.start()

    for head in range(heads):
        s.wide[head * BLK : (head + 1) * BLK, 0:width] = dot_tn(
            s.dqkv[heads + head], s.mixed[...]
        )
    totals.second()
    spread(1, True, 0)
    spread(2, False, 0)
    scatter_kv.step(C)
    for half in range(2):
        lines = slice(half * (rows // 2), (half + 1) * (rows // 2))
        relays[half][0].wait_recv()
        s.part_send[1, lines, :] = (
            s.part[2 * rows + lines.start : 2 * rows + lines.stop, :]
            + s.part_recv[2, lines, :].astype(f32)
        ).astype(bf16)
        relays[half][1].start()
    part_copies[0].start()
    scatter_kv.add(C)
    scatter_kv.step(Y)
    scatter_oq.add(Y)

    def chunk_back(part, half):
        slot = own // 2 * 2 + half
        place_in = 8 * my_rank + slot
        if part < 3:
            number = 32 * part + place_in
            owner, at = number // 3, number % 3
        else:
            owner, at = place_in, 3
        z = own % 2
        index = part * 2 + half
        source = s.blocks_a.at[(part + 1) % 4 // 2, slot, (part + 1) % 2]
        target = s.owned.at[z, at]
        far = remote_to(
            source, target, s.back_ss.at[index], s.back_rs.at[z * 4 + at],
            (owner // 16, owner % 16),
        )
        near = pltpu.make_async_copy(source, target, s.local_sem.at[index])
        return far, near, owner == me

    def chunks_back(parts, act):
        for part in parts:
            for half in range(2):
                far, near, stays = chunk_back(part, half)

                @pl.when(jnp.logical_not(stays))
                def _():
                    far.start() if act else far.wait_send()

                @pl.when(stays)
                def _():
                    near.start() if act else near.wait()

    chunks_back((0, 3), True)
    totals.third()
    for index in (1, 2):
        mlp_copies[index].wait_recv()
    mlp_branch = s.mlp[...] + s.mlp_recv[0].astype(f32) + s.mlp_recv[1].astype(f32)
    s.result[...] = (s.middle[...] + mod(gate_two) * mlp_branch).astype(bf16)
    normed_one, inverse_one = layer_norm(s.tokens[...].astype(f32))
    scatter_kv.add(Y)
    chunks_back((1, 2), True)
    totals.fourth()
    sums = totals.result()
    for index in range(6):
        for tile in range(width // BLK):
            s.tiles[index * (width // BLK) + tile] = sums[
                index : index + 1, tile * BLK : (tile + 1) * BLK
            ]
    for tile in range(width // BLK):
        s.gain_tiles[tile] = sums[6:9, tile * BLK : (tile + 1) * BLK]
    s.gain_tiles[width // BLK] = jnp.zeros((3, BLK), f32)
    s.vec_own[...] = jnp.zeros_like(s.vec_own)
    for tile in range(2):
        lanes = slice(tile * BLK, (tile + 1) * BLK)
        s.vec_own[0:1, lanes] = s.tiles[(9 * me) // 8 + tile]
        s.vec_own[9:12, lanes] = s.gain_tiles[(3 * me) // 16 + tile]
    s.sums[0:8, :] = pltpu.roll(s.vec_own[0:8, :], (256 - mod_shift) % 256, 1)
    s.sums[8:16, :] = pltpu.roll(s.vec_own[8:16, :], (256 - gain_shift) % 256, 1)
    s.grad_cond[...] = sums[9:10, 0:BLK]
    s.grad_r[0] = s.blocks_r[own_mlp]
    s.grad_e[0] = s.blocks_e[own_mlp]
    for scatter, target in ((scatter_r, s.grad_r), (scatter_e, s.grad_e)):
        scatter.copies[ZH].wait_recv()
        target[1] = scatter.inbox(6, 1)[0]
    part_copies[0].wait_recv()
    for half in range(2):
        relays[half][1].wait_recv()
    grad_mixed_one = (
        s.grad_mixed[...] + s.part_recv[0].astype(f32) + s.part_recv[1].astype(f32)
    )
    s.grad_tokens[...] = s.gmid[...] + norm_back(
        grad_mixed_one * mod(9), normed_one, inverse_one
    )

    chunks_back(range(4), False)
    for at in range(4):
        if at < 3:
            number = 3 * me + at
            part, place_in = number // 32, number % 32
        else:
            part, place_in = 3, me
        slot = place_in % 8
        for z in range(2):
            keeper = flat(member(place_in // 8, slot // 2 * 2 + z))

            @pl.when(keeper != me)
            def _():
                target = s.owned.at[z, at]
                remote(
                    target, target, s.back_ss.at[0], s.back_rs.at[z * 4 + at], C
                ).wait_recv()

    for copies in (
        kv_far, kv_near, cot_copies, mix_copies, att_copies, ga_copies, mlp_copies, token_copies,
        part_copies, *relays, *vec_steps,
    ):
        for copy in copies:
            copy.wait_send()
    for group in (
        gather_a, gather_er, spread_out, spread_ada, scatter_e, scatter_r, scatter_oq, scatter_kv, totals,
    ):
        group.finish()

    @pl.loop(0, heads)
    def _(head):
        kv_forward(head).wait_send()
        dkv_copy(0, head, C).wait_send()
        dkv_copy(1, head, ZL).wait_send()
        dkv_copy(2, head, C).wait_send()


def finish_kernel(
    result, grad_tokens, grad_cond, sums, grad_e, grad_r, owned, condition,
    result_out, tokens_out, cond_out, ada_out, ada_bias_out, first_out, second_out, project_out,
    output_out, expand_out, expand_bias_out, reduce_out, reduce_bias_out,
):
    width = result.shape[1]
    count = output_out.shape[0]
    piece = ada_out.shape[0]
    result_out[...] = result[...]
    tokens_out[...] = grad_tokens[...]
    cond_out[...] = grad_cond[...]
    first = lax.broadcasted_iota(jnp.int32, (8, piece), 0) == 0
    row = jnp.where(first, sums[0:8, 0:piece], 0.0)
    ada_out[...] = exact(
        row, jnp.broadcast_to(condition[...], (8, condition.shape[1])), ((0,), (0,))
    )
    ada_bias_out[...] = sums[0:1, 0:piece]
    first_out[...] = sums[9:10, 0:count]
    second_out[...] = sums[10:11, 0:count]
    reduce_bias_out[...] = sums[11:12, 0:count]
    both = owned[0].astype(f32) + owned[1].astype(f32)
    project_out[...] = both[0:3]
    output_out[...] = both[3]
    expand = grad_e[0].astype(f32) + grad_e[1].astype(f32)
    expand_out[...] = expand[:, 0:width]
    expand_bias_out[...] = to_row(expand[:, width : width + 1])
    reduce_out[...] = grad_r[0].astype(f32) + grad_r[1].astype(f32)


def rotary_blocks(length):
    half_dim = HEAD_DIM // 2
    frequency = np.exp(
        np.arange(half_dim, dtype=np.float32) * np.float32(-2.0 * math.log(10000.0) / HEAD_DIM)
    ).astype(np.float32)
    angles = (np.arange(length, dtype=np.float32)[:, None] * frequency[None, :]).astype(np.float32)
    cosine, sine = np.cos(angles.astype(np.float64)), np.sin(angles.astype(np.float64))
    one, zero = np.ones((length, HEAD_DIM)), np.zeros((length, HEAD_DIM))
    return np.concatenate([cosine, cosine, one, -sine, sine, zero], axis=1).astype(np.float32)


def on_device_fast(
    tokens, condition, ada_weight, ada_bias, first_gain, second_gain, project_weight,
    output_weight, expand_weight, expand_bias, reduce_weight, reduce_bias, cotangent,
):
    rows, width = tokens.shape
    group = 4 * rows
    heads = width // HEAD_DIM // 4
    per = reduce_weight.shape[0]
    units = 8 * per
    count = output_weight.shape[0]
    piece = ada_weight.shape[1]
    wide = width + BLK
    table = jnp.asarray(rotary_blocks(lax.axis_size("blk") * rows))
    line = condition[None, :]
    inputs = dict(
        tokens=tokens, cotangent=cotangent, condition=line, ada=ada_weight.T,
        ada_bias=ada_bias, first_gain=first_gain[None, :],
        second_gain=second_gain[None, :], reduce_bias=reduce_bias[None, :],
        expand_bias=expand_bias[None, :],
        project_weight=project_weight.T.reshape(3, count, width), output_weight=output_weight,
        expand_weight=expand_weight.T, reduce_weight=reduce_weight, table=table,
    )
    outputs = dict(
        result=((rows, width), bf16), grad_tokens=((rows, width), f32),
        grad_cond=((1, line.shape[1]), f32), sums=((16, 256), f32),
        grad_e=((2, per, wide), bf16), grad_r=((2, per, width), bf16),
        owned=((2, 4, count, width), bf16),
    )
    head_block = (group, BLK)
    kept = {
        name: (inputs[name].shape, inputs[name].dtype)
        for name in (
            "tokens", "condition", "ada", "ada_bias", "first_gain", "second_gain", "reduce_bias",
            "expand_bias", "project_weight",
        )
    }
    scratch = dict(
        **kept,
        table=((group, 2 * BLK), f32), vec_own=((16, 256), f32),
        vecs=((32, 4, 256), f32), mod_row=((1, 6 * width), f32), gain_rows=((3, wide), f32),
        mods=((16, width), f32), chunks=((8, 3, count, width), bf16),
        tok=((4, rows, width), bf16), cot=((4, rows, width), bf16),
        er=((8, per, wide + width), bf16),
        outw=((32, count, width), bf16), adaw=((32, count, width), bf16), ada_full=((6 * width, BLK), bf16), out_full=((width, width), bf16),
        weight=((2 * heads, BLK, width), bf16), mixed=((group, width), bf16),
        query=((heads,) + head_block, bf16), kv=((4, heads) + head_block, bf16),
        state_m=((heads, 1, group), f32), state_l=((heads, 1, group), f32),
        acc=((heads, BLK, group), f32), att=((heads, HEAD_DIM, group), bf16),
        logt=((heads, 1, group), f32), att_send=((4, heads, HEAD_DIM, rows), bf16),
        att_all=((4, heads, HEAD_DIM, rows), bf16), attn=((rows, width), f32),
        middle=((rows, width), f32), normed=((rows, width), f32), inverse=((rows, 1), f32),
        mix=((4, rows, wide), bf16), branch=((group, width), bf16),
        active=((group, units), bf16), grad_hid=((group, units), bf16),
        gm_send=((3, rows, width), bf16), gm_recv=((3, rows, width), bf16),
        mlp_send=((3, rows, width), bf16), mlp_recv=((3, rows, width), bf16),
        grad_mixed=((rows, width), f32), mlp=((rows, width), f32), gmid=((rows, width), f32),
        gattn=((4, rows, width), bf16), dout_send=((4, heads, HEAD_DIM, rows), bf16),
        dout_recv=((4, heads, HEAD_DIM, rows), bf16), rowsum=((16, width), f32),
        wide=((units, wide), f32), blocks_r=((8, per, width), bf16),
        blocks_e=((8, per, wide), bf16), blocks_a=((2, 8, 2, count, width), bf16),
        from_r=((7, per, width), bf16), from_e=((7, per, wide), bf16),
        from_a=((2, 6, 2, count, width), bf16), dout_t=((heads, BLK, group), bf16),
        dout=((heads,) + head_block, bf16), rdots=((heads, 1, group), f32),
        dq=((heads, BLK, group), f32), dkv=((heads,) + head_block, f32),
        dkv_send=((3 * heads,) + head_block, bf16), dkv_recv=((3 * heads,) + head_block, bf16),
        dqkv=((2 * heads,) + head_block, bf16), part=((group, width), f32),
        part_send=((3, rows, width), bf16), part_recv=((3, rows, width), bf16),
        plain=((group, wide), bf16), norm_sum=((8, width), f32),
        sum_halves=((2, 8, width), f32), sum_inbox=((3, 8, width), f32),
        sum_first=((4, 8, width), f32), sum_last=((4, 8, width), f32), tiles=((6 * width // BLK, 1, BLK), f32),
        gain_tiles=((width // BLK + 1, 3, BLK), f32),
        mlp_near=((rows, width), f32),
    )
    semaphores = dict(
        load_sem=16, table_sem=4, local_sem=8, chunk_ss=3, chunk_rs=3, vec_ss=7, vec_rs=7,
        tok_ss=4, tok_rs=4, a_ss=4, a_rs=4, er_ss=5, er_rs=5, o_ss=5, o_rs=5, ada_ss=5, ada_rs=5, cot_ss=4, cot_rs=4,
        kv_ss=3 * heads, kv_rs=3 * heads, att_ss=4, att_rs=4, mix_ss=4, mix_rs=4, gm_ss=4,
        gm_rs=4, mlp_ss=4, mlp_rs=4, dout_ss=4, dout_rs=4, ga_ss=4, ga_rs=4, sr_ss=3, sr_rs=3,
        se_ss=3, se_rs=3, soq_ss=2, soq_rs=2, skv_ss=2, skv_rs=2, dkv_ss=3 * heads,
        dkv_rs=3 * heads, part_ss=6, part_rs=6, back_ss=8, back_rs=8, sum_ss=8, sum_rs=8,
    )
    whole = pl.BlockSpec(memory_space=pltpu.VMEM)
    names = (*(name + "_hbm" for name in inputs), *outputs, *scratch, *semaphores)
    staged = pl.pallas_call(
        partial(block_kernel, names),
        out_shape=tuple(jax.ShapeDtypeStruct(*spec) for spec in outputs.values()),
        in_specs=[pl.BlockSpec(memory_space=pl.ANY)] * len(inputs),
        out_specs=tuple(whole for _ in outputs),
        scratch_shapes=[pltpu.VMEM(*spec) for spec in scratch.values()]
        + [pltpu.SemaphoreType.DMA((number,)) for number in semaphores.values()],
        compiler_params=pltpu.CompilerParams(
            collective_id=1, has_side_effects=True, vmem_limit_bytes=62 * 2**20
        ),
    )(*inputs.values())
    (
        result, grad_tokens, grad_condition, grad_ada, grad_ada_bias, grad_first, grad_second,
        grad_project, grad_output, grad_expand, grad_expand_bias, grad_reduce, grad_reduce_bias,
    ) = pl.pallas_call(
        finish_kernel,
        out_shape=tuple(
            jax.ShapeDtypeStruct(shape, kind)
            for shape, kind in (
                ((rows, width), bf16), ((rows, width), f32), (line.shape, f32),
                ((piece, line.shape[1]), f32), ((1, piece), f32), ((1, count), f32),
                ((1, count), f32), ((3, count, width), f32), ((count, width), f32),
                ((per, width), f32), ((1, per), f32), ((per, width), f32), ((1, count), f32),
            )
        ),
        in_specs=[whole] * 8,
        out_specs=(whole,) * 13,
    )(*staged, line)
    return (
        result,
        grad_tokens,
        grad_condition.reshape(-1),
        grad_ada.T,
        grad_ada_bias.reshape(-1),
        grad_first.reshape(-1),
        grad_second.reshape(-1),
        grad_project.reshape(3 * count, width).T,
        grad_output,
        grad_expand.T,
        grad_expand_bias.reshape(-1),
        grad_reduce,
        grad_reduce_bias.reshape(-1),
    )


def solution(mesh):
    return jax.shard_map(
        on_device_fast if mesh.shape["ulysses"] * mesh.shape["blk"] == 32 else on_device,
        mesh=mesh,
        in_specs=(
            P(BOTH, None),
            P(),
            P(None, BOTH),
            P(BOTH),
            P(BOTH),
            P(BOTH),
            P(None, BOTH),
            P(BOTH, None),
            P(None, BOTH),
            P(BOTH),
            P(BOTH, None),
            P(BOTH),
            P(BOTH, None),
        ),
        out_specs=(
            P(BOTH, None),
            P(BOTH, None),
            P(),
            P(None, BOTH),
            P(BOTH),
            P(BOTH),
            P(BOTH),
            P(None, BOTH),
            P(BOTH, None),
            P(None, BOTH),
            P(BOTH),
            P(BOTH, None),
            P(BOTH),
        ),
        check_vma=False,
    )
```

```python
from functools import partial
import itertools
import math
import types

import jax
import jax.numpy as jnp
import numpy as np
from jax import lax
from jax.experimental import pallas as pl
from jax.experimental.pallas import tpu as pltpu
from jax.sharding import PartitionSpec as P

HEAD_DIM = 64
BOTH = ("ulysses", "blk")


eps = 1e-05
highest = lax.Precision.HIGHEST


def layer_norm(value):
    center = value - jnp.mean(value, axis=-1, keepdims=True)
    inverse = lax.rsqrt(jnp.mean(center * center, axis=-1, keepdims=True) + eps)
    return (center * inverse, inverse)


def norm_back(grad_normed, normed, inverse):
    first = jnp.mean(grad_normed, axis=-1, keepdims=True)
    second = jnp.mean(grad_normed * normed, axis=-1, keepdims=True)
    return inverse * (grad_normed - first - normed * second)


def rotary_tables(positions, head_dim):
    half_dim = head_dim // 2
    frequency = jnp.exp(
        jnp.arange(half_dim, dtype=jnp.float32) * (-2.0 * math.log(10000.0) / head_dim)
    )
    angles = positions[:, None] * frequency[None, :]
    return (jnp.cos(angles)[:, None, :], jnp.sin(angles)[:, None, :])


def rotate(value, cosine, sine):
    half_dim = value.shape[-1] // 2
    first = value[..., :half_dim]
    second = value[..., half_dim:]
    return jnp.concatenate(
        [first * cosine - second * sine, second * cosine + first * sine], axis=-1
    )


def rotate_back(grad_value, cosine, sine):
    half_dim = grad_value.shape[-1] // 2
    first = grad_value[..., :half_dim]
    second = grad_value[..., half_dim:]
    return jnp.concatenate(
        [first * cosine + second * sine, second * cosine - first * sine], axis=-1
    )


def over_blocks(block_step, carried, pieces, key_block):
    length = pieces[0].shape[1]
    complete = length // key_block
    stacked = tuple(
        (
            jnp.moveaxis(
                member.reshape((member.shape[0], complete, key_block) + member.shape[2:]), 1, 0
            )
            for member in pieces
        )
    )
    offsets = jnp.arange(complete, dtype=jnp.int32) * key_block

    def scan_step(carried_in, inputs):
        return (block_step(carried_in, inputs[:-1], inputs[-1]), None)

    carried, unused = lax.scan(scan_step, carried, stacked + (offsets,))
    return carried


def on_device(
    tokens,
    condition,
    ada_weight,
    ada_bias,
    first_gain,
    second_gain,
    project_weight,
    output_weight,
    expand_weight,
    expand_bias,
    reduce_weight,
    reduce_bias,
    cotangent,
):
    row_count = tokens.shape[0]
    model_width = tokens.shape[1]
    cycle_size = lax.axis_size("blk")
    cycle_place = lax.axis_index("blk")
    seq_count = lax.axis_size("ulysses")
    (
        ada_full,
        ada_shift,
        gain_one,
        gain_two,
        project_full,
        output_full,
        expand_full,
        expand_shift,
        reduce_full,
        reduce_shift,
    ) = (
        lax.all_gather(ada_weight, BOTH, axis=1, tiled=True),
        lax.all_gather(ada_bias, BOTH, axis=0, tiled=True),
        lax.all_gather(first_gain, BOTH, axis=0, tiled=True),
        lax.all_gather(second_gain, BOTH, axis=0, tiled=True),
        lax.all_gather(project_weight, BOTH, axis=1, tiled=True),
        lax.all_gather(output_weight, BOTH, axis=0, tiled=True),
        lax.all_gather(expand_weight, BOTH, axis=1, tiled=True),
        lax.all_gather(expand_bias, BOTH, axis=0, tiled=True),
        lax.all_gather(reduce_weight, BOTH, axis=0, tiled=True),
        lax.all_gather(reduce_bias, BOTH, axis=0, tiled=True),
    )
    ada_float = ada_full.astype(jnp.float32)
    modulation = jnp.dot(condition, ada_float, precision=highest) + ada_shift.astype(jnp.float32)
    shift_one, scale_one, gate_one, shift_two, scale_two, gate_two = jnp.split(modulation, 6)
    gain_one_f = gain_one.astype(jnp.float32)
    gain_two_f = gain_two.astype(jnp.float32)
    inputs = tokens.astype(jnp.float32)
    normed_one, inverse_one = layer_norm(inputs)
    gain_first = gain_one_f * (1.0 + scale_one)
    mixed_one = (normed_one * gain_first + shift_one).astype(jnp.bfloat16)
    projected = jnp.dot(mixed_one, project_full, preferred_element_type=jnp.float32)
    packed = projected.astype(jnp.bfloat16).reshape(row_count, 3, model_width)
    regrouped = lax.all_to_all(packed, "ulysses", split_axis=2, concat_axis=0, tiled=True)
    local_rows = regrouped.shape[0]
    local_width = regrouped.shape[2]
    head_count = local_width // HEAD_DIM
    by_seq = regrouped.reshape(seq_count, row_count, 3, local_width)
    positions = cycle_place * row_count + jnp.arange(row_count, dtype=jnp.int32)
    cosine, sine = rotary_tables(positions.astype(jnp.float32), HEAD_DIM)
    query_rot = rotate(
        by_seq[:, :, 0].astype(jnp.float32).reshape(seq_count, row_count, head_count, HEAD_DIM),
        cosine,
        sine,
    ).astype(jnp.bfloat16)
    key_rot = rotate(
        by_seq[:, :, 1].astype(jnp.float32).reshape(seq_count, row_count, head_count, HEAD_DIM),
        cosine,
        sine,
    ).astype(jnp.bfloat16)
    value_flat = by_seq[:, :, 2]
    value_own = value_flat.reshape(seq_count, row_count, head_count, HEAD_DIM)
    key_flat = key_rot.reshape(seq_count, row_count, local_width)
    score_scale = HEAD_DIM ** (-0.5)
    key_block = row_count * -(-512 // row_count)

    def attend_step(carried, pieces, offset):
        maximum, denominator, weighted = carried
        key_rows = pieces[0].reshape(seq_count, -1, head_count, HEAD_DIM)
        value_rows = pieces[1].reshape(seq_count, -1, head_count, HEAD_DIM)
        scores = (
            jnp.einsum("sqhd,skhd->shqk", query_rot, key_rows, preferred_element_type=jnp.float32)
            * score_scale
        )
        new_maximum = jnp.maximum(maximum, jnp.max(scores, axis=-1))
        weights = jnp.exp(scores - new_maximum[..., None])
        factor = jnp.exp(maximum - new_maximum)
        denominator = denominator * factor + jnp.sum(weights, axis=-1)
        weighted = weighted * jnp.transpose(factor, (0, 2, 1))[..., None] + jnp.einsum(
            "shqk,skhd->sqhd",
            weights.astype(jnp.bfloat16),
            value_rows,
            preferred_element_type=jnp.float32,
        )
        return (new_maximum, denominator, weighted)

    start_state = (
        jnp.full((seq_count, head_count, row_count), -1e30, jnp.float32),
        jnp.zeros((seq_count, head_count, row_count), jnp.float32),
        jnp.zeros((seq_count, row_count, head_count, HEAD_DIM), jnp.float32),
    )
    maximum, denominator, weighted = over_blocks(
        attend_step,
        start_state,
        (
            lax.all_gather(key_flat, "blk", axis=1, tiled=True),
            lax.all_gather(value_flat, "blk", axis=1, tiled=True),
        ),
        key_block,
    )
    log_total = maximum + jnp.log(denominator)
    attended = (
        (weighted / jnp.transpose(denominator, (0, 2, 1))[..., None])
        .astype(jnp.bfloat16)
        .reshape(local_rows, local_width)
    )
    attended_tokens = lax.all_to_all(attended, "ulysses", split_axis=0, concat_axis=1, tiled=True)
    attn_branch = jnp.dot(attended_tokens, output_full, preferred_element_type=jnp.float32)
    middle = inputs + gate_one * attn_branch
    normed_two, inverse_two = layer_norm(middle)
    gain_second = gain_two_f * (1.0 + scale_two)
    mixed_two = (normed_two * gain_second + shift_two).astype(jnp.bfloat16)
    hidden = jnp.dot(
        mixed_two, expand_full, preferred_element_type=jnp.float32
    ) + expand_shift.astype(jnp.float32)
    activated, gelu_back = jax.vjp(partial(jax.nn.gelu, approximate=True), hidden)
    activated_low = activated.astype(jnp.bfloat16)
    mlp_branch = jnp.dot(
        activated_low, reduce_full, preferred_element_type=jnp.float32
    ) + reduce_shift.astype(jnp.float32)
    result = (middle + gate_two * mlp_branch).astype(jnp.bfloat16)
    grad_result = cotangent.astype(jnp.float32)
    grad_gate_two = jnp.sum(grad_result * mlp_branch, axis=0)
    grad_branch = (gate_two * grad_result).astype(jnp.bfloat16)
    grad_reduce = jnp.einsum(
        "tf,td->fd", activated_low, grad_branch, preferred_element_type=jnp.float32
    )
    grad_reduce_shift = jnp.sum(grad_branch.astype(jnp.float32), axis=0)
    grad_activated = jnp.einsum(
        "td,fd->tf", grad_branch, reduce_full, preferred_element_type=jnp.float32
    )
    grad_hidden = gelu_back(grad_activated)[0].astype(jnp.bfloat16)
    grad_expand = jnp.einsum(
        "td,tf->df", mixed_two, grad_hidden, preferred_element_type=jnp.float32
    )
    grad_expand_shift = jnp.sum(grad_hidden.astype(jnp.float32), axis=0)
    grad_mixed_two = jnp.einsum(
        "tf,df->td", grad_hidden, expand_full, preferred_element_type=jnp.float32
    )
    grad_shift_two = jnp.sum(grad_mixed_two, axis=0)
    grad_scale_two = jnp.sum(grad_mixed_two * normed_two * gain_two_f, axis=0)
    grad_gain_two = jnp.sum(grad_mixed_two * normed_two * (1.0 + scale_two), axis=0)
    grad_middle = grad_result + norm_back(grad_mixed_two * gain_second, normed_two, inverse_two)
    grad_gate_one = jnp.sum(grad_middle * attn_branch, axis=0)
    grad_attn = (gate_one * grad_middle).astype(jnp.bfloat16)
    grad_output = jnp.einsum(
        "tc,td->cd", attended_tokens, grad_attn, preferred_element_type=jnp.float32
    )
    grad_heads = jnp.einsum(
        "td,cd->tc", grad_attn, output_full, preferred_element_type=jnp.float32
    ).astype(jnp.bfloat16)
    grad_local = lax.all_to_all(grad_heads, "ulysses", split_axis=1, concat_axis=0, tiled=True)
    grad_local_heads = grad_local.reshape(seq_count, row_count, head_count, HEAD_DIM)
    row_dots = jnp.sum(
        (grad_local.astype(jnp.float32) * attended.astype(jnp.float32)).reshape(
            seq_count, row_count, head_count, HEAD_DIM
        ),
        axis=-1,
    )
    row_dots_t = jnp.transpose(row_dots, (0, 2, 1))

    def query_step(carried, pieces, offset):
        key_rows = pieces[0].reshape(seq_count, -1, head_count, HEAD_DIM)
        value_rows = pieces[1].reshape(seq_count, -1, head_count, HEAD_DIM)
        scores = (
            jnp.einsum("sqhd,skhd->shqk", query_rot, key_rows, preferred_element_type=jnp.float32)
            * score_scale
        )
        shares = jnp.exp(scores - log_total[..., None])
        grad_shares = jnp.einsum(
            "sqhd,skhd->shqk", grad_local_heads, value_rows, preferred_element_type=jnp.float32
        )
        grad_scores = (shares * (grad_shares - row_dots_t[..., None])).astype(jnp.bfloat16)
        return (
            carried
            + jnp.einsum(
                "shqk,skhd->sqhd", grad_scores, key_rows, preferred_element_type=jnp.float32
            )
            * score_scale
        )

    grad_query_rot = over_blocks(
        query_step,
        jnp.zeros((seq_count, row_count, head_count, HEAD_DIM), jnp.float32),
        (
            lax.all_gather(key_flat, "blk", axis=1, tiled=True),
            lax.all_gather(value_flat, "blk", axis=1, tiled=True),
        ),
        key_block,
    )

    def key_step(carried, pieces, offset):
        grad_keys_acc, grad_values_acc = carried
        query_rows = pieces[0].reshape(seq_count, -1, head_count, HEAD_DIM)
        slope_rows = pieces[1].reshape(seq_count, -1, head_count, HEAD_DIM)
        scores = (
            jnp.einsum("sqhd,skhd->shqk", query_rows, key_rot, preferred_element_type=jnp.float32)
            * score_scale
        )
        shares = jnp.exp(scores - jnp.transpose(pieces[2], (0, 2, 1))[..., None])
        grad_values_acc = grad_values_acc + jnp.einsum(
            "shqk,sqhd->skhd",
            shares.astype(jnp.bfloat16),
            slope_rows,
            preferred_element_type=jnp.float32,
        )
        grad_shares = jnp.einsum(
            "sqhd,skhd->shqk", slope_rows, value_own, preferred_element_type=jnp.float32
        )
        grad_scores = (
            shares * (grad_shares - jnp.transpose(pieces[3], (0, 2, 1))[..., None])
        ).astype(jnp.bfloat16)
        grad_keys_acc = (
            grad_keys_acc
            + jnp.einsum(
                "shqk,sqhd->skhd", grad_scores, query_rows, preferred_element_type=jnp.float32
            )
            * score_scale
        )
        return (grad_keys_acc, grad_values_acc)

    query_wide = query_rot.reshape(seq_count, row_count, local_width)
    slope_wide = grad_local.reshape(seq_count, row_count, local_width)
    key_init = (
        jnp.zeros((seq_count, row_count, head_count, HEAD_DIM), jnp.float32),
        jnp.zeros((seq_count, row_count, head_count, HEAD_DIM), jnp.float32),
    )
    grad_key_rot, grad_value_sum = over_blocks(
        key_step,
        key_init,
        (
            lax.all_gather(query_wide.astype(jnp.float32), "blk", axis=1, tiled=True).astype(
                jnp.bfloat16
            ),
            lax.all_gather(slope_wide.astype(jnp.float32), "blk", axis=1, tiled=True).astype(
                jnp.bfloat16
            ),
            lax.all_gather(jnp.transpose(log_total, (0, 2, 1)), "blk", axis=1, tiled=True),
            lax.all_gather(row_dots, "blk", axis=1, tiled=True),
        ),
        key_block,
    )
    grad_query = (
        rotate_back(grad_query_rot, cosine, sine)
        .astype(jnp.bfloat16)
        .reshape(local_rows, local_width)
    )
    grad_key = (
        rotate_back(grad_key_rot, cosine, sine)
        .astype(jnp.bfloat16)
        .reshape(local_rows, local_width)
    )
    grad_value = grad_value_sum.astype(jnp.bfloat16).reshape(local_rows, local_width)
    grad_packed = jnp.stack([grad_query, grad_key, grad_value], axis=1)
    grad_tokens_qkv = lax.all_to_all(
        grad_packed, "ulysses", split_axis=0, concat_axis=2, tiled=True
    ).reshape(row_count, 3 * model_width)
    grad_project = jnp.einsum(
        "tc,tk->ck", mixed_one, grad_tokens_qkv, preferred_element_type=jnp.float32
    )
    grad_mixed_one = jnp.einsum(
        "tk,ck->tc", grad_tokens_qkv, project_full, preferred_element_type=jnp.float32
    )
    grad_shift_one = jnp.sum(grad_mixed_one, axis=0)
    grad_scale_one = jnp.sum(grad_mixed_one * normed_one * gain_one_f, axis=0)
    grad_gain_one = jnp.sum(grad_mixed_one * normed_one * (1.0 + scale_one), axis=0)
    grad_input = grad_middle + norm_back(grad_mixed_one * gain_first, normed_one, inverse_one)
    mod_terms = jnp.concatenate(
        [
            grad_shift_one,
            grad_scale_one,
            grad_gate_one,
            grad_shift_two,
            grad_scale_two,
            grad_gate_two,
        ]
    )
    grad_modulation = lax.psum(mod_terms, BOTH)
    grad_condition = jnp.dot(ada_float, grad_modulation, precision=highest)
    piece_width = ada_weight.shape[1]
    flat_index = lax.axis_index("ulysses") * cycle_size + cycle_place
    mod_piece = lax.dynamic_slice_in_dim(grad_modulation, flat_index * piece_width, piece_width, 0)
    grad_ada = condition[:, None] * mod_piece[None, :]
    shards = (
        lax.psum_scatter(grad_gain_one, BOTH, scatter_dimension=0, tiled=True),
        lax.psum_scatter(grad_gain_two, BOTH, scatter_dimension=0, tiled=True),
        lax.psum_scatter(grad_project, BOTH, scatter_dimension=1, tiled=True),
        lax.psum_scatter(grad_output, BOTH, scatter_dimension=0, tiled=True),
        lax.psum_scatter(grad_expand, BOTH, scatter_dimension=1, tiled=True),
        lax.psum_scatter(grad_expand_shift, BOTH, scatter_dimension=0, tiled=True),
        lax.psum_scatter(grad_reduce, BOTH, scatter_dimension=0, tiled=True),
        lax.psum_scatter(grad_reduce_shift, BOTH, scatter_dimension=0, tiled=True),
    )
    return (
        result,
        grad_input,
        grad_condition,
        grad_ada,
        mod_piece,
        shards[0],
        shards[1],
        shards[2],
        shards[3],
        shards[4],
        shards[5],
        shards[6],
        shards[7],
    )


MESH = pl.DeviceIdType.MESH
Y, ZH, ZL, X, C = 16, 8, 4, 2, 1
ATTN = (0, X, ZH, X + ZH)
MLP = (0, X, ZL, X + ZL)
BLK = 128
f32 = jnp.float32
bf16 = jnp.bfloat16


def place():
    blk = lax.axis_index("blk")
    return (lax.axis_index("ulysses"), blk // 8, (blk // 4) % 2, (blk // 2) % 2, blk % 2)


def flip(offset):
    return tuple(
        1 - bit if (offset // weight) % 2 else bit
        for bit, weight in zip(place(), (Y, ZH, ZL, X, C))
    )


def device_at(y, zh, zl, x, c):
    return (y, zh * 8 + zl * 4 + x * 2 + c)


def peer(offset):
    return device_at(*flip(offset))


def peer_loop(offset):
    return device_at(
        *(
            (bit + (offset // weight) % 2) % 2
            for bit, weight in zip(place(), (Y, ZH, ZL, X, C))
        )
    )


def flat(device):
    return device[0] * 16 + device[1]


def share(offset, far):
    y, zh, zl, x, c = flip(offset)
    return c * 4 + y * 2 + (zl if far == ZL else zh)


def rank(offset):
    y, zh, zl, x, c = flip(offset)
    return zh * 2 + x


def member(which, slot):
    return device_at((slot // 2) % 2, which // 2, slot % 2, which % 2, slot // 4)


def greet(offsets):
    barrier = pltpu.get_barrier_semaphore()
    for offset in offsets:
        pl.semaphore_signal(barrier, inc=1, device_id=peer(offset), device_id_type=MESH)
    return lambda: pl.semaphore_wait(barrier, len(offsets))


def remote_to(source, target, send_sem, recv_sem, device):
    return pltpu.make_async_remote_copy(
        src_ref=source,
        dst_ref=target,
        send_sem=send_sem,
        recv_sem=recv_sem,
        device_id=device,
        device_id_type=MESH,
    )


def remote(source, target, send_sem, recv_sem, offset):
    return remote_to(source, target, send_sem, recv_sem, peer(offset))


def dot_nn(a, b):
    return jnp.dot(a, b, preferred_element_type=f32)


def dot_nt(a, b):
    return lax.dot_general(a, b, (((1,), (1,)), ((), ())), preferred_element_type=f32)


def dot_tn(a, b):
    return lax.dot_general(a, b, (((0,), (0,)), ((), ())), preferred_element_type=f32)


def exact(a, b, contract):
    return lax.dot_general(
        a, b, (contract, ((), ())), preferred_element_type=f32, precision=highest
    )


def column_sum(value):
    return jnp.sum(value, axis=0, keepdims=True)


class Gather:
    def __init__(self, view, send_sem, recv_sem, far, pieces):
        own, core = share(0, far), share(C, far)
        z, y = share(far, far), share(Y, far)
        both = share(Y + far, far)
        half, other = own // 4 * 4, core // 4 * 4

        def pair(mine, theirs, index, to, piece=lambda v: v):
            return tuple(
                remote(piece(where), piece(where), send_sem.at[index], recv_sem.at[index], to)
                for where in (mine, theirs)
            )

        self.y_own = pair(view(own, 1), view(y, 1), 0, Y)
        self.cores = pair(view(half, 4), view(other, 4), 1, C)
        self.over_z = [
            pair(view(own, 1), view(z, 1), 2 + 2 * index, far, piece)
            for index, piece in enumerate(pieces)
        ]
        self.over_y = [
            pair(view(z, 1), view(both, 1), 3 + 2 * index, Y, piece)
            for index, piece in enumerate(pieces)
        ]

    def near(self):
        self.y_own[0].start()

    def far(self, which=0):
        self.over_z[which][0].start()

    def second(self, which=0):
        self.over_z[which][1].wait_recv()
        self.over_y[which][0].start()

    def third(self):
        for _out, into in (self.y_own, *self.over_y):
            into.wait_recv()
        self.cores[0].start()

    def last(self):
        self.cores[1].wait_recv()

    def finish(self):
        for out, _into in (self.y_own, self.cores, *self.over_z, *self.over_y):
            out.wait_send()


class Spread:
    def __init__(self, view, place_of, order, send_sem, recv_sem):
        self.out, self.into = [], []
        size = 1
        for index, to in enumerate(order):
            mine, other = (place_of(flip(to_where)) // size * size for to_where in (0, to))
            sems = (send_sem.at[index], recv_sem.at[index])
            self.out.append(remote(view(mine, size), view(mine, size), *sems, to))
            self.into.append(remote(view(other, size), view(other, size), *sems, to))
            size *= 2

    def step(self, index):
        if index:
            self.into[index - 1].wait_recv()
        self.out[index].start()

    def last(self):
        self.into[-1].wait_recv()

    def finish(self):
        for copy in self.out:
            copy.wait_send()


class Scatter:
    def __init__(self, view, inbox, send_sem, recv_sem, far):
        self.view, self.inbox = view, inbox
        own = share(0, far)
        core, y, z = share(C, far), share(Y, far), share(far, far)
        self.plan = {
            C: (core // 4 * 4, own // 4 * 4, 4, 0), Y: (y // 2 * 2, own // 2 * 2, 2, 4),
            far: (z, own, 1, 6),
        }
        self.send_sem, self.recv_sem = send_sem, recv_sem
        self.copies = {}

    def step(self, to):
        goes, _stays, size, slot = self.plan[to]
        index = len(self.copies)
        self.copies[to] = remote(
            self.view(goes, size), self.inbox(slot, size), self.send_sem.at[index],
            self.recv_sem.at[index], to,
        )
        self.copies[to].start()

    def add(self, to):
        self.copies[to].wait_recv()
        _goes, stays, size, slot = self.plan[to]
        block = self.view(stays, size)
        block[...] = (
            block[...].astype(f32) + self.inbox(slot, size)[...].astype(f32)
        ).astype(bf16)

    def finish(self):
        for copy in self.copies.values():
            copy.wait_send()


class Total:
    def __init__(self, halves, inbox, first, last, send_sem, recv_sem):
        self.halves, self.inbox, self.first, self.last = halves, inbox, first, last
        y, zh, zl, x, c = place()
        self.core = c
        self.own = (y * 2 + zh, zl * 2 + x)
        sems = [(send_sem.at[index], recv_sem.at[index]) for index in range(8)]
        self.copies = [
            remote(ref.at[own], ref.at[own], *sems[3 * which + index], to)
            for which, (ref, own, offsets) in enumerate(
                ((first, self.own[0], (Y, ZH, Y + ZH)), (last, self.own[1], (ZL, X, ZL + X)))
            )
            for index, to in enumerate(offsets)
        ]
        self.copies.append(remote(halves.at[1 - c], inbox.at[0], *sems[6], C))
        self.copies.append(remote(inbox.at[1 + c], inbox.at[1 + c], *sems[7], C))

    def start(self):
        self.copies[6].start()

    def second(self):
        self.copies[6].wait_recv()
        self.first[self.own[0]] = self.halves[self.core] + self.inbox[0]
        for copy in self.copies[0:3]:
            copy.start()

    def third(self):
        for copy in self.copies[0:3]:
            copy.wait_recv()
        self.last[self.own[1]] = (
            self.first[0] + self.first[1] + self.first[2] + self.first[3]
        )
        for copy in self.copies[3:6]:
            copy.start()

    def fourth(self):
        for copy in self.copies[3:6]:
            copy.wait_recv()
        self.inbox[1 + self.core] = self.last[0] + self.last[1] + self.last[2] + self.last[3]
        self.copies[7].start()

    def result(self):
        self.copies[7].wait_recv()
        return jnp.concatenate([self.inbox[1], self.inbox[2]], axis=0)

    def finish(self):
        for copy in self.copies:
            copy.wait_send()


def turn(value, cosine, sine):
    lane = lax.broadcasted_iota(jnp.int32, value.shape, 1)
    swapped = jnp.where(
        lane < HEAD_DIM // 2,
        pltpu.roll(value, BLK - HEAD_DIM // 2, 1),
        pltpu.roll(value, HEAD_DIM // 2, 1),
    )
    return value * cosine + swapped * sine


def head_rows(first, count, low):
    for row in range(first, first + count, 8):
        yield row - first, row // HEAD_DIM, row % HEAD_DIM + (0 if low else HEAD_DIM)


def gelu_pair(hidden):
    scale = math.sqrt(2.0 / math.pi)
    square = hidden * hidden
    bend = jnp.tanh(scale * hidden * (1.0 + 0.044715 * square))
    half = 0.5 * (1.0 + bend)
    slope = half + 0.5 * hidden * (1.0 - bend * bend) * (
        scale * (1.0 + 3.0 * 0.044715 * square)
    )
    return hidden * half, slope


def to_column(row):
    count = row.shape[1]
    one = lax.broadcasted_iota(jnp.int32, (count, count), 0)
    two = lax.broadcasted_iota(jnp.int32, (count, count), 1)
    return jnp.sum(jnp.where(one == two, row, 0.0), axis=1, keepdims=True)


def to_row(column):
    count = column.shape[0]
    one = lax.broadcasted_iota(jnp.int32, (count, count), 0)
    two = lax.broadcasted_iota(jnp.int32, (count, count), 1)
    return jnp.sum(jnp.where(one == two, column, 0.0), axis=0, keepdims=True)


def block_kernel(names, *refs):
    s = types.SimpleNamespace(**dict(zip(names, refs)))
    rows, width = s.tokens.shape
    wide = width + BLK
    heads = s.query.shape[0]
    count = s.output_weight_hbm.shape[0]
    per = s.reduce_weight_hbm.shape[0]
    units = 8 * per
    scale = HEAD_DIM ** (-0.5)
    me = flat(peer(0))
    own, own_mlp = share(0, ZL), share(0, ZH)
    my_rank = rank(0)

    def here(slot):
        return slice(slot * rows, (slot + 1) * rows)

    loads = {}

    def load(name, target=None):
        number = len(loads)
        copy = pltpu.make_async_copy(
            getattr(s, name + "_hbm"), getattr(s, name) if target is None else target,
            s.load_sem.at[number],
        )
        copy.start()
        loads[name] = copy

    for name in (
        "ada", "condition", "ada_bias", "first_gain", "second_gain", "reduce_bias",
        "project_weight",
    ):
        load(name)
    def out_place(bits):
        y, zh, zl, x, c = bits
        return c * 16 + y * 8 + zh * 4 + zl * 2 + x

    entered = greet(range(1, 32))
    piece = s.ada.shape[0]
    for name in ("ada", "condition", "ada_bias", "first_gain", "second_gain", "reduce_bias"):
        loads[name].wait()
    for index in range(width // BLK):
        s.adaw[out_place(flip(0)), :, index * BLK : (index + 1) * BLK] = s.ada[
            index * count : (index + 1) * count, :
        ]
    s.vec_own[...] = jnp.zeros_like(s.vec_own)
    s.vec_own[0:8, 0:piece] = exact(
        jnp.broadcast_to(s.condition[...], (8, s.condition.shape[1])),
        s.ada[...].astype(f32), ((1,), (1,)),
    )
    s.vec_own[0:1, 0:piece] += s.ada_bias[...].astype(f32)
    for index, ref in enumerate((s.first_gain, s.second_gain, s.reduce_bias)):
        s.vec_own[8 + index : 9 + index, 0:count] = ref[...].astype(f32)
    mod_shift = (me % 8) * 16
    gain_shift = ((3 * me) % 16) * 8
    y, zh, zl, x, c = place()
    vec_own = y * 16 + x * 8 + c * 4 + zh * 2 + zl
    s.vecs[vec_own, 0:1, :] = pltpu.roll(s.vec_own[0:8, :], mod_shift, 1)[0:1, :]
    s.vecs[vec_own, 1:4, :] = pltpu.roll(s.vec_own[8:16, :], gain_shift, 1)[0:3, :]
    lane = lax.broadcasted_iota(jnp.int32, (rows, BLK), 1)
    ones = jnp.where(lane == 0, 1.0, 0.0).astype(bf16)
    for slot in range(4):
        s.mix[slot, :, width:] = ones
        s.plain[here(slot), width:] = ones
    loads["project_weight"].wait()
    entered()

    def token_copy(have, to):
        slot = ATTN.index(have + to)
        return remote(
            s.tok.at[ATTN.index(have)] if have else s.tokens, s.tok.at[slot],
            s.tok_ss.at[slot], s.tok_rs.at[slot], to,
        )

    token_copies = [token_copy(0, X), token_copy(0, ZH), token_copy(ZH, X)]
    vec_steps = []
    for index, (size, offsets) in enumerate(
        ((1, (ZL, ZH, ZL + ZH)), (4, (C, X, X + C)), (16, (Y,)))
    ):
        where = s.vecs.at[pl.ds(vec_own // size * size, size)]
        vec_steps.append(
            [
                remote(
                    where, where, s.vec_ss.at[3 * index + number], s.vec_rs.at[3 * index + number],
                    to,
                )
                for number, to in enumerate(offsets)
            ]
        )

    def vec_step(index):
        for copy in vec_steps[index - 1] if index else ():
            copy.wait_recv()
        for copy in vec_steps[index] if index < 3 else ():
            copy.start()

    vec_step(0)
    def chunk_out(index):
        number = 3 * me + index
        part, place_in = number // 32, number % 32
        slot = place_in % 8
        device = member(place_in // 8, slot)
        target = s.chunks.at[slot, part]
        far = remote_to(
            s.project_weight.at[index], target, s.chunk_ss.at[index], s.chunk_rs.at[index], device
        )
        near = pltpu.make_async_copy(s.project_weight.at[index], target, s.local_sem.at[index])
        return far, near, flat(device) == me

    for index in range(3):
        far, near, stays = chunk_out(index)

        @pl.when(jnp.logical_not(stays))
        def _():
            far.start()

        @pl.when(stays)
        def _():
            near.start()

    for name in ("tokens", "expand_bias"):
        load(name)
    load("expand_weight", s.er.at[own_mlp, :, pl.ds(0, width)])
    load("reduce_weight", s.er.at[own_mlp, :, pl.ds(wide, width)])

    load("output_weight", s.outw.at[out_place(flip(0))])
    load("cotangent", s.cot.at[0])
    tables = []
    for slot in range(4):
        start = pl.multiple_of(peer(ATTN[slot])[1] * rows, rows)
        copy = pltpu.make_async_copy(
            s.table_hbm.at[pl.ds(start, rows)], s.table.at[pl.ds(slot * rows, rows)],
            s.table_sem.at[slot],
        )
        copy.start()
        tables.append(copy)
    gather_er = Gather(
        lambda slot, size: s.er.at[pl.ds(slot, size)], s.er_ss, s.er_rs, ZH,
        (
            lambda v: v.at[:, :, pl.ds(wide, width)],
            lambda v: v.at[:, :, pl.ds(0, wide)],
        ),
    )
    loads["expand_bias"].wait()
    lane = lax.broadcasted_iota(jnp.int32, (per, BLK), 1)
    s.er[own_mlp, :, width:wide] = jnp.where(
        lane == 0, to_column(s.expand_bias[...].astype(f32)), 0.0
    ).astype(bf16)
    zero = jnp.zeros((HEAD_DIM, width), bf16)
    for head in range(heads):
        s.weight[head, HEAD_DIM:, :] = zero
    s.state_m[...] = jnp.full_like(s.state_m, -1e30)
    s.state_l[...] = jnp.zeros_like(s.state_l)
    s.acc[...] = jnp.zeros_like(s.acc)
    spread_out = Spread(
        lambda slot, size: s.outw.at[pl.ds(slot, size)], out_place, (X, ZL, ZH, Y, C),
        s.o_ss, s.o_rs,
    )
    spread_ada = Spread(
        lambda slot, size: s.adaw.at[pl.ds(slot, size)], out_place, (X, ZL, ZH, Y, C),
        s.ada_ss, s.ada_rs,
    )
    for name in ("expand_weight", "reduce_weight", "output_weight", "cotangent", "tokens"):
        loads[name].wait()
    vec_step(1)
    spread_out.step(0)
    spread_ada.step(0)

    for index in range(3):
        far, near, stays = chunk_out(index)

        @pl.when(jnp.logical_not(stays))
        def _():
            far.wait()

        @pl.when(stays)
        def _():
            near.wait()

    gather_a = Gather(
        lambda slot, size: s.chunks.at[pl.ds(slot, size)], s.a_ss, s.a_rs, ZL, (lambda v: v,)
    )
    def cot_copy(have, to):
        slot = MLP.index(have + to)
        return remote(
            s.cot.at[MLP.index(have)], s.cot.at[slot], s.cot_ss.at[slot], s.cot_rs.at[slot], to
        )

    cot_copies = [cot_copy(0, X), cot_copy(0, ZL), cot_copy(ZL, X)]
    gather_a.far()
    gather_a.near()
    token_copies[1].start()
    token_copies[0].start()
    vec_step(2)
    spread_out.step(1)
    spread_ada.step(1)
    gather_a.second()
    cot_copies[1].start()
    vec_step(3)
    s.mod_row[...] = jnp.zeros_like(s.mod_row)
    s.gain_rows[...] = jnp.zeros_like(s.gain_rows)
    for index in range(32):
        y, zh, zl, x, c = ((index // weight) % 2 for weight in (Y, ZH, ZL, X, C))
        found = y * 16 + x * 8 + c * 4 + zh * 2 + zl
        tile = (9 * index) // 8 * BLK
        s.mod_row[0:1, tile : tile + 2 * BLK] += s.vecs[found, 0:1, :]
        tile = (3 * index) // 16 * BLK
        s.gain_rows[0:3, tile : tile + 2 * BLK] += s.vecs[found, 1:4, :]
    shift_one, scale_one, gate_one, shift_two, scale_two, gate_two = range(6)
    for index in range(6):
        s.mods[index : index + 1, :] = s.mod_row[0:1, index * width : (index + 1) * width]
    s.mods[6:9, :] = s.gain_rows[0:3, 0:width]
    s.mods[9:10, :] = s.mods[6:7, :] * (1.0 + s.mods[scale_one : scale_one + 1, :])
    s.mods[10:11, :] = s.mods[7:8, :] * (1.0 + s.mods[scale_two : scale_two + 1, :])

    def mod(index):
        return s.mods[index : index + 1, :]

    for slot in range(4):
        if slot == 1 or slot == 3:
            token_copies[slot - 1].wait_recv()
        if slot == 2:
            token_copies[1].wait_recv()
            token_copies[2].start()
            cot_copies[0].start()
            spread_out.step(2)
            gather_er.far(0)
            gather_er.near()
            gather_a.third()
        source = s.tok[slot] if slot else s.tokens[...]
        normed, _unused = layer_norm(source.astype(f32))
        s.mixed[here(slot), :] = (normed * mod(9) + mod(shift_one)).astype(bf16)
        s.plain[here(slot), 0:width] = normed.astype(bf16)
    def assemble(part, base, low):
        for slot in range(8):
            for row, head, target in head_rows(slot * count, count, low):
                s.weight[base + head, target : target + 8, :] = s.chunks[
                    slot, part, row : row + 8, :
                ]

    gather_er.far(1)
    gather_a.last()
    assemble(1, heads, True)
    assemble(2, heads, False)
    for copy in tables:
        copy.wait()
    kv_far = [
        remote(s.kv.at[0, head], s.kv.at[2, head], s.kv_ss.at[head], s.kv_rs.at[head], ZL)
        for head in range(heads)
    ]
    kv_near = [
        remote(
            s.kv.at[0, head], s.kv.at[1, head], s.kv_ss.at[heads + head],
            s.kv_rs.at[heads + head], C,
        )
        for head in range(heads)
    ]
    for head in range(heads):
        both = dot_nt(s.mixed[...], s.weight[heads + head]).astype(bf16).astype(f32)
        s.kv[0, head] = turn(both, s.table[:, 0:BLK], s.table[:, BLK:]).astype(bf16)
        kv_far[head].start()
        kv_near[head].start()
    assemble(0, 0, True)
    for head in range(heads):
        query = dot_nt(s.mixed[...], s.weight[head]).astype(bf16).astype(f32)
        query = turn(query, s.table[:, 0:BLK], s.table[:, BLK:]).astype(bf16).astype(f32)
        s.query[head] = (query * scale).astype(bf16)
    cot_copies[1].wait_recv()
    cot_copies[2].start()
    spread_out.step(3)


    def attend(slot, head):
        keys = s.kv[slot, head]
        scores = dot_nt(keys, s.query[head])
        before = s.state_m[head]
        maximum = jnp.maximum(before, jnp.max(scores, axis=0, keepdims=True))
        weights = jnp.exp(scores - maximum)
        factor = jnp.exp(before - maximum)
        s.state_m[head] = maximum
        s.state_l[head] = s.state_l[head] * factor + column_sum(weights)
        s.acc[head] = s.acc[head] * factor + dot_tn(keys, weights.astype(bf16))

    for head in range(heads):
        kv_near[head].wait_recv()

    @pl.loop(0, heads)
    def _(head):
        attend(0, head)
        attend(1, head)

    gather_er.second(0)

    def kv_forward(head):
        return remote(
            s.kv.at[2, head], s.kv.at[3, head], s.kv_ss.at[2 * heads + head],
            s.kv_rs.at[2 * heads + head], C,
        )

    @pl.loop(0, heads)
    def _(head):
        remote(
            s.kv.at[0, head], s.kv.at[2, head], s.kv_ss.at[head], s.kv_rs.at[head], ZL
        ).wait_recv()
        forward = kv_forward(head)
        forward.start()

        @pl.when(head == 1)
        def _():
            gather_er.second(1)

        attend(2, head)
        forward.wait_recv()
        attend(3, head)
        value = (s.acc[head] / s.state_l[head]).astype(bf16)
        s.att[head] = value[HEAD_DIM:, :]
        s.logt[head] = s.state_m[head] + jnp.log(s.state_l[head])

    for slot in range(4):
        for head in range(heads):
            s.att_send[slot, head] = s.att[head, :, here(slot)]
    att_copies = [
        remote(
            s.att_send.at[slot], s.att_all.at[my_rank], s.att_ss.at[slot], s.att_rs.at[slot],
            ATTN[slot],
        )
        for slot in range(1, 4)
    ]
    for copy in att_copies:
        copy.start()
    s.att_all[my_rank] = s.att_send[0]
    spread_out.step(4)
    gather_er.third()
    spread_out.last()
    for y in range(2):
        for zh, zl, x, c in itertools.product(range(2), repeat=4):
            at = (y * 16 + zh * 8 + zl * 4 + x * 2 + c) * count
            s.out_full[at : at + count, :] = s.outw[c * 16 + y * 8 + zh * 4 + zl * 2 + x]
    for slot in range(1, 4):
        where = s.att_all.at[rank(ATTN[slot])]
        remote(where, where, s.att_ss.at[slot], s.att_rs.at[slot], ATTN[slot]).wait_recv()
    s.attn[...] = dot_tn(s.att_all[...].reshape(width, rows), s.out_full[...])
    s.middle[...] = s.tokens[...].astype(f32) + mod(gate_one) * s.attn[...]
    normed, inverse = layer_norm(s.middle[...])
    s.normed[...] = normed
    s.inverse[...] = inverse
    s.mix[0, :, :width] = (normed * mod(10) + mod(shift_two)).astype(bf16)
    def mix_copy(source, slot, number, lines, to):
        return remote(
            s.mix.at[source, lines, pl.ds(0, width)], s.mix.at[slot, lines, pl.ds(0, width)],
            s.mix_ss.at[number], s.mix_rs.at[number], to,
        )

    mix_copies = [
        mix_copy(0, 1, 0, pl.ds(0, rows), X),
        mix_copy(0, 2, 1, pl.ds(0, rows), ZL),
        mix_copy(1, 3, 2, pl.ds(0, rows // 2), ZL),
        mix_copy(2, 3, 3, pl.ds(rows // 2, rows // 2), X),
    ]
    for copy in mix_copies[0:2]:
        copy.start()
    for slot in range(4):
        if slot == 1 or slot == 3:
            cot_copies[slot - 1].wait_recv()
        s.branch[here(slot), :] = (mod(gate_two) * s.cot[slot].astype(f32)).astype(bf16)
    gather_er.last()

    def expand(lanes=wide):
        return s.er[:, :, 0:lanes].reshape(units, lanes)

    def reduce():
        return s.er[:, :, wide:].reshape(units, width)

    spread_ada.step(2)
    gm_copies = [
        remote(
            s.gm_send.at[slot - 1], s.gm_recv.at[slot - 1], s.gm_ss.at[slot], s.gm_rs.at[slot],
            MLP[slot],
        )
        for slot in range(1, 4)
    ]
    for first, last in ((0, 1), (1, 3), (3, 4)):
        if first == 1:
            for index in range(2):
                mix_copies[index].wait_recv()
                mix_copies[2 + index].start()
        elif first == 3:
            mix_copies[2].wait_recv()
            mix_copies[3].wait_recv()
        these = slice(first * rows, last * rows)
        mixed_two = s.mix[first:last].reshape((last - first) * rows, wide)
        activated, slope = gelu_pair(dot_nt(mixed_two, expand()))
        s.active[these, :] = activated.astype(bf16)
        grad_hidden = (dot_nt(s.branch[these, :], reduce()) * slope).astype(bf16)
        s.grad_hid[these, :] = grad_hidden
        gm_part = dot_nn(grad_hidden, expand(width))
        for slot in range(first, last):
            part = gm_part[(slot - first) * rows : (slot - first + 1) * rows, :]
            if slot:
                s.gm_send[slot - 1] = part.astype(bf16)
                gm_copies[slot - 1].start()
            else:
                s.grad_mixed[...] = part
    for index in range(units // BLK):
        lanes = slice(index * BLK, (index + 1) * BLK)
        s.wide[lanes, 0:width] = dot_tn(s.active[:, lanes], s.branch[...])
    for index in range(8):
        s.blocks_r[index] = s.wide[index * per : (index + 1) * per, 0:width].astype(bf16)
    scatter_r = Scatter(
        lambda slot, size: s.blocks_r.at[pl.ds(slot, size)],
        lambda slot, size: s.from_r.at[pl.ds(slot, size)], s.sr_ss, s.sr_rs, ZH
    )
    scatter_r.step(C)
    for index in range(units // BLK):
        lanes = slice(index * BLK, (index + 1) * BLK)
        s.wide[lanes, :] = dot_tn(
            s.grad_hid[:, lanes], s.mix[...].reshape(4 * rows, width + BLK)
        )
    scatter_r.add(C)
    scatter_r.step(Y)
    for index in range(8):
        s.blocks_e[index] = s.wide[index * per : (index + 1) * per, :].astype(bf16)
    scatter_e = Scatter(
        lambda slot, size: s.blocks_e.at[pl.ds(slot, size)],
        lambda slot, size: s.from_e.at[pl.ds(slot, size)], s.se_ss, s.se_rs, ZH
    )
    scatter_e.step(C)
    def mlp_copy(slot, number, to):
        return remote(
            s.mlp_send.at[slot], s.mlp_recv.at[number], s.mlp_ss.at[slot], s.mlp_rs.at[number], to
        )

    mlp_copies = [mlp_copy(2, 2, X), mlp_copy(0, 0, X), mlp_copy(1, 1, ZL)]

    def mlp_part(slot):
        return dot_nn(s.active[here(slot), :], reduce())

    s.mlp_send[2] = mlp_part(3).astype(bf16)
    s.mlp_send[0] = mlp_part(1).astype(bf16)
    s.mlp[...] = mlp_part(0) + mod(8)
    s.mlp_near[...] = mlp_part(2)
    for index in range(units // BLK):
        lanes = slice(index * BLK, (index + 1) * BLK)
        s.wide[lanes, 0:width] = dot_tn(s.active[:, lanes], s.cot[...].reshape(4 * rows, width))
    gate_sum = mod(8) * column_sum(s.cot[0].astype(f32))
    for index in range(8):
        gate_sum = gate_sum + column_sum(
            s.er[index, :, wide:].astype(f32) * s.wide[index * per : (index + 1) * per, 0:width]
        )
    s.rowsum[5:6, :] = gate_sum
    for copy in gm_copies:
        copy.wait()
    mlp_copies[0].start()
    grad_mixed = (
        s.grad_mixed[...]
        + s.gm_recv[0].astype(f32) + s.gm_recv[1].astype(f32) + s.gm_recv[2].astype(f32)
    )
    cot = s.cot[0].astype(f32)
    normed = s.normed[...]
    grad_middle = cot + norm_back(grad_mixed * mod(10), normed, s.inverse[...])
    s.gmid[...] = grad_middle
    grad_attn = (mod(gate_one) * grad_middle).astype(bf16)
    s.gattn[0] = grad_attn
    s.dout_send[...] = dot_nt(s.out_full[...], grad_attn).astype(bf16).reshape(
        s.dout_send.shape
    )
    dout_copies = [
        remote(
            s.dout_send.at[rank(ATTN[slot])], s.dout_recv.at[slot], s.dout_ss.at[slot],
            s.dout_rs.at[slot], ATTN[slot],
        )
        for slot in range(1, 4)
    ]
    for copy in dout_copies:
        copy.start()
    s.dout_recv[0] = s.dout_send[my_rank]
    def ga_copy(have, to):
        slot = ATTN.index(have + to)
        return remote(
            s.gattn.at[ATTN.index(have)], s.gattn.at[slot], s.ga_ss.at[slot], s.ga_rs.at[slot], to
        )

    ga_copies = [ga_copy(0, X), ga_copy(0, ZH), ga_copy(ZH, X)]
    weighted = column_sum(grad_mixed * normed)
    s.rowsum[2:3, :] = column_sum(grad_middle * s.attn[...])
    s.rowsum[3:4, :] = column_sum(grad_mixed)
    s.rowsum[4:5, :] = weighted * mod(7)
    s.rowsum[7:8, :] = weighted * (1.0 + mod(scale_two))
    s.rowsum[8:9, :] = column_sum(s.branch[here(0), :].astype(f32))
    scatter_e.add(C)
    scatter_e.step(Y)

    s.dout_t[...] = jnp.zeros_like(s.dout_t)
    for slot in range(4):
        if slot:
            dout_copies[slot - 1].wait()
        if slot == 3:
            ga_copies[1].start()
        for head in range(heads):
            s.dout_t[head, HEAD_DIM:, here(slot)] = s.dout_recv[slot, head]
    for head in range(heads):
        value = s.dout_t[head].astype(f32)
        s.dout[head] = value.T.astype(bf16)
        s.rdots[head] = column_sum(value[HEAD_DIM:, :] * s.att[head].astype(f32))
    scatter_r.add(Y)
    scatter_r.step(ZH)
    ga_copies[0].start()
    mlp_copies[1].start()
    s.dq[...] = jnp.zeros_like(s.dq)

    def back(slot, head):
        keys = s.kv[slot, head]
        query = s.query[head]
        shares = jnp.exp(dot_nt(keys, query) - s.logt[head])
        grad_shares = dot_nn(keys, s.dout_t[head])
        grad_scores = (shares * (grad_shares - s.rdots[head])).astype(bf16)
        s.dq[head] += dot_tn(keys, grad_scores)
        return dot_nn(grad_scores, query) + dot_nn(shares.astype(bf16), s.dout[head])

    def dkv_copy(stage, head, offset):
        index = stage * heads + head
        return remote(
            s.dkv_send.at[index], s.dkv_recv.at[index], s.dkv_ss.at[index], s.dkv_rs.at[index],
            offset,
        )

    @pl.loop(0, heads)
    def _(head):
        s.dkv_send[head] = back(3, head).astype(bf16)
        first = dkv_copy(0, head, C)
        first.start()
        part = back(2, head)
        first.wait_recv()
        s.dkv_send[heads + head] = (part + s.dkv_recv[head].astype(f32)).astype(bf16)
        dkv_copy(1, head, ZL).start()

    scatter_e.add(Y)
    scatter_e.step(ZH)
    spread_ada.step(3)

    @pl.loop(0, heads)
    def _(head):
        @pl.when(head == 1)
        def _():
            ga_copies[1].wait_recv()
            ga_copies[2].start()

        s.dkv_send[2 * heads + head] = back(1, head).astype(bf16)
        dkv_copy(2, head, C).start()
        s.dkv[head] = back(0, head)
        value = s.dq[head].T * scale
        s.dqkv[head] = turn(value, s.table[:, 0:BLK], -s.table[:, BLK:]).astype(bf16)

    spread_ada.step(4)
    query_part = dot_nn(s.dqkv[0], s.weight[0])
    for head in range(1, heads):
        query_part = query_part + dot_nn(s.dqkv[head], s.weight[head])
    s.part[...] = query_part
    ga_copies[0].wait_recv()
    ga_copies[2].wait_recv()
    gattn = s.gattn[...].reshape(4 * rows, width)

    def spread(part, low, of):
        for slot in range(8):
            for row, head, target in head_rows(slot * count, count, low):
                s.blocks_a[(part + 1) % 4 // 2, slot, (part + 1) % 2, row : row + 8, :] = s.wide[
                    of * heads * BLK + head * BLK + target
                    : of * heads * BLK + head * BLK + target + 8, 0:width
                ].astype(bf16)

    def scatter_pair(pair, ss, rs):
        return Scatter(
            lambda slot, size: s.blocks_a.at[pair, pl.ds(slot, size)],
            lambda slot, size: s.from_a.at[pair, pl.ds(slot, size)],
            ss, rs, ZL,
        )

    for head in range(heads):
        s.wide[head * BLK + HEAD_DIM : (head + 1) * BLK, 0:width] = dot_nn(s.att[head], gattn)
        at = (heads + head) * BLK
        s.wide[at : at + BLK, 0:width] = dot_tn(s.dqkv[head], s.mixed[...])
    spread(3, False, 0)
    spread(0, True, 1)
    scatter_oq = scatter_pair(0, s.soq_ss, s.soq_rs)
    scatter_kv = scatter_pair(1, s.skv_ss, s.skv_rs)
    scatter_oq.step(C)
    for head in range(heads):
        dkv_copy(2, head, C).wait_recv()
        s.dkv[head] += s.dkv_recv[2 * heads + head].astype(f32)
    for head in range(heads):
        dkv_copy(1, head, ZL).wait_recv()
        value = s.dkv[head] + s.dkv_recv[heads + head].astype(f32)
        s.dqkv[heads + head] = turn(value, s.table[:, 0:BLK], -s.table[:, BLK:]).astype(bf16)
    kv_part = s.part[...]
    for head in range(heads, 2 * heads):
        kv_part = kv_part + dot_nn(s.dqkv[head], s.weight[head])

    def part_copy(slot, number, to):
        return remote(
            s.part_send.at[slot], s.part_recv.at[number], s.part_ss.at[slot],
            s.part_rs.at[number], to,
        )

    def part_half(slot, number, to, half):
        lines = pl.ds(half * (rows // 2), rows // 2)
        return remote(
            s.part_send.at[slot, lines], s.part_recv.at[number, lines],
            s.part_ss.at[slot + 3 * half], s.part_rs.at[number + 3 * half], to,
        )

    relays = [(part_half(2, 2, X, half), part_half(1, 1, ZH, half)) for half in range(2)]
    part_copies = [part_copy(0, 0, X)]
    s.part_send[2] = kv_part[here(3), :].astype(bf16)
    for half in range(2):
        relays[half][0].start()
    mlp_copies[0].wait_recv()
    s.mlp_send[1] = (s.mlp_near[...] + s.mlp_recv[2].astype(f32)).astype(bf16)
    mlp_copies[2].start()
    s.part_send[0] = kv_part[here(1), :].astype(bf16)
    s.part[here(2), :] = kv_part[here(2), :]
    s.grad_mixed[...] = kv_part[here(0), :]

    scatter_oq.add(C)
    scatter_oq.step(Y)

    s.norm_sum[...] = jnp.zeros_like(s.norm_sum)
    s.rowsum[9:16, :] = jnp.zeros((7, width), f32)
    for head in range(2 * heads):
        moment = dot_tn(s.dqkv[head], s.plain[...])
        weights = s.weight[head].astype(f32)
        s.norm_sum[0:1, :] += column_sum(weights * moment[:, width : width + 1])
        s.norm_sum[1:2, :] += column_sum(weights * moment[:, 0:width])
    s.rowsum[0:1, :] = s.norm_sum[0:1, :]
    s.rowsum[1:2, :] = s.norm_sum[1:2, :] * mod(6)
    s.rowsum[6:7, :] = s.norm_sum[1:2, :] * (1.0 + mod(scale_one))
    spread_ada.last()
    for y in range(2):
        for zh, zl, x, c in itertools.product(range(2), repeat=4):
            at = (y * 16 + zh * 8 + zl * 4 + x * 2 + c) * piece
            for index in range(width // BLK):
                s.ada_full[at + index * count : at + (index + 1) * count, :] = s.adaw[
                    c * 16 + y * 8 + zh * 4 + zl * 2 + x, :,
                    index * BLK : (index + 1) * BLK,
                ]
    high = s.rowsum[0:8, :].astype(bf16)
    low = (s.rowsum[0:8, :] - high.astype(f32)).astype(bf16)
    both = jnp.concatenate([high, low], axis=0)
    terms = jnp.zeros((1, BLK), f32)
    for index in range(6):
        found = dot_nn(both, s.ada_full[index * width : (index + 1) * width, :])
        terms = terms + found[index : index + 1, :] + found[8 + index : 9 + index, :]
    s.rowsum[9:10, 0:BLK] = terms
    totals = Total(s.sum_halves, s.sum_inbox, s.sum_first, s.sum_last, s.sum_ss, s.sum_rs)
    s.sum_halves[0] = s.rowsum[0:8, :]
    s.sum_halves[1] = s.rowsum[8:16, :]
    totals.start()

    for head in range(heads):
        s.wide[head * BLK : (head + 1) * BLK, 0:width] = dot_tn(
            s.dqkv[heads + head], s.mixed[...]
        )
    totals.second()
    spread(1, True, 0)
    spread(2, False, 0)
    scatter_kv.step(C)
    for half in range(2):
        lines = slice(half * (rows // 2), (half + 1) * (rows // 2))
        relays[half][0].wait_recv()
        s.part_send[1, lines, :] = (
            s.part[2 * rows + lines.start : 2 * rows + lines.stop, :]
            + s.part_recv[2, lines, :].astype(f32)
        ).astype(bf16)
        relays[half][1].start()
    part_copies[0].start()
    scatter_kv.add(C)
    scatter_kv.step(Y)
    scatter_oq.add(Y)

    def chunk_back(part, half):
        slot = own // 2 * 2 + half
        place_in = 8 * my_rank + slot
        if part < 3:
            number = 32 * part + place_in
            owner, at = number // 3, number % 3
        else:
            owner, at = place_in, 3
        z = own % 2
        index = part * 2 + half
        source = s.blocks_a.at[(part + 1) % 4 // 2, slot, (part + 1) % 2]
        target = s.owned.at[z, at]
        far = remote_to(
            source, target, s.back_ss.at[index], s.back_rs.at[z * 4 + at],
            (owner // 16, owner % 16),
        )
        near = pltpu.make_async_copy(source, target, s.local_sem.at[index])
        return far, near, owner == me

    def chunks_back(parts, act):
        for part in parts:
            for half in range(2):
                far, near, stays = chunk_back(part, half)

                @pl.when(jnp.logical_not(stays))
                def _():
                    far.start() if act else far.wait_send()

                @pl.when(stays)
                def _():
                    near.start() if act else near.wait()

    chunks_back((0, 3), True)
    totals.third()
    for index in (1, 2):
        mlp_copies[index].wait_recv()
    mlp_branch = s.mlp[...] + s.mlp_recv[0].astype(f32) + s.mlp_recv[1].astype(f32)
    s.result[...] = (s.middle[...] + mod(gate_two) * mlp_branch).astype(bf16)
    normed_one, inverse_one = layer_norm(s.tokens[...].astype(f32))
    scatter_kv.add(Y)
    chunks_back((1, 2), True)
    totals.fourth()
    sums = totals.result()
    for index in range(6):
        for tile in range(width // BLK):
            s.tiles[index * (width // BLK) + tile] = sums[
                index : index + 1, tile * BLK : (tile + 1) * BLK
            ]
    for tile in range(width // BLK):
        s.gain_tiles[tile] = sums[6:9, tile * BLK : (tile + 1) * BLK]
    s.gain_tiles[width // BLK] = jnp.zeros((3, BLK), f32)
    s.vec_own[...] = jnp.zeros_like(s.vec_own)
    for tile in range(2):
        lanes = slice(tile * BLK, (tile + 1) * BLK)
        s.vec_own[0:1, lanes] = s.tiles[(9 * me) // 8 + tile]
        s.vec_own[9:12, lanes] = s.gain_tiles[(3 * me) // 16 + tile]
    s.sums[0:8, :] = pltpu.roll(s.vec_own[0:8, :], (256 - mod_shift) % 256, 1)
    s.sums[8:16, :] = pltpu.roll(s.vec_own[8:16, :], (256 - gain_shift) % 256, 1)
    s.grad_cond[...] = sums[9:10, 0:BLK]
    s.grad_r[0] = s.blocks_r[own_mlp]
    s.grad_e[0] = s.blocks_e[own_mlp]
    for scatter, target in ((scatter_r, s.grad_r), (scatter_e, s.grad_e)):
        scatter.copies[ZH].wait_recv()
        target[1] = scatter.inbox(6, 1)[0]
    part_copies[0].wait_recv()
    for half in range(2):
        relays[half][1].wait_recv()
    grad_mixed_one = (
        s.grad_mixed[...] + s.part_recv[0].astype(f32) + s.part_recv[1].astype(f32)
    )
    s.grad_tokens[...] = s.gmid[...] + norm_back(
        grad_mixed_one * mod(9), normed_one, inverse_one
    )

    chunks_back(range(4), False)
    for at in range(4):
        if at < 3:
            number = 3 * me + at
            part, place_in = number // 32, number % 32
        else:
            part, place_in = 3, me
        slot = place_in % 8
        for z in range(2):
            keeper = flat(member(place_in // 8, slot // 2 * 2 + z))

            @pl.when(keeper != me)
            def _():
                target = s.owned.at[z, at]
                remote(
                    target, target, s.back_ss.at[0], s.back_rs.at[z * 4 + at], C
                ).wait_recv()

    for copies in (
        kv_far, kv_near, cot_copies, mix_copies, att_copies, ga_copies, mlp_copies, token_copies,
        part_copies, *relays, *vec_steps,
    ):
        for copy in copies:
            copy.wait_send()
    for group in (
        gather_a, gather_er, spread_out, spread_ada, scatter_e, scatter_r, scatter_oq, scatter_kv, totals,
    ):
        group.finish()

    @pl.loop(0, heads)
    def _(head):
        kv_forward(head).wait_send()
        dkv_copy(0, head, C).wait_send()
        dkv_copy(1, head, ZL).wait_send()
        dkv_copy(2, head, C).wait_send()


def finish_kernel(
    result, grad_tokens, grad_cond, sums, grad_e, grad_r, owned, condition,
    result_out, tokens_out, cond_out, ada_out, ada_bias_out, first_out, second_out, project_out,
    output_out, expand_out, expand_bias_out, reduce_out, reduce_bias_out,
):
    width = result.shape[1]
    count = output_out.shape[0]
    piece = ada_out.shape[0]
    result_out[...] = result[...]
    tokens_out[...] = grad_tokens[...]
    cond_out[...] = grad_cond[...]
    first = lax.broadcasted_iota(jnp.int32, (8, piece), 0) == 0
    row = jnp.where(first, sums[0:8, 0:piece], 0.0)
    ada_out[...] = exact(
        row, jnp.broadcast_to(condition[...], (8, condition.shape[1])), ((0,), (0,))
    )
    ada_bias_out[...] = sums[0:1, 0:piece]
    first_out[...] = sums[9:10, 0:count]
    second_out[...] = sums[10:11, 0:count]
    reduce_bias_out[...] = sums[11:12, 0:count]
    both = owned[0].astype(f32) + owned[1].astype(f32)
    project_out[...] = both[0:3]
    output_out[...] = both[3]
    expand = grad_e[0].astype(f32) + grad_e[1].astype(f32)
    expand_out[...] = expand[:, 0:width]
    expand_bias_out[...] = to_row(expand[:, width : width + 1])
    reduce_out[...] = grad_r[0].astype(f32) + grad_r[1].astype(f32)


def rotary_blocks(length):
    half_dim = HEAD_DIM // 2
    frequency = np.exp(
        np.arange(half_dim, dtype=np.float32) * np.float32(-2.0 * math.log(10000.0) / HEAD_DIM)
    ).astype(np.float32)
    angles = (np.arange(length, dtype=np.float32)[:, None] * frequency[None, :]).astype(np.float32)
    cosine, sine = np.cos(angles.astype(np.float64)), np.sin(angles.astype(np.float64))
    one, zero = np.ones((length, HEAD_DIM)), np.zeros((length, HEAD_DIM))
    return np.concatenate([cosine, cosine, one, -sine, sine, zero], axis=1).astype(np.float32)


def on_device_fast(
    tokens, condition, ada_weight, ada_bias, first_gain, second_gain, project_weight,
    output_weight, expand_weight, expand_bias, reduce_weight, reduce_bias, cotangent,
):
    rows, width = tokens.shape
    group = 4 * rows
    heads = width // HEAD_DIM // 4
    per = reduce_weight.shape[0]
    units = 8 * per
    count = output_weight.shape[0]
    piece = ada_weight.shape[1]
    wide = width + BLK
    table = jnp.asarray(rotary_blocks(lax.axis_size("blk") * rows))
    line = condition[None, :]
    inputs = dict(
        tokens=tokens, cotangent=cotangent, condition=line, ada=ada_weight.T,
        ada_bias=ada_bias, first_gain=first_gain[None, :],
        second_gain=second_gain[None, :], reduce_bias=reduce_bias[None, :],
        expand_bias=expand_bias[None, :],
        project_weight=project_weight.T.reshape(3, count, width), output_weight=output_weight,
        expand_weight=expand_weight.T, reduce_weight=reduce_weight, table=table,
    )
    outputs = dict(
        result=((rows, width), bf16), grad_tokens=((rows, width), f32),
        grad_cond=((1, line.shape[1]), f32), sums=((16, 256), f32),
        grad_e=((2, per, wide), bf16), grad_r=((2, per, width), bf16),
        owned=((2, 4, count, width), bf16),
    )
    head_block = (group, BLK)
    kept = {
        name: (inputs[name].shape, inputs[name].dtype)
        for name in (
            "tokens", "condition", "ada", "ada_bias", "first_gain", "second_gain", "reduce_bias",
            "expand_bias", "project_weight",
        )
    }
    scratch = dict(
        **kept,
        table=((group, 2 * BLK), f32), vec_own=((16, 256), f32),
        vecs=((32, 4, 256), f32), mod_row=((1, 6 * width), f32), gain_rows=((3, wide), f32),
        mods=((16, width), f32), chunks=((8, 3, count, width), bf16),
        tok=((4, rows, width), bf16), cot=((4, rows, width), bf16),
        er=((8, per, wide + width), bf16),
        outw=((32, count, width), bf16), adaw=((32, count, width), bf16), ada_full=((6 * width, BLK), bf16), out_full=((width, width), bf16),
        weight=((2 * heads, BLK, width), bf16), mixed=((group, width), bf16),
        query=((heads,) + head_block, bf16), kv=((4, heads) + head_block, bf16),
        state_m=((heads, 1, group), f32), state_l=((heads, 1, group), f32),
        acc=((heads, BLK, group), f32), att=((heads, HEAD_DIM, group), bf16),
        logt=((heads, 1, group), f32), att_send=((4, heads, HEAD_DIM, rows), bf16),
        att_all=((4, heads, HEAD_DIM, rows), bf16), attn=((rows, width), f32),
        middle=((rows, width), f32), normed=((rows, width), f32), inverse=((rows, 1), f32),
        mix=((4, rows, wide), bf16), branch=((group, width), bf16),
        active=((group, units), bf16), grad_hid=((group, units), bf16),
        gm_send=((3, rows, width), bf16), gm_recv=((3, rows, width), bf16),
        mlp_send=((3, rows, width), bf16), mlp_recv=((3, rows, width), bf16),
        grad_mixed=((rows, width), f32), mlp=((rows, width), f32), gmid=((rows, width), f32),
        gattn=((4, rows, width), bf16), dout_send=((4, heads, HEAD_DIM, rows), bf16),
        dout_recv=((4, heads, HEAD_DIM, rows), bf16), rowsum=((16, width), f32),
        wide=((units, wide), f32), blocks_r=((8, per, width), bf16),
        blocks_e=((8, per, wide), bf16), blocks_a=((2, 8, 2, count, width), bf16),
        from_r=((7, per, width), bf16), from_e=((7, per, wide), bf16),
        from_a=((2, 6, 2, count, width), bf16), dout_t=((heads, BLK, group), bf16),
        dout=((heads,) + head_block, bf16), rdots=((heads, 1, group), f32),
        dq=((heads, BLK, group), f32), dkv=((heads,) + head_block, f32),
        dkv_send=((3 * heads,) + head_block, bf16), dkv_recv=((3 * heads,) + head_block, bf16),
        dqkv=((2 * heads,) + head_block, bf16), part=((group, width), f32),
        part_send=((3, rows, width), bf16), part_recv=((3, rows, width), bf16),
        plain=((group, wide), bf16), norm_sum=((8, width), f32),
        sum_halves=((2, 8, width), f32), sum_inbox=((3, 8, width), f32),
        sum_first=((4, 8, width), f32), sum_last=((4, 8, width), f32), tiles=((6 * width // BLK, 1, BLK), f32),
        gain_tiles=((width // BLK + 1, 3, BLK), f32),
        mlp_near=((rows, width), f32),
    )
    semaphores = dict(
        load_sem=16, table_sem=4, local_sem=8, chunk_ss=3, chunk_rs=3, vec_ss=7, vec_rs=7,
        tok_ss=4, tok_rs=4, a_ss=4, a_rs=4, er_ss=6, er_rs=6, o_ss=5, o_rs=5, ada_ss=5, ada_rs=5, cot_ss=4, cot_rs=4,
        kv_ss=3 * heads, kv_rs=3 * heads, att_ss=4, att_rs=4, mix_ss=4, mix_rs=4, gm_ss=4,
        gm_rs=4, mlp_ss=4, mlp_rs=4, dout_ss=4, dout_rs=4, ga_ss=4, ga_rs=4, sr_ss=3, sr_rs=3,
        se_ss=3, se_rs=3, soq_ss=2, soq_rs=2, skv_ss=2, skv_rs=2, dkv_ss=3 * heads,
        dkv_rs=3 * heads, part_ss=6, part_rs=6, back_ss=8, back_rs=8, sum_ss=8, sum_rs=8,
    )
    whole = pl.BlockSpec(memory_space=pltpu.VMEM)
    names = (*(name + "_hbm" for name in inputs), *outputs, *scratch, *semaphores)
    staged = pl.pallas_call(
        partial(block_kernel, names),
        out_shape=tuple(jax.ShapeDtypeStruct(*spec) for spec in outputs.values()),
        in_specs=[pl.BlockSpec(memory_space=pl.ANY)] * len(inputs),
        out_specs=tuple(whole for _ in outputs),
        scratch_shapes=[pltpu.VMEM(*spec) for spec in scratch.values()]
        + [pltpu.SemaphoreType.DMA((number,)) for number in semaphores.values()],
        compiler_params=pltpu.CompilerParams(
            collective_id=1, has_side_effects=True, vmem_limit_bytes=62 * 2**20
        ),
    )(*inputs.values())
    (
        result, grad_tokens, grad_condition, grad_ada, grad_ada_bias, grad_first, grad_second,
        grad_project, grad_output, grad_expand, grad_expand_bias, grad_reduce, grad_reduce_bias,
    ) = pl.pallas_call(
        finish_kernel,
        out_shape=tuple(
            jax.ShapeDtypeStruct(shape, kind)
            for shape, kind in (
                ((rows, width), bf16), ((rows, width), f32), (line.shape, f32),
                ((piece, line.shape[1]), f32), ((1, piece), f32), ((1, count), f32),
                ((1, count), f32), ((3, count, width), f32), ((count, width), f32),
                ((per, width), f32), ((1, per), f32), ((per, width), f32), ((1, count), f32),
            )
        ),
        in_specs=[whole] * 8,
        out_specs=(whole,) * 13,
    )(*staged, line)
    return (
        result,
        grad_tokens,
        grad_condition.reshape(-1),
        grad_ada.T,
        grad_ada_bias.reshape(-1),
        grad_first.reshape(-1),
        grad_second.reshape(-1),
        grad_project.reshape(3 * count, width).T,
        grad_output,
        grad_expand.T,
        grad_expand_bias.reshape(-1),
        grad_reduce,
        grad_reduce_bias.reshape(-1),
    )


def solution(mesh):
    return jax.shard_map(
        on_device_fast if mesh.shape["ulysses"] * mesh.shape["blk"] == 32 else on_device,
        mesh=mesh,
        in_specs=(
            P(BOTH, None),
            P(),
            P(None, BOTH),
            P(BOTH),
            P(BOTH),
            P(BOTH),
            P(None, BOTH),
            P(BOTH, None),
            P(None, BOTH),
            P(BOTH),
            P(BOTH, None),
            P(BOTH),
            P(BOTH, None),
        ),
        out_specs=(
            P(BOTH, None),
            P(BOTH, None),
            P(),
            P(None, BOTH),
            P(BOTH),
            P(BOTH),
            P(BOTH),
            P(None, BOTH),
            P(BOTH, None),
            P(None, BOTH),
            P(BOTH),
            P(BOTH, None),
            P(BOTH),
        ),
        check_vma=False,
    )
```

```python
from functools import partial
import itertools
import math
import types

import jax
import jax.numpy as jnp
import numpy as np
from jax import lax
from jax.experimental import pallas as pl
from jax.experimental.pallas import tpu as pltpu
from jax.sharding import PartitionSpec as P

HEAD_DIM = 64
BOTH = ("ulysses", "blk")


eps = 1e-05
highest = lax.Precision.HIGHEST


def layer_norm(value):
    center = value - jnp.mean(value, axis=-1, keepdims=True)
    inverse = lax.rsqrt(jnp.mean(center * center, axis=-1, keepdims=True) + eps)
    return (center * inverse, inverse)


def norm_back(grad_normed, normed, inverse):
    first = jnp.mean(grad_normed, axis=-1, keepdims=True)
    second = jnp.mean(grad_normed * normed, axis=-1, keepdims=True)
    return inverse * (grad_normed - first - normed * second)


def rotary_tables(positions, head_dim):
    half_dim = head_dim // 2
    frequency = jnp.exp(
        jnp.arange(half_dim, dtype=jnp.float32) * (-2.0 * math.log(10000.0) / head_dim)
    )
    angles = positions[:, None] * frequency[None, :]
    return (jnp.cos(angles)[:, None, :], jnp.sin(angles)[:, None, :])


def rotate(value, cosine, sine):
    half_dim = value.shape[-1] // 2
    first = value[..., :half_dim]
    second = value[..., half_dim:]
    return jnp.concatenate(
        [first * cosine - second * sine, second * cosine + first * sine], axis=-1
    )


def rotate_back(grad_value, cosine, sine):
    half_dim = grad_value.shape[-1] // 2
    first = grad_value[..., :half_dim]
    second = grad_value[..., half_dim:]
    return jnp.concatenate(
        [first * cosine + second * sine, second * cosine - first * sine], axis=-1
    )


def over_blocks(block_step, carried, pieces, key_block):
    length = pieces[0].shape[1]
    complete = length // key_block
    stacked = tuple(
        (
            jnp.moveaxis(
                member.reshape((member.shape[0], complete, key_block) + member.shape[2:]), 1, 0
            )
            for member in pieces
        )
    )
    offsets = jnp.arange(complete, dtype=jnp.int32) * key_block

    def scan_step(carried_in, inputs):
        return (block_step(carried_in, inputs[:-1], inputs[-1]), None)

    carried, unused = lax.scan(scan_step, carried, stacked + (offsets,))
    return carried


def on_device(
    tokens,
    condition,
    ada_weight,
    ada_bias,
    first_gain,
    second_gain,
    project_weight,
    output_weight,
    expand_weight,
    expand_bias,
    reduce_weight,
    reduce_bias,
    cotangent,
):
    row_count = tokens.shape[0]
    model_width = tokens.shape[1]
    cycle_size = lax.axis_size("blk")
    cycle_place = lax.axis_index("blk")
    seq_count = lax.axis_size("ulysses")
    (
        ada_full,
        ada_shift,
        gain_one,
        gain_two,
        project_full,
        output_full,
        expand_full,
        expand_shift,
        reduce_full,
        reduce_shift,
    ) = (
        lax.all_gather(ada_weight, BOTH, axis=1, tiled=True),
        lax.all_gather(ada_bias, BOTH, axis=0, tiled=True),
        lax.all_gather(first_gain, BOTH, axis=0, tiled=True),
        lax.all_gather(second_gain, BOTH, axis=0, tiled=True),
        lax.all_gather(project_weight, BOTH, axis=1, tiled=True),
        lax.all_gather(output_weight, BOTH, axis=0, tiled=True),
        lax.all_gather(expand_weight, BOTH, axis=1, tiled=True),
        lax.all_gather(expand_bias, BOTH, axis=0, tiled=True),
        lax.all_gather(reduce_weight, BOTH, axis=0, tiled=True),
        lax.all_gather(reduce_bias, BOTH, axis=0, tiled=True),
    )
    ada_float = ada_full.astype(jnp.float32)
    modulation = jnp.dot(condition, ada_float, precision=highest) + ada_shift.astype(jnp.float32)
    shift_one, scale_one, gate_one, shift_two, scale_two, gate_two = jnp.split(modulation, 6)
    gain_one_f = gain_one.astype(jnp.float32)
    gain_two_f = gain_two.astype(jnp.float32)
    inputs = tokens.astype(jnp.float32)
    normed_one, inverse_one = layer_norm(inputs)
    gain_first = gain_one_f * (1.0 + scale_one)
    mixed_one = (normed_one * gain_first + shift_one).astype(jnp.bfloat16)
    projected = jnp.dot(mixed_one, project_full, preferred_element_type=jnp.float32)
    packed = projected.astype(jnp.bfloat16).reshape(row_count, 3, model_width)
    regrouped = lax.all_to_all(packed, "ulysses", split_axis=2, concat_axis=0, tiled=True)
    local_rows = regrouped.shape[0]
    local_width = regrouped.shape[2]
    head_count = local_width // HEAD_DIM
    by_seq = regrouped.reshape(seq_count, row_count, 3, local_width)
    positions = cycle_place * row_count + jnp.arange(row_count, dtype=jnp.int32)
    cosine, sine = rotary_tables(positions.astype(jnp.float32), HEAD_DIM)
    query_rot = rotate(
        by_seq[:, :, 0].astype(jnp.float32).reshape(seq_count, row_count, head_count, HEAD_DIM),
        cosine,
        sine,
    ).astype(jnp.bfloat16)
    key_rot = rotate(
        by_seq[:, :, 1].astype(jnp.float32).reshape(seq_count, row_count, head_count, HEAD_DIM),
        cosine,
        sine,
    ).astype(jnp.bfloat16)
    value_flat = by_seq[:, :, 2]
    value_own = value_flat.reshape(seq_count, row_count, head_count, HEAD_DIM)
    key_flat = key_rot.reshape(seq_count, row_count, local_width)
    score_scale = HEAD_DIM ** (-0.5)
    key_block = row_count * -(-512 // row_count)

    def attend_step(carried, pieces, offset):
        maximum, denominator, weighted = carried
        key_rows = pieces[0].reshape(seq_count, -1, head_count, HEAD_DIM)
        value_rows = pieces[1].reshape(seq_count, -1, head_count, HEAD_DIM)
        scores = (
            jnp.einsum("sqhd,skhd->shqk", query_rot, key_rows, preferred_element_type=jnp.float32)
            * score_scale
        )
        new_maximum = jnp.maximum(maximum, jnp.max(scores, axis=-1))
        weights = jnp.exp(scores - new_maximum[..., None])
        factor = jnp.exp(maximum - new_maximum)
        denominator = denominator * factor + jnp.sum(weights, axis=-1)
        weighted = weighted * jnp.transpose(factor, (0, 2, 1))[..., None] + jnp.einsum(
            "shqk,skhd->sqhd",
            weights.astype(jnp.bfloat16),
            value_rows,
            preferred_element_type=jnp.float32,
        )
        return (new_maximum, denominator, weighted)

    start_state = (
        jnp.full((seq_count, head_count, row_count), -1e30, jnp.float32),
        jnp.zeros((seq_count, head_count, row_count), jnp.float32),
        jnp.zeros((seq_count, row_count, head_count, HEAD_DIM), jnp.float32),
    )
    maximum, denominator, weighted = over_blocks(
        attend_step,
        start_state,
        (
            lax.all_gather(key_flat, "blk", axis=1, tiled=True),
            lax.all_gather(value_flat, "blk", axis=1, tiled=True),
        ),
        key_block,
    )
    log_total = maximum + jnp.log(denominator)
    attended = (
        (weighted / jnp.transpose(denominator, (0, 2, 1))[..., None])
        .astype(jnp.bfloat16)
        .reshape(local_rows, local_width)
    )
    attended_tokens = lax.all_to_all(attended, "ulysses", split_axis=0, concat_axis=1, tiled=True)
    attn_branch = jnp.dot(attended_tokens, output_full, preferred_element_type=jnp.float32)
    middle = inputs + gate_one * attn_branch
    normed_two, inverse_two = layer_norm(middle)
    gain_second = gain_two_f * (1.0 + scale_two)
    mixed_two = (normed_two * gain_second + shift_two).astype(jnp.bfloat16)
    hidden = jnp.dot(
        mixed_two, expand_full, preferred_element_type=jnp.float32
    ) + expand_shift.astype(jnp.float32)
    activated, gelu_back = jax.vjp(partial(jax.nn.gelu, approximate=True), hidden)
    activated_low = activated.astype(jnp.bfloat16)
    mlp_branch = jnp.dot(
        activated_low, reduce_full, preferred_element_type=jnp.float32
    ) + reduce_shift.astype(jnp.float32)
    result = (middle + gate_two * mlp_branch).astype(jnp.bfloat16)
    grad_result = cotangent.astype(jnp.float32)
    grad_gate_two = jnp.sum(grad_result * mlp_branch, axis=0)
    grad_branch = (gate_two * grad_result).astype(jnp.bfloat16)
    grad_reduce = jnp.einsum(
        "tf,td->fd", activated_low, grad_branch, preferred_element_type=jnp.float32
    )
    grad_reduce_shift = jnp.sum(grad_branch.astype(jnp.float32), axis=0)
    grad_activated = jnp.einsum(
        "td,fd->tf", grad_branch, reduce_full, preferred_element_type=jnp.float32
    )
    grad_hidden = gelu_back(grad_activated)[0].astype(jnp.bfloat16)
    grad_expand = jnp.einsum(
        "td,tf->df", mixed_two, grad_hidden, preferred_element_type=jnp.float32
    )
    grad_expand_shift = jnp.sum(grad_hidden.astype(jnp.float32), axis=0)
    grad_mixed_two = jnp.einsum(
        "tf,df->td", grad_hidden, expand_full, preferred_element_type=jnp.float32
    )
    grad_shift_two = jnp.sum(grad_mixed_two, axis=0)
    grad_scale_two = jnp.sum(grad_mixed_two * normed_two * gain_two_f, axis=0)
    grad_gain_two = jnp.sum(grad_mixed_two * normed_two * (1.0 + scale_two), axis=0)
    grad_middle = grad_result + norm_back(grad_mixed_two * gain_second, normed_two, inverse_two)
    grad_gate_one = jnp.sum(grad_middle * attn_branch, axis=0)
    grad_attn = (gate_one * grad_middle).astype(jnp.bfloat16)
    grad_output = jnp.einsum(
        "tc,td->cd", attended_tokens, grad_attn, preferred_element_type=jnp.float32
    )
    grad_heads = jnp.einsum(
        "td,cd->tc", grad_attn, output_full, preferred_element_type=jnp.float32
    ).astype(jnp.bfloat16)
    grad_local = lax.all_to_all(grad_heads, "ulysses", split_axis=1, concat_axis=0, tiled=True)
    grad_local_heads = grad_local.reshape(seq_count, row_count, head_count, HEAD_DIM)
    row_dots = jnp.sum(
        (grad_local.astype(jnp.float32) * attended.astype(jnp.float32)).reshape(
            seq_count, row_count, head_count, HEAD_DIM
        ),
        axis=-1,
    )
    row_dots_t = jnp.transpose(row_dots, (0, 2, 1))

    def query_step(carried, pieces, offset):
        key_rows = pieces[0].reshape(seq_count, -1, head_count, HEAD_DIM)
        value_rows = pieces[1].reshape(seq_count, -1, head_count, HEAD_DIM)
        scores = (
            jnp.einsum("sqhd,skhd->shqk", query_rot, key_rows, preferred_element_type=jnp.float32)
            * score_scale
        )
        shares = jnp.exp(scores - log_total[..., None])
        grad_shares = jnp.einsum(
            "sqhd,skhd->shqk", grad_local_heads, value_rows, preferred_element_type=jnp.float32
        )
        grad_scores = (shares * (grad_shares - row_dots_t[..., None])).astype(jnp.bfloat16)
        return (
            carried
            + jnp.einsum(
                "shqk,skhd->sqhd", grad_scores, key_rows, preferred_element_type=jnp.float32
            )
            * score_scale
        )

    grad_query_rot = over_blocks(
        query_step,
        jnp.zeros((seq_count, row_count, head_count, HEAD_DIM), jnp.float32),
        (
            lax.all_gather(key_flat, "blk", axis=1, tiled=True),
            lax.all_gather(value_flat, "blk", axis=1, tiled=True),
        ),
        key_block,
    )

    def key_step(carried, pieces, offset):
        grad_keys_acc, grad_values_acc = carried
        query_rows = pieces[0].reshape(seq_count, -1, head_count, HEAD_DIM)
        slope_rows = pieces[1].reshape(seq_count, -1, head_count, HEAD_DIM)
        scores = (
            jnp.einsum("sqhd,skhd->shqk", query_rows, key_rot, preferred_element_type=jnp.float32)
            * score_scale
        )
        shares = jnp.exp(scores - jnp.transpose(pieces[2], (0, 2, 1))[..., None])
        grad_values_acc = grad_values_acc + jnp.einsum(
            "shqk,sqhd->skhd",
            shares.astype(jnp.bfloat16),
            slope_rows,
            preferred_element_type=jnp.float32,
        )
        grad_shares = jnp.einsum(
            "sqhd,skhd->shqk", slope_rows, value_own, preferred_element_type=jnp.float32
        )
        grad_scores = (
            shares * (grad_shares - jnp.transpose(pieces[3], (0, 2, 1))[..., None])
        ).astype(jnp.bfloat16)
        grad_keys_acc = (
            grad_keys_acc
            + jnp.einsum(
                "shqk,sqhd->skhd", grad_scores, query_rows, preferred_element_type=jnp.float32
            )
            * score_scale
        )
        return (grad_keys_acc, grad_values_acc)

    query_wide = query_rot.reshape(seq_count, row_count, local_width)
    slope_wide = grad_local.reshape(seq_count, row_count, local_width)
    key_init = (
        jnp.zeros((seq_count, row_count, head_count, HEAD_DIM), jnp.float32),
        jnp.zeros((seq_count, row_count, head_count, HEAD_DIM), jnp.float32),
    )
    grad_key_rot, grad_value_sum = over_blocks(
        key_step,
        key_init,
        (
            lax.all_gather(query_wide.astype(jnp.float32), "blk", axis=1, tiled=True).astype(
                jnp.bfloat16
            ),
            lax.all_gather(slope_wide.astype(jnp.float32), "blk", axis=1, tiled=True).astype(
                jnp.bfloat16
            ),
            lax.all_gather(jnp.transpose(log_total, (0, 2, 1)), "blk", axis=1, tiled=True),
            lax.all_gather(row_dots, "blk", axis=1, tiled=True),
        ),
        key_block,
    )
    grad_query = (
        rotate_back(grad_query_rot, cosine, sine)
        .astype(jnp.bfloat16)
        .reshape(local_rows, local_width)
    )
    grad_key = (
        rotate_back(grad_key_rot, cosine, sine)
        .astype(jnp.bfloat16)
        .reshape(local_rows, local_width)
    )
    grad_value = grad_value_sum.astype(jnp.bfloat16).reshape(local_rows, local_width)
    grad_packed = jnp.stack([grad_query, grad_key, grad_value], axis=1)
    grad_tokens_qkv = lax.all_to_all(
        grad_packed, "ulysses", split_axis=0, concat_axis=2, tiled=True
    ).reshape(row_count, 3 * model_width)
    grad_project = jnp.einsum(
        "tc,tk->ck", mixed_one, grad_tokens_qkv, preferred_element_type=jnp.float32
    )
    grad_mixed_one = jnp.einsum(
        "tk,ck->tc", grad_tokens_qkv, project_full, preferred_element_type=jnp.float32
    )
    grad_shift_one = jnp.sum(grad_mixed_one, axis=0)
    grad_scale_one = jnp.sum(grad_mixed_one * normed_one * gain_one_f, axis=0)
    grad_gain_one = jnp.sum(grad_mixed_one * normed_one * (1.0 + scale_one), axis=0)
    grad_input = grad_middle + norm_back(grad_mixed_one * gain_first, normed_one, inverse_one)
    mod_terms = jnp.concatenate(
        [
            grad_shift_one,
            grad_scale_one,
            grad_gate_one,
            grad_shift_two,
            grad_scale_two,
            grad_gate_two,
        ]
    )
    grad_modulation = lax.psum(mod_terms, BOTH)
    grad_condition = jnp.dot(ada_float, grad_modulation, precision=highest)
    piece_width = ada_weight.shape[1]
    flat_index = lax.axis_index("ulysses") * cycle_size + cycle_place
    mod_piece = lax.dynamic_slice_in_dim(grad_modulation, flat_index * piece_width, piece_width, 0)
    grad_ada = condition[:, None] * mod_piece[None, :]
    shards = (
        lax.psum_scatter(grad_gain_one, BOTH, scatter_dimension=0, tiled=True),
        lax.psum_scatter(grad_gain_two, BOTH, scatter_dimension=0, tiled=True),
        lax.psum_scatter(grad_project, BOTH, scatter_dimension=1, tiled=True),
        lax.psum_scatter(grad_output, BOTH, scatter_dimension=0, tiled=True),
        lax.psum_scatter(grad_expand, BOTH, scatter_dimension=1, tiled=True),
        lax.psum_scatter(grad_expand_shift, BOTH, scatter_dimension=0, tiled=True),
        lax.psum_scatter(grad_reduce, BOTH, scatter_dimension=0, tiled=True),
        lax.psum_scatter(grad_reduce_shift, BOTH, scatter_dimension=0, tiled=True),
    )
    return (
        result,
        grad_input,
        grad_condition,
        grad_ada,
        mod_piece,
        shards[0],
        shards[1],
        shards[2],
        shards[3],
        shards[4],
        shards[5],
        shards[6],
        shards[7],
    )


MESH = pl.DeviceIdType.MESH
Y, ZH, ZL, X, C = 16, 8, 4, 2, 1
ATTN = (0, X, ZH, X + ZH)
MLP = (0, X, ZL, X + ZL)
BLK = 128
f32 = jnp.float32
bf16 = jnp.bfloat16


def place():
    blk = lax.axis_index("blk")
    return (lax.axis_index("ulysses"), blk // 8, (blk // 4) % 2, (blk // 2) % 2, blk % 2)


def flip(offset):
    return tuple(
        1 - bit if (offset // weight) % 2 else bit
        for bit, weight in zip(place(), (Y, ZH, ZL, X, C))
    )


def device_at(y, zh, zl, x, c):
    return (y, zh * 8 + zl * 4 + x * 2 + c)


def peer(offset):
    return device_at(*flip(offset))


def peer_loop(offset):
    return device_at(
        *(
            (bit + (offset // weight) % 2) % 2
            for bit, weight in zip(place(), (Y, ZH, ZL, X, C))
        )
    )


def flat(device):
    return device[0] * 16 + device[1]


def share(offset, far):
    y, zh, zl, x, c = flip(offset)
    return c * 4 + y * 2 + (zl if far == ZL else zh)


def rank(offset):
    y, zh, zl, x, c = flip(offset)
    return zh * 2 + x


def member(which, slot):
    return device_at((slot // 2) % 2, which // 2, slot % 2, which % 2, slot // 4)


def greet(offsets):
    barrier = pltpu.get_barrier_semaphore()
    for offset in offsets:
        pl.semaphore_signal(barrier, inc=1, device_id=peer(offset), device_id_type=MESH)
    return lambda: pl.semaphore_wait(barrier, len(offsets))


def remote_to(source, target, send_sem, recv_sem, device):
    return pltpu.make_async_remote_copy(
        src_ref=source,
        dst_ref=target,
        send_sem=send_sem,
        recv_sem=recv_sem,
        device_id=device,
        device_id_type=MESH,
    )


def remote(source, target, send_sem, recv_sem, offset):
    return remote_to(source, target, send_sem, recv_sem, peer(offset))


def dot_nn(a, b):
    return jnp.dot(a, b, preferred_element_type=f32)


def dot_nt(a, b):
    return lax.dot_general(a, b, (((1,), (1,)), ((), ())), preferred_element_type=f32)


def dot_tn(a, b):
    return lax.dot_general(a, b, (((0,), (0,)), ((), ())), preferred_element_type=f32)


def exact(a, b, contract):
    return lax.dot_general(
        a, b, (contract, ((), ())), preferred_element_type=f32, precision=highest
    )


def column_sum(value):
    return jnp.sum(value, axis=0, keepdims=True)


class Gather:
    def __init__(self, view, send_sem, recv_sem, far, pieces):
        own, core = share(0, far), share(C, far)
        z, y = share(far, far), share(Y, far)
        both = share(Y + far, far)
        half, other = own // 4 * 4, core // 4 * 4

        def pair(mine, theirs, index, to, piece=lambda v: v):
            return tuple(
                remote(piece(where), piece(where), send_sem.at[index], recv_sem.at[index], to)
                for where in (mine, theirs)
            )

        self.y_own = pair(view(own, 1), view(y, 1), 0, Y)
        self.cores = pair(view(half, 4), view(other, 4), 1, C)
        self.over_z = [
            pair(view(own, 1), view(z, 1), 2 + 2 * index, far, piece)
            for index, piece in enumerate(pieces)
        ]
        self.over_y = [
            pair(view(z, 1), view(both, 1), 3 + 2 * index, Y, piece)
            for index, piece in enumerate(pieces)
        ]

    def near(self):
        self.y_own[0].start()

    def far(self, which=0):
        self.over_z[which][0].start()

    def second(self, which=0):
        self.over_z[which][1].wait_recv()
        self.over_y[which][0].start()

    def third(self):
        for _out, into in (self.y_own, *self.over_y):
            into.wait_recv()
        self.cores[0].start()

    def last(self):
        self.cores[1].wait_recv()

    def finish(self):
        for out, _into in (self.y_own, self.cores, *self.over_z, *self.over_y):
            out.wait_send()


class Spread:
    def __init__(self, view, place_of, order, send_sem, recv_sem):
        self.out, self.into = [], []
        size = 1
        for index, to in enumerate(order):
            mine, other = (place_of(flip(to_where)) // size * size for to_where in (0, to))
            sems = (send_sem.at[index], recv_sem.at[index])
            self.out.append(remote(view(mine, size), view(mine, size), *sems, to))
            self.into.append(remote(view(other, size), view(other, size), *sems, to))
            size *= 2

    def step(self, index):
        if index:
            self.into[index - 1].wait_recv()
        self.out[index].start()

    def last(self):
        self.into[-1].wait_recv()

    def finish(self):
        for copy in self.out:
            copy.wait_send()


class Scatter:
    def __init__(self, view, inbox, send_sem, recv_sem, far):
        self.view, self.inbox = view, inbox
        own = share(0, far)
        core, y, z = share(C, far), share(Y, far), share(far, far)
        self.plan = {
            C: (core // 4 * 4, own // 4 * 4, 4, 0), Y: (y // 2 * 2, own // 2 * 2, 2, 4),
            far: (z, own, 1, 6),
        }
        self.send_sem, self.recv_sem = send_sem, recv_sem
        self.copies = {}

    def step(self, to):
        goes, _stays, size, slot = self.plan[to]
        index = len(self.copies)
        self.copies[to] = remote(
            self.view(goes, size), self.inbox(slot, size), self.send_sem.at[index],
            self.recv_sem.at[index], to,
        )
        self.copies[to].start()

    def add(self, to):
        self.copies[to].wait_recv()
        _goes, stays, size, slot = self.plan[to]
        block = self.view(stays, size)
        block[...] = (
            block[...].astype(f32) + self.inbox(slot, size)[...].astype(f32)
        ).astype(bf16)

    def finish(self):
        for copy in self.copies.values():
            copy.wait_send()


class Total:
    def __init__(self, halves, inbox, first, last, send_sem, recv_sem):
        self.halves, self.inbox, self.first, self.last = halves, inbox, first, last
        y, zh, zl, x, c = place()
        self.core = c
        self.own = (y * 2 + zh, zl * 2 + x)
        sems = [(send_sem.at[index], recv_sem.at[index]) for index in range(8)]
        self.copies = [
            remote(ref.at[own], ref.at[own], *sems[3 * which + index], to)
            for which, (ref, own, offsets) in enumerate(
                ((first, self.own[0], (Y, ZH, Y + ZH)), (last, self.own[1], (ZL, X, ZL + X)))
            )
            for index, to in enumerate(offsets)
        ]
        self.copies.append(remote(halves.at[1 - c], inbox.at[0], *sems[6], C))
        self.copies.append(remote(inbox.at[1 + c], inbox.at[1 + c], *sems[7], C))

    def start(self):
        self.copies[6].start()

    def second(self):
        self.copies[6].wait_recv()
        self.first[self.own[0]] = self.halves[self.core] + self.inbox[0]
        for copy in self.copies[0:3]:
            copy.start()

    def third(self):
        for copy in self.copies[0:3]:
            copy.wait_recv()
        self.last[self.own[1]] = (
            self.first[0] + self.first[1] + self.first[2] + self.first[3]
        )
        for copy in self.copies[3:6]:
            copy.start()

    def fourth(self):
        for copy in self.copies[3:6]:
            copy.wait_recv()
        self.inbox[1 + self.core] = self.last[0] + self.last[1] + self.last[2] + self.last[3]
        self.copies[7].start()

    def result(self):
        self.copies[7].wait_recv()
        return jnp.concatenate([self.inbox[1], self.inbox[2]], axis=0)

    def finish(self):
        for copy in self.copies:
            copy.wait_send()


def turn(value, cosine, sine):
    lane = lax.broadcasted_iota(jnp.int32, value.shape, 1)
    swapped = jnp.where(
        lane < HEAD_DIM // 2,
        pltpu.roll(value, BLK - HEAD_DIM // 2, 1),
        pltpu.roll(value, HEAD_DIM // 2, 1),
    )
    return value * cosine + swapped * sine


def head_rows(first, count, low):
    for row in range(first, first + count, 8):
        yield row - first, row // HEAD_DIM, row % HEAD_DIM + (0 if low else HEAD_DIM)


def gelu_pair(hidden):
    scale = math.sqrt(2.0 / math.pi)
    square = hidden * hidden
    bend = jnp.tanh(scale * hidden * (1.0 + 0.044715 * square))
    half = 0.5 * (1.0 + bend)
    slope = half + 0.5 * hidden * (1.0 - bend * bend) * (
        scale * (1.0 + 3.0 * 0.044715 * square)
    )
    return hidden * half, slope


def to_column(row):
    count = row.shape[1]
    one = lax.broadcasted_iota(jnp.int32, (count, count), 0)
    two = lax.broadcasted_iota(jnp.int32, (count, count), 1)
    return jnp.sum(jnp.where(one == two, row, 0.0), axis=1, keepdims=True)


def to_row(column):
    count = column.shape[0]
    one = lax.broadcasted_iota(jnp.int32, (count, count), 0)
    two = lax.broadcasted_iota(jnp.int32, (count, count), 1)
    return jnp.sum(jnp.where(one == two, column, 0.0), axis=0, keepdims=True)


def block_kernel(names, *refs):
    s = types.SimpleNamespace(**dict(zip(names, refs)))
    rows, width = s.tokens.shape
    wide = width + BLK
    heads = s.query.shape[0]
    count = s.output_weight_hbm.shape[0]
    per = s.reduce_weight_hbm.shape[0]
    units = 8 * per
    scale = HEAD_DIM ** (-0.5)
    me = flat(peer(0))
    own, own_mlp = share(0, ZL), share(0, ZH)
    my_rank = rank(0)

    def here(slot):
        return slice(slot * rows, (slot + 1) * rows)

    loads = {}

    def load(name, target=None):
        number = len(loads)
        copy = pltpu.make_async_copy(
            getattr(s, name + "_hbm"), getattr(s, name) if target is None else target,
            s.load_sem.at[number],
        )
        copy.start()
        loads[name] = copy

    for name in (
        "ada", "condition", "ada_bias", "first_gain", "second_gain", "reduce_bias",
        "project_weight",
    ):
        load(name)
    def out_place(bits):
        y, zh, zl, x, c = bits
        return c * 16 + y * 8 + zh * 4 + zl * 2 + x

    entered = greet(range(1, 32))
    piece = s.ada.shape[0]
    for name in ("ada", "condition", "ada_bias", "first_gain", "second_gain", "reduce_bias"):
        loads[name].wait()
    for index in range(width // BLK):
        s.adaw[out_place(flip(0)), :, index * BLK : (index + 1) * BLK] = s.ada[
            index * count : (index + 1) * count, :
        ]
    s.vec_own[...] = jnp.zeros_like(s.vec_own)
    s.vec_own[0:8, 0:piece] = exact(
        jnp.broadcast_to(s.condition[...], (8, s.condition.shape[1])),
        s.ada[...].astype(f32), ((1,), (1,)),
    )
    s.vec_own[0:1, 0:piece] += s.ada_bias[...].astype(f32)
    for index, ref in enumerate((s.first_gain, s.second_gain, s.reduce_bias)):
        s.vec_own[8 + index : 9 + index, 0:count] = ref[...].astype(f32)
    mod_shift = (me % 8) * 16
    gain_shift = ((3 * me) % 16) * 8
    y, zh, zl, x, c = place()
    vec_own = y * 16 + x * 8 + c * 4 + zh * 2 + zl
    s.vecs[vec_own, 0:1, :] = pltpu.roll(s.vec_own[0:8, :], mod_shift, 1)[0:1, :]
    s.vecs[vec_own, 1:4, :] = pltpu.roll(s.vec_own[8:16, :], gain_shift, 1)[0:3, :]
    lane = lax.broadcasted_iota(jnp.int32, (rows, BLK), 1)
    ones = jnp.where(lane == 0, 1.0, 0.0).astype(bf16)
    for slot in range(4):
        s.mix[slot, :, width:] = ones
        s.plain[here(slot), width:] = ones
    loads["project_weight"].wait()
    entered()

    def token_copy(have, to):
        slot = ATTN.index(have + to)
        return remote(
            s.tok.at[ATTN.index(have)] if have else s.tokens, s.tok.at[slot],
            s.tok_ss.at[slot], s.tok_rs.at[slot], to,
        )

    def token_half(have, to, half, number):
        lines = pl.ds(half * (rows // 2), rows // 2)
        slot = ATTN.index(have + to)
        source = s.tok.at[ATTN.index(have), lines] if have else s.tokens.at[lines]
        return remote(
            source, s.tok.at[slot, lines], s.tok_ss.at[number], s.tok_rs.at[number], to
        )

    token_copies = [token_copy(0, X)]
    token_z = [token_half(0, ZH, half, 2 + half) for half in range(2)]
    token_on = [token_half(ZH, X, half, 4 + half) for half in range(2)]
    vec_steps = []
    for index, (size, offsets) in enumerate(
        ((1, (ZL, ZH, ZL + ZH)), (4, (C, X, X + C)), (16, (Y,)))
    ):
        where = s.vecs.at[pl.ds(vec_own // size * size, size)]
        vec_steps.append(
            [
                remote(
                    where, where, s.vec_ss.at[3 * index + number], s.vec_rs.at[3 * index + number],
                    to,
                )
                for number, to in enumerate(offsets)
            ]
        )

    def vec_step(index):
        for copy in vec_steps[index - 1] if index else ():
            copy.wait_recv()
        for copy in vec_steps[index] if index < 3 else ():
            copy.start()

    vec_step(0)
    def chunk_out(index):
        number = 3 * me + index
        part, place_in = number // 32, number % 32
        slot = place_in % 8
        device = member(place_in // 8, slot)
        target = s.chunks.at[slot, part]
        far = remote_to(
            s.project_weight.at[index], target, s.chunk_ss.at[index], s.chunk_rs.at[index], device
        )
        near = pltpu.make_async_copy(s.project_weight.at[index], target, s.local_sem.at[index])
        return far, near, flat(device) == me

    for index in range(3):
        far, near, stays = chunk_out(index)

        @pl.when(jnp.logical_not(stays))
        def _():
            far.start()

        @pl.when(stays)
        def _():
            near.start()

    for name in ("tokens", "expand_bias"):
        load(name)
    load("expand_weight", s.er.at[own_mlp, :, pl.ds(0, width)])
    load("reduce_weight", s.er.at[own_mlp, :, pl.ds(wide, width)])

    load("output_weight", s.outw.at[out_place(flip(0))])
    load("cotangent", s.cot.at[0])
    tables = []
    for slot in range(4):
        start = pl.multiple_of(peer(ATTN[slot])[1] * rows, rows)
        copy = pltpu.make_async_copy(
            s.table_hbm.at[pl.ds(start, rows)], s.table.at[pl.ds(slot * rows, rows)],
            s.table_sem.at[slot],
        )
        copy.start()
        tables.append(copy)
    gather_er = Gather(
        lambda slot, size: s.er.at[pl.ds(slot, size)], s.er_ss, s.er_rs, ZH,
        (
            lambda v: v.at[:, :, pl.ds(wide, width)],
            lambda v: v.at[:, :, pl.ds(0, wide)],
        ),
    )
    loads["expand_bias"].wait()
    lane = lax.broadcasted_iota(jnp.int32, (per, BLK), 1)
    s.er[own_mlp, :, width:wide] = jnp.where(
        lane == 0, to_column(s.expand_bias[...].astype(f32)), 0.0
    ).astype(bf16)
    zero = jnp.zeros((HEAD_DIM, width), bf16)
    for head in range(heads):
        s.weight[head, HEAD_DIM:, :] = zero
    s.state_m[...] = jnp.full_like(s.state_m, -1e30)
    s.state_l[...] = jnp.zeros_like(s.state_l)
    s.acc[...] = jnp.zeros_like(s.acc)
    spread_out = Spread(
        lambda slot, size: s.outw.at[pl.ds(slot, size)], out_place, (X, ZL, ZH, Y, C),
        s.o_ss, s.o_rs,
    )
    spread_ada = Spread(
        lambda slot, size: s.adaw.at[pl.ds(slot, size)], out_place, (X, ZL, ZH, Y, C),
        s.ada_ss, s.ada_rs,
    )
    for name in ("expand_weight", "reduce_weight", "output_weight", "cotangent", "tokens"):
        loads[name].wait()
    vec_step(1)
    spread_out.step(0)
    spread_ada.step(0)

    for index in range(3):
        far, near, stays = chunk_out(index)

        @pl.when(jnp.logical_not(stays))
        def _():
            far.wait()

        @pl.when(stays)
        def _():
            near.wait()

    gather_a = Gather(
        lambda slot, size: s.chunks.at[pl.ds(slot, size)], s.a_ss, s.a_rs, ZL, (lambda v: v,)
    )
    def cot_copy(have, to):
        slot = MLP.index(have + to)
        return remote(
            s.cot.at[MLP.index(have)], s.cot.at[slot], s.cot_ss.at[slot], s.cot_rs.at[slot], to
        )

    cot_copies = [cot_copy(0, X), cot_copy(0, ZL), cot_copy(ZL, X)]
    gather_a.far()
    gather_a.near()
    token_z[0].start()
    token_z[1].start()
    token_copies[0].start()
    vec_step(2)
    spread_out.step(1)
    spread_ada.step(1)
    gather_a.second()
    cot_copies[1].start()
    vec_step(3)
    s.mod_row[...] = jnp.zeros_like(s.mod_row)
    s.gain_rows[...] = jnp.zeros_like(s.gain_rows)
    for index in range(32):
        y, zh, zl, x, c = ((index // weight) % 2 for weight in (Y, ZH, ZL, X, C))
        found = y * 16 + x * 8 + c * 4 + zh * 2 + zl
        tile = (9 * index) // 8 * BLK
        s.mod_row[0:1, tile : tile + 2 * BLK] += s.vecs[found, 0:1, :]
        tile = (3 * index) // 16 * BLK
        s.gain_rows[0:3, tile : tile + 2 * BLK] += s.vecs[found, 1:4, :]
    shift_one, scale_one, gate_one, shift_two, scale_two, gate_two = range(6)
    for index in range(6):
        s.mods[index : index + 1, :] = s.mod_row[0:1, index * width : (index + 1) * width]
    s.mods[6:9, :] = s.gain_rows[0:3, 0:width]
    s.mods[9:10, :] = s.mods[6:7, :] * (1.0 + s.mods[scale_one : scale_one + 1, :])
    s.mods[10:11, :] = s.mods[7:8, :] * (1.0 + s.mods[scale_two : scale_two + 1, :])

    def mod(index):
        return s.mods[index : index + 1, :]

    for slot in range(4):
        if slot == 1:
            token_copies[0].wait_recv()
        if slot == 3:
            token_on[0].wait_recv()
            token_on[1].wait_recv()
        if slot == 2:
            token_z[0].wait_recv()
            token_z[1].wait_recv()
            token_on[0].start()
            token_on[1].start()
            cot_copies[0].start()
            spread_out.step(2)
            gather_er.far(0)
            gather_er.near()
            gather_a.third()
        source = s.tok[slot] if slot else s.tokens[...]
        normed, _unused = layer_norm(source.astype(f32))
        s.mixed[here(slot), :] = (normed * mod(9) + mod(shift_one)).astype(bf16)
        s.plain[here(slot), 0:width] = normed.astype(bf16)
    def assemble(part, base, low):
        for slot in range(8):
            for row, head, target in head_rows(slot * count, count, low):
                s.weight[base + head, target : target + 8, :] = s.chunks[
                    slot, part, row : row + 8, :
                ]

    gather_er.far(1)
    gather_a.last()
    assemble(1, heads, True)
    assemble(2, heads, False)
    for copy in tables:
        copy.wait()
    kv_far = [
        remote(s.kv.at[0, head], s.kv.at[2, head], s.kv_ss.at[head], s.kv_rs.at[head], ZL)
        for head in range(heads)
    ]
    kv_near = [
        remote(
            s.kv.at[0, head], s.kv.at[1, head], s.kv_ss.at[heads + head],
            s.kv_rs.at[heads + head], C,
        )
        for head in range(heads)
    ]
    for head in range(heads):
        both = dot_nt(s.mixed[...], s.weight[heads + head]).astype(bf16).astype(f32)
        s.kv[0, head] = turn(both, s.table[:, 0:BLK], s.table[:, BLK:]).astype(bf16)
        kv_far[head].start()
        kv_near[head].start()
    assemble(0, 0, True)
    for head in range(heads):
        query = dot_nt(s.mixed[...], s.weight[head]).astype(bf16).astype(f32)
        query = turn(query, s.table[:, 0:BLK], s.table[:, BLK:]).astype(bf16).astype(f32)
        s.query[head] = (query * scale).astype(bf16)
    cot_copies[1].wait_recv()
    cot_copies[2].start()


    def attend(slot, head, count_of=1):
        keys = s.kv[slot : slot + count_of, head].reshape(count_of * 4 * rows, BLK)
        scores = dot_nt(keys, s.query[head])
        before = s.state_m[head]
        maximum = jnp.maximum(before, jnp.max(scores, axis=0, keepdims=True))
        weights = jnp.exp(scores - maximum)
        factor = jnp.exp(before - maximum)
        s.state_m[head] = maximum
        s.state_l[head] = s.state_l[head] * factor + column_sum(weights)
        s.acc[head] = s.acc[head] * factor + dot_tn(keys, weights.astype(bf16))

    for head in range(heads):
        kv_near[head].wait_recv()

    @pl.loop(0, heads)
    def _(head):
        attend(0, head, 2)

        @pl.when(head == 0)
        def _():
            spread_out.step(3)


    gather_er.second(0)

    def kv_forward(head):
        return remote(
            s.kv.at[2, head], s.kv.at[3, head], s.kv_ss.at[2 * heads + head],
            s.kv_rs.at[2 * heads + head], C,
        )

    def finish_head(head):
        forwards[head].wait_recv()
        attend(3, head)
        value = (s.acc[head] / s.state_l[head]).astype(bf16)
        s.att[head] = value[HEAD_DIM:, :]
        s.logt[head] = s.state_m[head] + jnp.log(s.state_l[head])

    forwards = []
    for head in range(heads):
        kv_far[head].wait_recv()
        forwards.append(kv_forward(head))
        forwards[head].start()
        attend(2, head)
        if head == 1:
            gather_er.second(1)
        if head:
            finish_head(head - 1)
    finish_head(heads - 1)

    for slot in range(4):
        for head in range(heads):
            s.att_send[slot, head] = s.att[head, :, here(slot)]
    att_copies = [
        remote(
            s.att_send.at[slot], s.att_all.at[my_rank], s.att_ss.at[slot], s.att_rs.at[slot],
            ATTN[slot],
        )
        for slot in range(1, 4)
    ]
    for copy in att_copies:
        copy.start()
    s.att_all[my_rank] = s.att_send[0]
    spread_out.step(4)
    gather_er.third()
    spread_out.last()
    for y in range(2):
        for zh, zl, x, c in itertools.product(range(2), repeat=4):
            at = (y * 16 + zh * 8 + zl * 4 + x * 2 + c) * count
            s.out_full[at : at + count, :] = s.outw[c * 16 + y * 8 + zh * 4 + zl * 2 + x]
    for slot in range(1, 4):
        where = s.att_all.at[rank(ATTN[slot])]
        remote(where, where, s.att_ss.at[slot], s.att_rs.at[slot], ATTN[slot]).wait_recv()
    s.attn[...] = dot_tn(s.att_all[...].reshape(width, rows), s.out_full[...])
    s.middle[...] = s.tokens[...].astype(f32) + mod(gate_one) * s.attn[...]
    normed, inverse = layer_norm(s.middle[...])
    s.normed[...] = normed
    s.inverse[...] = inverse
    s.mix[0, :, :width] = (normed * mod(10) + mod(shift_two)).astype(bf16)
    def mix_copy(source, slot, number, lines, to):
        return remote(
            s.mix.at[source, lines, pl.ds(0, width)], s.mix.at[slot, lines, pl.ds(0, width)],
            s.mix_ss.at[number], s.mix_rs.at[number], to,
        )

    mix_copies = [
        mix_copy(0, 1, 0, pl.ds(0, rows), X),
        mix_copy(0, 2, 1, pl.ds(0, rows), ZL),
        mix_copy(1, 3, 2, pl.ds(0, rows // 2), ZL),
        mix_copy(2, 3, 3, pl.ds(rows // 2, rows // 2), X),
    ]
    for copy in mix_copies[0:2]:
        copy.start()
    for slot in range(4):
        if slot == 1 or slot == 3:
            cot_copies[slot - 1].wait_recv()
        s.branch[here(slot), :] = (mod(gate_two) * s.cot[slot].astype(f32)).astype(bf16)
    gather_er.last()

    def expand(lanes=wide):
        return s.er[:, :, 0:lanes].reshape(units, lanes)

    def reduce():
        return s.er[:, :, wide:].reshape(units, width)

    spread_ada.step(2)
    gm_copies = [
        remote(
            s.gm_send.at[slot - 1], s.gm_recv.at[slot - 1], s.gm_ss.at[slot], s.gm_rs.at[slot],
            MLP[slot],
        )
        for slot in range(1, 4)
    ]
    for first, last in ((0, 1), (1, 3), (3, 4)):
        if first == 1:
            for index in range(2):
                mix_copies[index].wait_recv()
                mix_copies[2 + index].start()
        elif first == 3:
            mix_copies[2].wait_recv()
            mix_copies[3].wait_recv()
        these = slice(first * rows, last * rows)
        mixed_two = s.mix[first:last].reshape((last - first) * rows, wide)
        activated, slope = gelu_pair(dot_nt(mixed_two, expand()))
        s.active[these, :] = activated.astype(bf16)
        grad_hidden = (dot_nt(s.branch[these, :], reduce()) * slope).astype(bf16)
        s.grad_hid[these, :] = grad_hidden
        gm_part = dot_nn(grad_hidden, expand(width))
        for slot in range(first, last):
            part = gm_part[(slot - first) * rows : (slot - first + 1) * rows, :]
            if slot:
                s.gm_send[slot - 1] = part.astype(bf16)
                gm_copies[slot - 1].start()
            else:
                s.grad_mixed[...] = part
    for index in range(units // BLK):
        lanes = slice(index * BLK, (index + 1) * BLK)
        s.wide[lanes, 0:width] = dot_tn(s.active[:, lanes], s.branch[...])
    for index in range(8):
        s.blocks_r[index] = s.wide[index * per : (index + 1) * per, 0:width].astype(bf16)
    scatter_r = Scatter(
        lambda slot, size: s.blocks_r.at[pl.ds(slot, size)],
        lambda slot, size: s.from_r.at[pl.ds(slot, size)], s.sr_ss, s.sr_rs, ZH
    )
    scatter_r.step(C)
    for index in range(units // BLK):
        lanes = slice(index * BLK, (index + 1) * BLK)
        s.wide[lanes, :] = dot_tn(
            s.grad_hid[:, lanes], s.mix[...].reshape(4 * rows, width + BLK)
        )
    scatter_r.add(C)
    scatter_r.step(Y)
    for index in range(8):
        s.blocks_e[index] = s.wide[index * per : (index + 1) * per, :].astype(bf16)
    scatter_e = Scatter(
        lambda slot, size: s.blocks_e.at[pl.ds(slot, size)],
        lambda slot, size: s.from_e.at[pl.ds(slot, size)], s.se_ss, s.se_rs, ZH
    )
    scatter_e.step(C)
    def mlp_copy(slot, number, to):
        return remote(
            s.mlp_send.at[slot], s.mlp_recv.at[number], s.mlp_ss.at[slot], s.mlp_rs.at[number], to
        )

    mlp_copies = [mlp_copy(2, 2, X), mlp_copy(0, 0, X), mlp_copy(1, 1, ZL)]

    def mlp_part(slot):
        return dot_nn(s.active[here(slot), :], reduce())

    s.mlp_send[2] = mlp_part(3).astype(bf16)
    s.mlp_send[0] = mlp_part(1).astype(bf16)
    s.mlp[...] = mlp_part(0) + mod(8)
    s.mlp_near[...] = mlp_part(2)
    for index in range(units // BLK):
        lanes = slice(index * BLK, (index + 1) * BLK)
        s.wide[lanes, 0:width] = dot_tn(s.active[:, lanes], s.cot[...].reshape(4 * rows, width))
    gate_sum = mod(8) * column_sum(s.cot[0].astype(f32))
    for index in range(8):
        gate_sum = gate_sum + column_sum(
            s.er[index, :, wide:].astype(f32) * s.wide[index * per : (index + 1) * per, 0:width]
        )
    s.rowsum[5:6, :] = gate_sum
    for copy in gm_copies:
        copy.wait()
    mlp_copies[0].start()
    grad_mixed = (
        s.grad_mixed[...]
        + s.gm_recv[0].astype(f32) + s.gm_recv[1].astype(f32) + s.gm_recv[2].astype(f32)
    )
    cot = s.cot[0].astype(f32)
    normed = s.normed[...]
    grad_middle = cot + norm_back(grad_mixed * mod(10), normed, s.inverse[...])
    s.gmid[...] = grad_middle
    grad_attn = (mod(gate_one) * grad_middle).astype(bf16)
    s.gattn[0] = grad_attn
    s.dout_send[...] = dot_nt(s.out_full[...], grad_attn).astype(bf16).reshape(
        s.dout_send.shape
    )
    dout_copies = [
        remote(
            s.dout_send.at[rank(ATTN[slot])], s.dout_recv.at[slot], s.dout_ss.at[slot],
            s.dout_rs.at[slot], ATTN[slot],
        )
        for slot in range(1, 4)
    ]
    for copy in dout_copies:
        copy.start()
    s.dout_recv[0] = s.dout_send[my_rank]
    def ga_copy(have, to):
        slot = ATTN.index(have + to)
        return remote(
            s.gattn.at[ATTN.index(have)], s.gattn.at[slot], s.ga_ss.at[slot], s.ga_rs.at[slot], to
        )

    ga_copies = [ga_copy(0, X), ga_copy(0, ZH), ga_copy(ZH, X)]
    weighted = column_sum(grad_mixed * normed)
    s.rowsum[2:3, :] = column_sum(grad_middle * s.attn[...])
    s.rowsum[3:4, :] = column_sum(grad_mixed)
    s.rowsum[4:5, :] = weighted * mod(7)
    s.rowsum[7:8, :] = weighted * (1.0 + mod(scale_two))
    s.rowsum[8:9, :] = column_sum(s.branch[here(0), :].astype(f32))
    scatter_e.add(C)
    scatter_e.step(Y)

    s.dout_t[...] = jnp.zeros_like(s.dout_t)
    for slot in range(4):
        if slot:
            dout_copies[slot - 1].wait()
        if slot == 3:
            ga_copies[1].start()
        for head in range(heads):
            s.dout_t[head, HEAD_DIM:, here(slot)] = s.dout_recv[slot, head]
    for head in range(heads):
        value = s.dout_t[head].astype(f32)
        s.dout[head] = value.T.astype(bf16)
        s.rdots[head] = column_sum(value[HEAD_DIM:, :] * s.att[head].astype(f32))
    scatter_r.add(Y)
    scatter_r.step(ZH)
    ga_copies[0].start()
    mlp_copies[1].start()
    s.dq[...] = jnp.zeros_like(s.dq)

    def back(slot, head):
        keys = s.kv[slot : slot + 2, head].reshape(2 * 4 * rows, BLK)
        query = s.query[head]
        shares = jnp.exp(dot_nt(keys, query) - s.logt[head])
        grad_shares = dot_nn(keys, s.dout_t[head])
        grad_scores = (shares * (grad_shares - s.rdots[head])).astype(bf16)
        s.dq[head] += dot_tn(keys, grad_scores)
        return dot_nn(grad_scores, query) + dot_nn(shares.astype(bf16), s.dout[head])

    def dkv_copy(stage, head, offset):
        index = stage * heads + head
        return remote(
            s.dkv_send.at[index], s.dkv_recv.at[index], s.dkv_ss.at[index], s.dkv_rs.at[index],
            offset,
        )

    @pl.loop(0, heads)
    def _(head):
        both = back(2, head)
        s.dkv_send[head] = both[4 * rows :].astype(bf16)
        first = dkv_copy(0, head, C)
        first.start()
        part = both[: 4 * rows]
        first.wait_recv()
        s.dkv_send[heads + head] = (part + s.dkv_recv[head].astype(f32)).astype(bf16)
        dkv_copy(1, head, ZL).start()

    scatter_e.add(Y)
    scatter_e.step(ZH)
    spread_ada.step(3)

    @pl.loop(0, heads)
    def _(head):
        @pl.when(head == 2)
        def _():
            ga_copies[1].wait_recv()
            ga_copies[2].start()

        both = back(0, head)
        s.dkv_send[2 * heads + head] = both[4 * rows :].astype(bf16)
        dkv_copy(2, head, C).start()
        s.dkv[head] = both[: 4 * rows]
        value = s.dq[head].T * scale
        s.dqkv[head] = turn(value, s.table[:, 0:BLK], -s.table[:, BLK:]).astype(bf16)

    query_part = dot_nn(s.dqkv[0], s.weight[0])
    for head in range(1, heads):
        query_part = query_part + dot_nn(s.dqkv[head], s.weight[head])
    s.part[...] = query_part
    def spread(part, low, of):
        for slot in range(8):
            for row, head, target in head_rows(slot * count, count, low):
                s.blocks_a[(part + 1) % 4 // 2, slot, (part + 1) % 2, row : row + 8, :] = s.wide[
                    of * heads * BLK + head * BLK + target
                    : of * heads * BLK + head * BLK + target + 8, 0:width
                ].astype(bf16)

    def scatter_pair(pair, ss, rs):
        return Scatter(
            lambda slot, size: s.blocks_a.at[pair, pl.ds(slot, size)],
            lambda slot, size: s.from_a.at[pair, pl.ds(slot, size)],
            ss, rs, ZL,
        )

    for head in range(heads):
        at = (heads + head) * BLK
        s.wide[at : at + BLK, 0:width] = dot_tn(s.dqkv[head], s.mixed[...])
    spread(0, True, 1)
    ga_copies[0].wait_recv()
    ga_copies[2].wait_recv()
    gattn = s.gattn[...].reshape(4 * rows, width)

    for head in range(heads):
        s.wide[head * BLK + HEAD_DIM : (head + 1) * BLK, 0:width] = dot_nn(s.att[head], gattn)
    spread(3, False, 0)
    scatter_oq = scatter_pair(0, s.soq_ss, s.soq_rs)
    scatter_kv = scatter_pair(1, s.skv_ss, s.skv_rs)
    scatter_oq.step(C)
    for head in range(heads):
        dkv_copy(2, head, C).wait_recv()
        s.dkv[head] += s.dkv_recv[2 * heads + head].astype(f32)
    for head in range(heads):
        dkv_copy(1, head, ZL).wait_recv()
        value = s.dkv[head] + s.dkv_recv[heads + head].astype(f32)
        s.dqkv[heads + head] = turn(value, s.table[:, 0:BLK], -s.table[:, BLK:]).astype(bf16)
    spread_ada.step(4)
    kv_part = s.part[...]
    for head in range(heads, 2 * heads):
        kv_part = kv_part + dot_nn(s.dqkv[head], s.weight[head])

    def part_copy(slot, number, to):
        return remote(
            s.part_send.at[slot], s.part_recv.at[number], s.part_ss.at[slot],
            s.part_rs.at[number], to,
        )

    def part_half(slot, number, to, half):
        lines = pl.ds(half * (rows // 2), rows // 2)
        return remote(
            s.part_send.at[slot, lines], s.part_recv.at[number, lines],
            s.part_ss.at[slot + 3 * half], s.part_rs.at[number + 3 * half], to,
        )

    relays = [(part_half(2, 2, X, half), part_half(1, 1, ZH, half)) for half in range(2)]
    part_copies = [part_copy(0, 0, X)]
    s.part_send[2] = kv_part[here(3), :].astype(bf16)
    for half in range(2):
        relays[half][0].start()
    mlp_copies[0].wait_recv()
    s.mlp_send[1] = (s.mlp_near[...] + s.mlp_recv[2].astype(f32)).astype(bf16)
    mlp_copies[2].start()
    s.part_send[0] = kv_part[here(1), :].astype(bf16)
    s.part[here(2), :] = kv_part[here(2), :]
    s.grad_mixed[...] = kv_part[here(0), :]

    scatter_oq.add(C)
    scatter_oq.step(Y)

    s.norm_sum[...] = jnp.zeros_like(s.norm_sum)
    s.rowsum[9:16, :] = jnp.zeros((7, width), f32)
    for head in range(2 * heads):
        moment = dot_tn(s.dqkv[head], s.plain[...])
        weights = s.weight[head].astype(f32)
        s.norm_sum[0:1, :] += column_sum(weights * moment[:, width : width + 1])
        s.norm_sum[1:2, :] += column_sum(weights * moment[:, 0:width])
    s.rowsum[0:1, :] = s.norm_sum[0:1, :]
    s.rowsum[1:2, :] = s.norm_sum[1:2, :] * mod(6)
    s.rowsum[6:7, :] = s.norm_sum[1:2, :] * (1.0 + mod(scale_one))
    spread_ada.last()
    for y in range(2):
        for zh, zl, x, c in itertools.product(range(2), repeat=4):
            at = (y * 16 + zh * 8 + zl * 4 + x * 2 + c) * piece
            for index in range(width // BLK):
                s.ada_full[at + index * count : at + (index + 1) * count, :] = s.adaw[
                    c * 16 + y * 8 + zh * 4 + zl * 2 + x, :,
                    index * BLK : (index + 1) * BLK,
                ]
    high = s.rowsum[0:8, :].astype(bf16)
    low = (s.rowsum[0:8, :] - high.astype(f32)).astype(bf16)
    both = jnp.concatenate([high, low], axis=0)
    terms = jnp.zeros((1, BLK), f32)
    for index in range(6):
        found = dot_nn(both, s.ada_full[index * width : (index + 1) * width, :])
        terms = terms + found[index : index + 1, :] + found[8 + index : 9 + index, :]
    s.rowsum[9:10, 0:BLK] = terms
    totals = Total(s.sum_halves, s.sum_inbox, s.sum_first, s.sum_last, s.sum_ss, s.sum_rs)
    s.sum_halves[0] = s.rowsum[0:8, :]
    s.sum_halves[1] = s.rowsum[8:16, :]
    totals.start()

    for head in range(heads):
        s.wide[head * BLK : (head + 1) * BLK, 0:width] = dot_tn(
            s.dqkv[heads + head], s.mixed[...]
        )
    totals.second()
    spread(1, True, 0)
    spread(2, False, 0)
    scatter_kv.step(C)
    for half in range(2):
        lines = slice(half * (rows // 2), (half + 1) * (rows // 2))
        relays[half][0].wait_recv()
        s.part_send[1, lines, :] = (
            s.part[2 * rows + lines.start : 2 * rows + lines.stop, :]
            + s.part_recv[2, lines, :].astype(f32)
        ).astype(bf16)
        relays[half][1].start()
    part_copies[0].start()
    scatter_kv.add(C)
    scatter_kv.step(Y)
    scatter_oq.add(Y)

    def chunk_back(part, half):
        slot = own // 2 * 2 + half
        place_in = 8 * my_rank + slot
        if part < 3:
            number = 32 * part + place_in
            owner, at = number // 3, number % 3
        else:
            owner, at = place_in, 3
        z = own % 2
        index = part * 2 + half
        source = s.blocks_a.at[(part + 1) % 4 // 2, slot, (part + 1) % 2]
        target = s.owned.at[z, at]
        far = remote_to(
            source, target, s.back_ss.at[index], s.back_rs.at[z * 4 + at],
            (owner // 16, owner % 16),
        )
        near = pltpu.make_async_copy(source, target, s.local_sem.at[index])
        return far, near, owner == me

    def chunks_back(parts, act):
        for part in parts:
            for half in range(2):
                far, near, stays = chunk_back(part, half)

                @pl.when(jnp.logical_not(stays))
                def _():
                    far.start() if act else far.wait_send()

                @pl.when(stays)
                def _():
                    near.start() if act else near.wait()

    chunks_back((0, 3), True)
    for copies in (
        kv_far, kv_near, cot_copies, mix_copies, att_copies, ga_copies, mlp_copies,
        token_copies, token_z, token_on, *vec_steps,
    ):
        for copy in copies:
            copy.wait_send()
    for group in (gather_a, gather_er, spread_out, spread_ada, scatter_e, scatter_r):
        group.finish()

    @pl.loop(0, heads)
    def _(head):
        kv_forward(head).wait_send()
        dkv_copy(0, head, C).wait_send()
        dkv_copy(1, head, ZL).wait_send()
        dkv_copy(2, head, C).wait_send()

    totals.third()
    for index in (1, 2):
        mlp_copies[index].wait_recv()
    mlp_branch = s.mlp[...] + s.mlp_recv[0].astype(f32) + s.mlp_recv[1].astype(f32)
    s.result[...] = (s.middle[...] + mod(gate_two) * mlp_branch).astype(bf16)
    normed_one, inverse_one = layer_norm(s.tokens[...].astype(f32))
    scatter_kv.add(Y)
    chunks_back((1, 2), True)
    totals.fourth()
    s.grad_r[0] = s.blocks_r[own_mlp]
    s.grad_e[0] = s.blocks_e[own_mlp]
    for scatter, target in ((scatter_r, s.grad_r), (scatter_e, s.grad_e)):
        scatter.copies[ZH].wait_recv()
        target[1] = scatter.inbox(6, 1)[0]
    part_copies[0].wait_recv()
    for half in range(2):
        relays[half][1].wait_recv()
    grad_mixed_one = (
        s.grad_mixed[...] + s.part_recv[0].astype(f32) + s.part_recv[1].astype(f32)
    )
    s.grad_tokens[...] = s.gmid[...] + norm_back(
        grad_mixed_one * mod(9), normed_one, inverse_one
    )

    sums = totals.result()
    for index in range(6):
        for tile in range(width // BLK):
            s.tiles[index * (width // BLK) + tile] = sums[
                index : index + 1, tile * BLK : (tile + 1) * BLK
            ]
    for tile in range(width // BLK):
        s.gain_tiles[tile] = sums[6:9, tile * BLK : (tile + 1) * BLK]
    s.gain_tiles[width // BLK] = jnp.zeros((3, BLK), f32)
    s.vec_own[...] = jnp.zeros_like(s.vec_own)
    for tile in range(2):
        lanes = slice(tile * BLK, (tile + 1) * BLK)
        s.vec_own[0:1, lanes] = s.tiles[(9 * me) // 8 + tile]
        s.vec_own[9:12, lanes] = s.gain_tiles[(3 * me) // 16 + tile]
    s.sums[0:8, :] = pltpu.roll(s.vec_own[0:8, :], (256 - mod_shift) % 256, 1)
    s.sums[8:16, :] = pltpu.roll(s.vec_own[8:16, :], (256 - gain_shift) % 256, 1)
    s.grad_cond[...] = sums[9:10, 0:BLK]

    chunks_back(range(4), False)
    for at in range(4):
        if at < 3:
            number = 3 * me + at
            part, place_in = number // 32, number % 32
        else:
            part, place_in = 3, me
        slot = place_in % 8
        for z in range(2):
            keeper = flat(member(place_in // 8, slot // 2 * 2 + z))

            @pl.when(keeper != me)
            def _():
                target = s.owned.at[z, at]
                remote(
                    target, target, s.back_ss.at[0], s.back_rs.at[z * 4 + at], C
                ).wait_recv()

    for copies in (part_copies, *relays):
        for copy in copies:
            copy.wait_send()
    for group in (scatter_oq, scatter_kv, totals):
        group.finish()


def finish_kernel(
    result, grad_tokens, grad_cond, sums, grad_e, grad_r, owned, condition,
    result_out, tokens_out, cond_out, ada_out, ada_bias_out, first_out, second_out, project_out,
    output_out, expand_out, expand_bias_out, reduce_out, reduce_bias_out,
):
    width = result.shape[1]
    count = output_out.shape[0]
    piece = ada_out.shape[0]
    result_out[...] = result[...]
    tokens_out[...] = grad_tokens[...]
    cond_out[...] = grad_cond[...]
    first = lax.broadcasted_iota(jnp.int32, (8, piece), 0) == 0
    row = jnp.where(first, sums[0:8, 0:piece], 0.0)
    ada_out[...] = exact(
        row, jnp.broadcast_to(condition[...], (8, condition.shape[1])), ((0,), (0,))
    )
    ada_bias_out[...] = sums[0:1, 0:piece]
    first_out[...] = sums[9:10, 0:count]
    second_out[...] = sums[10:11, 0:count]
    reduce_bias_out[...] = sums[11:12, 0:count]
    both = owned[0].astype(f32) + owned[1].astype(f32)
    project_out[...] = both[0:3]
    output_out[...] = both[3]
    expand = grad_e[0].astype(f32) + grad_e[1].astype(f32)
    expand_out[...] = expand[:, 0:width]
    expand_bias_out[...] = to_row(expand[:, width : width + 1])
    reduce_out[...] = grad_r[0].astype(f32) + grad_r[1].astype(f32)


def rotary_blocks(length):
    half_dim = HEAD_DIM // 2
    frequency = np.exp(
        np.arange(half_dim, dtype=np.float32) * np.float32(-2.0 * math.log(10000.0) / HEAD_DIM)
    ).astype(np.float32)
    angles = (np.arange(length, dtype=np.float32)[:, None] * frequency[None, :]).astype(np.float32)
    cosine, sine = np.cos(angles.astype(np.float64)), np.sin(angles.astype(np.float64))
    one, zero = np.ones((length, HEAD_DIM)), np.zeros((length, HEAD_DIM))
    return np.concatenate([cosine, cosine, one, -sine, sine, zero], axis=1).astype(np.float32)


def on_device_fast(
    tokens, condition, ada_weight, ada_bias, first_gain, second_gain, project_weight,
    output_weight, expand_weight, expand_bias, reduce_weight, reduce_bias, cotangent,
):
    rows, width = tokens.shape
    group = 4 * rows
    heads = width // HEAD_DIM // 4
    per = reduce_weight.shape[0]
    units = 8 * per
    count = output_weight.shape[0]
    piece = ada_weight.shape[1]
    wide = width + BLK
    table = jnp.asarray(rotary_blocks(lax.axis_size("blk") * rows))
    line = condition[None, :]
    inputs = dict(
        tokens=tokens, cotangent=cotangent, condition=line, ada=ada_weight.T,
        ada_bias=ada_bias, first_gain=first_gain[None, :],
        second_gain=second_gain[None, :], reduce_bias=reduce_bias[None, :],
        expand_bias=expand_bias[None, :],
        project_weight=project_weight.T.reshape(3, count, width), output_weight=output_weight,
        expand_weight=expand_weight.T, reduce_weight=reduce_weight, table=table,
    )
    outputs = dict(
        result=((rows, width), bf16), grad_tokens=((rows, width), f32),
        grad_cond=((1, line.shape[1]), f32), sums=((16, 256), f32),
        grad_e=((2, per, wide), bf16), grad_r=((2, per, width), bf16),
        owned=((2, 4, count, width), bf16),
    )
    head_block = (group, BLK)
    kept = {
        name: (inputs[name].shape, inputs[name].dtype)
        for name in (
            "tokens", "condition", "ada", "ada_bias", "first_gain", "second_gain", "reduce_bias",
            "expand_bias", "project_weight",
        )
    }
    scratch = dict(
        **kept,
        table=((group, 2 * BLK), f32), vec_own=((16, 256), f32),
        vecs=((32, 4, 256), f32), mod_row=((1, 6 * width), f32), gain_rows=((3, wide), f32),
        mods=((16, width), f32), chunks=((8, 3, count, width), bf16),
        tok=((4, rows, width), bf16), cot=((4, rows, width), bf16),
        er=((8, per, wide + width), bf16),
        outw=((32, count, width), bf16), adaw=((32, count, width), bf16), ada_full=((6 * width, BLK), bf16), out_full=((width, width), bf16),
        weight=((2 * heads, BLK, width), bf16), mixed=((group, width), bf16),
        query=((heads,) + head_block, bf16), kv=((4, heads) + head_block, bf16),
        state_m=((heads, 1, group), f32), state_l=((heads, 1, group), f32),
        acc=((heads, BLK, group), f32), att=((heads, HEAD_DIM, group), bf16),
        logt=((heads, 1, group), f32), att_send=((4, heads, HEAD_DIM, rows), bf16),
        att_all=((4, heads, HEAD_DIM, rows), bf16), attn=((rows, width), f32),
        middle=((rows, width), f32), normed=((rows, width), f32), inverse=((rows, 1), f32),
        mix=((4, rows, wide), bf16), branch=((group, width), bf16),
        active=((group, units), bf16), grad_hid=((group, units), bf16),
        gm_send=((3, rows, width), bf16), gm_recv=((3, rows, width), bf16),
        mlp_send=((3, rows, width), bf16), mlp_recv=((3, rows, width), bf16),
        grad_mixed=((rows, width), f32), mlp=((rows, width), f32), gmid=((rows, width), f32),
        gattn=((4, rows, width), bf16), dout_send=((4, heads, HEAD_DIM, rows), bf16),
        dout_recv=((4, heads, HEAD_DIM, rows), bf16), rowsum=((16, width), f32),
        wide=((units, wide), f32), blocks_r=((8, per, width), bf16),
        blocks_e=((8, per, wide), bf16), blocks_a=((2, 8, 2, count, width), bf16),
        from_r=((7, per, width), bf16), from_e=((7, per, wide), bf16),
        from_a=((2, 6, 2, count, width), bf16), dout_t=((heads, BLK, group), bf16),
        dout=((heads,) + head_block, bf16), rdots=((heads, 1, group), f32),
        dq=((heads, BLK, group), f32), dkv=((heads,) + head_block, f32),
        dkv_send=((3 * heads,) + head_block, bf16), dkv_recv=((3 * heads,) + head_block, bf16),
        dqkv=((2 * heads,) + head_block, bf16), part=((group, width), f32),
        part_send=((3, rows, width), bf16), part_recv=((3, rows, width), bf16),
        plain=((group, wide), bf16), norm_sum=((8, width), f32),
        sum_halves=((2, 8, width), f32), sum_inbox=((3, 8, width), f32),
        sum_first=((4, 8, width), f32), sum_last=((4, 8, width), f32), tiles=((6 * width // BLK, 1, BLK), f32),
        gain_tiles=((width // BLK + 1, 3, BLK), f32),
        mlp_near=((rows, width), f32),
    )
    semaphores = dict(
        load_sem=16, table_sem=4, local_sem=8, chunk_ss=3, chunk_rs=3, vec_ss=7, vec_rs=7,
        tok_ss=6, tok_rs=6, a_ss=4, a_rs=4, er_ss=6, er_rs=6, o_ss=5, o_rs=5, ada_ss=5, ada_rs=5, cot_ss=4, cot_rs=4,
        kv_ss=3 * heads, kv_rs=3 * heads, att_ss=4, att_rs=4, mix_ss=4, mix_rs=4, gm_ss=4,
        gm_rs=4, mlp_ss=4, mlp_rs=4, dout_ss=4, dout_rs=4, ga_ss=4, ga_rs=4, sr_ss=3, sr_rs=3,
        se_ss=3, se_rs=3, soq_ss=2, soq_rs=2, skv_ss=2, skv_rs=2, dkv_ss=3 * heads,
        dkv_rs=3 * heads, part_ss=6, part_rs=6, back_ss=8, back_rs=8, sum_ss=8, sum_rs=8,
    )
    whole = pl.BlockSpec(memory_space=pltpu.VMEM)
    names = (*(name + "_hbm" for name in inputs), *outputs, *scratch, *semaphores)
    staged = pl.pallas_call(
        partial(block_kernel, names),
        out_shape=tuple(jax.ShapeDtypeStruct(*spec) for spec in outputs.values()),
        in_specs=[pl.BlockSpec(memory_space=pl.ANY)] * len(inputs),
        out_specs=tuple(whole for _ in outputs),
        scratch_shapes=[pltpu.VMEM(*spec) for spec in scratch.values()]
        + [pltpu.SemaphoreType.DMA((number,)) for number in semaphores.values()],
        compiler_params=pltpu.CompilerParams(
            collective_id=1, has_side_effects=True, vmem_limit_bytes=62 * 2**20
        ),
    )(*inputs.values())
    (
        result, grad_tokens, grad_condition, grad_ada, grad_ada_bias, grad_first, grad_second,
        grad_project, grad_output, grad_expand, grad_expand_bias, grad_reduce, grad_reduce_bias,
    ) = pl.pallas_call(
        finish_kernel,
        out_shape=tuple(
            jax.ShapeDtypeStruct(shape, kind)
            for shape, kind in (
                ((rows, width), bf16), ((rows, width), f32), (line.shape, f32),
                ((piece, line.shape[1]), f32), ((1, piece), f32), ((1, count), f32),
                ((1, count), f32), ((3, count, width), f32), ((count, width), f32),
                ((per, width), f32), ((1, per), f32), ((per, width), f32), ((1, count), f32),
            )
        ),
        in_specs=[whole] * 8,
        out_specs=(whole,) * 13,
    )(*staged, line)
    return (
        result,
        grad_tokens,
        grad_condition.reshape(-1),
        grad_ada.T,
        grad_ada_bias.reshape(-1),
        grad_first.reshape(-1),
        grad_second.reshape(-1),
        grad_project.reshape(3 * count, width).T,
        grad_output,
        grad_expand.T,
        grad_expand_bias.reshape(-1),
        grad_reduce,
        grad_reduce_bias.reshape(-1),
    )


def solution(mesh):
    return jax.shard_map(
        on_device_fast if mesh.shape["ulysses"] * mesh.shape["blk"] == 32 else on_device,
        mesh=mesh,
        in_specs=(
            P(BOTH, None),
            P(),
            P(None, BOTH),
            P(BOTH),
            P(BOTH),
            P(BOTH),
            P(None, BOTH),
            P(BOTH, None),
            P(None, BOTH),
            P(BOTH),
            P(BOTH, None),
            P(BOTH),
            P(BOTH, None),
        ),
        out_specs=(
            P(BOTH, None),
            P(BOTH, None),
            P(),
            P(None, BOTH),
            P(BOTH),
            P(BOTH),
            P(BOTH),
            P(None, BOTH),
            P(BOTH, None),
            P(None, BOTH),
            P(BOTH),
            P(BOTH, None),
            P(BOTH),
        ),
        check_vma=False,
    )
```

```python
from functools import partial
import itertools
import math
import types

import jax
import jax.numpy as jnp
import numpy as np
from jax import lax
from jax.experimental import pallas as pl
from jax.experimental.pallas import tpu as pltpu
from jax.sharding import PartitionSpec as P

HEAD_DIM = 64
BOTH = ("ulysses", "blk")


eps = 1e-05
highest = lax.Precision.HIGHEST


def layer_norm(value):
    center = value - jnp.mean(value, axis=-1, keepdims=True)
    inverse = lax.rsqrt(jnp.mean(center * center, axis=-1, keepdims=True) + eps)
    return (center * inverse, inverse)


def norm_back(grad_normed, normed, inverse):
    first = jnp.mean(grad_normed, axis=-1, keepdims=True)
    second = jnp.mean(grad_normed * normed, axis=-1, keepdims=True)
    return inverse * (grad_normed - first - normed * second)


def rotary_tables(positions, head_dim):
    half_dim = head_dim // 2
    frequency = jnp.exp(
        jnp.arange(half_dim, dtype=jnp.float32) * (-2.0 * math.log(10000.0) / head_dim)
    )
    angles = positions[:, None] * frequency[None, :]
    return (jnp.cos(angles)[:, None, :], jnp.sin(angles)[:, None, :])


def rotate(value, cosine, sine):
    half_dim = value.shape[-1] // 2
    first = value[..., :half_dim]
    second = value[..., half_dim:]
    return jnp.concatenate(
        [first * cosine - second * sine, second * cosine + first * sine], axis=-1
    )


def rotate_back(grad_value, cosine, sine):
    half_dim = grad_value.shape[-1] // 2
    first = grad_value[..., :half_dim]
    second = grad_value[..., half_dim:]
    return jnp.concatenate(
        [first * cosine + second * sine, second * cosine - first * sine], axis=-1
    )


def over_blocks(block_step, carried, pieces, key_block):
    length = pieces[0].shape[1]
    complete = length // key_block
    stacked = tuple(
        (
            jnp.moveaxis(
                member.reshape((member.shape[0], complete, key_block) + member.shape[2:]), 1, 0
            )
            for member in pieces
        )
    )
    offsets = jnp.arange(complete, dtype=jnp.int32) * key_block

    def scan_step(carried_in, inputs):
        return (block_step(carried_in, inputs[:-1], inputs[-1]), None)

    carried, unused = lax.scan(scan_step, carried, stacked + (offsets,))
    return carried


def on_device(
    tokens,
    condition,
    ada_weight,
    ada_bias,
    first_gain,
    second_gain,
    project_weight,
    output_weight,
    expand_weight,
    expand_bias,
    reduce_weight,
    reduce_bias,
    cotangent,
):
    row_count = tokens.shape[0]
    model_width = tokens.shape[1]
    cycle_size = lax.axis_size("blk")
    cycle_place = lax.axis_index("blk")
    seq_count = lax.axis_size("ulysses")
    (
        ada_full,
        ada_shift,
        gain_one,
        gain_two,
        project_full,
        output_full,
        expand_full,
        expand_shift,
        reduce_full,
        reduce_shift,
    ) = (
        lax.all_gather(ada_weight, BOTH, axis=1, tiled=True),
        lax.all_gather(ada_bias, BOTH, axis=0, tiled=True),
        lax.all_gather(first_gain, BOTH, axis=0, tiled=True),
        lax.all_gather(second_gain, BOTH, axis=0, tiled=True),
        lax.all_gather(project_weight, BOTH, axis=1, tiled=True),
        lax.all_gather(output_weight, BOTH, axis=0, tiled=True),
        lax.all_gather(expand_weight, BOTH, axis=1, tiled=True),
        lax.all_gather(expand_bias, BOTH, axis=0, tiled=True),
        lax.all_gather(reduce_weight, BOTH, axis=0, tiled=True),
        lax.all_gather(reduce_bias, BOTH, axis=0, tiled=True),
    )
    ada_float = ada_full.astype(jnp.float32)
    modulation = jnp.dot(condition, ada_float, precision=highest) + ada_shift.astype(jnp.float32)
    shift_one, scale_one, gate_one, shift_two, scale_two, gate_two = jnp.split(modulation, 6)
    gain_one_f = gain_one.astype(jnp.float32)
    gain_two_f = gain_two.astype(jnp.float32)
    inputs = tokens.astype(jnp.float32)
    normed_one, inverse_one = layer_norm(inputs)
    gain_first = gain_one_f * (1.0 + scale_one)
    mixed_one = (normed_one * gain_first + shift_one).astype(jnp.bfloat16)
    projected = jnp.dot(mixed_one, project_full, preferred_element_type=jnp.float32)
    packed = projected.astype(jnp.bfloat16).reshape(row_count, 3, model_width)
    regrouped = lax.all_to_all(packed, "ulysses", split_axis=2, concat_axis=0, tiled=True)
    local_rows = regrouped.shape[0]
    local_width = regrouped.shape[2]
    head_count = local_width // HEAD_DIM
    by_seq = regrouped.reshape(seq_count, row_count, 3, local_width)
    positions = cycle_place * row_count + jnp.arange(row_count, dtype=jnp.int32)
    cosine, sine = rotary_tables(positions.astype(jnp.float32), HEAD_DIM)
    query_rot = rotate(
        by_seq[:, :, 0].astype(jnp.float32).reshape(seq_count, row_count, head_count, HEAD_DIM),
        cosine,
        sine,
    ).astype(jnp.bfloat16)
    key_rot = rotate(
        by_seq[:, :, 1].astype(jnp.float32).reshape(seq_count, row_count, head_count, HEAD_DIM),
        cosine,
        sine,
    ).astype(jnp.bfloat16)
    value_flat = by_seq[:, :, 2]
    value_own = value_flat.reshape(seq_count, row_count, head_count, HEAD_DIM)
    key_flat = key_rot.reshape(seq_count, row_count, local_width)
    score_scale = HEAD_DIM ** (-0.5)
    key_block = row_count * -(-512 // row_count)

    def attend_step(carried, pieces, offset):
        maximum, denominator, weighted = carried
        key_rows = pieces[0].reshape(seq_count, -1, head_count, HEAD_DIM)
        value_rows = pieces[1].reshape(seq_count, -1, head_count, HEAD_DIM)
        scores = (
            jnp.einsum("sqhd,skhd->shqk", query_rot, key_rows, preferred_element_type=jnp.float32)
            * score_scale
        )
        new_maximum = jnp.maximum(maximum, jnp.max(scores, axis=-1))
        weights = jnp.exp(scores - new_maximum[..., None])
        factor = jnp.exp(maximum - new_maximum)
        denominator = denominator * factor + jnp.sum(weights, axis=-1)
        weighted = weighted * jnp.transpose(factor, (0, 2, 1))[..., None] + jnp.einsum(
            "shqk,skhd->sqhd",
            weights.astype(jnp.bfloat16),
            value_rows,
            preferred_element_type=jnp.float32,
        )
        return (new_maximum, denominator, weighted)

    start_state = (
        jnp.full((seq_count, head_count, row_count), -1e30, jnp.float32),
        jnp.zeros((seq_count, head_count, row_count), jnp.float32),
        jnp.zeros((seq_count, row_count, head_count, HEAD_DIM), jnp.float32),
    )
    maximum, denominator, weighted = over_blocks(
        attend_step,
        start_state,
        (
            lax.all_gather(key_flat, "blk", axis=1, tiled=True),
            lax.all_gather(value_flat, "blk", axis=1, tiled=True),
        ),
        key_block,
    )
    log_total = maximum + jnp.log(denominator)
    attended = (
        (weighted / jnp.transpose(denominator, (0, 2, 1))[..., None])
        .astype(jnp.bfloat16)
        .reshape(local_rows, local_width)
    )
    attended_tokens = lax.all_to_all(attended, "ulysses", split_axis=0, concat_axis=1, tiled=True)
    attn_branch = jnp.dot(attended_tokens, output_full, preferred_element_type=jnp.float32)
    middle = inputs + gate_one * attn_branch
    normed_two, inverse_two = layer_norm(middle)
    gain_second = gain_two_f * (1.0 + scale_two)
    mixed_two = (normed_two * gain_second + shift_two).astype(jnp.bfloat16)
    hidden = jnp.dot(
        mixed_two, expand_full, preferred_element_type=jnp.float32
    ) + expand_shift.astype(jnp.float32)
    activated, gelu_back = jax.vjp(partial(jax.nn.gelu, approximate=True), hidden)
    activated_low = activated.astype(jnp.bfloat16)
    mlp_branch = jnp.dot(
        activated_low, reduce_full, preferred_element_type=jnp.float32
    ) + reduce_shift.astype(jnp.float32)
    result = (middle + gate_two * mlp_branch).astype(jnp.bfloat16)
    grad_result = cotangent.astype(jnp.float32)
    grad_gate_two = jnp.sum(grad_result * mlp_branch, axis=0)
    grad_branch = (gate_two * grad_result).astype(jnp.bfloat16)
    grad_reduce = jnp.einsum(
        "tf,td->fd", activated_low, grad_branch, preferred_element_type=jnp.float32
    )
    grad_reduce_shift = jnp.sum(grad_branch.astype(jnp.float32), axis=0)
    grad_activated = jnp.einsum(
        "td,fd->tf", grad_branch, reduce_full, preferred_element_type=jnp.float32
    )
    grad_hidden = gelu_back(grad_activated)[0].astype(jnp.bfloat16)
    grad_expand = jnp.einsum(
        "td,tf->df", mixed_two, grad_hidden, preferred_element_type=jnp.float32
    )
    grad_expand_shift = jnp.sum(grad_hidden.astype(jnp.float32), axis=0)
    grad_mixed_two = jnp.einsum(
        "tf,df->td", grad_hidden, expand_full, preferred_element_type=jnp.float32
    )
    grad_shift_two = jnp.sum(grad_mixed_two, axis=0)
    grad_scale_two = jnp.sum(grad_mixed_two * normed_two * gain_two_f, axis=0)
    grad_gain_two = jnp.sum(grad_mixed_two * normed_two * (1.0 + scale_two), axis=0)
    grad_middle = grad_result + norm_back(grad_mixed_two * gain_second, normed_two, inverse_two)
    grad_gate_one = jnp.sum(grad_middle * attn_branch, axis=0)
    grad_attn = (gate_one * grad_middle).astype(jnp.bfloat16)
    grad_output = jnp.einsum(
        "tc,td->cd", attended_tokens, grad_attn, preferred_element_type=jnp.float32
    )
    grad_heads = jnp.einsum(
        "td,cd->tc", grad_attn, output_full, preferred_element_type=jnp.float32
    ).astype(jnp.bfloat16)
    grad_local = lax.all_to_all(grad_heads, "ulysses", split_axis=1, concat_axis=0, tiled=True)
    grad_local_heads = grad_local.reshape(seq_count, row_count, head_count, HEAD_DIM)
    row_dots = jnp.sum(
        (grad_local.astype(jnp.float32) * attended.astype(jnp.float32)).reshape(
            seq_count, row_count, head_count, HEAD_DIM
        ),
        axis=-1,
    )
    row_dots_t = jnp.transpose(row_dots, (0, 2, 1))

    def query_step(carried, pieces, offset):
        key_rows = pieces[0].reshape(seq_count, -1, head_count, HEAD_DIM)
        value_rows = pieces[1].reshape(seq_count, -1, head_count, HEAD_DIM)
        scores = (
            jnp.einsum("sqhd,skhd->shqk", query_rot, key_rows, preferred_element_type=jnp.float32)
            * score_scale
        )
        shares = jnp.exp(scores - log_total[..., None])
        grad_shares = jnp.einsum(
            "sqhd,skhd->shqk", grad_local_heads, value_rows, preferred_element_type=jnp.float32
        )
        grad_scores = (shares * (grad_shares - row_dots_t[..., None])).astype(jnp.bfloat16)
        return (
            carried
            + jnp.einsum(
                "shqk,skhd->sqhd", grad_scores, key_rows, preferred_element_type=jnp.float32
            )
            * score_scale
        )

    grad_query_rot = over_blocks(
        query_step,
        jnp.zeros((seq_count, row_count, head_count, HEAD_DIM), jnp.float32),
        (
            lax.all_gather(key_flat, "blk", axis=1, tiled=True),
            lax.all_gather(value_flat, "blk", axis=1, tiled=True),
        ),
        key_block,
    )

    def key_step(carried, pieces, offset):
        grad_keys_acc, grad_values_acc = carried
        query_rows = pieces[0].reshape(seq_count, -1, head_count, HEAD_DIM)
        slope_rows = pieces[1].reshape(seq_count, -1, head_count, HEAD_DIM)
        scores = (
            jnp.einsum("sqhd,skhd->shqk", query_rows, key_rot, preferred_element_type=jnp.float32)
            * score_scale
        )
        shares = jnp.exp(scores - jnp.transpose(pieces[2], (0, 2, 1))[..., None])
        grad_values_acc = grad_values_acc + jnp.einsum(
            "shqk,sqhd->skhd",
            shares.astype(jnp.bfloat16),
            slope_rows,
            preferred_element_type=jnp.float32,
        )
        grad_shares = jnp.einsum(
            "sqhd,skhd->shqk", slope_rows, value_own, preferred_element_type=jnp.float32
        )
        grad_scores = (
            shares * (grad_shares - jnp.transpose(pieces[3], (0, 2, 1))[..., None])
        ).astype(jnp.bfloat16)
        grad_keys_acc = (
            grad_keys_acc
            + jnp.einsum(
                "shqk,sqhd->skhd", grad_scores, query_rows, preferred_element_type=jnp.float32
            )
            * score_scale
        )
        return (grad_keys_acc, grad_values_acc)

    query_wide = query_rot.reshape(seq_count, row_count, local_width)
    slope_wide = grad_local.reshape(seq_count, row_count, local_width)
    key_init = (
        jnp.zeros((seq_count, row_count, head_count, HEAD_DIM), jnp.float32),
        jnp.zeros((seq_count, row_count, head_count, HEAD_DIM), jnp.float32),
    )
    grad_key_rot, grad_value_sum = over_blocks(
        key_step,
        key_init,
        (
            lax.all_gather(query_wide.astype(jnp.float32), "blk", axis=1, tiled=True).astype(
                jnp.bfloat16
            ),
            lax.all_gather(slope_wide.astype(jnp.float32), "blk", axis=1, tiled=True).astype(
                jnp.bfloat16
            ),
            lax.all_gather(jnp.transpose(log_total, (0, 2, 1)), "blk", axis=1, tiled=True),
            lax.all_gather(row_dots, "blk", axis=1, tiled=True),
        ),
        key_block,
    )
    grad_query = (
        rotate_back(grad_query_rot, cosine, sine)
        .astype(jnp.bfloat16)
        .reshape(local_rows, local_width)
    )
    grad_key = (
        rotate_back(grad_key_rot, cosine, sine)
        .astype(jnp.bfloat16)
        .reshape(local_rows, local_width)
    )
    grad_value = grad_value_sum.astype(jnp.bfloat16).reshape(local_rows, local_width)
    grad_packed = jnp.stack([grad_query, grad_key, grad_value], axis=1)
    grad_tokens_qkv = lax.all_to_all(
        grad_packed, "ulysses", split_axis=0, concat_axis=2, tiled=True
    ).reshape(row_count, 3 * model_width)
    grad_project = jnp.einsum(
        "tc,tk->ck", mixed_one, grad_tokens_qkv, preferred_element_type=jnp.float32
    )
    grad_mixed_one = jnp.einsum(
        "tk,ck->tc", grad_tokens_qkv, project_full, preferred_element_type=jnp.float32
    )
    grad_shift_one = jnp.sum(grad_mixed_one, axis=0)
    grad_scale_one = jnp.sum(grad_mixed_one * normed_one * gain_one_f, axis=0)
    grad_gain_one = jnp.sum(grad_mixed_one * normed_one * (1.0 + scale_one), axis=0)
    grad_input = grad_middle + norm_back(grad_mixed_one * gain_first, normed_one, inverse_one)
    mod_terms = jnp.concatenate(
        [
            grad_shift_one,
            grad_scale_one,
            grad_gate_one,
            grad_shift_two,
            grad_scale_two,
            grad_gate_two,
        ]
    )
    grad_modulation = lax.psum(mod_terms, BOTH)
    grad_condition = jnp.dot(ada_float, grad_modulation, precision=highest)
    piece_width = ada_weight.shape[1]
    flat_index = lax.axis_index("ulysses") * cycle_size + cycle_place
    mod_piece = lax.dynamic_slice_in_dim(grad_modulation, flat_index * piece_width, piece_width, 0)
    grad_ada = condition[:, None] * mod_piece[None, :]
    shards = (
        lax.psum_scatter(grad_gain_one, BOTH, scatter_dimension=0, tiled=True),
        lax.psum_scatter(grad_gain_two, BOTH, scatter_dimension=0, tiled=True),
        lax.psum_scatter(grad_project, BOTH, scatter_dimension=1, tiled=True),
        lax.psum_scatter(grad_output, BOTH, scatter_dimension=0, tiled=True),
        lax.psum_scatter(grad_expand, BOTH, scatter_dimension=1, tiled=True),
        lax.psum_scatter(grad_expand_shift, BOTH, scatter_dimension=0, tiled=True),
        lax.psum_scatter(grad_reduce, BOTH, scatter_dimension=0, tiled=True),
        lax.psum_scatter(grad_reduce_shift, BOTH, scatter_dimension=0, tiled=True),
    )
    return (
        result,
        grad_input,
        grad_condition,
        grad_ada,
        mod_piece,
        shards[0],
        shards[1],
        shards[2],
        shards[3],
        shards[4],
        shards[5],
        shards[6],
        shards[7],
    )


MESH = pl.DeviceIdType.MESH
Y, ZH, ZL, X, C = 16, 8, 4, 2, 1
ATTN = (0, X, ZH, X + ZH)
MLP = (0, X, ZL, X + ZL)
BLK = 128
f32 = jnp.float32
bf16 = jnp.bfloat16


def place():
    blk = lax.axis_index("blk")
    return (lax.axis_index("ulysses"), blk // 8, (blk // 4) % 2, (blk // 2) % 2, blk % 2)


def flip(offset):
    return tuple(
        1 - bit if (offset // weight) % 2 else bit
        for bit, weight in zip(place(), (Y, ZH, ZL, X, C))
    )


def device_at(y, zh, zl, x, c):
    return (y, zh * 8 + zl * 4 + x * 2 + c)


def peer(offset):
    return device_at(*flip(offset))


def peer_loop(offset):
    return device_at(
        *(
            (bit + (offset // weight) % 2) % 2
            for bit, weight in zip(place(), (Y, ZH, ZL, X, C))
        )
    )


def flat(device):
    return device[0] * 16 + device[1]


def share(offset, far):
    y, zh, zl, x, c = flip(offset)
    return c * 4 + y * 2 + (zl if far == ZL else zh)


def rank(offset):
    y, zh, zl, x, c = flip(offset)
    return zh * 2 + x


def member(which, slot):
    return device_at((slot // 2) % 2, which // 2, slot % 2, which % 2, slot // 4)


def greet(offsets):
    barrier = pltpu.get_barrier_semaphore()
    for offset in offsets:
        pl.semaphore_signal(barrier, inc=1, device_id=peer(offset), device_id_type=MESH)
    return lambda: pl.semaphore_wait(barrier, len(offsets))


def remote_to(source, target, send_sem, recv_sem, device):
    return pltpu.make_async_remote_copy(
        src_ref=source,
        dst_ref=target,
        send_sem=send_sem,
        recv_sem=recv_sem,
        device_id=device,
        device_id_type=MESH,
    )


def remote(source, target, send_sem, recv_sem, offset):
    return remote_to(source, target, send_sem, recv_sem, peer(offset))


def dot_nn(a, b):
    return jnp.dot(a, b, preferred_element_type=f32)


def dot_nt(a, b):
    return lax.dot_general(a, b, (((1,), (1,)), ((), ())), preferred_element_type=f32)


def dot_tn(a, b):
    return lax.dot_general(a, b, (((0,), (0,)), ((), ())), preferred_element_type=f32)


def exact(a, b, contract):
    return lax.dot_general(
        a, b, (contract, ((), ())), preferred_element_type=f32, precision=highest
    )


def column_sum(value):
    return jnp.sum(value, axis=0, keepdims=True)


class Gather:
    def __init__(self, view, send_sem, recv_sem, far, pieces):
        own, core = share(0, far), share(C, far)
        z, y = share(far, far), share(Y, far)
        both = share(Y + far, far)
        half, other = own // 4 * 4, core // 4 * 4

        def pair(mine, theirs, index, to, piece=lambda v: v):
            return tuple(
                remote(piece(where), piece(where), send_sem.at[index], recv_sem.at[index], to)
                for where in (mine, theirs)
            )

        self.y_own = pair(view(own, 1), view(y, 1), 0, Y)
        self.cores = pair(view(half, 4), view(other, 4), 1, C)
        self.over_z = [
            pair(view(own, 1), view(z, 1), 2 + 2 * index, far, piece)
            for index, piece in enumerate(pieces)
        ]
        self.over_y = [
            pair(view(z, 1), view(both, 1), 3 + 2 * index, Y, piece)
            for index, piece in enumerate(pieces)
        ]

    def near(self):
        self.y_own[0].start()

    def far(self, which=0):
        self.over_z[which][0].start()

    def second(self, which=0):
        self.over_z[which][1].wait_recv()
        self.over_y[which][0].start()

    def third(self):
        for _out, into in (self.y_own, *self.over_y):
            into.wait_recv()
        self.cores[0].start()

    def last(self):
        self.cores[1].wait_recv()

    def finish(self):
        for out, _into in (self.y_own, self.cores, *self.over_z, *self.over_y):
            out.wait_send()


class Spread:
    def __init__(self, view, place_of, order, send_sem, recv_sem):
        self.out, self.into = [], []
        size = 1
        for index, to in enumerate(order):
            mine, other = (place_of(flip(to_where)) // size * size for to_where in (0, to))
            sems = (send_sem.at[index], recv_sem.at[index])
            self.out.append(remote(view(mine, size), view(mine, size), *sems, to))
            self.into.append(remote(view(other, size), view(other, size), *sems, to))
            size *= 2

    def step(self, index):
        if index:
            self.into[index - 1].wait_recv()
        self.out[index].start()

    def last(self):
        self.into[-1].wait_recv()

    def finish(self):
        for copy in self.out:
            copy.wait_send()


class Scatter:
    def __init__(self, view, inbox, send_sem, recv_sem, far):
        self.view, self.inbox = view, inbox
        own = share(0, far)
        core, y, z = share(C, far), share(Y, far), share(far, far)
        self.plan = {
            C: (core // 4 * 4, own // 4 * 4, 4, 0), Y: (y // 2 * 2, own // 2 * 2, 2, 4),
            far: (z, own, 1, 6),
        }
        self.send_sem, self.recv_sem = send_sem, recv_sem
        self.copies = {}

    def step(self, to):
        goes, _stays, size, slot = self.plan[to]
        index = len(self.copies)
        self.copies[to] = remote(
            self.view(goes, size), self.inbox(slot, size), self.send_sem.at[index],
            self.recv_sem.at[index], to,
        )
        self.copies[to].start()

    def add(self, to):
        self.copies[to].wait_recv()
        _goes, stays, size, slot = self.plan[to]
        block = self.view(stays, size)
        block[...] = (
            block[...].astype(f32) + self.inbox(slot, size)[...].astype(f32)
        ).astype(bf16)

    def finish(self):
        for copy in self.copies.values():
            copy.wait_send()


class Total:
    def __init__(self, halves, inbox, first, last, send_sem, recv_sem):
        self.halves, self.inbox, self.first, self.last = halves, inbox, first, last
        y, zh, zl, x, c = place()
        self.core = c
        self.own = (y * 2 + zh, zl * 2 + x)
        sems = [(send_sem.at[index], recv_sem.at[index]) for index in range(8)]
        self.copies = [
            remote(ref.at[own], ref.at[own], *sems[3 * which + index], to)
            for which, (ref, own, offsets) in enumerate(
                ((first, self.own[0], (Y, ZH, Y + ZH)), (last, self.own[1], (ZL, X, ZL + X)))
            )
            for index, to in enumerate(offsets)
        ]
        self.copies.append(remote(halves.at[1 - c], inbox.at[0], *sems[6], C))
        self.copies.append(remote(inbox.at[1 + c], inbox.at[1 + c], *sems[7], C))

    def start(self):
        self.copies[6].start()

    def second(self):
        self.copies[6].wait_recv()
        self.first[self.own[0]] = self.halves[self.core] + self.inbox[0]
        for copy in self.copies[0:3]:
            copy.start()

    def third(self):
        for copy in self.copies[0:3]:
            copy.wait_recv()
        self.last[self.own[1]] = (
            self.first[0] + self.first[1] + self.first[2] + self.first[3]
        )
        for copy in self.copies[3:6]:
            copy.start()

    def fourth(self):
        for copy in self.copies[3:6]:
            copy.wait_recv()
        self.inbox[1 + self.core] = self.last[0] + self.last[1] + self.last[2] + self.last[3]
        self.copies[7].start()

    def result(self):
        self.copies[7].wait_recv()
        return jnp.concatenate([self.inbox[1], self.inbox[2]], axis=0)

    def finish(self):
        for copy in self.copies:
            copy.wait_send()


def turn(value, cosine, sine):
    lane = lax.broadcasted_iota(jnp.int32, value.shape, 1)
    swapped = jnp.where(
        lane < HEAD_DIM // 2,
        pltpu.roll(value, BLK - HEAD_DIM // 2, 1),
        pltpu.roll(value, HEAD_DIM // 2, 1),
    )
    return value * cosine + swapped * sine


def head_rows(first, count, low):
    for row in range(first, first + count, 8):
        yield row - first, row // HEAD_DIM, row % HEAD_DIM + (0 if low else HEAD_DIM)


def gelu_pair(hidden):
    scale = math.sqrt(2.0 / math.pi)
    square = hidden * hidden
    bend = jnp.tanh(scale * hidden * (1.0 + 0.044715 * square))
    half = 0.5 * (1.0 + bend)
    slope = half + 0.5 * hidden * (1.0 - bend * bend) * (
        scale * (1.0 + 3.0 * 0.044715 * square)
    )
    return hidden * half, slope


def to_column(row):
    count = row.shape[1]
    one = lax.broadcasted_iota(jnp.int32, (count, count), 0)
    two = lax.broadcasted_iota(jnp.int32, (count, count), 1)
    return jnp.sum(jnp.where(one == two, row, 0.0), axis=1, keepdims=True)


def to_row(column):
    count = column.shape[0]
    one = lax.broadcasted_iota(jnp.int32, (count, count), 0)
    two = lax.broadcasted_iota(jnp.int32, (count, count), 1)
    return jnp.sum(jnp.where(one == two, column, 0.0), axis=0, keepdims=True)


def block_kernel(names, *refs):
    s = types.SimpleNamespace(**dict(zip(names, refs)))
    rows, width = s.tokens.shape
    wide = width + BLK
    heads = s.query.shape[0]
    count = s.output_weight_hbm.shape[0]
    per = s.reduce_weight_hbm.shape[0]
    units = 8 * per
    scale = HEAD_DIM ** (-0.5)
    me = flat(peer(0))
    own, own_mlp = share(0, ZL), share(0, ZH)
    my_rank = rank(0)

    def here(slot):
        return slice(slot * rows, (slot + 1) * rows)

    loads = {}

    def load(name, target=None):
        number = len(loads)
        copy = pltpu.make_async_copy(
            getattr(s, name + "_hbm"), getattr(s, name) if target is None else target,
            s.load_sem.at[number],
        )
        copy.start()
        loads[name] = copy

    for name in (
        "ada", "condition", "ada_bias", "first_gain", "second_gain", "reduce_bias",
        "project_weight",
    ):
        load(name)
    def out_place(bits):
        y, zh, zl, x, c = bits
        return c * 16 + y * 8 + zh * 4 + zl * 2 + x

    entered = greet(range(1, 32))
    piece = s.ada.shape[0]
    for name in ("ada", "condition", "ada_bias", "first_gain", "second_gain", "reduce_bias"):
        loads[name].wait()
    for index in range(width // BLK):
        s.adaw[out_place(flip(0)), :, index * BLK : (index + 1) * BLK] = s.ada[
            index * count : (index + 1) * count, :
        ]
    s.vec_own[...] = jnp.zeros_like(s.vec_own)
    s.vec_own[0:8, 0:piece] = exact(
        jnp.broadcast_to(s.condition[...], (8, s.condition.shape[1])),
        s.ada[...].astype(f32), ((1,), (1,)),
    )
    s.vec_own[0:1, 0:piece] += s.ada_bias[...].astype(f32)
    for index, ref in enumerate((s.first_gain, s.second_gain, s.reduce_bias)):
        s.vec_own[8 + index : 9 + index, 0:count] = ref[...].astype(f32)
    mod_shift = (me % 8) * 16
    gain_shift = ((3 * me) % 16) * 8
    y, zh, zl, x, c = place()
    vec_own = y * 16 + x * 8 + c * 4 + zh * 2 + zl
    s.vecs[vec_own, 0:1, :] = pltpu.roll(s.vec_own[0:8, :], mod_shift, 1)[0:1, :]
    s.vecs[vec_own, 1:4, :] = pltpu.roll(s.vec_own[8:16, :], gain_shift, 1)[0:3, :]
    lane = lax.broadcasted_iota(jnp.int32, (rows, BLK), 1)
    ones = jnp.where(lane == 0, 1.0, 0.0).astype(bf16)
    for slot in range(4):
        s.mix[slot, :, width:] = ones
        s.plain[here(slot), width:] = ones
    loads["project_weight"].wait()
    entered()

    def token_copy(have, to):
        slot = ATTN.index(have + to)
        return remote(
            s.tok.at[ATTN.index(have)] if have else s.tokens, s.tok.at[slot],
            s.tok_ss.at[slot], s.tok_rs.at[slot], to,
        )

    def token_half(have, to, half, number):
        lines = pl.ds(half * (rows // 2), rows // 2)
        slot = ATTN.index(have + to)
        source = s.tok.at[ATTN.index(have), lines] if have else s.tokens.at[lines]
        return remote(
            source, s.tok.at[slot, lines], s.tok_ss.at[number], s.tok_rs.at[number], to
        )

    token_copies = [token_copy(0, X)]
    token_z = [token_half(0, ZH, half, 2 + half) for half in range(2)]
    token_on = [token_half(ZH, X, half, 4 + half) for half in range(2)]
    vec_steps = []
    for index, (size, offsets) in enumerate(
        ((1, (ZL, ZH, ZL + ZH)), (4, (C, X, X + C)), (16, (Y,)))
    ):
        where = s.vecs.at[pl.ds(vec_own // size * size, size)]
        vec_steps.append(
            [
                remote(
                    where, where, s.vec_ss.at[3 * index + number], s.vec_rs.at[3 * index + number],
                    to,
                )
                for number, to in enumerate(offsets)
            ]
        )

    def vec_step(index):
        for copy in vec_steps[index - 1] if index else ():
            copy.wait_recv()
        for copy in vec_steps[index] if index < 3 else ():
            copy.start()

    vec_step(0)
    def chunk_out(index):
        number = 3 * me + index
        part, place_in = number // 32, number % 32
        slot = place_in % 8
        device = member(place_in // 8, slot)
        target = s.chunks.at[slot, part]
        far = remote_to(
            s.project_weight.at[index], target, s.chunk_ss.at[index], s.chunk_rs.at[index], device
        )
        near = pltpu.make_async_copy(s.project_weight.at[index], target, s.local_sem.at[index])
        return far, near, flat(device) == me

    for index in range(3):
        far, near, stays = chunk_out(index)

        @pl.when(jnp.logical_not(stays))
        def _():
            far.start()

        @pl.when(stays)
        def _():
            near.start()

    for name in ("tokens", "expand_bias"):
        load(name)
    load("expand_weight", s.er.at[own_mlp, :, pl.ds(0, width)])
    load("reduce_weight", s.er.at[own_mlp, :, pl.ds(wide, width)])

    load("output_weight", s.outw.at[out_place(flip(0))])
    load("cotangent", s.cot.at[0])
    tables = []
    for slot in range(4):
        start = pl.multiple_of(peer(ATTN[slot])[1] * rows, rows)
        copy = pltpu.make_async_copy(
            s.table_hbm.at[pl.ds(start, rows)], s.table.at[pl.ds(slot * rows, rows)],
            s.table_sem.at[slot],
        )
        copy.start()
        tables.append(copy)
    gather_er = Gather(
        lambda slot, size: s.er.at[pl.ds(slot, size)], s.er_ss, s.er_rs, ZH,
        (
            lambda v: v.at[:, :, pl.ds(wide, width)],
            lambda v: v.at[:, :, pl.ds(0, wide)],
        ),
    )
    loads["expand_bias"].wait()
    lane = lax.broadcasted_iota(jnp.int32, (per, BLK), 1)
    s.er[own_mlp, :, width:wide] = jnp.where(
        lane == 0, to_column(s.expand_bias[...].astype(f32)), 0.0
    ).astype(bf16)
    zero = jnp.zeros((HEAD_DIM, width), bf16)
    for head in range(heads):
        s.weight[head, HEAD_DIM:, :] = zero
    s.state_m[...] = jnp.full_like(s.state_m, -1e30)
    s.state_l[...] = jnp.zeros_like(s.state_l)
    s.acc[...] = jnp.zeros_like(s.acc)
    spread_out = Spread(
        lambda slot, size: s.outw.at[pl.ds(slot, size)], out_place, (X, ZL, ZH, Y, C),
        s.o_ss, s.o_rs,
    )
    spread_ada = Spread(
        lambda slot, size: s.adaw.at[pl.ds(slot, size)], out_place, (X, ZL, ZH, Y, C),
        s.ada_ss, s.ada_rs,
    )
    for name in ("expand_weight", "reduce_weight", "output_weight", "cotangent", "tokens"):
        loads[name].wait()
    vec_step(1)
    spread_out.step(0)
    spread_ada.step(0)

    for index in range(3):
        far, near, stays = chunk_out(index)

        @pl.when(jnp.logical_not(stays))
        def _():
            far.wait()

        @pl.when(stays)
        def _():
            near.wait()

    gather_a = Gather(
        lambda slot, size: s.chunks.at[pl.ds(slot, size)], s.a_ss, s.a_rs, ZL, (lambda v: v,)
    )
    def cot_copy(have, to):
        slot = MLP.index(have + to)
        return remote(
            s.cot.at[MLP.index(have)], s.cot.at[slot], s.cot_ss.at[slot], s.cot_rs.at[slot], to
        )

    cot_copies = [cot_copy(0, X), cot_copy(0, ZL), cot_copy(ZL, X)]
    gather_a.far()
    gather_a.near()
    token_z[0].start()
    token_z[1].start()
    token_copies[0].start()
    vec_step(2)
    spread_out.step(1)
    spread_ada.step(1)
    gather_a.second()
    cot_copies[1].start()
    vec_step(3)
    s.mod_row[...] = jnp.zeros_like(s.mod_row)
    s.gain_rows[...] = jnp.zeros_like(s.gain_rows)
    for index in range(32):
        y, zh, zl, x, c = ((index // weight) % 2 for weight in (Y, ZH, ZL, X, C))
        found = y * 16 + x * 8 + c * 4 + zh * 2 + zl
        tile = (9 * index) // 8 * BLK
        s.mod_row[0:1, tile : tile + 2 * BLK] += s.vecs[found, 0:1, :]
        tile = (3 * index) // 16 * BLK
        s.gain_rows[0:3, tile : tile + 2 * BLK] += s.vecs[found, 1:4, :]
    shift_one, scale_one, gate_one, shift_two, scale_two, gate_two = range(6)
    for index in range(6):
        s.mods[index : index + 1, :] = s.mod_row[0:1, index * width : (index + 1) * width]
    s.mods[6:9, :] = s.gain_rows[0:3, 0:width]
    s.mods[9:10, :] = s.mods[6:7, :] * (1.0 + s.mods[scale_one : scale_one + 1, :])
    s.mods[10:11, :] = s.mods[7:8, :] * (1.0 + s.mods[scale_two : scale_two + 1, :])

    def mod(index):
        return s.mods[index : index + 1, :]

    for slot in range(4):
        if slot == 1:
            token_copies[0].wait_recv()
        if slot == 3:
            token_on[0].wait_recv()
            token_on[1].wait_recv()
        if slot == 2:
            token_z[0].wait_recv()
            token_z[1].wait_recv()
            token_on[0].start()
            token_on[1].start()
            cot_copies[0].start()
            spread_out.step(2)
            gather_er.far(0)
            gather_er.near()
            gather_a.third()
        source = s.tok[slot] if slot else s.tokens[...]
        normed, _unused = layer_norm(source.astype(f32))
        s.mixed[here(slot), :] = (normed * mod(9) + mod(shift_one)).astype(bf16)
        s.plain[here(slot), 0:width] = normed.astype(bf16)
    def assemble(part, base, low):
        for slot in range(8):
            for row, head, target in head_rows(slot * count, count, low):
                s.weight[base + head, target : target + 8, :] = s.chunks[
                    slot, part, row : row + 8, :
                ]

    gather_er.far(1)
    gather_a.last()
    assemble(1, heads, True)
    assemble(2, heads, False)
    for copy in tables:
        copy.wait()
    kv_far = [
        remote(s.kv.at[0, head], s.kv.at[2, head], s.kv_ss.at[head], s.kv_rs.at[head], ZL)
        for head in range(heads)
    ]
    kv_near = [
        remote(
            s.kv.at[0, head], s.kv.at[1, head], s.kv_ss.at[heads + head],
            s.kv_rs.at[heads + head], C,
        )
        for head in range(heads)
    ]
    for head in range(heads):
        both = dot_nt(s.mixed[...], s.weight[heads + head]).astype(bf16).astype(f32)
        s.kv[0, head] = turn(both, s.table[:, 0:BLK], s.table[:, BLK:]).astype(bf16)
        kv_far[head].start()
        kv_near[head].start()
    assemble(0, 0, True)
    for head in range(heads):
        query = dot_nt(s.mixed[...], s.weight[head]).astype(bf16).astype(f32)
        query = turn(query, s.table[:, 0:BLK], s.table[:, BLK:]).astype(bf16).astype(f32)
        s.query[head] = (query * scale).astype(bf16)
    cot_copies[1].wait_recv()
    cot_copies[2].start()


    def attend(slot, head, count_of=1):
        keys = s.kv[slot : slot + count_of, head].reshape(count_of * 4 * rows, BLK)
        scores = dot_nt(keys, s.query[head])
        before = s.state_m[head]
        maximum = jnp.maximum(before, jnp.max(scores, axis=0, keepdims=True))
        weights = jnp.exp(scores - maximum)
        factor = jnp.exp(before - maximum)
        s.state_m[head] = maximum
        s.state_l[head] = s.state_l[head] * factor + column_sum(weights)
        s.acc[head] = s.acc[head] * factor + dot_tn(keys, weights.astype(bf16))

    for head in range(heads):
        kv_near[head].wait_recv()

    @pl.loop(0, heads)
    def _(head):
        attend(0, head, 2)

        @pl.when(head == 0)
        def _():
            spread_out.step(3)


    gather_er.second(0)

    def kv_forward(head):
        return remote(
            s.kv.at[2, head], s.kv.at[3, head], s.kv_ss.at[2 * heads + head],
            s.kv_rs.at[2 * heads + head], C,
        )

    def finish_head(head):
        forwards[head].wait_recv()
        attend(3, head)
        value = (s.acc[head] / s.state_l[head]).astype(bf16)
        s.att[head] = value[HEAD_DIM:, :]
        s.logt[head] = s.state_m[head] + jnp.log(s.state_l[head])

    forwards = []
    for head in range(heads):
        kv_far[head].wait_recv()
        forwards.append(kv_forward(head))
        forwards[head].start()
        attend(2, head)
        if head == 1:
            gather_er.second(1)
        if head:
            finish_head(head - 1)
    finish_head(heads - 1)

    for slot in range(4):
        for head in range(heads):
            s.att_send[slot, head] = s.att[head, :, here(slot)]
    att_copies = [
        remote(
            s.att_send.at[slot], s.att_all.at[my_rank], s.att_ss.at[slot], s.att_rs.at[slot],
            ATTN[slot],
        )
        for slot in range(1, 4)
    ]
    for copy in att_copies:
        copy.start()
    s.att_all[my_rank] = s.att_send[0]
    spread_out.step(4)
    gather_er.third()
    spread_out.last()
    for y in range(2):
        for zh, zl, x, c in itertools.product(range(2), repeat=4):
            at = (y * 16 + zh * 8 + zl * 4 + x * 2 + c) * count
            s.out_full[at : at + count, :] = s.outw[c * 16 + y * 8 + zh * 4 + zl * 2 + x]
    for slot in range(1, 4):
        where = s.att_all.at[rank(ATTN[slot])]
        remote(where, where, s.att_ss.at[slot], s.att_rs.at[slot], ATTN[slot]).wait_recv()
    s.attn[...] = dot_tn(s.att_all[...].reshape(width, rows), s.out_full[...])
    s.middle[...] = s.tokens[...].astype(f32) + mod(gate_one) * s.attn[...]
    normed, inverse = layer_norm(s.middle[...])
    s.normed[...] = normed
    s.inverse[...] = inverse
    s.mix[0, :, :width] = (normed * mod(10) + mod(shift_two)).astype(bf16)
    def mix_copy(source, slot, number, lines, to):
        return remote(
            s.mix.at[source, lines, pl.ds(0, width)], s.mix.at[slot, lines, pl.ds(0, width)],
            s.mix_ss.at[number], s.mix_rs.at[number], to,
        )

    mix_copies = [
        mix_copy(0, 1, 0, pl.ds(0, rows), X),
        mix_copy(0, 2, 1, pl.ds(0, rows), ZL),
        mix_copy(1, 3, 2, pl.ds(0, rows // 2), ZL),
        mix_copy(2, 3, 3, pl.ds(rows // 2, rows // 2), X),
    ]
    for copy in mix_copies[0:2]:
        copy.start()
    for slot in range(4):
        if slot == 1 or slot == 3:
            cot_copies[slot - 1].wait_recv()
        s.branch[here(slot), :] = (mod(gate_two) * s.cot[slot].astype(f32)).astype(bf16)
    gather_er.last()

    def expand(lanes=wide):
        return s.er[:, :, 0:lanes].reshape(units, lanes)

    def reduce():
        return s.er[:, :, wide:].reshape(units, width)

    spread_ada.step(2)
    gm_copies = [
        remote(
            s.gm_send.at[slot - 1], s.gm_recv.at[slot - 1], s.gm_ss.at[slot], s.gm_rs.at[slot],
            MLP[slot],
        )
        for slot in range(1, 4)
    ]
    for first, last in ((0, 1), (1, 3), (3, 4)):
        if first == 1:
            for index in range(2):
                mix_copies[index].wait_recv()
                mix_copies[2 + index].start()
        elif first == 3:
            mix_copies[2].wait_recv()
            mix_copies[3].wait_recv()
        these = slice(first * rows, last * rows)
        mixed_two = s.mix[first:last].reshape((last - first) * rows, wide)
        activated, slope = gelu_pair(dot_nt(mixed_two, expand()))
        s.active[these, :] = activated.astype(bf16)
        grad_hidden = (dot_nt(s.branch[these, :], reduce()) * slope).astype(bf16)
        s.grad_hid[these, :] = grad_hidden
        gm_part = dot_nn(grad_hidden, expand(width))
        for slot in range(first, last):
            part = gm_part[(slot - first) * rows : (slot - first + 1) * rows, :]
            if slot:
                s.gm_send[slot - 1] = part.astype(bf16)
                gm_copies[slot - 1].start()
            else:
                s.grad_mixed[...] = part
    for index in range(units // BLK):
        lanes = slice(index * BLK, (index + 1) * BLK)
        s.wide[lanes, 0:width] = dot_tn(s.active[:, lanes], s.branch[...])
    for index in range(8):
        s.blocks_r[index] = s.wide[index * per : (index + 1) * per, 0:width].astype(bf16)
    scatter_r = Scatter(
        lambda slot, size: s.blocks_r.at[pl.ds(slot, size)],
        lambda slot, size: s.from_r.at[pl.ds(slot, size)], s.sr_ss, s.sr_rs, ZH
    )
    scatter_r.step(C)
    for index in range(units // BLK):
        lanes = slice(index * BLK, (index + 1) * BLK)
        s.wide[lanes, :] = dot_tn(
            s.grad_hid[:, lanes], s.mix[...].reshape(4 * rows, width + BLK)
        )
    scatter_r.add(C)
    scatter_r.step(Y)
    for index in range(8):
        s.blocks_e[index] = s.wide[index * per : (index + 1) * per, :].astype(bf16)
    scatter_e = Scatter(
        lambda slot, size: s.blocks_e.at[pl.ds(slot, size)],
        lambda slot, size: s.from_e.at[pl.ds(slot, size)], s.se_ss, s.se_rs, ZH
    )
    scatter_e.step(C)
    def mlp_copy(slot, number, to):
        return remote(
            s.mlp_send.at[slot], s.mlp_recv.at[number], s.mlp_ss.at[slot], s.mlp_rs.at[number], to
        )

    mlp_copies = [mlp_copy(2, 2, X), mlp_copy(0, 0, X), mlp_copy(1, 1, ZL)]

    def mlp_part(slot):
        return dot_nn(s.active[here(slot), :], reduce())

    s.mlp_send[2] = mlp_part(3).astype(bf16)
    s.mlp_send[0] = mlp_part(1).astype(bf16)
    s.mlp[...] = mlp_part(0) + mod(8)
    s.mlp_near[...] = mlp_part(2)
    for index in range(units // BLK):
        lanes = slice(index * BLK, (index + 1) * BLK)
        s.wide[lanes, 0:width] = dot_tn(s.active[:, lanes], s.cot[...].reshape(4 * rows, width))
    gate_sum = mod(8) * column_sum(s.cot[0].astype(f32))
    for index in range(8):
        gate_sum = gate_sum + column_sum(
            s.er[index, :, wide:].astype(f32) * s.wide[index * per : (index + 1) * per, 0:width]
        )
    s.rowsum[5:6, :] = gate_sum
    for copy in gm_copies:
        copy.wait()
    grad_mixed = (
        s.grad_mixed[...]
        + s.gm_recv[0].astype(f32) + s.gm_recv[1].astype(f32) + s.gm_recv[2].astype(f32)
    )
    cot = s.cot[0].astype(f32)
    normed = s.normed[...]
    grad_middle = cot + norm_back(grad_mixed * mod(10), normed, s.inverse[...])
    s.gmid[...] = grad_middle
    grad_attn = (mod(gate_one) * grad_middle).astype(bf16)
    s.gattn[0] = grad_attn
    s.dout_send[...] = dot_nt(s.out_full[...], grad_attn).astype(bf16).reshape(
        s.dout_send.shape
    )
    dout_copies = [
        remote(
            s.dout_send.at[rank(ATTN[slot])], s.dout_recv.at[slot], s.dout_ss.at[slot],
            s.dout_rs.at[slot], ATTN[slot],
        )
        for slot in range(1, 4)
    ]
    for copy in dout_copies:
        copy.start()
    s.dout_recv[0] = s.dout_send[my_rank]
    def ga_copy(have, to):
        slot = ATTN.index(have + to)
        return remote(
            s.gattn.at[ATTN.index(have)], s.gattn.at[slot], s.ga_ss.at[slot], s.ga_rs.at[slot], to
        )

    ga_copies = [ga_copy(0, X), ga_copy(0, ZH), ga_copy(ZH, X)]
    weighted = column_sum(grad_mixed * normed)
    s.rowsum[2:3, :] = column_sum(grad_middle * s.attn[...])
    s.rowsum[3:4, :] = column_sum(grad_mixed)
    s.rowsum[4:5, :] = weighted * mod(7)
    s.rowsum[7:8, :] = weighted * (1.0 + mod(scale_two))
    s.rowsum[8:9, :] = column_sum(s.branch[here(0), :].astype(f32))
    scatter_e.add(C)
    scatter_e.step(Y)

    s.dout_t[...] = jnp.zeros_like(s.dout_t)
    for slot in range(4):
        if slot:
            dout_copies[slot - 1].wait()
        if slot == 3:
            ga_copies[1].start()
        for head in range(heads):
            s.dout_t[head, HEAD_DIM:, here(slot)] = s.dout_recv[slot, head]
    for head in range(heads):
        value = s.dout_t[head].astype(f32)
        s.dout[head] = value.T.astype(bf16)
        s.rdots[head] = column_sum(value[HEAD_DIM:, :] * s.att[head].astype(f32))
    scatter_r.add(Y)
    scatter_r.step(ZH)
    ga_copies[0].start()
    mlp_copies[0].start()
    mlp_copies[1].start()
    s.dq[...] = jnp.zeros_like(s.dq)

    def back(slot, head):
        keys = s.kv[slot : slot + 2, head].reshape(2 * 4 * rows, BLK)
        query = s.query[head]
        shares = jnp.exp(dot_nt(keys, query) - s.logt[head])
        grad_shares = dot_nn(keys, s.dout_t[head])
        grad_scores = (shares * (grad_shares - s.rdots[head])).astype(bf16)
        s.dq[head] += dot_tn(keys, grad_scores)
        return dot_nn(grad_scores, query) + dot_nn(shares.astype(bf16), s.dout[head])

    def dkv_copy(stage, head, offset):
        index = stage * heads + head
        return remote(
            s.dkv_send.at[index], s.dkv_recv.at[index], s.dkv_ss.at[index], s.dkv_rs.at[index],
            offset,
        )

    @pl.loop(0, heads)
    def _(head):
        both = back(2, head)
        s.dkv_send[head] = both[4 * rows :].astype(bf16)
        first = dkv_copy(0, head, C)
        first.start()
        part = both[: 4 * rows]
        first.wait_recv()
        s.dkv_send[heads + head] = (part + s.dkv_recv[head].astype(f32)).astype(bf16)
        dkv_copy(1, head, ZL).start()

    scatter_e.add(Y)
    scatter_e.step(ZH)
    spread_ada.step(3)

    @pl.loop(0, heads)
    def _(head):
        @pl.when(head == 2)
        def _():
            ga_copies[1].wait_recv()
            ga_copies[2].start()

        both = back(0, head)
        s.dkv_send[2 * heads + head] = both[4 * rows :].astype(bf16)
        dkv_copy(2, head, C).start()
        s.dkv[head] = both[: 4 * rows]
        value = s.dq[head].T * scale
        s.dqkv[head] = turn(value, s.table[:, 0:BLK], -s.table[:, BLK:]).astype(bf16)

    spread_ada.step(4)
    query_part = dot_nn(s.dqkv[0], s.weight[0])
    for head in range(1, heads):
        query_part = query_part + dot_nn(s.dqkv[head], s.weight[head])
    s.part[...] = query_part
    def spread(part, low, of):
        for slot in range(8):
            for row, head, target in head_rows(slot * count, count, low):
                s.blocks_a[(part + 1) % 4 // 2, slot, (part + 1) % 2, row : row + 8, :] = s.wide[
                    of * heads * BLK + head * BLK + target
                    : of * heads * BLK + head * BLK + target + 8, 0:width
                ].astype(bf16)

    def scatter_pair(pair, ss, rs):
        return Scatter(
            lambda slot, size: s.blocks_a.at[pair, pl.ds(slot, size)],
            lambda slot, size: s.from_a.at[pair, pl.ds(slot, size)],
            ss, rs, ZL,
        )

    for head in range(heads):
        at = (heads + head) * BLK
        s.wide[at : at + BLK, 0:width] = dot_tn(s.dqkv[head], s.mixed[...])
    spread(0, True, 1)
    ga_copies[0].wait_recv()
    ga_copies[2].wait_recv()
    gattn = s.gattn[...].reshape(4 * rows, width)

    for head in range(heads):
        s.wide[head * BLK + HEAD_DIM : (head + 1) * BLK, 0:width] = dot_nn(s.att[head], gattn)
    spread(3, False, 0)
    scatter_oq = scatter_pair(0, s.soq_ss, s.soq_rs)
    scatter_kv = scatter_pair(1, s.skv_ss, s.skv_rs)
    scatter_oq.step(C)
    s.norm_sum[...] = jnp.zeros_like(s.norm_sum)
    s.rowsum[9:16, :] = jnp.zeros((7, width), f32)

    def norm_sums(which):
        for head in which:
            moment = dot_tn(s.dqkv[head], s.plain[...])
            weights = s.weight[head].astype(f32)
            s.norm_sum[0:1, :] += column_sum(weights * moment[:, width : width + 1])
            s.norm_sum[1:2, :] += column_sum(weights * moment[:, 0:width])

    norm_sums(range(heads))
    spread_ada.last()
    for y in range(2):
        for zh, zl, x, c in itertools.product(range(2), repeat=4):
            at = (y * 16 + zh * 8 + zl * 4 + x * 2 + c) * piece
            for index in range(width // BLK):
                s.ada_full[at + index * count : at + (index + 1) * count, :] = s.adaw[
                    c * 16 + y * 8 + zh * 4 + zl * 2 + x, :,
                    index * BLK : (index + 1) * BLK,
                ]
    for head in range(heads):
        dkv_copy(2, head, C).wait_recv()
        s.dkv[head] += s.dkv_recv[2 * heads + head].astype(f32)
    for head in range(heads):
        dkv_copy(1, head, ZL).wait_recv()
        value = s.dkv[head] + s.dkv_recv[heads + head].astype(f32)
        s.dqkv[heads + head] = turn(value, s.table[:, 0:BLK], -s.table[:, BLK:]).astype(bf16)
    kv_part = s.part[...]
    for head in range(heads, 2 * heads):
        kv_part = kv_part + dot_nn(s.dqkv[head], s.weight[head])

    def part_copy(slot, number, to):
        return remote(
            s.part_send.at[slot], s.part_recv.at[number], s.part_ss.at[slot],
            s.part_rs.at[number], to,
        )

    def part_half(slot, number, to, half):
        lines = pl.ds(half * (rows // 2), rows // 2)
        return remote(
            s.part_send.at[slot, lines], s.part_recv.at[number, lines],
            s.part_ss.at[slot + 3 * half], s.part_rs.at[number + 3 * half], to,
        )

    relays = [(part_half(2, 2, X, half), part_half(1, 1, ZH, half)) for half in range(2)]
    part_copies = [part_copy(0, 0, X)]
    s.part_send[2] = kv_part[here(3), :].astype(bf16)
    for half in range(2):
        relays[half][0].start()
    mlp_copies[0].wait_recv()
    s.mlp_send[1] = (s.mlp_near[...] + s.mlp_recv[2].astype(f32)).astype(bf16)
    mlp_copies[2].start()
    s.part_send[0] = kv_part[here(1), :].astype(bf16)
    s.part[here(2), :] = kv_part[here(2), :]
    s.grad_mixed[...] = kv_part[here(0), :]

    scatter_oq.add(C)
    scatter_oq.step(Y)

    norm_sums(range(heads, 2 * heads))
    s.rowsum[0:1, :] = s.norm_sum[0:1, :]
    s.rowsum[1:2, :] = s.norm_sum[1:2, :] * mod(6)
    s.rowsum[6:7, :] = s.norm_sum[1:2, :] * (1.0 + mod(scale_one))
    high = s.rowsum[0:8, :].astype(bf16)
    low = (s.rowsum[0:8, :] - high.astype(f32)).astype(bf16)
    both = jnp.concatenate([high, low], axis=0)
    terms = jnp.zeros((1, BLK), f32)
    for index in range(6):
        found = dot_nn(both, s.ada_full[index * width : (index + 1) * width, :])
        terms = terms + found[index : index + 1, :] + found[8 + index : 9 + index, :]
    s.rowsum[9:10, 0:BLK] = terms
    totals = Total(s.sum_halves, s.sum_inbox, s.sum_first, s.sum_last, s.sum_ss, s.sum_rs)
    s.sum_halves[0] = s.rowsum[0:8, :]
    s.sum_halves[1] = s.rowsum[8:16, :]
    totals.start()

    for head in range(heads):
        s.wide[head * BLK : (head + 1) * BLK, 0:width] = dot_tn(
            s.dqkv[heads + head], s.mixed[...]
        )
    totals.second()
    spread(1, True, 0)
    spread(2, False, 0)
    scatter_kv.step(C)
    for half in range(2):
        lines = slice(half * (rows // 2), (half + 1) * (rows // 2))
        relays[half][0].wait_recv()
        s.part_send[1, lines, :] = (
            s.part[2 * rows + lines.start : 2 * rows + lines.stop, :]
            + s.part_recv[2, lines, :].astype(f32)
        ).astype(bf16)
        relays[half][1].start()
    part_copies[0].start()
    scatter_kv.add(C)
    scatter_kv.step(Y)
    scatter_oq.add(Y)

    def chunk_back(part, half):
        slot = own // 2 * 2 + half
        place_in = 8 * my_rank + slot
        if part < 3:
            number = 32 * part + place_in
            owner, at = number // 3, number % 3
        else:
            owner, at = place_in, 3
        z = own % 2
        index = part * 2 + half
        source = s.blocks_a.at[(part + 1) % 4 // 2, slot, (part + 1) % 2]
        target = s.owned.at[z, at]
        far = remote_to(
            source, target, s.back_ss.at[index], s.back_rs.at[z * 4 + at],
            (owner // 16, owner % 16),
        )
        near = pltpu.make_async_copy(source, target, s.local_sem.at[index])
        return far, near, owner == me

    def chunks_back(parts, act):
        for part in parts:
            for half in range(2):
                far, near, stays = chunk_back(part, half)

                @pl.when(jnp.logical_not(stays))
                def _():
                    far.start() if act else far.wait_send()

                @pl.when(stays)
                def _():
                    near.start() if act else near.wait()

    chunks_back((0, 3), True)
    for copies in (
        kv_far, kv_near, cot_copies, mix_copies, att_copies, ga_copies, mlp_copies,
        token_copies, token_z, token_on, *vec_steps,
    ):
        for copy in copies:
            copy.wait_send()
    for group in (gather_a, gather_er, spread_out, spread_ada, scatter_e, scatter_r):
        group.finish()

    @pl.loop(0, heads)
    def _(head):
        kv_forward(head).wait_send()
        dkv_copy(0, head, C).wait_send()
        dkv_copy(1, head, ZL).wait_send()
        dkv_copy(2, head, C).wait_send()

    totals.third()
    for index in (1, 2):
        mlp_copies[index].wait_recv()
    mlp_branch = s.mlp[...] + s.mlp_recv[0].astype(f32) + s.mlp_recv[1].astype(f32)
    s.result[...] = (s.middle[...] + mod(gate_two) * mlp_branch).astype(bf16)
    normed_one, inverse_one = layer_norm(s.tokens[...].astype(f32))
    scatter_kv.add(Y)
    chunks_back((1, 2), True)
    totals.fourth()
    s.grad_r[0] = s.blocks_r[own_mlp]
    s.grad_e[0] = s.blocks_e[own_mlp]
    for scatter, target in ((scatter_r, s.grad_r), (scatter_e, s.grad_e)):
        scatter.copies[ZH].wait_recv()
        target[1] = scatter.inbox(6, 1)[0]
    part_copies[0].wait_recv()
    for half in range(2):
        relays[half][1].wait_recv()
    grad_mixed_one = (
        s.grad_mixed[...] + s.part_recv[0].astype(f32) + s.part_recv[1].astype(f32)
    )
    s.grad_tokens[...] = s.gmid[...] + norm_back(
        grad_mixed_one * mod(9), normed_one, inverse_one
    )

    sums = totals.result()
    for index in range(6):
        for tile in range(width // BLK):
            s.tiles[index * (width // BLK) + tile] = sums[
                index : index + 1, tile * BLK : (tile + 1) * BLK
            ]
    for tile in range(width // BLK):
        s.gain_tiles[tile] = sums[6:9, tile * BLK : (tile + 1) * BLK]
    s.gain_tiles[width // BLK] = jnp.zeros((3, BLK), f32)
    s.vec_own[...] = jnp.zeros_like(s.vec_own)
    for tile in range(2):
        lanes = slice(tile * BLK, (tile + 1) * BLK)
        s.vec_own[0:1, lanes] = s.tiles[(9 * me) // 8 + tile]
        s.vec_own[9:12, lanes] = s.gain_tiles[(3 * me) // 16 + tile]
    s.sums[0:8, :] = pltpu.roll(s.vec_own[0:8, :], (256 - mod_shift) % 256, 1)
    s.sums[8:16, :] = pltpu.roll(s.vec_own[8:16, :], (256 - gain_shift) % 256, 1)
    s.grad_cond[...] = sums[9:10, 0:BLK]

    chunks_back(range(4), False)
    for at in range(4):
        if at < 3:
            number = 3 * me + at
            part, place_in = number // 32, number % 32
        else:
            part, place_in = 3, me
        slot = place_in % 8
        for z in range(2):
            keeper = flat(member(place_in // 8, slot // 2 * 2 + z))

            @pl.when(keeper != me)
            def _():
                target = s.owned.at[z, at]
                remote(
                    target, target, s.back_ss.at[0], s.back_rs.at[z * 4 + at], C
                ).wait_recv()

    for copies in (part_copies, *relays):
        for copy in copies:
            copy.wait_send()
    for group in (scatter_oq, scatter_kv, totals):
        group.finish()


def finish_kernel(
    result, grad_tokens, grad_cond, sums, grad_e, grad_r, owned, condition,
    result_out, tokens_out, cond_out, ada_out, ada_bias_out, first_out, second_out, project_out,
    output_out, expand_out, expand_bias_out, reduce_out, reduce_bias_out,
):
    width = result.shape[1]
    count = output_out.shape[0]
    piece = ada_out.shape[0]
    result_out[...] = result[...]
    tokens_out[...] = grad_tokens[...]
    cond_out[...] = grad_cond[...]
    first = lax.broadcasted_iota(jnp.int32, (8, piece), 0) == 0
    row = jnp.where(first, sums[0:8, 0:piece], 0.0)
    ada_out[...] = exact(
        row, jnp.broadcast_to(condition[...], (8, condition.shape[1])), ((0,), (0,))
    )
    ada_bias_out[...] = sums[0:1, 0:piece]
    first_out[...] = sums[9:10, 0:count]
    second_out[...] = sums[10:11, 0:count]
    reduce_bias_out[...] = sums[11:12, 0:count]
    both = owned[0].astype(f32) + owned[1].astype(f32)
    project_out[...] = both[0:3]
    output_out[...] = both[3]
    expand = grad_e[0].astype(f32) + grad_e[1].astype(f32)
    expand_out[...] = expand[:, 0:width]
    expand_bias_out[...] = to_row(expand[:, width : width + 1])
    reduce_out[...] = grad_r[0].astype(f32) + grad_r[1].astype(f32)


def rotary_blocks(length):
    half_dim = HEAD_DIM // 2
    frequency = np.exp(
        np.arange(half_dim, dtype=np.float32) * np.float32(-2.0 * math.log(10000.0) / HEAD_DIM)
    ).astype(np.float32)
    angles = (np.arange(length, dtype=np.float32)[:, None] * frequency[None, :]).astype(np.float32)
    cosine, sine = np.cos(angles.astype(np.float64)), np.sin(angles.astype(np.float64))
    one, zero = np.ones((length, HEAD_DIM)), np.zeros((length, HEAD_DIM))
    return np.concatenate([cosine, cosine, one, -sine, sine, zero], axis=1).astype(np.float32)


def on_device_fast(
    tokens, condition, ada_weight, ada_bias, first_gain, second_gain, project_weight,
    output_weight, expand_weight, expand_bias, reduce_weight, reduce_bias, cotangent,
):
    rows, width = tokens.shape
    group = 4 * rows
    heads = width // HEAD_DIM // 4
    per = reduce_weight.shape[0]
    units = 8 * per
    count = output_weight.shape[0]
    piece = ada_weight.shape[1]
    wide = width + BLK
    table = jnp.asarray(rotary_blocks(lax.axis_size("blk") * rows))
    line = condition[None, :]
    inputs = dict(
        tokens=tokens, cotangent=cotangent, condition=line, ada=ada_weight.T,
        ada_bias=ada_bias, first_gain=first_gain[None, :],
        second_gain=second_gain[None, :], reduce_bias=reduce_bias[None, :],
        expand_bias=expand_bias[None, :],
        project_weight=project_weight.T.reshape(3, count, width), output_weight=output_weight,
        expand_weight=expand_weight.T, reduce_weight=reduce_weight, table=table,
    )
    outputs = dict(
        result=((rows, width), bf16), grad_tokens=((rows, width), f32),
        grad_cond=((1, line.shape[1]), f32), sums=((16, 256), f32),
        grad_e=((2, per, wide), bf16), grad_r=((2, per, width), bf16),
        owned=((2, 4, count, width), bf16),
    )
    head_block = (group, BLK)
    kept = {
        name: (inputs[name].shape, inputs[name].dtype)
        for name in (
            "tokens", "condition", "ada", "ada_bias", "first_gain", "second_gain", "reduce_bias",
            "expand_bias", "project_weight",
        )
    }
    scratch = dict(
        **kept,
        table=((group, 2 * BLK), f32), vec_own=((16, 256), f32),
        vecs=((32, 4, 256), f32), mod_row=((1, 6 * width), f32), gain_rows=((3, wide), f32),
        mods=((16, width), f32), chunks=((8, 3, count, width), bf16),
        tok=((4, rows, width), bf16), cot=((4, rows, width), bf16),
        er=((8, per, wide + width), bf16),
        outw=((32, count, width), bf16), adaw=((32, count, width), bf16), ada_full=((6 * width, BLK), bf16), out_full=((width, width), bf16),
        weight=((2 * heads, BLK, width), bf16), mixed=((group, width), bf16),
        query=((heads,) + head_block, bf16), kv=((4, heads) + head_block, bf16),
        state_m=((heads, 1, group), f32), state_l=((heads, 1, group), f32),
        acc=((heads, BLK, group), f32), att=((heads, HEAD_DIM, group), bf16),
        logt=((heads, 1, group), f32), att_send=((4, heads, HEAD_DIM, rows), bf16),
        att_all=((4, heads, HEAD_DIM, rows), bf16), attn=((rows, width), f32),
        middle=((rows, width), f32), normed=((rows, width), f32), inverse=((rows, 1), f32),
        mix=((4, rows, wide), bf16), branch=((group, width), bf16),
        active=((group, units), bf16), grad_hid=((group, units), bf16),
        gm_send=((3, rows, width), bf16), gm_recv=((3, rows, width), bf16),
        mlp_send=((3, rows, width), bf16), mlp_recv=((3, rows, width), bf16),
        grad_mixed=((rows, width), f32), mlp=((rows, width), f32), gmid=((rows, width), f32),
        gattn=((4, rows, width), bf16), dout_send=((4, heads, HEAD_DIM, rows), bf16),
        dout_recv=((4, heads, HEAD_DIM, rows), bf16), rowsum=((16, width), f32),
        wide=((units, wide), f32), blocks_r=((8, per, width), bf16),
        blocks_e=((8, per, wide), bf16), blocks_a=((2, 8, 2, count, width), bf16),
        from_r=((7, per, width), bf16), from_e=((7, per, wide), bf16),
        from_a=((2, 6, 2, count, width), bf16), dout_t=((heads, BLK, group), bf16),
        dout=((heads,) + head_block, bf16), rdots=((heads, 1, group), f32),
        dq=((heads, BLK, group), f32), dkv=((heads,) + head_block, f32),
        dkv_send=((3 * heads,) + head_block, bf16), dkv_recv=((3 * heads,) + head_block, bf16),
        dqkv=((2 * heads,) + head_block, bf16), part=((group, width), f32),
        part_send=((3, rows, width), bf16), part_recv=((3, rows, width), bf16),
        plain=((group, wide), bf16), norm_sum=((8, width), f32),
        sum_halves=((2, 8, width), f32), sum_inbox=((3, 8, width), f32),
        sum_first=((4, 8, width), f32), sum_last=((4, 8, width), f32), tiles=((6 * width // BLK, 1, BLK), f32),
        gain_tiles=((width // BLK + 1, 3, BLK), f32),
        mlp_near=((rows, width), f32),
    )
    semaphores = dict(
        load_sem=16, table_sem=4, local_sem=8, chunk_ss=3, chunk_rs=3, vec_ss=7, vec_rs=7,
        tok_ss=6, tok_rs=6, a_ss=4, a_rs=4, er_ss=6, er_rs=6, o_ss=5, o_rs=5, ada_ss=5, ada_rs=5, cot_ss=4, cot_rs=4,
        kv_ss=3 * heads, kv_rs=3 * heads, att_ss=4, att_rs=4, mix_ss=4, mix_rs=4, gm_ss=4,
        gm_rs=4, mlp_ss=4, mlp_rs=4, dout_ss=4, dout_rs=4, ga_ss=4, ga_rs=4, sr_ss=3, sr_rs=3,
        se_ss=3, se_rs=3, soq_ss=2, soq_rs=2, skv_ss=2, skv_rs=2, dkv_ss=3 * heads,
        dkv_rs=3 * heads, part_ss=6, part_rs=6, back_ss=8, back_rs=8, sum_ss=8, sum_rs=8,
    )
    whole = pl.BlockSpec(memory_space=pltpu.VMEM)
    names = (*(name + "_hbm" for name in inputs), *outputs, *scratch, *semaphores)
    staged = pl.pallas_call(
        partial(block_kernel, names),
        out_shape=tuple(jax.ShapeDtypeStruct(*spec) for spec in outputs.values()),
        in_specs=[pl.BlockSpec(memory_space=pl.ANY)] * len(inputs),
        out_specs=tuple(whole for _ in outputs),
        scratch_shapes=[pltpu.VMEM(*spec) for spec in scratch.values()]
        + [pltpu.SemaphoreType.DMA((number,)) for number in semaphores.values()],
        compiler_params=pltpu.CompilerParams(
            collective_id=1, has_side_effects=True, vmem_limit_bytes=62 * 2**20
        ),
    )(*inputs.values())
    (
        result, grad_tokens, grad_condition, grad_ada, grad_ada_bias, grad_first, grad_second,
        grad_project, grad_output, grad_expand, grad_expand_bias, grad_reduce, grad_reduce_bias,
    ) = pl.pallas_call(
        finish_kernel,
        out_shape=tuple(
            jax.ShapeDtypeStruct(shape, kind)
            for shape, kind in (
                ((rows, width), bf16), ((rows, width), f32), (line.shape, f32),
                ((piece, line.shape[1]), f32), ((1, piece), f32), ((1, count), f32),
                ((1, count), f32), ((3, count, width), f32), ((count, width), f32),
                ((per, width), f32), ((1, per), f32), ((per, width), f32), ((1, count), f32),
            )
        ),
        in_specs=[whole] * 8,
        out_specs=(whole,) * 13,
    )(*staged, line)
    return (
        result,
        grad_tokens,
        grad_condition.reshape(-1),
        grad_ada.T,
        grad_ada_bias.reshape(-1),
        grad_first.reshape(-1),
        grad_second.reshape(-1),
        grad_project.reshape(3 * count, width).T,
        grad_output,
        grad_expand.T,
        grad_expand_bias.reshape(-1),
        grad_reduce,
        grad_reduce_bias.reshape(-1),
    )


def solution(mesh):
    return jax.shard_map(
        on_device_fast if mesh.shape["ulysses"] * mesh.shape["blk"] == 32 else on_device,
        mesh=mesh,
        in_specs=(
            P(BOTH, None),
            P(),
            P(None, BOTH),
            P(BOTH),
            P(BOTH),
            P(BOTH),
            P(None, BOTH),
            P(BOTH, None),
            P(None, BOTH),
            P(BOTH),
            P(BOTH, None),
            P(BOTH),
            P(BOTH, None),
        ),
        out_specs=(
            P(BOTH, None),
            P(BOTH, None),
            P(),
            P(None, BOTH),
            P(BOTH),
            P(BOTH),
            P(BOTH),
            P(None, BOTH),
            P(BOTH, None),
            P(None, BOTH),
            P(BOTH),
            P(BOTH, None),
            P(BOTH),
        ),
        check_vma=False,
    )
```
